32 devices in a mesh: dp: 8 (over y, x, core), rep: 4 (over z).
Axes of the slice: x: 2, y: 2, z: 4, core: 2. Of those that a mesh axis runs over, the one named last changes fastest.
Arguments:
- inputs: bfloat16 [32, 1044, 512], P(('dp', 'rep')), may hold values from -6 to 6
- segments: int32 [32, 1024], P(('dp', 'rep')), may hold values from 0 to 3, never falling along the last dimension, each value on 1 to 512 neighbouring positions
- cotangent: bfloat16 [32, 1044, 512], P(('dp', 'rep')), may hold values from -6 to 6
- attend_in: float32 [512, 1536], P(('dp', 'rep'))
- attend_out: float32 [512, 512], P(('dp', 'rep'))
- expand: float32 [512, 2048], P(('dp', 'rep'))
- contract: float32 [2048, 512], P(('dp', 'rep'))
- layer_norms: float32 [4, 512], P(None, ('dp', 'rep'))
- moment_in: float32 [512, 1536], P(('dp', 'rep')), may hold values from -512 to 512
- moment_out: float32 [512, 512], P(('dp', 'rep')), may hold values from -112 to 112
- moment_expand: float32 [512, 2048], P(('dp', 'rep')), may hold values from -320 to 320
- moment_contract: float32 [2048, 512], P(('dp', 'rep')), may hold values from -640 to 640
- moment_norms: float32 [4, 512], P(None, ('dp', 'rep')), may hold values from -1024 to 1024
- square_in: float32 [512, 1536], P(('dp', 'rep')), may hold values from 8352 to 33408
- square_out: float32 [512, 512], P(('dp', 'rep')), may hold values from 334 to 1336
- square_expand: float32 [512, 2048], P(('dp', 'rep')), may hold values from 3037 to 12148
- square_contract: float32 [2048, 512], P(('dp', 'rep')), may hold values from 12026 to 48107
- square_norms: float32 [4, 512], P(None, ('dp', 'rep')), may hold values from 33408 to 133632
Outputs:
- outputs: bfloat16 [32, 1044, 512], P(('dp', 'rep'))
- input_gradient: bfloat16 [32, 1044, 512], P(('dp', 'rep'))
- updated_in: float32 [512, 1536], P(('dp', 'rep'))
- updated_out: float32 [512, 512], P(('dp', 'rep'))
- updated_expand: float32 [512, 2048], P(('dp', 'rep'))
- updated_contract: float32 [2048, 512], P(('dp', 'rep'))
- updated_norms: float32 [4, 512], P(None, ('dp', 'rep'))
- momentum_in: float32 [512, 1536], P(('dp', 'rep'))
- momentum_out: float32 [512, 512], P(('dp', 'rep'))
- momentum_expand: float32 [512, 2048], P(('dp', 'rep'))
- momentum_contract: float32 [2048, 512], P(('dp', 'rep'))
- momentum_norms: float32 [4, 512], P(None, ('dp', 'rep'))
- variance_in: float32 [512, 1536], P(('dp', 'rep'))
- variance_out: float32 [512, 512], P(('dp', 'rep'))
- variance_expand: float32 [512, 2048], P(('dp', 'rep'))
- variance_contract: float32 [2048, 512], P(('dp', 'rep'))
- variance_norms: float32 [4, 512], P(None, ('dp', 'rep'))
- trust_table: float32 [3, 5], replicated
The draws below stay inside these ranges and needn't reach their ends.
Inputs may be any that keep to these rules, and one draw needn't show every extreme that they name: `segments`: along a row the ids never fall; every id occurs, a segment holds at most 512 positions and in every row one holds exactly that many.
All inputs are finite; a program needn't handle non-finite values.
Results may differ from the reference program's by a relative error of at most 0.019.
The reference program's roundings to bfloat16 on the way count: a program that leaves them out, or rounds other values in their place, can miss the bound.
Values may be sent and summed in bfloat16 or wider, within the bound.
No kernel may reach another device: no remote copies, remote signals or barrier semaphores. Data moves between devices by JAX's collectives and lax.ppermute only.
A program may use at most 128 MiB of HBM per device.

```python
import math
import jax
import jax.numpy as jnp
import numpy as np
from jax import lax

D = 512
HEADS = 8
HEAD_DIM = 64
FF = 2048
SEQ = 1024
SEGS = 4
ROWS = 1044
SEQS = 32
ROWS_ALL = 33408


def ramp_scale(count):
    index = jnp.arange(count, dtype=jnp.float32)
    return jnp.exp(math.log(3.0) * (index / max(count - 1, 1) - 0.5))


def matrix_draw(key, rows, cols, fan_in):
    base = jax.random.truncated_normal(key, -4.0, 4.0, (rows, cols), jnp.float32)
    return base * fan_in ** (-0.5) * ramp_scale(rows)[:, None]


def draw_attend_in(key, part):
    return matrix_draw(key, D, 3 * D, D)


def draw_attend_out(key, part):
    return matrix_draw(key, D, D, D // 32)


def draw_expand(key, part):
    return matrix_draw(key, D, FF, D)


def draw_contract(key, part):
    return matrix_draw(key, FF, D, FF)


def draw_layer_norms(key, part):
    base = jax.random.truncated_normal(key, -4.0, 4.0, (4, D), jnp.float32)
    offset = jnp.array([[1.0], [0.0], [1.0], [0.0]], jnp.float32)
    spread = jnp.array([[0.15], [0.2], [0.15], [0.2]], jnp.float32)
    return (offset + spread * base) * ramp_scale(D)[None, :]


def block_levels(own_key, dims, split, smallest, top_value):
    level = 1.0
    for axis_at, blocks in split:
        steps = jax.random.uniform(jax.random.fold_in(jax.random.fold_in(own_key, 6), axis_at), (blocks,), jnp.float32, smallest / len(split), top_value / len(split))
        level = level * jnp.repeat(jnp.exp(steps), dims[axis_at] // blocks).reshape((-1,) + (1,) * (len(dims) - 1 - axis_at))
    return level


def length_profile(count, total, reach, lean):
    loads = [(1 << 20) // math.isqrt(standing ** lean) + 1 for standing in range(2, count + 1)]
    rest, holding = total - reach - (count - 1), [1] * (count - 1)
    while rest > 0:
        free = [i for i in range(count - 1) if holding[i] < reach]
        whole, remaining = sum([loads[i] for i in free]), rest
        for i in free:
            addition = min(reach - holding[i], max(1, remaining * loads[i] // whole), rest)
            holding[i] = holding[i] + addition
            rest = rest - addition
    return np.array([reach] + holding)


def ragged(key, count, total, most, slope):
    if count == 2:
        one = jax.random.randint(key, (), max(1, total - most), min(most, total - 1) + 1)
        return jnp.stack([one, total - one])
    tallies = jnp.asarray(length_profile(count, total, most, slope), jnp.int32)
    pairs = (count - 1) // 2
    source_of, taker = tallies[1:1 + 2 * pairs:2], tallies[2:2 + 2 * pairs:2]
    room = jnp.minimum(source_of - 1, most - taker)
    shifted = jax.random.randint(jax.random.fold_in(key, 1), (pairs,), 0, 1 << 20) % (room + 1)
    tallies = tallies.at[1:1 + 2 * pairs:2].set(source_of - shifted).at[2:2 + 2 * pairs:2].set(taker + shifted)
    return tallies[jax.random.permutation(jax.random.fold_in(key, 2), count)]


def scatter_about(key, shape, scale, reach, cuts=(), kind=jnp.bfloat16):
    values = jax.random.normal(key, shape, jnp.float32) * scale
    if len(cuts) > 0:
        values = block_levels(key, shape, cuts, -0.22, 0.18) * values
    return jnp.clip(values, min=-reach, max=reach).astype(kind)


def setup_inputs(seed: int = 0) -> dict:
    arg_keys = jax.random.split(jax.random.key(seed), 19)
    inputs = scatter_about(arg_keys[0], (SEQS, ROWS, D), 1.0, 6.0, ((0, 32),))
    segments = jax.vmap(lambda own: jnp.searchsorted(jnp.cumsum(ragged(own, SEGS, SEQ, SEQ // 2, 1)), jnp.arange(SEQ), side="right"))(jax.random.split(arg_keys[1], SEQS)).reshape((SEQS, SEQ)).astype(jnp.int32)
    cotangent = scatter_about(arg_keys[2], (SEQS, ROWS, D), 1.0, 6.0, ((0, 32),))
    attend_in = draw_attend_in(jax.random.fold_in(arg_keys[18], 71), 0)
    attend_out = draw_attend_out(jax.random.fold_in(arg_keys[18], 71), 0)
    expand = draw_expand(jax.random.fold_in(arg_keys[18], 71), 0)
    contract = draw_contract(jax.random.fold_in(arg_keys[18], 71), 0)
    layer_norms = draw_layer_norms(jax.random.fold_in(arg_keys[18], 71), 0)
    moment_in = scatter_about(arg_keys[8], (D, 3 * D), ((ROWS_ALL // 4) ** 0.5), 512.0, ((0, 32),), jnp.float32)
    moment_out = scatter_about(arg_keys[9], (D, D), ((ROWS_ALL // 100) ** 0.5), 112.0, ((0, 32),), jnp.float32)
    moment_expand = scatter_about(arg_keys[10], (D, FF), ((ROWS_ALL // 11) ** 0.5), 320.0, ((0, 32),), jnp.float32)
    moment_contract = scatter_about(arg_keys[11], (FF, D), ((ROWS_ALL * 9 // 25) ** 0.5), 640.0, ((0, 32),), jnp.float32)
    moment_norms = scatter_about(arg_keys[12], (4, D), (ROWS_ALL ** 0.5), 1024.0, ((1, 32),), jnp.float32)
    square_in = jnp.clip(jnp.exp(math.log(33408.0) - 1.3862944 * jax.random.uniform(arg_keys[13], (D, 3 * D), jnp.float32) ** block_levels(arg_keys[13], (D, 3 * D), ((0, 32),), -0.2, 0.2)), 8352.0, 33408.0)
    square_out = jnp.clip(jnp.exp(math.log(1336.0) - 1.3862944 * jax.random.uniform(arg_keys[14], (D, D), jnp.float32) ** block_levels(arg_keys[14], (D, D), ((0, 32),), -0.2, 0.2)), 334.0, 1336.0)
    square_expand = jnp.clip(jnp.exp(math.log(12148.0) - 1.3862944 * jax.random.uniform(arg_keys[15], (D, FF), jnp.float32) ** block_levels(arg_keys[15], (D, FF), ((0, 32),), -0.2, 0.2)), 3037.0, 12148.0)
    square_contract = jnp.clip(jnp.exp(math.log(48107.0) - 1.3863567 * jax.random.uniform(arg_keys[16], (FF, D), jnp.float32) ** block_levels(arg_keys[16], (FF, D), ((0, 32),), -0.2, 0.2)), 12026.0, 48107.0)
    square_norms = jnp.clip(jnp.exp(math.log(133632.0) - 1.3862944 * jax.random.uniform(arg_keys[17], (4, D), jnp.float32) ** block_levels(arg_keys[17], (4, D), ((1, 32),), -0.2, 0.2)), 33408.0, 133632.0)
    return {"inputs": inputs, "segments": segments, "cotangent": cotangent, "attend_in": attend_in, "attend_out": attend_out, "expand": expand, "contract": contract, "layer_norms": layer_norms, "moment_in": moment_in, "moment_out": moment_out, "moment_expand": moment_expand, "moment_contract": moment_contract, "moment_norms": moment_norms, "square_in": square_in, "square_out": square_out, "square_expand": square_expand, "square_contract": square_contract, "square_norms": square_norms}


EPSILON = 1e-05
ADAM_EPSILON = 1e-06
DECAY = 0.01
RATE = 0.5
BETA = 0.5
NEGATIVE = -1e+30
HIGH = lax.Precision.HIGHEST

@jax.custom_vjp
def low(v):
    return lax.optimization_barrier(v.astype(jnp.bfloat16)).astype(jnp.float32)

@jax.custom_vjp
def low_back(v):
    return v

def low_keep(v):
    return (low(v), None)

def low_pass(kept, grad):
    return (grad,)

def back_keep(v):
    return (v, None)

def back_low(kept, grad):
    return (low(grad),)
low.defvjp(low_keep, low_pass)
low_back.defvjp(back_keep, back_low)

def layer_norm(values, gain, bias):
    center = values - lax.optimization_barrier(jnp.mean(values, axis=-1, keepdims=True))
    scale = lax.rsqrt(lax.optimization_barrier(jnp.mean(center * center, axis=-1, keepdims=True)) + EPSILON)
    return center * scale * gain + bias

def allowed_mask(segment_row, rows):
    memory = rows - segment_row.shape[0]
    labels = jnp.concatenate([jnp.full((memory,), -1, jnp.int32), segment_row.astype(jnp.int32)])
    return (labels[:, None] == labels[None, :]) | (labels[:, None] < 0) | (labels[None, :] < 0)

def sequence_forward(weights, values, segment_row):
    attend_in, attend_out, expand, contract, norms = weights
    rows = values.shape[0]
    allowed = allowed_mask(segment_row, rows)
    first = low(layer_norm(values, norms[0], norms[1]))
    packed = low(low_back(jnp.dot(first, attend_in, precision=HIGH)))
    parts = packed.reshape(rows, 3, HEADS, HEAD_DIM)
    queries = parts[:, 0]
    keys = parts[:, 1]
    head_values = parts[:, 2]
    scores = jnp.einsum('qhd,khd->hqk', queries, keys, precision=HIGH) / math.sqrt(HEAD_DIM)
    scores = jnp.where(allowed[None], low_back(scores), NEGATIVE)
    highest = lax.optimization_barrier(jnp.max(scores, axis=-1, keepdims=True))
    raised = jnp.exp(scores - highest)
    attention = low(raised / lax.optimization_barrier(jnp.sum(raised, axis=-1, keepdims=True)))
    mixed = jnp.einsum('hqk,khd->qhd', attention, head_values, precision=HIGH).reshape(rows, -1)
    mixed = low(low_back(mixed))
    middle = values + low_back(jnp.dot(mixed, attend_out, precision=HIGH))
    second = low(layer_norm(middle, norms[2], norms[3]))
    hidden = low_back(jnp.dot(second, expand, precision=HIGH))
    active = low(jax.nn.gelu(hidden, approximate=True))
    return middle + low_back(jnp.dot(active, contract, precision=HIGH))

def reference(inputs, segments, cotangent, attend_in, attend_out, expand, contract, layer_norms, moment_in, moment_out, moment_expand, moment_contract, moment_norms, square_in, square_out, square_expand, square_contract, square_norms):
    masters = (attend_in, attend_out, expand, contract, layer_norms)

    def forward_all(weights, start):
        lowered = tuple((low(weight) for weight in weights))

        def one_sequence(items):
            return sequence_forward(lowered, items[0], items[1])
        return lax.map(jax.checkpoint(one_sequence), (start, segments))
    start = inputs.astype(jnp.float32)
    result, pull = jax.vjp(forward_all, masters, start)
    grads, grad_input = pull(cotangent.astype(jnp.float32))
    firsts = (moment_in, moment_out, moment_expand, moment_contract, moment_norms)
    seconds = (square_in, square_out, square_expand, square_contract, square_norms)
    updated = []
    momenta = []
    variances = []
    weight_norms = []
    update_norms = []
    ratios = []
    for weight, gradient, first, second in zip(masters, grads, firsts, seconds):
        momentum = BETA * first + (1.0 - BETA) * gradient
        variance = BETA * second + (1.0 - BETA) * gradient * gradient
        direction = momentum / (jnp.sqrt(variance) + ADAM_EPSILON) + DECAY * weight
        weight_norm = jnp.sqrt(jnp.sum(weight * weight))
        update_norm = jnp.sqrt(jnp.sum(direction * direction))
        ratio = weight_norm / update_norm
        updated.append(weight - RATE * ratio * direction)
        momenta.append(momentum)
        variances.append(variance)
        weight_norms.append(weight_norm)
        update_norms.append(update_norm)
        ratios.append(ratio)
    trust_table = jnp.stack([jnp.stack(weight_norms), jnp.stack(update_norms), jnp.stack(ratios)])
    return (result.astype(jnp.bfloat16), grad_input.astype(jnp.bfloat16), updated[0], updated[1], updated[2], updated[3], updated[4], momenta[0], momenta[1], momenta[2], momenta[3], momenta[4], variances[0], variances[1], variances[2], variances[3], variances[4], trust_table)
```

```python
from functools import partial
import math

import jax
import jax.numpy as jnp
from jax import lax
from jax.sharding import PartitionSpec as P

HEADS = 8
HEAD_DIM = 64


EPSILON = 1e-05
ADAM_EPSILON = 1e-06
DECAY = 0.01
RATE = 0.5
BETA = 0.5
NEGATIVE = -1e30


def layer_norm(values, gain, bias):
    center = values - jnp.mean(values, axis=-1, keepdims=True)
    scale = lax.rsqrt(jnp.mean(center * center, axis=-1, keepdims=True) + EPSILON)
    normed = center * scale
    return (normed * gain + bias, normed, scale)


def norm_backward(grad_out, normed, scale, gain):
    scaled = grad_out * gain
    grad_in = scale * (
        scaled
        - jnp.mean(scaled, axis=-1, keepdims=True)
        - normed * jnp.mean(scaled * normed, axis=-1, keepdims=True)
    )
    return (grad_in, jnp.sum(grad_out * normed, axis=0), jnp.sum(grad_out, axis=0))


def allowed_mask(segment_row, rows):
    memory = rows - segment_row.shape[0]
    labels = jnp.concatenate([jnp.full((memory,), -1, jnp.int32), segment_row])
    return (labels[:, None] == labels[None, :]) | (labels[:, None] < 0) | (labels[None, :] < 0)


def head_scores(queries, keys, allowed):
    scores = jnp.einsum("qd,kd->qk", queries, keys, preferred_element_type=jnp.float32)
    return jnp.where(allowed, scores * (1.0 / math.sqrt(HEAD_DIM)), NEGATIVE)


def forward_sequence(weights, values_in, segment_row):
    attend_in, attend_out, expand, contract, norms = weights
    gains = norms.astype(jnp.float32)
    rows = values_in.shape[0]
    allowed = allowed_mask(segment_row, rows)
    start = values_in.astype(jnp.float32)
    first_norm, normed_one, scale_one = layer_norm(start, gains[0], gains[1])
    first_low = first_norm.astype(jnp.bfloat16)
    packed = jnp.dot(first_low, attend_in, preferred_element_type=jnp.float32).astype(jnp.bfloat16)
    parts = packed.reshape(rows, 3, HEADS, HEAD_DIM).transpose(1, 2, 0, 3)

    def one_head(triple):
        queries, keys, values = triple
        scores = head_scores(queries, keys, allowed)
        highest = jnp.max(scores, axis=-1, keepdims=True)
        raised = jnp.exp(scores - highest)
        total = jnp.sum(raised, axis=-1, keepdims=True)
        attention = (raised / total).astype(jnp.bfloat16)
        return (
            jnp.dot(attention, values, preferred_element_type=jnp.float32),
            highest + jnp.log(total),
        )

    mixed_heads, log_totals = lax.map(one_head, (parts[0], parts[1], parts[2]))
    mixed = mixed_heads.transpose(1, 0, 2).reshape(rows, -1).astype(jnp.bfloat16)
    middle = start + jnp.dot(mixed, attend_out, preferred_element_type=jnp.float32)
    second_norm, normed_two, scale_two = layer_norm(middle, gains[2], gains[3])
    second_low = second_norm.astype(jnp.bfloat16)
    hidden = jnp.dot(second_low, expand, preferred_element_type=jnp.float32)
    active = jax.nn.gelu(hidden, approximate=True).astype(jnp.bfloat16)
    result = middle + jnp.dot(active, contract, preferred_element_type=jnp.float32)
    saved = (
        allowed,
        gains,
        normed_one,
        scale_one,
        first_low,
        parts,
        log_totals,
        mixed,
        normed_two,
        scale_two,
        second_low,
        hidden,
        active,
    )
    return (result, saved)


def backward_sequence(weights, values_in, segment_row, cotangent):
    attend_in, attend_out, expand, contract, norms = weights
    result, saved = forward_sequence(weights, values_in, segment_row)
    (
        allowed,
        gains,
        normed_one,
        scale_one,
        first_low,
        parts,
        log_totals,
        mixed,
        normed_two,
        scale_two,
        second_low,
        hidden,
        active,
    ) = saved
    rows = values_in.shape[0]
    grad_out = cotangent.astype(jnp.float32)
    grad_low = grad_out.astype(jnp.bfloat16)
    grad_contract = jnp.einsum("rf,rd->fd", active, grad_low, preferred_element_type=jnp.float32)
    grad_active = jnp.einsum("rd,fd->rf", grad_low, contract, preferred_element_type=jnp.float32)
    gelu_value, gelu_back = jax.vjp(partial(jax.nn.gelu, approximate=True), hidden)
    grad_hidden = gelu_back(grad_active)[0].astype(jnp.bfloat16)
    grad_expand = jnp.einsum(
        "rd,rf->df", second_low, grad_hidden, preferred_element_type=jnp.float32
    )
    grad_second = jnp.einsum("rf,df->rd", grad_hidden, expand, preferred_element_type=jnp.float32)
    back_two, gain_two, bias_two = norm_backward(grad_second, normed_two, scale_two, gains[2])
    grad_middle = grad_out + back_two
    middle_low = grad_middle.astype(jnp.bfloat16)
    grad_attend_out = jnp.einsum("rd,re->de", mixed, middle_low, preferred_element_type=jnp.float32)
    grad_mixed = jnp.einsum(
        "re,de->rd", middle_low, attend_out, preferred_element_type=jnp.float32
    ).astype(jnp.bfloat16)
    upstream_heads = grad_mixed.reshape(rows, HEADS, HEAD_DIM).transpose(1, 0, 2)
    factor = 1.0 / math.sqrt(HEAD_DIM)

    def head_back(items):
        queries, keys, values, upstream, log_total = items
        scores = head_scores(queries, keys, allowed)
        attention = jnp.exp(scores - log_total)
        grad_attention = jnp.einsum(
            "qd,kd->qk", upstream, values, preferred_element_type=jnp.float32
        )
        inner = jnp.sum(attention * grad_attention, axis=-1, keepdims=True)
        grad_scores = (attention * (grad_attention - inner)).astype(jnp.bfloat16)
        grad_queries = jnp.dot(grad_scores, keys, preferred_element_type=jnp.float32) * factor
        grad_keys = (
            jnp.einsum("qk,qd->kd", grad_scores, queries, preferred_element_type=jnp.float32)
            * factor
        )
        grad_values = jnp.einsum(
            "qk,qd->kd",
            attention.astype(jnp.bfloat16),
            upstream,
            preferred_element_type=jnp.float32,
        )
        return jnp.stack([grad_queries, grad_keys, grad_values])

    head_grads = lax.map(head_back, (parts[0], parts[1], parts[2], upstream_heads, log_totals))
    grad_packed = head_grads.transpose(2, 1, 0, 3).reshape(rows, -1).astype(jnp.bfloat16)
    grad_attend_in = jnp.einsum(
        "rd,re->de", first_low, grad_packed, preferred_element_type=jnp.float32
    )
    grad_first = jnp.einsum("re,de->rd", grad_packed, attend_in, preferred_element_type=jnp.float32)
    back_one, gain_one, bias_one = norm_backward(grad_first, normed_one, scale_one, gains[0])
    grad_input = (grad_middle + back_one).astype(jnp.bfloat16)
    grad_norms = jnp.stack([gain_one, bias_one, gain_two, bias_two])
    return (result, grad_input, (grad_attend_in, grad_attend_out, grad_expand, grad_contract, grad_norms))


AXES = ("dp", "rep")


class Layout:
    def __init__(self, mesh):
        self.dp = mesh.shape["dp"]
        self.rep = mesh.shape["rep"]
        self.plane = self.dp // 2

    def permute(self, value, move):
        pairs = []
        for p in range(self.plane):
            for c in range(2):
                for z in range(self.rep):
                    q, d, w = move(p, c, z)
                    pairs.append(((p * 2 + c) * self.rep + z, (q * 2 + d) * self.rep + w))
        return lax.ppermute(value, AXES, pairs)

    def to_core(self, value):
        return self.permute(value, lambda p, c, z: (p, 1 - c, z))

    def to_plane(self, value, m):
        return self.permute(value, lambda p, c, z: (p ^ m, c, z))

    def to_rep(self, value, k):
        return self.permute(value, lambda p, c, z: (p, c, (z + k) % self.rep))

    def place(self):
        dp = lax.axis_index("dp")
        return dp // 2, dp % 2, lax.axis_index("rep")


def pick(value, index, axis):
    return lax.dynamic_index_in_dim(value, index, axis, keepdims=False)


def gather_rows(lay, shard):
    rows, cols = shard.shape
    p, c, z = lay.place()
    column = jnp.zeros((lay.rep, rows, cols), shard.dtype)
    column = lax.dynamic_update_index_in_dim(column, shard, z, 0)
    for k in range(1, lay.rep):
        column = lax.dynamic_update_index_in_dim(column, lay.to_rep(shard, k), (z - k) % lay.rep, 0)
    column = column.reshape(lay.rep * rows, cols)
    plane = jnp.zeros((lay.plane, lay.rep * rows, cols), shard.dtype)
    plane = lax.dynamic_update_index_in_dim(plane, column, p, 0)
    for m in range(1, lay.plane):
        plane = lax.dynamic_update_index_in_dim(plane, lay.to_plane(column, m), p ^ m, 0)
    other = lay.to_core(plane)
    first = jnp.where(c == 0, plane, other)
    second = jnp.where(c == 0, other, plane)
    return jnp.stack([first, second], axis=1).reshape(-1, cols)


def scatter_rows(lay, total):
    cols = total.shape[1]
    p, c, z = lay.place()
    split = total.reshape(lay.plane, 2, -1, cols)
    sent = lay.to_core(pick(split, 1 - c, 1).astype(jnp.bfloat16))
    chip = pick(split, c, 1) + sent.astype(jnp.float32)
    low = chip.astype(jnp.bfloat16)
    column = pick(chip, p, 0)
    for m in range(1, lay.plane):
        column = column + lay.to_plane(pick(low, p ^ m, 0), m).astype(jnp.float32)
    column = column.reshape(lay.rep, -1, cols)
    low = column.astype(jnp.bfloat16)
    own = pick(column, z, 0)
    for k in range(1, lay.rep):
        own = own + lay.to_rep(pick(low, (z + k) % lay.rep, 0), k).astype(jnp.float32)
    return own


def sum_all(lay, row):
    count = lay.dp * lay.rep
    spread = jnp.broadcast_to(row[None, None, :], (count, 1, row.shape[0]))
    return jnp.sum(lax.all_to_all(spread, AXES, 0, 0), axis=(0, 1))


def body(
    lay,
    inputs,
    segments,
    cotangent,
    attend_in,
    attend_out,
    expand,
    contract,
    layer_norms,
    moment_in,
    moment_out,
    moment_expand,
    moment_contract,
    moment_norms,
    square_in,
    square_out,
    square_expand,
    square_contract,
    square_norms,
):
    masters = (attend_in, attend_out, expand, contract, layer_norms)
    local_weight_sums = jnp.stack([jnp.sum(weight * weight) for weight in masters])
    lowered = [weight.astype(jnp.bfloat16) for weight in masters]
    norm_rows = jnp.pad(lowered[4].T, ((0, 0), (0, 124)))
    first = gather_rows(lay, jnp.concatenate([lowered[0], norm_rows], axis=1))
    second = gather_rows(lay, jnp.concatenate([lowered[1], lowered[2]], axis=1))
    third = gather_rows(lay, lowered[3])
    width = attend_in.shape[1]
    gathered = (
        first[:, :width],
        second[:, : attend_out.shape[1]],
        second[:, attend_out.shape[1] :],
        third,
        first[:, width : width + 4].T,
    )
    outputs, input_gradient, summed = backward_sequence(gathered, inputs[0], segments[0], cotangent[0])
    outputs = outputs.astype(jnp.bfloat16)[None]
    input_gradient = input_gradient[None]
    last = scatter_rows(lay, jnp.concatenate([summed[0], jnp.pad(summed[4].T, ((0, 0), (0, 124)))], axis=1))
    middle = scatter_rows(lay, jnp.concatenate([summed[1], summed[2]], axis=1))
    reduced = (
        last[:, :width],
        middle[:, : attend_out.shape[1]],
        middle[:, attend_out.shape[1] :],
        scatter_rows(lay, summed[3]),
        last[:, width : width + 4].T,
    )
    firsts = (moment_in, moment_out, moment_expand, moment_contract, moment_norms)
    seconds = (square_in, square_out, square_expand, square_contract, square_norms)
    momenta = []
    variances = []
    directions = []
    for weight, gradient, first, second in zip(masters, reduced, firsts, seconds):
        momentum = BETA * first + (1.0 - BETA) * gradient
        variance = BETA * second + (1.0 - BETA) * gradient * gradient
        momenta.append(momentum)
        variances.append(variance)
        directions.append(momentum / (jnp.sqrt(variance) + ADAM_EPSILON) + DECAY * weight)
    local_update_sums = jnp.stack([jnp.sum(direction * direction) for direction in directions])
    sums = sum_all(lay, jnp.pad(jnp.concatenate([local_weight_sums, local_update_sums]), (0, 118)))
    weight_sums, update_sums = sums[:5], sums[5:10]
    weight_norms = jnp.sqrt(weight_sums)
    update_norms = jnp.sqrt(update_sums)
    ratios = weight_norms / update_norms
    updated = [
        weight - RATE * ratios[index] * direction
        for index, (weight, direction) in enumerate(zip(masters, directions))
    ]
    trust_table = jnp.stack([weight_norms, update_norms, ratios])
    return (
        outputs,
        input_gradient,
        updated[0],
        updated[1],
        updated[2],
        updated[3],
        updated[4],
        momenta[0],
        momenta[1],
        momenta[2],
        momenta[3],
        momenta[4],
        variances[0],
        variances[1],
        variances[2],
        variances[3],
        variances[4],
        trust_table,
    )


def solution(mesh):
    placed = (
        P(("dp", "rep"), None, None),
        P(("dp", "rep"), None),
        P(("dp", "rep"), None, None),
        P(("dp", "rep"), None),
        P(("dp", "rep"), None),
        P(("dp", "rep"), None),
        P(("dp", "rep"), None),
        P(None, ("dp", "rep")),
        P(("dp", "rep"), None),
        P(("dp", "rep"), None),
        P(("dp", "rep"), None),
        P(("dp", "rep"), None),
        P(None, ("dp", "rep")),
        P(("dp", "rep"), None),
        P(("dp", "rep"), None),
        P(("dp", "rep"), None),
        P(("dp", "rep"), None),
        P(None, ("dp", "rep")),
    )
    return jax.shard_map(
        partial(body, Layout(mesh)),
        mesh=mesh,
        in_specs=placed,
        out_specs=(
            P(("dp", "rep"), None, None),
            P(("dp", "rep"), None, None),
            P(("dp", "rep"), None),
            P(("dp", "rep"), None),
            P(("dp", "rep"), None),
            P(("dp", "rep"), None),
            P(None, ("dp", "rep")),
            P(("dp", "rep"), None),
            P(("dp", "rep"), None),
            P(("dp", "rep"), None),
            P(("dp", "rep"), None),
            P(None, ("dp", "rep")),
            P(("dp", "rep"), None),
            P(("dp", "rep"), None),
            P(("dp", "rep"), None),
            P(("dp", "rep"), None),
            P(None, ("dp", "rep")),
            P(),
        ),
        check_vma=False,
    )
```

```python
from functools import partial
import math

import jax
import jax.numpy as jnp
from jax import lax
from jax.experimental import pallas as pl
from jax.experimental.pallas import tpu as pltpu
from jax.sharding import PartitionSpec as P

HEADS = 8
HEAD_DIM = 64


EPSILON = 1e-05
ADAM_EPSILON = 1e-06
DECAY = 0.01
RATE = 0.5
BETA = 0.5
PAD = 12
LANES = 128
HALF = 64
BIG = 1e30
FEATS = 4
TILE = 256
THIN = 32
VMEM = pltpu.MemorySpace.VMEM


def params():
    return pltpu.CompilerParams(vmem_limit_bytes=62 * 1024 * 1024)


def dot(a, b, ca, cb):
    return lax.dot_general(a, b, (((ca,), (cb,)), ((), ())), preferred_element_type=jnp.float32)


def normalize(values):
    center = values - jnp.mean(values, axis=-1, keepdims=True)
    scale = lax.rsqrt(jnp.mean(center * center, axis=-1, keepdims=True) + EPSILON)
    return center * scale, scale


def core_index():
    return lax.rem(lax.axis_index("dp"), 2)


def assemble(own_ref, other_ref, full_ref):
    plane, rows, _ = own_ref.shape
    core = core_index()
    for p in range(plane):
        at = pl.multiple_of((2 * p + core) * rows, rows)
        full_ref[pl.ds(at, rows), :] = own_ref[p]
        at = pl.multiple_of((2 * p + 1 - core) * rows, rows)
        full_ref[pl.ds(at, rows), :] = other_ref[p]


def split_rows(full_ref, keep_ref, send_ref, lanes):
    plane, rows, _ = keep_ref.shape
    core = core_index()
    for p in range(plane):
        at = pl.multiple_of((2 * p + core) * rows, rows)
        keep_ref[p, :, lanes] = full_ref[pl.ds(at, rows), :]
        at = pl.multiple_of((2 * p + 1 - core) * rows, rows)
        send_ref[p, :, lanes] = full_ref[pl.ds(at, rows), :].astype(jnp.bfloat16)


def row_chunks(rows, size):
    return [(at, min(size, rows - at)) for at in range(0, rows, size)]


def attend_kernel(x, labels, own, other, qx, kx, vx, mixed, gains, weight, qs, ext):
    rows = x.shape[0]
    width = mixed.shape[1]
    assemble(own, other, weight)
    gains[...] = jnp.transpose(weight[:, 3 * width :].astype(jnp.float32))[:8]
    gain, bias = gains[0:1], gains[1:2]
    for at, size in row_chunks(rows, 352):
        span = pl.ds(at, size)
        normed, _ = normalize(x[span].astype(jnp.float32))
        first = (normed * gain + bias).astype(jnp.bfloat16)
        lane = lax.broadcasted_iota(jnp.int32, (size, LANES), 1)
        low = lane < HALF
        feature = lane % HALF
        label = jnp.broadcast_to(labels[span], (size, LANES))
        blocked = ((feature < FEATS) & (label >= 0) & (feature != label)) | (feature == FEATS)
        query_side = jnp.where(blocked, -BIG, 0.0)
        marked = ((feature < FEATS) & (feature == label)) | ((feature == FEATS) & (label == -2))
        key_side = jnp.where(marked | (feature > FEATS), 1.0, 0.0)
        for pair in range(width // LANES):
            columns = slice(pair * LANES, (pair + 1) * LANES)
            for kind, (target, side) in enumerate(((qs, query_side), (kx, key_side), (vx, jnp.ones_like(key_side)))):
                part = dot(first, weight[:, kind * width + pair * LANES : kind * width + (pair + 1) * LANES], 1, 0)
                part = part.astype(jnp.bfloat16).astype(jnp.float32)
                if kind == 0:
                    part = part * (1.0 / math.sqrt(HEAD_DIM))
                target[span, 2 * pair * LANES : (2 * pair + 1) * LANES] = jnp.where(low, part, side).astype(jnp.bfloat16)
                target[span, (2 * pair + 1) * LANES : (2 * pair + 2) * LANES] = jnp.where(low, side, part).astype(jnp.bfloat16)

    def one_pair(pair, carry):
        columns = pl.ds(pl.multiple_of(pair * LANES, LANES), LANES)
        for at, size in row_chunks(rows, TILE):
            span = pl.ds(at, size)
            lane = lax.broadcasted_iota(jnp.int32, (size, LANES), 1)
            low = lane < HALF
            feature = lane % HALF
            got = []
            for side in range(2):
                head = pl.ds(pl.multiple_of((2 * pair + side) * LANES, LANES), LANES)
                queries = qs[span, head]
                scores = dot(queries, kx[:, head], 1, 1)
                highest = jnp.max(scores, axis=1, keepdims=True)
                raised = jnp.exp(scores - highest).astype(jnp.bfloat16)
                found = dot(raised, vx[:, head], 1, 0)
                total = -(highest + jnp.log(found))
                first = total.astype(jnp.bfloat16).astype(jnp.float32)
                second = (total - first).astype(jnp.bfloat16).astype(jnp.float32)
                third = total - first - second
                values = jnp.where(feature == 5, first, jnp.where(feature == 6, second, third))
                place = (feature > FEATS) & (feature < 8) & (low if side else ~low)
                qx[span, head] = jnp.where(place, values, queries.astype(jnp.float32)).astype(jnp.bfloat16)
                got.append(found)
            over = pltpu.roll(jnp.where(low, got[1], got[0]), HALF, 1)
            mixed[span, columns] = (jnp.where(low, got[0], got[1]) / over).astype(jnp.bfloat16)
        return carry

    lax.fori_loop(0, width // LANES, one_pair, 0)


def attend(x, labels, own, other):
    rows, width = x.shape
    wide = jax.ShapeDtypeStruct((rows, 2 * width), jnp.bfloat16)
    depth = own.shape[0] * 2 * own.shape[1]
    return pl.pallas_call(
        attend_kernel,
        out_shape=(
            wide,
            wide,
            wide,
            jax.ShapeDtypeStruct((rows, width), jnp.bfloat16),
            jax.ShapeDtypeStruct((8, width), jnp.float32),
        ),
        in_specs=[pl.BlockSpec(memory_space=VMEM)] * 4,
        out_specs=[pl.BlockSpec(memory_space=VMEM)] * 5,
        scratch_shapes=[
            pltpu.VMEM((depth, own.shape[2]), jnp.bfloat16),
            pltpu.VMEM((rows, 2 * width), jnp.bfloat16),
            pltpu.VMEM((8, LANES), jnp.float32),
        ],
        compiler_params=params(),
        name="attend",
    )(x, labels, own, other)


def attend_back_kernel(qx, kx, vx, dox, packed, total):
    rows = qx.shape[0]
    width = packed.shape[1] // 3

    def one_pair(pair, carry):
        heads = [pl.ds(pl.multiple_of((2 * pair + side) * LANES, LANES), LANES) for side in range(2)]
        spots = [pl.ds(pl.multiple_of(kind * width + pair * LANES, LANES), LANES) for kind in range(3)]
        for at, size in row_chunks(rows, TILE):
            span = pl.ds(at, size)
            low = lax.broadcasted_iota(jnp.int32, (size, LANES), 1) < HALF
            got = []
            for side in range(2):
                head = heads[side]
                keys = kx[span, head]
                queries = qx[:, head]
                upstream = dox[:, head]
                attention = jnp.exp(dot(keys, queries, 1, 1))
                grad = dot(vx[span, head], upstream, 1, 1)
                scores = (attention * grad).astype(jnp.bfloat16)
                got.append((dot(scores, queries, 1, 0), dot(attention.astype(jnp.bfloat16), upstream, 1, 0)))
                part = dot(scores, keys, 0, 0)
                if at == 0:
                    total[side] = part
                else:
                    total[side] += part
            packed[span, spots[1]] = jnp.where(low, got[0][0], got[1][0]).astype(jnp.bfloat16)
            packed[span, spots[2]] = jnp.where(low, got[0][1], got[1][1]).astype(jnp.bfloat16)
        low = lax.broadcasted_iota(jnp.int32, (rows, LANES), 1) < HALF
        packed[:, spots[0]] = (jnp.where(low, total[0], total[1]) * (1.0 / math.sqrt(HEAD_DIM))).astype(jnp.bfloat16)
        return carry

    lax.fori_loop(0, width // LANES, one_pair, 0)


def attend_back(qx, kx, vx, dox):
    rows, wide = qx.shape
    return pl.pallas_call(
        attend_back_kernel,
        out_shape=jax.ShapeDtypeStruct((rows, 3 * wide // 2), jnp.bfloat16),
        in_specs=[pl.BlockSpec(memory_space=VMEM)] * 4,
        out_specs=pl.BlockSpec(memory_space=VMEM),
        scratch_shapes=[pltpu.VMEM((2, rows, LANES), jnp.float32)],
        compiler_params=params(),
        name="attend_back",
    )(qx, kx, vx, dox)


def norm_back(grad, normed, scale, gain):
    scaled = grad * gain
    return scale * (
        scaled
        - jnp.mean(scaled, axis=-1, keepdims=True)
        - normed * jnp.mean(scaled * normed, axis=-1, keepdims=True)
    )


def feed_kernel(
    x, mixed, dy, gains, own2, other2, own3, other3,
    outputs, dox, middle_grad, keep2, send2, keep3, send3, norm_grads,
    wide, contract, active, hidden_grad, second, middle_low, block,
):
    rows, width = x.shape
    hidden = contract.shape[0]
    assemble(own2, other2, wide)
    assemble(own3, other3, contract)
    gain, bias = gains[2:3], gains[3:4]
    gain_sum = jnp.zeros((1, width), jnp.float32)
    bias_sum = jnp.zeros((1, width), jnp.float32)
    for at, size in row_chunks(rows, 352):
        span = pl.ds(at, size)
        middle = x[span].astype(jnp.float32) + dot(mixed[span], wide[:, :width], 1, 0)
        normed, scale = normalize(middle)
        low = (normed * gain + bias).astype(jnp.bfloat16)
        second[span] = low
        result = middle
        back = jnp.zeros_like(middle)
        for start in range(0, hidden, 512):
            part = slice(start, start + 512)
            from_expand = wide[:, width + start : width + start + 512]
            up = dot(low, from_expand, 1, 0)
            square = up * up
            bend = jnp.tanh(0.7978845608028654 * up * (1.0 + 0.044715 * square))
            half = 0.5 * (1.0 + bend)
            act = (up * half).astype(jnp.bfloat16)
            active[span, part] = act
            slope = half + 0.5 * up * (1.0 - bend * bend) * (0.7978845608028654 * (1.0 + 3 * 0.044715 * square))
            down = (dot(dy[span], contract[part], 1, 1) * slope).astype(jnp.bfloat16)
            hidden_grad[span, part] = down
            result = result + dot(act, contract[part], 1, 0)
            back = back + dot(down, from_expand, 1, 1)
        outputs[span] = result.astype(jnp.bfloat16)
        gain_sum = gain_sum + jnp.sum(back * normed, axis=0, keepdims=True)
        bias_sum = bias_sum + jnp.sum(back, axis=0, keepdims=True)
        grad = dy[span].astype(jnp.float32) + norm_back(back, normed, scale, gain)
        middle_grad[span] = grad
        grad_low = grad.astype(jnp.bfloat16)
        middle_low[span] = grad_low
        mixed_grad = dot(grad_low, wide[:, :width], 1, 1).astype(jnp.bfloat16).astype(jnp.float32)
        lane = lax.broadcasted_iota(jnp.int32, (size, LANES), 1)
        left = lane < HALF
        feature = lane % HALF
        for pair in range(width // LANES):
            columns = slice(pair * LANES, (pair + 1) * LANES)
            piece = mixed_grad[:, columns]
            product = piece * mixed[span, columns].astype(jnp.float32)
            for side in range(2):
                mine = left if side == 0 else ~left
                delta = -jnp.sum(jnp.where(mine, product, 0.0), axis=1, keepdims=True)
                one = delta.astype(jnp.bfloat16).astype(jnp.float32)
                two = (delta - one).astype(jnp.bfloat16).astype(jnp.float32)
                three = delta - one - two
                extra = jnp.where(feature == 0, one, jnp.where(feature == 1, two, jnp.where(feature == 2, three, 0.0)))
                head = (2 * pair + side) * LANES
                dox[span, head : head + LANES] = jnp.where(mine, piece, extra).astype(jnp.bfloat16)
    norm_grads[...] = jnp.concatenate([gain_sum, bias_sum, jnp.zeros((6, width), jnp.float32)], axis=0)
    plane, deep, _ = keep3.shape
    each = 512 // (2 * deep)
    for start in range(0, plane, each):
        at = 2 * deep * start
        block[...] = dot(active[:, at : at + 512], dy[...], 0, 0)
        planes = pl.ds(start, each)
        split_rows(block, keep3.at[planes], send3.at[planes], slice(0, width))
    block[...] = dot(mixed[...], middle_low[...], 0, 0)
    split_rows(block, keep2, send2, slice(0, width))
    for start in range(0, hidden, 512):
        block[...] = dot(second[...], hidden_grad[:, start : start + 512], 0, 0)
        split_rows(block, keep2, send2, slice(width + start, width + start + 512))


def feed(x, mixed, dy, gains, own2, other2, own3, other3):
    rows, width = x.shape
    hidden = own3.shape[0] * 2 * own3.shape[1]
    return pl.pallas_call(
        feed_kernel,
        out_shape=(
            jax.ShapeDtypeStruct((rows, width), jnp.bfloat16),
            jax.ShapeDtypeStruct((rows, 2 * width), jnp.bfloat16),
            jax.ShapeDtypeStruct((rows, width), jnp.float32),
            jax.ShapeDtypeStruct(own2.shape, jnp.float32),
            jax.ShapeDtypeStruct(own2.shape, jnp.bfloat16),
            jax.ShapeDtypeStruct(own3.shape, jnp.float32),
            jax.ShapeDtypeStruct(own3.shape, jnp.bfloat16),
            jax.ShapeDtypeStruct((8, width), jnp.float32),
        ),
        in_specs=[pl.BlockSpec(memory_space=VMEM)] * 8,
        out_specs=[pl.BlockSpec(memory_space=VMEM)] * 8,
        scratch_shapes=[
            pltpu.VMEM((width, own2.shape[2]), jnp.bfloat16),
            pltpu.VMEM((hidden, width), jnp.bfloat16),
            pltpu.VMEM((rows, hidden), jnp.bfloat16),
            pltpu.VMEM((rows, hidden), jnp.bfloat16),
            pltpu.VMEM((rows, width), jnp.bfloat16),
            pltpu.VMEM((rows, width), jnp.bfloat16),
            pltpu.VMEM((width, 512), jnp.float32),
        ],
        compiler_params=params(),
        name="feed",
    )(x, mixed, dy, gains, own2, other2, own3, other3)


def project_back_kernel(x, packed, gains, keep, send, first, block):
    rows, width = x.shape
    gain, bias = gains[0:1], gains[1:2]
    for at, size in row_chunks(rows, 352):
        span = pl.ds(at, size)
        normed, _ = normalize(x[span].astype(jnp.float32))
        first[span] = (normed * gain + bias).astype(jnp.bfloat16)
    for start in range(0, packed.shape[1], 512):
        block[...] = dot(first[...], packed[:, start : start + 512], 0, 0)
        split_rows(block, keep, send, slice(start, start + 512))


def project_back(x, packed, gains, plane, deep):
    rows, width = x.shape
    shape = (plane, deep, packed.shape[1])
    return pl.pallas_call(
        project_back_kernel,
        out_shape=(jax.ShapeDtypeStruct(shape, jnp.float32), jax.ShapeDtypeStruct(shape, jnp.bfloat16)),
        in_specs=[pl.BlockSpec(memory_space=VMEM)] * 3,
        out_specs=[pl.BlockSpec(memory_space=VMEM)] * 2,
        scratch_shapes=[pltpu.VMEM((rows, width), jnp.bfloat16), pltpu.VMEM((width, 512), jnp.float32)],
        compiler_params=params(),
        name="project_back",
    )(x, packed, gains)


def input_back_kernel(x, packed, gains, own, other, middle_grad, grad_in, norm_grads, weight):
    rows, width = x.shape
    assemble(own, other, weight)
    gain = gains[0:1]
    gain_sum = jnp.zeros((1, width), jnp.float32)
    bias_sum = jnp.zeros((1, width), jnp.float32)
    for at, size in row_chunks(rows, 352):
        span = pl.ds(at, size)
        normed, scale = normalize(x[span].astype(jnp.float32))
        back = dot(packed[span], weight[:, : 3 * width], 1, 1)
        gain_sum = gain_sum + jnp.sum(back * normed, axis=0, keepdims=True)
        bias_sum = bias_sum + jnp.sum(back, axis=0, keepdims=True)
        grad_in[span] = (middle_grad[span] + norm_back(back, normed, scale, gain)).astype(jnp.bfloat16)
    norm_grads[...] = jnp.concatenate([gain_sum, bias_sum, jnp.zeros((6, width), jnp.float32)], axis=0)


def input_back(x, packed, gains, own, other, middle_grad):
    rows, width = x.shape
    return pl.pallas_call(
        input_back_kernel,
        out_shape=(jax.ShapeDtypeStruct((rows, width), jnp.bfloat16), jax.ShapeDtypeStruct((8, width), jnp.float32)),
        in_specs=[pl.BlockSpec(memory_space=VMEM)] * 6,
        out_specs=[pl.BlockSpec(memory_space=VMEM)] * 2,
        scratch_shapes=[pltpu.VMEM((width, own.shape[2]), jnp.bfloat16)],
        compiler_params=params(),
        name="input_back",
    )(x, packed, gains, own, other, middle_grad)


AXES = ("dp", "rep")


class Layout:
    def __init__(self, mesh):
        self.dp = mesh.shape["dp"]
        self.rep = mesh.shape["rep"]
        self.plane = self.dp // 2

    def permute(self, value, move):
        pairs = []
        for p in range(self.plane):
            for c in range(2):
                for z in range(self.rep):
                    q, d, w = move(p, c, z)
                    pairs.append(((p * 2 + c) * self.rep + z, (q * 2 + d) * self.rep + w))
        return lax.ppermute(value, AXES, pairs)

    def to_core(self, value):
        return self.permute(value, lambda p, c, z: (p, 1 - c, z))

    def to_plane(self, value, m):
        return self.permute(value, lambda p, c, z: (p ^ m, c, z))

    def to_rep(self, value, k):
        return self.permute(value, lambda p, c, z: (p, c, (z + k) % self.rep))

    def place(self):
        dp = lax.axis_index("dp")
        return dp // 2, dp % 2, lax.axis_index("rep")


def pick(value, index, axis):
    return lax.dynamic_index_in_dim(value, index, axis, keepdims=False)


def gather_rows(lay, shard):
    rows, cols = shard.shape
    p, c, z = lay.place()
    column = jnp.zeros((lay.rep, rows, cols), shard.dtype)
    column = lax.dynamic_update_index_in_dim(column, shard, z, 0)
    for k in range(1, lay.rep):
        column = lax.dynamic_update_index_in_dim(column, lay.to_rep(shard, k), (z - k) % lay.rep, 0)
    column = column.reshape(lay.rep * rows, cols)
    plane = jnp.zeros((lay.plane, lay.rep * rows, cols), shard.dtype)
    plane = lax.dynamic_update_index_in_dim(plane, column, p, 0)
    for m in range(1, lay.plane):
        plane = lax.dynamic_update_index_in_dim(plane, lay.to_plane(column, m), p ^ m, 0)
    return plane, lay.to_core(plane)


def scatter_rows(lay, keep, send):
    cols = keep.shape[-1]
    p, c, z = lay.place()
    chip = keep + lay.to_core(send).astype(jnp.float32)
    low = chip.astype(jnp.bfloat16)
    column = pick(chip, p, 0)
    for m in range(1, lay.plane):
        column = column + lay.to_plane(pick(low, p ^ m, 0), m).astype(jnp.float32)
    column = column.reshape(lay.rep, -1, cols)
    low = column.astype(jnp.bfloat16)
    own = pick(column, z, 0)
    for k in range(1, lay.rep):
        own = own + lay.to_rep(pick(low, (z + k) % lay.rep, 0), k).astype(jnp.float32)
    return own


def exchange(lay, value):
    return lax.all_to_all(value, AXES, 0, 0)


def sum_all(lay, row):
    count = lay.dp * lay.rep
    spread = jnp.broadcast_to(row[None, None, :], (count, 1, row.shape[0]))
    return jnp.sum(exchange(lay, spread), axis=(0, 1))


def body(
    lay,
    inputs,
    segments,
    cotangent,
    attend_in,
    attend_out,
    expand,
    contract,
    layer_norms,
    moment_in,
    moment_out,
    moment_expand,
    moment_contract,
    moment_norms,
    square_in,
    square_out,
    square_expand,
    square_contract,
    square_norms,
):
    masters = (attend_in, attend_out, expand, contract, layer_norms)
    width = attend_in.shape[1]
    depth = attend_out.shape[1]
    count = lay.dp * lay.rep
    local_weight_sums = jnp.stack([jnp.sum(weight * weight) for weight in masters])
    lowered = [weight.astype(jnp.bfloat16) for weight in masters]
    norm_rows = jnp.pad(lowered[4].T, ((0, 0), (0, LANES - 4)))
    own1, other1 = gather_rows(lay, jnp.concatenate([lowered[0], norm_rows], axis=1))
    own2, other2 = gather_rows(lay, jnp.concatenate([lowered[1], lowered[2]], axis=1))
    own3, other3 = gather_rows(lay, lowered[3])
    rows = inputs.shape[1]
    memory = rows - segments.shape[1]
    pad = -rows % 32
    labels = jnp.concatenate(
        [jnp.full((memory,), -1, jnp.int32), segments[0], jnp.full((pad,), -2, jnp.int32)]
    )[:, None]
    x = jnp.pad(inputs[0], ((0, pad), (0, 0)))
    dy = jnp.pad(cotangent[0], ((0, pad), (0, 0)))
    qx, kx, vx, mixed, gains = attend(x, labels, own1, other1)
    outputs, dox, middle_grad, keep2, send2, keep3, send3, second_norms = feed(
        x, mixed, dy, gains, own2, other2, own3, other3
    )
    reduced3 = scatter_rows(lay, keep3, send3)
    reduced2 = scatter_rows(lay, keep2, send2)
    packed = attend_back(qx, kx, vx, dox)
    keep1, send1 = project_back(x, packed, gains, lay.plane, own1.shape[1])
    reduced1 = scatter_rows(lay, keep1, send1)
    input_gradient, first_norms = input_back(x, packed, gains, own1, other1, middle_grad)
    norm_grads = jnp.concatenate([first_norms[:2], second_norms[:2]], axis=0)
    norm_grads = jnp.sum(exchange(lay, norm_grads.reshape(4, count, -1).transpose(1, 0, 2)), axis=0)
    outputs = outputs[None, :rows]
    input_gradient = input_gradient[None, :rows]
    reduced = (reduced1, reduced2[:, :depth], reduced2[:, depth:], reduced3, norm_grads)
    firsts = (moment_in, moment_out, moment_expand, moment_contract, moment_norms)
    seconds = (square_in, square_out, square_expand, square_contract, square_norms)
    momenta = []
    variances = []
    directions = []
    for weight, gradient, first, second in zip(masters, reduced, firsts, seconds):
        momentum = BETA * first + (1.0 - BETA) * gradient
        variance = BETA * second + (1.0 - BETA) * gradient * gradient
        momenta.append(momentum)
        variances.append(variance)
        directions.append(momentum / (jnp.sqrt(variance) + ADAM_EPSILON) + DECAY * weight)
    local_update_sums = jnp.stack([jnp.sum(direction * direction) for direction in directions])
    sums = sum_all(lay, jnp.pad(jnp.concatenate([local_weight_sums, local_update_sums]), (0, LANES - 10)))
    weight_norms = jnp.sqrt(sums[:5])
    update_norms = jnp.sqrt(sums[5:10])
    ratios = weight_norms / update_norms
    updated = [
        weight - RATE * ratios[index] * direction
        for index, (weight, direction) in enumerate(zip(masters, directions))
    ]
    trust_table = jnp.stack([weight_norms, update_norms, ratios])
    return (outputs, input_gradient, *updated, *momenta, *variances, trust_table)


def solution(mesh):
    placed = (
        P(("dp", "rep"), None, None),
        P(("dp", "rep"), None),
        P(("dp", "rep"), None, None),
        P(("dp", "rep"), None),
        P(("dp", "rep"), None),
        P(("dp", "rep"), None),
        P(("dp", "rep"), None),
        P(None, ("dp", "rep")),
        P(("dp", "rep"), None),
        P(("dp", "rep"), None),
        P(("dp", "rep"), None),
        P(("dp", "rep"), None),
        P(None, ("dp", "rep")),
        P(("dp", "rep"), None),
        P(("dp", "rep"), None),
        P(("dp", "rep"), None),
        P(("dp", "rep"), None),
        P(None, ("dp", "rep")),
    )
    return jax.shard_map(
        partial(body, Layout(mesh)),
        mesh=mesh,
        in_specs=placed,
        out_specs=(
            P(("dp", "rep"), None, None),
            P(("dp", "rep"), None, None),
            P(("dp", "rep"), None),
            P(("dp", "rep"), None),
            P(("dp", "rep"), None),
            P(("dp", "rep"), None),
            P(None, ("dp", "rep")),
            P(("dp", "rep"), None),
            P(("dp", "rep"), None),
            P(("dp", "rep"), None),
            P(("dp", "rep"), None),
            P(None, ("dp", "rep")),
            P(("dp", "rep"), None),
            P(("dp", "rep"), None),
            P(("dp", "rep"), None),
            P(("dp", "rep"), None),
            P(None, ("dp", "rep")),
            P(),
        ),
        check_vma=False,
    )
```

```python
from functools import partial
import math

import jax
import jax.numpy as jnp
from jax import lax
from jax.experimental import pallas as pl
from jax.experimental.pallas import tpu as pltpu
from jax.sharding import PartitionSpec as P

HEADS = 8
HEAD_DIM = 64


EPSILON = 1e-05
ADAM_EPSILON = 1e-06
DECAY = 0.01
RATE = 0.5
BETA = 0.5
PAD = 12
LANES = 128
HALF = 64
BIG = 1e30
FEATS = 4
TILE = 256
THIN = 32
VMEM = pltpu.MemorySpace.VMEM


def params():
    return pltpu.CompilerParams(vmem_limit_bytes=62 * 1024 * 1024)


def cost(microseconds):
    return pl.CostEstimate(flops=int(microseconds * 9e8), bytes_accessed=int(microseconds * 3e6), transcendentals=0)


def dot(a, b, ca, cb):
    return lax.dot_general(a, b, (((ca,), (cb,)), ((), ())), preferred_element_type=jnp.float32)


def normalize(values):
    center = values - jnp.mean(values, axis=-1, keepdims=True)
    scale = lax.rsqrt(jnp.mean(center * center, axis=-1, keepdims=True) + EPSILON)
    return center * scale, scale


def core_index():
    return lax.rem(lax.axis_index("dp"), 2)


def plane_index():
    return lax.div(lax.axis_index("dp"), 2)


def block_at(m, other, rows):
    core = core_index()
    side = 1 - core if other else core
    return pl.multiple_of((2 * (plane_index() ^ m) + side) * rows, rows)


def assemble(pieces, full_ref, columns):
    plane = len(pieces) // 2
    for i, piece in enumerate(pieces):
        at = block_at(i % plane, i >= plane, piece.shape[0])
        full_ref[pl.ds(at, piece.shape[0]), :] = piece[:, columns]


def assemble_deep(pieces, full_ref, first, reps):
    plane = len(pieces) // 2
    width = full_ref.shape[1]
    for i, piece in enumerate(pieces):
        rows = piece.shape[0] // reps
        at = block_at(i % plane, i >= plane, 4 * piece.shape[0])
        for z in range(reps):
            for j in range(4):
                source = piece[z * rows : (z + 1) * rows, first + j * width : first + (j + 1) * width]
                full_ref[pl.ds(at + (4 * z + j) * rows, rows), :] = source


def split_rows(full_ref, keep_ref, send_ref, lanes):
    plane, rows, _ = keep_ref.shape
    core = core_index()
    for p in range(plane):
        at = pl.multiple_of((2 * p + core) * rows, rows)
        keep_ref[p, :, lanes] = full_ref[pl.ds(at, rows), :]
        at = pl.multiple_of((2 * p + 1 - core) * rows, rows)
        send_ref[p, :, lanes] = full_ref[pl.ds(at, rows), :].astype(jnp.bfloat16)


def split_deep(full_ref, keep_ref, send_ref, first, reps):
    plane, rows, _ = keep_ref.shape
    width = full_ref.shape[1]
    core = core_index()
    each = rows // reps
    for p in range(plane):
        for side, target in ((core, keep_ref), (1 - core, send_ref)):
            base = pl.multiple_of((2 * p + side) * 4 * rows, 4 * rows)
            for z in range(reps):
                for j in range(4):
                    source = full_ref[pl.ds(base + (4 * z + j) * each, each), :]
                    columns = slice(first + j * width, first + (j + 1) * width)
                    target[p, z * each : (z + 1) * each, columns] = source.astype(target.dtype)


def row_chunks(rows, size):
    return [(at, min(size, rows - at)) for at in range(0, rows, size)]


def attend_kernel(count, x, labels, *refs):
    pieces = refs[:count]
    qx, kx, vx, mixed, gains, weight, qs = refs[count:]
    rows = x.shape[0]
    width = mixed.shape[1]
    assemble(pieces, weight, slice(None))
    gains[...] = jnp.transpose(weight[:, 3 * width :].astype(jnp.float32))[:8]
    gain, bias = gains[0:1], gains[1:2]
    for at, size in row_chunks(rows, 352):
        span = pl.ds(at, size)
        normed, _ = normalize(x[span].astype(jnp.float32))
        first = (normed * gain + bias).astype(jnp.bfloat16)
        lane = lax.broadcasted_iota(jnp.int32, (size, LANES), 1)
        low = lane < HALF
        feature = lane % HALF
        label = jnp.broadcast_to(labels[span], (size, LANES))
        blocked = ((feature < FEATS) & (label >= 0) & (feature != label)) | (feature == FEATS)
        query_side = jnp.where(blocked, -BIG, 0.0)
        marked = ((feature < FEATS) & (feature == label)) | ((feature == FEATS) & (label == -2))
        key_side = jnp.where(marked | (feature > FEATS), 1.0, 0.0)
        for pair in range(width // LANES):
            columns = slice(pair * LANES, (pair + 1) * LANES)
            for kind, (target, side) in enumerate(((qs, query_side), (kx, key_side), (vx, jnp.ones_like(key_side)))):
                part = dot(first, weight[:, kind * width + pair * LANES : kind * width + (pair + 1) * LANES], 1, 0)
                part = part.astype(jnp.bfloat16).astype(jnp.float32)
                if kind == 0:
                    part = part * (1.0 / math.sqrt(HEAD_DIM))
                target[span, 2 * pair * LANES : (2 * pair + 1) * LANES] = jnp.where(low, part, side).astype(jnp.bfloat16)
                target[span, (2 * pair + 1) * LANES : (2 * pair + 2) * LANES] = jnp.where(low, side, part).astype(jnp.bfloat16)

    def one_pair(pair, carry):
        columns = pl.ds(pl.multiple_of(pair * LANES, LANES), LANES)
        for at, size in row_chunks(rows, TILE):
            span = pl.ds(at, size)
            lane = lax.broadcasted_iota(jnp.int32, (size, LANES), 1)
            low = lane < HALF
            feature = lane % HALF
            got = []
            for side in range(2):
                head = pl.ds(pl.multiple_of((2 * pair + side) * LANES, LANES), LANES)
                queries = qs[span, head]
                scores = dot(queries, kx[:, head], 1, 1)
                highest = jnp.max(scores, axis=1, keepdims=True)
                raised = jnp.exp(scores - highest).astype(jnp.bfloat16)
                found = dot(raised, vx[:, head], 1, 0)
                total = -(highest + jnp.log(found))
                first = total.astype(jnp.bfloat16).astype(jnp.float32)
                second = (total - first).astype(jnp.bfloat16).astype(jnp.float32)
                third = total - first - second
                values = jnp.where(feature == 5, first, jnp.where(feature == 6, second, third))
                place = (feature > FEATS) & (feature < 8) & (low if side else ~low)
                qx[span, head] = jnp.where(place, values, queries.astype(jnp.float32)).astype(jnp.bfloat16)
                got.append(found)
            over = pltpu.roll(jnp.where(low, got[1], got[0]), HALF, 1)
            mixed[span, columns] = (jnp.where(low, got[0], got[1]) / over).astype(jnp.bfloat16)
        return carry

    lax.fori_loop(0, width // LANES, one_pair, 0)


def attend(x, labels, pieces):
    rows, width = x.shape
    wide = jax.ShapeDtypeStruct((rows, 2 * width), jnp.bfloat16)
    depth = len(pieces) * pieces[0].shape[0]
    return pl.pallas_call(
        partial(attend_kernel, len(pieces)),
        out_shape=(
            wide,
            wide,
            wide,
            jax.ShapeDtypeStruct((rows, width), jnp.bfloat16),
            jax.ShapeDtypeStruct((8, width), jnp.float32),
        ),
        in_specs=[pl.BlockSpec(memory_space=VMEM)] * (2 + len(pieces)),
        out_specs=[pl.BlockSpec(memory_space=VMEM)] * 5,
        scratch_shapes=[
            pltpu.VMEM((depth, pieces[0].shape[1]), jnp.bfloat16),
            pltpu.VMEM((rows, 2 * width), jnp.bfloat16),
        ],
        compiler_params=params(),
        cost_estimate=cost(25),
        name="attend",
    )(x, labels, *pieces)


def attend_back_kernel(qx, kx, vx, dox, packed, total):
    rows = qx.shape[0]
    width = packed.shape[1] // 3

    def one_pair(pair, carry):
        heads = [pl.ds(pl.multiple_of((2 * pair + side) * LANES, LANES), LANES) for side in range(2)]
        spots = [pl.ds(pl.multiple_of(kind * width + pair * LANES, LANES), LANES) for kind in range(3)]
        for at, size in row_chunks(rows, TILE):
            span = pl.ds(at, size)
            low = lax.broadcasted_iota(jnp.int32, (size, LANES), 1) < HALF
            got = []
            for side in range(2):
                head = heads[side]
                keys = kx[span, head]
                queries = qx[:, head]
                upstream = dox[:, head]
                attention = jnp.exp(dot(keys, queries, 1, 1))
                grad = dot(vx[span, head], upstream, 1, 1)
                scores = (attention * grad).astype(jnp.bfloat16)
                got.append((dot(scores, queries, 1, 0), dot(attention.astype(jnp.bfloat16), upstream, 1, 0)))
                part = dot(scores, keys, 0, 0)
                if at == 0:
                    total[side] = part
                else:
                    total[side] += part
            packed[span, spots[1]] = jnp.where(low, got[0][0], got[1][0]).astype(jnp.bfloat16)
            packed[span, spots[2]] = jnp.where(low, got[0][1], got[1][1]).astype(jnp.bfloat16)
        low = lax.broadcasted_iota(jnp.int32, (rows, LANES), 1) < HALF
        packed[:, spots[0]] = (jnp.where(low, total[0], total[1]) * (1.0 / math.sqrt(HEAD_DIM))).astype(jnp.bfloat16)
        return carry

    lax.fori_loop(0, width // LANES, one_pair, 0)


def attend_back(qx, kx, vx, dox):
    rows, wide = qx.shape
    return pl.pallas_call(
        attend_back_kernel,
        out_shape=jax.ShapeDtypeStruct((rows, 3 * wide // 2), jnp.bfloat16),
        in_specs=[pl.BlockSpec(memory_space=VMEM)] * 4,
        out_specs=pl.BlockSpec(memory_space=VMEM),
        scratch_shapes=[pltpu.VMEM((2, rows, LANES), jnp.float32)],
        compiler_params=params(),
        cost_estimate=cost(34),
        name="attend_back",
    )(qx, kx, vx, dox)


def norm_back(grad, normed, scale, gain):
    scaled = grad * gain
    return scale * (
        scaled
        - jnp.mean(scaled, axis=-1, keepdims=True)
        - normed * jnp.mean(scaled * normed, axis=-1, keepdims=True)
    )


def feed_kernel(reps, count, deep_count, x, mixed, dy, gains, *refs):
    pieces = refs[:count]
    deep_pieces = refs[count : count + deep_count]
    outputs, dox, middle_grad, keep2, send2, norm_grads, *deep_out = refs[count + deep_count : -7]
    wide, contract, active, hidden_grad, second, middle_low, block = refs[-7:]
    rows, width = x.shape
    hidden = contract.shape[0]
    wide_part = slice(0, width + hidden)
    assemble(pieces, wide, wide_part)
    if deep_count:
        assemble(deep_pieces, contract, slice(None))
    else:
        assemble_deep(pieces, contract, width + hidden, reps)
    gain, bias = gains[2:3], gains[3:4]
    gain_sum = jnp.zeros((1, width), jnp.float32)
    bias_sum = jnp.zeros((1, width), jnp.float32)
    for at, size in row_chunks(rows, 352):
        span = pl.ds(at, size)
        middle = x[span].astype(jnp.float32) + dot(mixed[span], wide[:, :width], 1, 0)
        normed, scale = normalize(middle)
        low = (normed * gain + bias).astype(jnp.bfloat16)
        second[span] = low
        result = middle
        back = jnp.zeros_like(middle)
        for start in range(0, hidden, 512):
            part = slice(start, start + 512)
            from_expand = wide[:, width + start : width + start + 512]
            up = dot(low, from_expand, 1, 0)
            square = up * up
            bend = jnp.tanh(0.7978845608028654 * up * (1.0 + 0.044715 * square))
            half = 0.5 * (1.0 + bend)
            act = (up * half).astype(jnp.bfloat16)
            active[span, part] = act
            slope = half + 0.5 * up * (1.0 - bend * bend) * (0.7978845608028654 * (1.0 + 3 * 0.044715 * square))
            down = (dot(dy[span], contract[part], 1, 1) * slope).astype(jnp.bfloat16)
            hidden_grad[span, part] = down
            result = result + dot(act, contract[part], 1, 0)
            back = back + dot(down, from_expand, 1, 1)
        outputs[span] = result.astype(jnp.bfloat16)
        gain_sum = gain_sum + jnp.sum(back * normed, axis=0, keepdims=True)
        bias_sum = bias_sum + jnp.sum(back, axis=0, keepdims=True)
        grad = dy[span].astype(jnp.float32) + norm_back(back, normed, scale, gain)
        middle_grad[span] = grad
        grad_low = grad.astype(jnp.bfloat16)
        middle_low[span] = grad_low
        mixed_grad = dot(grad_low, wide[:, :width], 1, 1).astype(jnp.bfloat16).astype(jnp.float32)
        lane = lax.broadcasted_iota(jnp.int32, (size, LANES), 1)
        left = lane < HALF
        feature = lane % HALF
        for pair in range(width // LANES):
            columns = slice(pair * LANES, (pair + 1) * LANES)
            piece = mixed_grad[:, columns]
            product = piece * mixed[span, columns].astype(jnp.float32)
            for side in range(2):
                mine = left if side == 0 else ~left
                delta = -jnp.sum(jnp.where(mine, product, 0.0), axis=1, keepdims=True)
                one = delta.astype(jnp.bfloat16).astype(jnp.float32)
                two = (delta - one).astype(jnp.bfloat16).astype(jnp.float32)
                three = delta - one - two
                extra = jnp.where(feature == 0, one, jnp.where(feature == 1, two, jnp.where(feature == 2, three, 0.0)))
                head = (2 * pair + side) * LANES
                dox[span, head : head + LANES] = jnp.where(mine, piece, extra).astype(jnp.bfloat16)
    norm_grads[...] = jnp.concatenate([gain_sum, bias_sum, jnp.zeros((6, width), jnp.float32)], axis=0)
    plane = keep2.shape[0]
    deep = hidden // (2 * plane)
    each = 512 // (2 * deep)
    for start in range(0, plane, each):
        at = 2 * deep * start
        block[...] = dot(active[:, at : at + 512], dy[...], 0, 0)
        planes = pl.ds(start, each)
        if deep_count:
            split_rows(block, deep_out[0].at[planes], deep_out[1].at[planes], slice(0, width))
        else:
            split_deep(block, keep2.at[planes], send2.at[planes], width + hidden, reps)
    block[...] = dot(mixed[...], middle_low[...], 0, 0)
    split_rows(block, keep2, send2, slice(0, width))
    for start in range(0, hidden, 512):
        block[...] = dot(second[...], hidden_grad[:, start : start + 512], 0, 0)
        split_rows(block, keep2, send2, slice(width + start, width + start + 512))


def feed(reps, x, mixed, dy, gains, pieces, deep_pieces):
    rows, width = x.shape
    plane = len(pieces) // 2
    deep = pieces[0].shape[0]
    columns = pieces[0].shape[1]
    hidden = 4 * width
    out_shape = [
        jax.ShapeDtypeStruct((rows, width), jnp.bfloat16),
        jax.ShapeDtypeStruct((rows, 2 * width), jnp.bfloat16),
        jax.ShapeDtypeStruct((rows, width), jnp.float32),
        jax.ShapeDtypeStruct((plane, deep, columns), jnp.float32),
        jax.ShapeDtypeStruct((plane, deep, columns), jnp.bfloat16),
        jax.ShapeDtypeStruct((8, width), jnp.float32),
    ]
    if deep_pieces:
        out_shape.append(jax.ShapeDtypeStruct((plane, 4 * deep, width), jnp.float32))
        out_shape.append(jax.ShapeDtypeStruct((plane, 4 * deep, width), jnp.bfloat16))
    return pl.pallas_call(
        partial(feed_kernel, reps, len(pieces), len(deep_pieces)),
        out_shape=out_shape,
        in_specs=[pl.BlockSpec(memory_space=VMEM)] * (4 + len(pieces) + len(deep_pieces)),
        out_specs=[pl.BlockSpec(memory_space=VMEM)] * len(out_shape),
        scratch_shapes=[
            pltpu.VMEM((width, width + hidden), jnp.bfloat16),
            pltpu.VMEM((hidden, width), jnp.bfloat16),
            pltpu.VMEM((rows, hidden), jnp.bfloat16),
            pltpu.VMEM((rows, hidden), jnp.bfloat16),
            pltpu.VMEM((rows, width), jnp.bfloat16),
            pltpu.VMEM((rows, width), jnp.bfloat16),
            pltpu.VMEM((width, 512), jnp.float32),
        ],
        compiler_params=params(),
        cost_estimate=cost(28),
        name="feed",
    )(x, mixed, dy, gains, *pieces, *deep_pieces)


def project_back_kernel(x, packed, gains, keep, send, first, block):
    rows, width = x.shape
    gain, bias = gains[0:1], gains[1:2]
    for at, size in row_chunks(rows, 352):
        span = pl.ds(at, size)
        normed, _ = normalize(x[span].astype(jnp.float32))
        first[span] = (normed * gain + bias).astype(jnp.bfloat16)
    for start in range(0, packed.shape[1], 512):
        block[...] = dot(first[...], packed[:, start : start + 512], 0, 0)
        split_rows(block, keep, send, slice(start, start + 512))


def project_back(x, packed, gains, plane, deep):
    rows, width = x.shape
    shape = (plane, deep, packed.shape[1])
    return pl.pallas_call(
        project_back_kernel,
        out_shape=(jax.ShapeDtypeStruct(shape, jnp.float32), jax.ShapeDtypeStruct(shape, jnp.bfloat16)),
        in_specs=[pl.BlockSpec(memory_space=VMEM)] * 3,
        out_specs=[pl.BlockSpec(memory_space=VMEM)] * 2,
        scratch_shapes=[pltpu.VMEM((rows, width), jnp.bfloat16), pltpu.VMEM((width, 512), jnp.float32)],
        compiler_params=params(),
        cost_estimate=cost(6),
        name="project_back",
    )(x, packed, gains)


def input_back_kernel(x, packed, gains, middle_grad, *refs):
    pieces = refs[:-3]
    grad_in, norm_grads, weight = refs[-3:]
    rows, width = x.shape
    assemble(pieces, weight, slice(None))
    gain = gains[0:1]
    gain_sum = jnp.zeros((1, width), jnp.float32)
    bias_sum = jnp.zeros((1, width), jnp.float32)
    for at, size in row_chunks(rows, 352):
        span = pl.ds(at, size)
        normed, scale = normalize(x[span].astype(jnp.float32))
        back = dot(packed[span], weight[:, : 3 * width], 1, 1)
        gain_sum = gain_sum + jnp.sum(back * normed, axis=0, keepdims=True)
        bias_sum = bias_sum + jnp.sum(back, axis=0, keepdims=True)
        grad_in[span] = (middle_grad[span] + norm_back(back, normed, scale, gain)).astype(jnp.bfloat16)
    norm_grads[...] = jnp.concatenate([gain_sum, bias_sum, jnp.zeros((6, width), jnp.float32)], axis=0)


def input_back(x, packed, gains, middle_grad, pieces):
    rows, width = x.shape
    return pl.pallas_call(
        input_back_kernel,
        out_shape=(jax.ShapeDtypeStruct((rows, width), jnp.bfloat16), jax.ShapeDtypeStruct((8, width), jnp.float32)),
        in_specs=[pl.BlockSpec(memory_space=VMEM)] * (4 + len(pieces)),
        out_specs=[pl.BlockSpec(memory_space=VMEM)] * 2,
        scratch_shapes=[pltpu.VMEM((width, pieces[0].shape[1]), jnp.bfloat16)],
        compiler_params=params(),
        cost_estimate=cost(6),
        name="input_back",
    )(x, packed, gains, middle_grad, *pieces)


def column_kernel(*refs):
    reps = len(refs) - 1
    out = refs[-1]
    z = lax.axis_index("rep")
    rows = refs[0].shape[0]
    got = [ref[...].astype(jnp.float32) for ref in refs[:-1]]
    parts = []
    for j in range(reps):
        part = got[0]
        for k in range(1, reps):
            part = jnp.where(lax.rem(z + reps - k, reps) == j, got[k], part)
        parts.append(part)
    out[...] = jnp.concatenate(parts, axis=0).astype(out.dtype)


def column_of(shards):
    rows, cols = shards[0].shape
    reps = len(shards)
    return pl.pallas_call(
        column_kernel,
        out_shape=jax.ShapeDtypeStruct((reps * rows, cols), shards[0].dtype),
        in_specs=[pl.BlockSpec(memory_space=VMEM)] * reps,
        out_specs=pl.BlockSpec(memory_space=VMEM),
        cost_estimate=cost(1),
        name="column",
    )(*shards)


def chip_sum_kernel(keep, got, own, *low):
    p = plane_index()
    own[...] = keep[p] + got[p].astype(jnp.float32)
    for m, ref in enumerate(low, 1):
        ref[...] = (keep[p ^ m] + got[p ^ m].astype(jnp.float32)).astype(jnp.bfloat16)


def chip_sum(keep, got):
    plane, rows, cols = keep.shape
    block = 512
    part = pl.BlockSpec((rows, block), lambda i: (0, i))
    whole = pl.BlockSpec((plane, rows, block), lambda i: (0, 0, i))
    return pl.pallas_call(
        chip_sum_kernel,
        grid=(cols // block,),
        out_shape=[jax.ShapeDtypeStruct((rows, cols), jnp.float32)]
        + [jax.ShapeDtypeStruct((rows, cols), jnp.bfloat16)] * (plane - 1),
        in_specs=[whole, whole],
        out_specs=[part] * plane,
        cost_estimate=cost(2),
        name="chip_sum",
    )(keep, got)


def plane_sum_kernel(own, *refs):
    plane = sum(1 for ref in refs if ref.shape == own.shape) + 1
    got, out, low = refs[: plane - 1], refs[plane - 1], refs[plane:]
    reps = len(low) + 1
    rows = out.shape[0]
    z = lax.axis_index("rep")
    total = own[...]
    for ref in got:
        total = total + ref[...].astype(jnp.float32)
    for k, ref in enumerate((out, *low)):
        part = total[:rows]
        for j in range(1, reps):
            part = jnp.where(lax.rem(z + k, reps) == j, total[j * rows : (j + 1) * rows], part)
        ref[...] = part.astype(ref.dtype)


def plane_sum(own, got, reps):
    rows, cols = own.shape
    block = 512
    part = pl.BlockSpec((rows, block), lambda i: (0, i))
    small = pl.BlockSpec((rows // reps, block), lambda i: (0, i))
    return pl.pallas_call(
        plane_sum_kernel,
        grid=(cols // block,),
        out_shape=[jax.ShapeDtypeStruct((rows // reps, cols), jnp.float32)]
        + [jax.ShapeDtypeStruct((rows // reps, cols), jnp.bfloat16)] * (reps - 1),
        in_specs=[part] * (1 + len(got)),
        out_specs=[small] * reps,
        cost_estimate=cost(2),
        name="plane_sum",
    )(own, *got)


def full_sum(value):
    return jnp.sum(jnp.sum(value, axis=1, keepdims=True), axis=0, keepdims=True)


def moments_kernel(pieces_of, first_index, reps, *refs):
    n = len(pieces_of)
    grads = refs[: reps if reps else 1]
    if reps:
        total = grads[0][...]
        for ref in grads[1:]:
            total = total + ref[...].astype(jnp.float32)
        extra = refs[reps]
        arrays = refs[reps + 1 :]
    weights, firsts, seconds = arrays[:n], arrays[n : 2 * n], arrays[2 * n : 3 * n]
    momenta, variances, directions = arrays[3 * n : 4 * n], arrays[4 * n : 5 * n], arrays[5 * n : 6 * n]
    sums = arrays[6 * n]
    lane = lax.broadcasted_iota(jnp.int32, (1, LANES), 1)
    row = jnp.zeros((1, LANES), jnp.float32)
    for i, parts in enumerate(pieces_of):
        weight_sum = jnp.zeros((1, 1), jnp.float32)
        step_sum = jnp.zeros((1, 1), jnp.float32)
        for at, size, columns in parts:
            rows = slice(at, at + size)
            gradient = extra[...] if columns is None else total[:, columns[0] : columns[1]]
            weight = weights[i][rows]
            momentum = BETA * firsts[i][rows] + (1.0 - BETA) * gradient
            variance = BETA * seconds[i][rows] + (1.0 - BETA) * gradient * gradient
            direction = momentum / (jnp.sqrt(variance) + ADAM_EPSILON) + DECAY * weight
            momenta[i][rows] = momentum
            variances[i][rows] = variance
            directions[i][rows] = direction
            weight_sum = weight_sum + full_sum(weight * weight)
            step_sum = step_sum + full_sum(direction * direction)
        row = jnp.where(lane == first_index[i], weight_sum, row)
        row = jnp.where(lane == 5 + first_index[i], step_sum, row)
    sums[...] = row


def moments(pieces_of, first_index, grads, extra, weights, firsts, seconds):
    arrays = [*grads, extra, *weights, *firsts, *seconds]
    shapes = [jax.ShapeDtypeStruct(weight.shape, jnp.float32) for weight in weights]
    outs = pl.pallas_call(
        partial(moments_kernel, pieces_of, first_index, len(grads)),
        out_shape=shapes * 3 + [jax.ShapeDtypeStruct((1, LANES), jnp.float32)],
        in_specs=[pl.BlockSpec(memory_space=VMEM)] * len(arrays),
        out_specs=[pl.BlockSpec(memory_space=VMEM)] * (3 * len(weights) + 1),
        cost_estimate=cost(2),
        name="moments",
    )(*arrays)
    n = len(weights)
    return outs[:n], outs[n : 2 * n], outs[2 * n : 3 * n], outs[3 * n]


def update_kernel(n, sums, *refs):
    weights, directions, updated, table = refs[:n], refs[n : 2 * n], refs[2 * n : 3 * n], refs[3 * n]
    norms = jnp.sqrt(jnp.sum(sums[...], axis=0, keepdims=True))
    row = lax.broadcasted_iota(jnp.int32, table.shape, 0)
    lane = lax.broadcasted_iota(jnp.int32, table.shape, 1)
    out = jnp.zeros(table.shape, jnp.float32)
    for i in range(n):
        weight_norm = norms[:, i : i + 1]
        step_norm = norms[:, 5 + i : 6 + i]
        ratio = weight_norm / step_norm
        updated[i][...] = weights[i][...] - RATE * ratio * directions[i][...]
        column = jnp.where(row == 0, weight_norm, jnp.where(row == 1, step_norm, ratio))
        out = jnp.where(lane == i, column, out)
    table[...] = out


def update(sums, weights, directions):
    n = len(weights)
    outs = pl.pallas_call(
        partial(update_kernel, n),
        out_shape=[jax.ShapeDtypeStruct(weight.shape, jnp.float32) for weight in weights]
        + [jax.ShapeDtypeStruct((8, LANES), jnp.float32)],
        in_specs=[pl.BlockSpec(memory_space=VMEM)] * (1 + 2 * n),
        out_specs=[pl.BlockSpec(memory_space=VMEM)] * (n + 1),
        cost_estimate=cost(2),
        name="update",
    )(sums, *weights, *directions)
    return outs[:n], outs[n][:3, :n]


AXES = ("dp", "rep")


class Layout:
    def __init__(self, mesh):
        self.dp = mesh.shape["dp"]
        self.rep = mesh.shape["rep"]
        self.plane = self.dp // 2

    def permute(self, value, move):
        pairs = []
        for p in range(self.plane):
            for c in range(2):
                for z in range(self.rep):
                    q, d, w = move(p, c, z)
                    pairs.append(((p * 2 + c) * self.rep + z, (q * 2 + d) * self.rep + w))
        return lax.ppermute(value, AXES, pairs)

    def to_core(self, value):
        return self.permute(value, lambda p, c, z: (p, 1 - c, z))

    def to_plane(self, value, m):
        return self.permute(value, lambda p, c, z: (p ^ m, c, z))

    def to_rep(self, value, k):
        return self.permute(value, lambda p, c, z: (p, c, (z + k) % self.rep))

    def place(self):
        dp = lax.axis_index("dp")
        return dp // 2, dp % 2, lax.axis_index("rep")


def over_rep(lay, shard):
    return [shard] + [lay.to_rep(shard, k) for k in range(1, lay.rep)]


def over_plane(lay, column):
    return [column] + [lay.to_plane(column, m) for m in range(1, lay.plane)]


def over_core(lay, blocks):
    return blocks + [lay.to_core(block) for block in blocks]


def after(values, others):
    count = len(values)
    return list(lax.optimization_barrier((*values, *others))[:count])


def exchange(lay, value):
    return lax.all_to_all(value, AXES, 0, 0)


def body(
    lay,
    inputs,
    segments,
    cotangent,
    attend_in,
    attend_out,
    expand,
    contract,
    layer_norms,
    moment_in,
    moment_out,
    moment_expand,
    moment_contract,
    moment_norms,
    square_in,
    square_out,
    square_expand,
    square_contract,
    square_norms,
):
    masters = (attend_in, attend_out, expand, contract, layer_norms)
    width = attend_in.shape[1]
    depth = attend_out.shape[1]
    hidden = expand.shape[1]
    own = attend_in.shape[0]
    count = lay.dp * lay.rep
    plain = own % 16 == 0
    norm_rows = jnp.pad(layer_norms.astype(jnp.bfloat16).T, ((0, 0), (0, LANES - 4)))
    shard1 = jnp.concatenate([attend_in.astype(jnp.bfloat16), norm_rows], axis=1)
    column1 = over_rep(lay, shard1)
    rows = inputs.shape[1]
    memory = rows - segments.shape[1]
    pad = -rows % 32
    attend_out_, expand_, contract_, inputs_, cotangent_, segments_ = after(
        [attend_out, expand, contract, inputs, cotangent, segments], [shard1]
    )
    labels = jnp.concatenate(
        [jnp.full((memory,), -1, jnp.int32), segments_[0], jnp.full((pad,), -2, jnp.int32)]
    )[:, None]
    x = jnp.pad(inputs_[0], ((0, pad), (0, 0)))
    dy = jnp.pad(cotangent_[0], ((0, pad), (0, 0)))
    deep = [contract_[j * own : (j + 1) * own] for j in range(4)]
    shard2 = jnp.concatenate([part.astype(jnp.bfloat16) for part in (attend_out_, expand_, *deep)], axis=1)
    x, dy, labels, shard2 = after([x, dy, labels, shard2], [])
    column2 = over_rep(lay, shard2)
    blocks1 = over_plane(lay, column_of(column1))
    blocks2 = over_plane(lay, column_of(after(column2, blocks1)))
    pieces1 = over_core(lay, blocks1)
    *pieces1, x, labels = after([*pieces1, x, labels], blocks2[:1])
    qx, kx, vx, mixed, gains = attend(x, labels, pieces1)
    pieces2 = over_core(lay, blocks2)
    deep_pieces = []
    if not plain:
        first = depth + hidden
        for piece in pieces2:
            part = piece[:, first:].reshape(lay.rep, own, 4, depth).transpose(0, 2, 1, 3)
            deep_pieces.append(part.reshape(-1, depth))
    outputs, dox, middle_grad, keep2, send2, second_norms, *deep_out = feed(
        lay.rep, x, mixed, dy, gains, pieces2, deep_pieces
    )
    if not plain:
        keep2, send2 = [
            jnp.concatenate(
                [
                    wide[:, :, : depth + hidden],
                    part.reshape(lay.plane, lay.rep, 4, own, depth).transpose(0, 1, 3, 2, 4).reshape(lay.plane, -1, 4 * depth),
                ],
                axis=2,
            )
            for wide, part in zip((keep2, send2), deep_out)
        ]
    own2, *low2 = chip_sum(keep2, lay.to_core(send2))
    got2 = [lay.to_plane(part, m) for m, part in enumerate(low2, 1)]
    (dox,) = after([dox], low2)
    packed = attend_back(qx, kx, vx, dox)
    own2, *got2 = after([own2, *got2], [packed])
    own2, *low2 = plane_sum(own2, got2, lay.rep)
    got2 = [lay.to_rep(part, k) for k, part in enumerate(low2, 1)]
    (packed_,) = after([packed], low2)
    keep1, send1 = project_back(x, packed_, gains, lay.plane, lay.rep * own)
    own1, *low1 = chip_sum(keep1, lay.to_core(send1))
    got1 = [lay.to_plane(part, m) for m, part in enumerate(low1, 1)]
    (packed_,) = after([packed], low1)
    input_gradient, first_norms = input_back(x, packed_, gains, middle_grad, pieces1)
    norm_grads = jnp.concatenate([first_norms[:2], second_norms[:2]], axis=0)
    norm_grads = jnp.sum(exchange(lay, norm_grads.reshape(4, count, -1).transpose(1, 0, 2)), axis=0)
    own2, *got2 = after([own2, *got2], [first_norms])
    spans = [[(0, own, (0, depth))], [(0, own, (depth, depth + hidden))]]
    spans.append([(j * own, own, (depth + hidden + j * depth, depth + hidden + (j + 1) * depth)) for j in range(4)])
    momenta2, variances2, directions2, sums2 = moments(
        spans, (1, 2, 3), [own2, *got2], jnp.zeros((8, LANES), jnp.float32), masters[1:4],
        (moment_out, moment_expand, moment_contract), (square_out, square_expand, square_contract),
    )
    own1, *got1 = after([own1, *got1], [sums2])
    own1, *low1 = plane_sum(own1, got1, lay.rep)
    got1 = [lay.to_rep(part, k) for k, part in enumerate(low1, 1)]
    momenta1, variances1, directions1, sums1 = moments(
        [[(0, own, (0, width))], [(0, 4, None)]], (0, 4), [own1, *got1], norm_grads, (attend_in, layer_norms),
        (moment_in, moment_norms), (square_in, square_norms),
    )
    sums = exchange(lay, jnp.broadcast_to((sums1 + sums2)[None], (count, 1, LANES)))
    directions = (directions1[0], *directions2, directions1[1])
    updated, trust_table = update(sums[:, 0], masters, directions)
    outputs = outputs[None, :rows]
    input_gradient = input_gradient[None, :rows]
    momenta = (momenta1[0], *momenta2, momenta1[1])
    variances = (variances1[0], *variances2, variances1[1])
    return (outputs, input_gradient, *updated, *momenta, *variances, trust_table)


def solution(mesh):
    placed = (
        P(("dp", "rep"), None, None),
        P(("dp", "rep"), None),
        P(("dp", "rep"), None, None),
        P(("dp", "rep"), None),
        P(("dp", "rep"), None),
        P(("dp", "rep"), None),
        P(("dp", "rep"), None),
        P(None, ("dp", "rep")),
        P(("dp", "rep"), None),
        P(("dp", "rep"), None),
        P(("dp", "rep"), None),
        P(("dp", "rep"), None),
        P(None, ("dp", "rep")),
        P(("dp", "rep"), None),
        P(("dp", "rep"), None),
        P(("dp", "rep"), None),
        P(("dp", "rep"), None),
        P(None, ("dp", "rep")),
    )
    return jax.shard_map(
        partial(body, Layout(mesh)),
        mesh=mesh,
        in_specs=placed,
        out_specs=(
            P(("dp", "rep"), None, None),
            P(("dp", "rep"), None, None),
            P(("dp", "rep"), None),
            P(("dp", "rep"), None),
            P(("dp", "rep"), None),
            P(("dp", "rep"), None),
            P(None, ("dp", "rep")),
            P(("dp", "rep"), None),
            P(("dp", "rep"), None),
            P(("dp", "rep"), None),
            P(("dp", "rep"), None),
            P(None, ("dp", "rep")),
            P(("dp", "rep"), None),
            P(("dp", "rep"), None),
            P(("dp", "rep"), None),
            P(("dp", "rep"), None),
            P(None, ("dp", "rep")),
            P(),
        ),
        check_vma=False,
    )
```

```python
from functools import partial
import math

import jax
import jax.numpy as jnp
from jax import lax
from jax.experimental import pallas as pl
from jax.experimental.pallas import tpu as pltpu
from jax.sharding import PartitionSpec as P

HEADS = 8
HEAD_DIM = 64


EPSILON = 1e-05
ADAM_EPSILON = 1e-06
DECAY = 0.01
RATE = 0.5
BETA = 0.5
PAD = 12
LANES = 128
HALF = 64
BIG = 1e30
FEATS = 4
TILE = 256
THIN = 32
VMEM = pltpu.MemorySpace.VMEM


def params(mebibytes):
    return pltpu.CompilerParams(vmem_limit_bytes=mebibytes * 1024 * 1024)


def dot(a, b, ca, cb):
    return lax.dot_general(a, b, (((ca,), (cb,)), ((), ())), preferred_element_type=jnp.float32)


def normalize(values):
    center = values - jnp.mean(values, axis=-1, keepdims=True)
    scale = lax.rsqrt(jnp.mean(center * center, axis=-1, keepdims=True) + EPSILON)
    return center * scale, scale


def core_index():
    return lax.rem(lax.axis_index("dp"), 2)


def plane_index():
    return lax.div(lax.axis_index("dp"), 2)


def block_at(m, other, rows):
    core = core_index()
    side = 1 - core if other else core
    return pl.multiple_of((2 * (plane_index() ^ m) + side) * rows, rows)


def assemble(pieces, full_ref, columns):
    plane = len(pieces) // 2
    for i, piece in enumerate(pieces):
        at = block_at(i % plane, i >= plane, piece.shape[0])
        full_ref[pl.ds(at, piece.shape[0]), :] = piece[:, columns]


def assemble_deep(pieces, full_ref, first, reps):
    plane = len(pieces) // 2
    width = full_ref.shape[1]
    for i, piece in enumerate(pieces):
        rows = piece.shape[0] // reps
        at = block_at(i % plane, i >= plane, 4 * piece.shape[0])
        for z in range(reps):
            for j in range(4):
                source = piece[z * rows : (z + 1) * rows, first + j * width : first + (j + 1) * width]
                full_ref[pl.ds(at + (4 * z + j) * rows, rows), :] = source


def split_rows(full_ref, keep_ref, send_ref, lanes):
    plane, rows, _ = keep_ref.shape
    core = core_index()
    for p in range(plane):
        at = pl.multiple_of((2 * p + core) * rows, rows)
        keep_ref[p, :, lanes] = full_ref[pl.ds(at, rows), :]
        at = pl.multiple_of((2 * p + 1 - core) * rows, rows)
        send_ref[p, :, lanes] = full_ref[pl.ds(at, rows), :].astype(jnp.bfloat16)


def split_deep(full_ref, keep_ref, send_ref, first, reps):
    plane, rows, _ = keep_ref.shape
    width = full_ref.shape[1]
    core = core_index()
    each = rows // reps
    for p in range(plane):
        for side, target in ((core, keep_ref), (1 - core, send_ref)):
            base = pl.multiple_of((2 * p + side) * 4 * rows, 4 * rows)
            for z in range(reps):
                for j in range(4):
                    source = full_ref[pl.ds(base + (4 * z + j) * each, each), :]
                    columns = slice(first + j * width, first + (j + 1) * width)
                    target[p, z * each : (z + 1) * each, columns] = source.astype(target.dtype)


def row_chunks(rows, size):
    return [(at, min(size, rows - at)) for at in range(0, rows, size)]


def attend_kernel(count, x, labels, *refs):
    pieces = refs[:count]
    qx, kx, vx, mixed, gains, weight, qs = refs[count:]
    rows = x.shape[0]
    width = mixed.shape[1]
    assemble(pieces, weight, slice(None))
    gains[...] = jnp.transpose(weight[:, 3 * width :].astype(jnp.float32))[:8]
    gain, bias = gains[0:1], gains[1:2]
    for at, size in row_chunks(rows, 352):
        span = pl.ds(at, size)
        normed, _ = normalize(x[span].astype(jnp.float32))
        first = (normed * gain + bias).astype(jnp.bfloat16)
        lane = lax.broadcasted_iota(jnp.int32, (size, LANES), 1)
        low = lane < HALF
        feature = lane % HALF
        label = labels[span]
        blocked = ((feature < FEATS) & (label >= 0) & (feature != label)) | (feature == FEATS)
        query_side = jnp.where(blocked, -BIG, 0.0)
        marked = ((feature < FEATS) & (feature == label)) | ((feature == FEATS) & (label == -2))
        key_side = jnp.where(marked | (feature > FEATS), 1.0, 0.0)
        for pair in range(width // LANES):
            columns = slice(pair * LANES, (pair + 1) * LANES)
            for kind, (target, side) in enumerate(((qs, query_side), (kx, key_side), (vx, jnp.ones_like(key_side)))):
                part = dot(first, weight[:, kind * width + pair * LANES : kind * width + (pair + 1) * LANES], 1, 0)
                part = part.astype(jnp.bfloat16).astype(jnp.float32)
                if kind == 0:
                    part = part * (1.0 / math.sqrt(HEAD_DIM))
                target[span, 2 * pair * LANES : (2 * pair + 1) * LANES] = jnp.where(low, part, side).astype(jnp.bfloat16)
                target[span, (2 * pair + 1) * LANES : (2 * pair + 2) * LANES] = jnp.where(low, side, part).astype(jnp.bfloat16)

    def one_pair(pair, carry):
        columns = pl.ds(pl.multiple_of(pair * LANES, LANES), LANES)
        for at, size in row_chunks(rows, TILE):
            span = pl.ds(at, size)
            lane = lax.broadcasted_iota(jnp.int32, (size, LANES), 1)
            low = lane < HALF
            feature = lane % HALF
            got = []
            for side in range(2):
                head = pl.ds(pl.multiple_of((2 * pair + side) * LANES, LANES), LANES)
                queries = qs[span, head]
                scores = dot(queries, kx[:, head], 1, 1)
                highest = jnp.max(scores, axis=1, keepdims=True)
                raised = jnp.exp(scores - highest).astype(jnp.bfloat16)
                found = dot(raised, vx[:, head], 1, 0)
                total = -(highest + jnp.log(found))
                first = total.astype(jnp.bfloat16).astype(jnp.float32)
                second = (total - first).astype(jnp.bfloat16).astype(jnp.float32)
                third = total - first - second
                values = jnp.where(feature == 5, first, jnp.where(feature == 6, second, third))
                place = (feature > FEATS) & (feature < 8) & (low if side else ~low)
                qx[span, head] = jnp.where(place, values, queries.astype(jnp.float32)).astype(jnp.bfloat16)
                got.append(found)
            over = pltpu.roll(jnp.where(low, got[1], got[0]), HALF, 1)
            mixed[span, columns] = (jnp.where(low, got[0], got[1]) / over).astype(jnp.bfloat16)
        return carry

    lax.fori_loop(0, width // LANES, one_pair, 0)


def attend(x, labels, pieces):
    rows, width = x.shape
    wide = jax.ShapeDtypeStruct((rows, 2 * width), jnp.bfloat16)
    depth = len(pieces) * pieces[0].shape[0]
    return pl.pallas_call(
        partial(attend_kernel, len(pieces)),
        out_shape=(
            wide,
            wide,
            wide,
            jax.ShapeDtypeStruct((rows, width), jnp.bfloat16),
            jax.ShapeDtypeStruct((8, width), jnp.float32),
        ),
        in_specs=[pl.BlockSpec(memory_space=VMEM)] * (2 + len(pieces)),
        out_specs=[pl.BlockSpec(memory_space=VMEM)] * 5,
        scratch_shapes=[
            pltpu.VMEM((depth, pieces[0].shape[1]), jnp.bfloat16),
            pltpu.VMEM((rows, 2 * width), jnp.bfloat16),
        ],
        compiler_params=params(26),
        name="attend",
    )(x, labels, *pieces)


def attend_back_kernel(qx, kx, vx, dox, packed, total):
    rows = qx.shape[0]
    width = packed.shape[1] // 3

    def one_pair(pair, carry):
        heads = [pl.ds(pl.multiple_of((2 * pair + side) * LANES, LANES), LANES) for side in range(2)]
        spots = [pl.ds(pl.multiple_of(kind * width + pair * LANES, LANES), LANES) for kind in range(3)]
        for at, size in row_chunks(rows, TILE):
            span = pl.ds(at, size)
            low = lax.broadcasted_iota(jnp.int32, (size, LANES), 1) < HALF
            got = []
            for side in range(2):
                head = heads[side]
                keys = kx[span, head]
                queries = qx[:, head]
                upstream = dox[:, head]
                attention = jnp.exp(dot(keys, queries, 1, 1))
                grad = dot(vx[span, head], upstream, 1, 1)
                scores = (attention * grad).astype(jnp.bfloat16)
                got.append((dot(scores, queries, 1, 0), dot(attention.astype(jnp.bfloat16), upstream, 1, 0)))
                part = dot(scores, keys, 0, 0)
                if at == 0:
                    total[side] = part
                else:
                    total[side] += part
            packed[span, spots[1]] = jnp.where(low, got[0][0], got[1][0]).astype(jnp.bfloat16)
            packed[span, spots[2]] = jnp.where(low, got[0][1], got[1][1]).astype(jnp.bfloat16)
        low = lax.broadcasted_iota(jnp.int32, (rows, LANES), 1) < HALF
        packed[:, spots[0]] = (jnp.where(low, total[0], total[1]) * (1.0 / math.sqrt(HEAD_DIM))).astype(jnp.bfloat16)
        return carry

    lax.fori_loop(0, width // LANES, one_pair, 0)


def attend_back(qx, kx, vx, dox):
    rows, wide = qx.shape
    return pl.pallas_call(
        attend_back_kernel,
        out_shape=jax.ShapeDtypeStruct((rows, 3 * wide // 2), jnp.bfloat16),
        in_specs=[pl.BlockSpec(memory_space=VMEM)] * 4,
        out_specs=pl.BlockSpec(memory_space=VMEM),
        scratch_shapes=[pltpu.VMEM((2, rows, LANES), jnp.float32)],
        compiler_params=params(24),
        name="attend_back",
    )(qx, kx, vx, dox)


def norm_back(grad, normed, scale, gain):
    scaled = grad * gain
    return scale * (
        scaled
        - jnp.mean(scaled, axis=-1, keepdims=True)
        - normed * jnp.mean(scaled * normed, axis=-1, keepdims=True)
    )


def feed_kernel(reps, count, deep_count, x, mixed, dy, gains, *refs):
    pieces = refs[:count]
    deep_pieces = refs[count : count + deep_count]
    outputs, dox, middle_grad, keep2, send2, norm_grads, *deep_out = refs[count + deep_count : -7]
    wide, contract, active, hidden_grad, second, middle_low, block = refs[-7:]
    rows, width = x.shape
    hidden = contract.shape[0]
    wide_part = slice(0, width + hidden)
    assemble(pieces, wide, wide_part)
    if deep_count:
        assemble(deep_pieces, contract, slice(None))
    else:
        assemble_deep(pieces, contract, width + hidden, reps)
    gain, bias = gains[2:3], gains[3:4]
    gain_sum = jnp.zeros((1, width), jnp.float32)
    bias_sum = jnp.zeros((1, width), jnp.float32)
    for at, size in row_chunks(rows, 352):
        span = pl.ds(at, size)
        middle = x[span].astype(jnp.float32) + dot(mixed[span], wide[:, :width], 1, 0)
        normed, scale = normalize(middle)
        low = (normed * gain + bias).astype(jnp.bfloat16)
        second[span] = low
        result = middle
        back = jnp.zeros_like(middle)
        for start in range(0, hidden, 512):
            part = slice(start, start + 512)
            from_expand = wide[:, width + start : width + start + 512]
            up = dot(low, from_expand, 1, 0)
            square = up * up
            bend = jnp.tanh(0.7978845608028654 * up * (1.0 + 0.044715 * square))
            half = 0.5 * (1.0 + bend)
            act = (up * half).astype(jnp.bfloat16)
            active[span, part] = act
            slope = half + 0.5 * up * (1.0 - bend * bend) * (0.7978845608028654 * (1.0 + 3 * 0.044715 * square))
            down = (dot(dy[span], contract[part], 1, 1) * slope).astype(jnp.bfloat16)
            hidden_grad[span, part] = down
            result = result + dot(act, contract[part], 1, 0)
            back = back + dot(down, from_expand, 1, 1)
        outputs[span] = result.astype(jnp.bfloat16)
        gain_sum = gain_sum + jnp.sum(back * normed, axis=0, keepdims=True)
        bias_sum = bias_sum + jnp.sum(back, axis=0, keepdims=True)
        grad = dy[span].astype(jnp.float32) + norm_back(back, normed, scale, gain)
        middle_grad[span] = grad
        grad_low = grad.astype(jnp.bfloat16)
        middle_low[span] = grad_low
        mixed_grad = dot(grad_low, wide[:, :width], 1, 1).astype(jnp.bfloat16).astype(jnp.float32)
        lane = lax.broadcasted_iota(jnp.int32, (size, LANES), 1)
        left = lane < HALF
        feature = lane % HALF
        for pair in range(width // LANES):
            columns = slice(pair * LANES, (pair + 1) * LANES)
            piece = mixed_grad[:, columns]
            product = piece * mixed[span, columns].astype(jnp.float32)
            for side in range(2):
                mine = left if side == 0 else ~left
                delta = -jnp.sum(jnp.where(mine, product, 0.0), axis=1, keepdims=True)
                one = delta.astype(jnp.bfloat16).astype(jnp.float32)
                two = (delta - one).astype(jnp.bfloat16).astype(jnp.float32)
                three = delta - one - two
                extra = jnp.where(feature == 0, one, jnp.where(feature == 1, two, jnp.where(feature == 2, three, 0.0)))
                head = (2 * pair + side) * LANES
                dox[span, head : head + LANES] = jnp.where(mine, piece, extra).astype(jnp.bfloat16)
    norm_grads[...] = jnp.concatenate([gain_sum, bias_sum, jnp.zeros((6, width), jnp.float32)], axis=0)
    plane = keep2.shape[0]
    deep = hidden // (2 * plane)
    each = 512 // (2 * deep)
    for start in range(0, plane, each):
        at = 2 * deep * start
        block[...] = dot(active[:, at : at + 512], dy[...], 0, 0)
        planes = pl.ds(start, each)
        if deep_count:
            split_rows(block, deep_out[0].at[planes], deep_out[1].at[planes], slice(0, width))
        else:
            split_deep(block, keep2.at[planes], send2.at[planes], width + hidden, reps)
    block[...] = dot(mixed[...], middle_low[...], 0, 0)
    split_rows(block, keep2, send2, slice(0, width))
    for start in range(0, hidden, 512):
        block[...] = dot(second[...], hidden_grad[:, start : start + 512], 0, 0)
        split_rows(block, keep2, send2, slice(width + start, width + start + 512))


def feed(reps, x, mixed, dy, gains, pieces, deep_pieces):
    rows, width = x.shape
    plane = len(pieces) // 2
    deep = pieces[0].shape[0]
    columns = pieces[0].shape[1]
    hidden = 4 * width
    out_shape = [
        jax.ShapeDtypeStruct((rows, width), jnp.bfloat16),
        jax.ShapeDtypeStruct((rows, 2 * width), jnp.bfloat16),
        jax.ShapeDtypeStruct((rows, width), jnp.float32),
        jax.ShapeDtypeStruct((plane, deep, columns), jnp.float32),
        jax.ShapeDtypeStruct((plane, deep, columns), jnp.bfloat16),
        jax.ShapeDtypeStruct((8, width), jnp.float32),
    ]
    if deep_pieces:
        out_shape.append(jax.ShapeDtypeStruct((plane, 4 * deep, width), jnp.float32))
        out_shape.append(jax.ShapeDtypeStruct((plane, 4 * deep, width), jnp.bfloat16))
    return pl.pallas_call(
        partial(feed_kernel, reps, len(pieces), len(deep_pieces)),
        out_shape=out_shape,
        in_specs=[pl.BlockSpec(memory_space=VMEM)] * (4 + len(pieces) + len(deep_pieces)),
        out_specs=[pl.BlockSpec(memory_space=VMEM)] * len(out_shape),
        scratch_shapes=[
            pltpu.VMEM((width, width + hidden), jnp.bfloat16),
            pltpu.VMEM((hidden, width), jnp.bfloat16),
            pltpu.VMEM((rows, hidden), jnp.bfloat16),
            pltpu.VMEM((rows, hidden), jnp.bfloat16),
            pltpu.VMEM((rows, width), jnp.bfloat16),
            pltpu.VMEM((rows, width), jnp.bfloat16),
            pltpu.VMEM((width, 512), jnp.float32),
        ],
        compiler_params=params(46),
        name="feed",
    )(x, mixed, dy, gains, *pieces, *deep_pieces)


def project_back_kernel(x, packed, gains, keep, send, first, block):
    rows, width = x.shape
    gain, bias = gains[0:1], gains[1:2]
    for at, size in row_chunks(rows, 352):
        span = pl.ds(at, size)
        normed, _ = normalize(x[span].astype(jnp.float32))
        first[span] = (normed * gain + bias).astype(jnp.bfloat16)
    for start in range(0, packed.shape[1], 512):
        block[...] = dot(first[...], packed[:, start : start + 512], 0, 0)
        split_rows(block, keep, send, slice(start, start + 512))


def project_back(x, packed, gains, plane, deep):
    rows, width = x.shape
    shape = (plane, deep, packed.shape[1])
    return pl.pallas_call(
        project_back_kernel,
        out_shape=(jax.ShapeDtypeStruct(shape, jnp.float32), jax.ShapeDtypeStruct(shape, jnp.bfloat16)),
        in_specs=[pl.BlockSpec(memory_space=VMEM)] * 3,
        out_specs=[pl.BlockSpec(memory_space=VMEM)] * 2,
        scratch_shapes=[pltpu.VMEM((rows, width), jnp.bfloat16), pltpu.VMEM((width, 512), jnp.float32)],
        compiler_params=params(16),
        name="project_back",
    )(x, packed, gains)


def input_back_kernel(x, packed, gains, middle_grad, *refs):
    pieces = refs[:-3]
    grad_in, norm_grads, weight = refs[-3:]
    rows, width = x.shape
    assemble(pieces, weight, slice(None))
    gain = gains[0:1]
    gain_sum = jnp.zeros((1, width), jnp.float32)
    bias_sum = jnp.zeros((1, width), jnp.float32)
    for at, size in row_chunks(rows, 352):
        span = pl.ds(at, size)
        normed, scale = normalize(x[span].astype(jnp.float32))
        back = dot(packed[span], weight[:, : 3 * width], 1, 1)
        gain_sum = gain_sum + jnp.sum(back * normed, axis=0, keepdims=True)
        bias_sum = bias_sum + jnp.sum(back, axis=0, keepdims=True)
        grad_in[span] = (middle_grad[span] + norm_back(back, normed, scale, gain)).astype(jnp.bfloat16)
    norm_grads[...] = jnp.concatenate([gain_sum, bias_sum, jnp.zeros((6, width), jnp.float32)], axis=0)


def input_back(x, packed, gains, middle_grad, pieces):
    rows, width = x.shape
    return pl.pallas_call(
        input_back_kernel,
        out_shape=(jax.ShapeDtypeStruct((rows, width), jnp.bfloat16), jax.ShapeDtypeStruct((8, width), jnp.float32)),
        in_specs=[pl.BlockSpec(memory_space=VMEM)] * (4 + len(pieces)),
        out_specs=[pl.BlockSpec(memory_space=VMEM)] * 2,
        scratch_shapes=[pltpu.VMEM((width, pieces[0].shape[1]), jnp.bfloat16)],
        compiler_params=params(18),
        name="input_back",
    )(x, packed, gains, middle_grad, *pieces)


def column_kernel(*refs):
    reps = len(refs) - 1
    out = refs[-1]
    z = lax.axis_index("rep")
    rows = refs[0].shape[0]
    got = [ref[...].astype(jnp.float32) for ref in refs[:-1]]
    parts = []
    for j in range(reps):
        part = got[0]
        for k in range(1, reps):
            part = jnp.where(lax.rem(z + reps - k, reps) == j, got[k], part)
        parts.append(part)
    out[...] = jnp.concatenate(parts, axis=0).astype(out.dtype)


def column_of(shards):
    rows, cols = shards[0].shape
    reps = len(shards)
    return pl.pallas_call(
        column_kernel,
        out_shape=jax.ShapeDtypeStruct((reps * rows, cols), shards[0].dtype),
        in_specs=[pl.BlockSpec(memory_space=VMEM)] * reps,
        out_specs=pl.BlockSpec(memory_space=VMEM),
        compiler_params=params(4),
        name="column",
    )(*shards)


def chip_sum_kernel(keep, got, own, *low):
    p = plane_index()
    own[...] = keep[p] + got[p].astype(jnp.float32)
    for m, ref in enumerate(low, 1):
        ref[...] = (keep[p ^ m] + got[p ^ m].astype(jnp.float32)).astype(jnp.bfloat16)


def chip_sum(keep, got):
    plane, rows, cols = keep.shape
    block = 1536
    part = pl.BlockSpec((rows, block), lambda i: (0, i))
    whole = pl.BlockSpec((plane, rows, block), lambda i: (0, 0, i))
    return pl.pallas_call(
        chip_sum_kernel,
        grid=(cols // block,),
        out_shape=[jax.ShapeDtypeStruct((rows, cols), jnp.float32)]
        + [jax.ShapeDtypeStruct((rows, cols), jnp.bfloat16)] * (plane - 1),
        in_specs=[whole, whole],
        out_specs=[part] * plane,
        compiler_params=params(12),
        name="chip_sum",
    )(keep, got)


def plane_sum_kernel(own, *refs):
    plane = sum(1 for ref in refs if ref.shape == own.shape) + 1
    got, out, low = refs[: plane - 1], refs[plane - 1], refs[plane:]
    reps = len(low) + 1
    rows = out.shape[0]
    z = lax.axis_index("rep")
    total = own[...]
    for ref in got:
        total = total + ref[...].astype(jnp.float32)
    for k, ref in enumerate((out, *low)):
        part = total[:rows]
        for j in range(1, reps):
            part = jnp.where(lax.rem(z + k, reps) == j, total[j * rows : (j + 1) * rows], part)
        ref[...] = part.astype(ref.dtype)


def plane_sum(own, got, reps):
    rows, cols = own.shape
    block = 1536
    part = pl.BlockSpec((rows, block), lambda i: (0, i))
    small = pl.BlockSpec((rows // reps, block), lambda i: (0, i))
    return pl.pallas_call(
        plane_sum_kernel,
        grid=(cols // block,),
        out_shape=[jax.ShapeDtypeStruct((rows // reps, cols), jnp.float32)]
        + [jax.ShapeDtypeStruct((rows // reps, cols), jnp.bfloat16)] * (reps - 1),
        in_specs=[part] * (1 + len(got)),
        out_specs=[small] * reps,
        compiler_params=params(10),
        name="plane_sum",
    )(own, *got)


def full_sum(value):
    return jnp.sum(jnp.sum(value, axis=1, keepdims=True), axis=0, keepdims=True)


def moments_kernel(pieces_of, first_index, reps, *refs):
    n = len(pieces_of)
    grads = refs[: reps if reps else 1]
    if reps:
        total = grads[0][...]
        for ref in grads[1:]:
            total = total + ref[...].astype(jnp.float32)
        extra = refs[reps]
        arrays = refs[reps + 1 :]
    weights, firsts, seconds = arrays[:n], arrays[n : 2 * n], arrays[2 * n : 3 * n]
    momenta, variances, directions = arrays[3 * n : 4 * n], arrays[4 * n : 5 * n], arrays[5 * n : 6 * n]
    sums = arrays[6 * n]
    lane = lax.broadcasted_iota(jnp.int32, (1, LANES), 1)
    row = jnp.zeros((1, LANES), jnp.float32)
    for i, parts in enumerate(pieces_of):
        weight_sum = jnp.zeros((1, 1), jnp.float32)
        step_sum = jnp.zeros((1, 1), jnp.float32)
        for at, size, columns in parts:
            rows = slice(at, at + size)
            gradient = extra[...] if columns is None else total[:, columns[0] : columns[1]]
            weight = weights[i][rows]
            momentum = BETA * firsts[i][rows] + (1.0 - BETA) * gradient
            variance = BETA * seconds[i][rows] + (1.0 - BETA) * gradient * gradient
            direction = momentum / (jnp.sqrt(variance) + ADAM_EPSILON) + DECAY * weight
            momenta[i][rows] = momentum
            variances[i][rows] = variance
            directions[i][rows] = direction
            weight_sum = weight_sum + full_sum(weight * weight)
            step_sum = step_sum + full_sum(direction * direction)
        row = jnp.where(lane == first_index[i], weight_sum, row)
        row = jnp.where(lane == 5 + first_index[i], step_sum, row)
    sums[...] = row


def moments(pieces_of, first_index, grads, extra, weights, firsts, seconds):
    arrays = [*grads, extra, *weights, *firsts, *seconds]
    shapes = [jax.ShapeDtypeStruct(weight.shape, jnp.float32) for weight in weights]
    outs = pl.pallas_call(
        partial(moments_kernel, pieces_of, first_index, len(grads)),
        out_shape=shapes * 3 + [jax.ShapeDtypeStruct((1, LANES), jnp.float32)],
        in_specs=[pl.BlockSpec(memory_space=VMEM)] * len(arrays),
        out_specs=[pl.BlockSpec(memory_space=VMEM)] * (3 * len(weights) + 1),
        compiler_params=params(8),
        name="moments",
    )(*arrays)
    n = len(weights)
    return outs[:n], outs[n : 2 * n], outs[2 * n : 3 * n], outs[3 * n]


def update_kernel(n, sums, *refs):
    weights, directions, updated, table = refs[:n], refs[n : 2 * n], refs[2 * n : 3 * n], refs[3 * n]
    norms = jnp.sqrt(jnp.sum(sums[...], axis=0, keepdims=True))
    row = lax.broadcasted_iota(jnp.int32, table.shape, 0)
    lane = lax.broadcasted_iota(jnp.int32, table.shape, 1)
    out = jnp.zeros(table.shape, jnp.float32)
    for i in range(n):
        weight_norm = norms[:, i : i + 1]
        step_norm = norms[:, 5 + i : 6 + i]
        ratio = weight_norm / step_norm
        updated[i][...] = weights[i][...] - RATE * ratio * directions[i][...]
        column = jnp.where(row == 0, weight_norm, jnp.where(row == 1, step_norm, ratio))
        out = jnp.where(lane == i, column, out)
    table[...] = out


def update(sums, weights, directions):
    n = len(weights)
    outs = pl.pallas_call(
        partial(update_kernel, n),
        out_shape=[jax.ShapeDtypeStruct(weight.shape, jnp.float32) for weight in weights]
        + [jax.ShapeDtypeStruct((8, LANES), jnp.float32)],
        in_specs=[pl.BlockSpec(memory_space=VMEM)] * (1 + 2 * n),
        out_specs=[pl.BlockSpec(memory_space=VMEM)] * (n + 1),
        compiler_params=params(6),
        name="update",
    )(sums, *weights, *directions)
    return outs[:n], outs[n][:3, :n]


AXES = ("dp", "rep")


class Layout:
    def __init__(self, mesh):
        self.dp = mesh.shape["dp"]
        self.rep = mesh.shape["rep"]
        self.plane = self.dp // 2

    def permute(self, value, move):
        pairs = []
        for p in range(self.plane):
            for c in range(2):
                for z in range(self.rep):
                    q, d, w = move(p, c, z)
                    pairs.append(((p * 2 + c) * self.rep + z, (q * 2 + d) * self.rep + w))
        return lax.ppermute(value, AXES, pairs)

    def to_core(self, value):
        return self.permute(value, lambda p, c, z: (p, 1 - c, z))

    def to_plane(self, value, m):
        return self.permute(value, lambda p, c, z: (p ^ m, c, z))

    def to_rep(self, value, k):
        return self.permute(value, lambda p, c, z: (p, c, (z + k) % self.rep))

    def place(self):
        dp = lax.axis_index("dp")
        return dp // 2, dp % 2, lax.axis_index("rep")


def over_rep(lay, shard):
    return [shard] + [lay.to_rep(shard, k) for k in range(1, lay.rep)]


def over_plane(lay, column):
    return [column] + [lay.to_plane(column, m) for m in range(1, lay.plane)]


def over_core(lay, blocks):
    return blocks + [lay.to_core(block) for block in blocks]


def after(values, others):
    count = len(values)
    return list(lax.optimization_barrier((*values, *others))[:count])


def exchange(lay, value):
    return lax.all_to_all(value, AXES, 0, 0)


def body(
    lay,
    inputs,
    segments,
    cotangent,
    attend_in,
    attend_out,
    expand,
    contract,
    layer_norms,
    moment_in,
    moment_out,
    moment_expand,
    moment_contract,
    moment_norms,
    square_in,
    square_out,
    square_expand,
    square_contract,
    square_norms,
):
    masters = (attend_in, attend_out, expand, contract, layer_norms)
    width = attend_in.shape[1]
    depth = attend_out.shape[1]
    hidden = expand.shape[1]
    own = attend_in.shape[0]
    count = lay.dp * lay.rep
    plain = own % 16 == 0
    norm_rows = jnp.pad(layer_norms.astype(jnp.bfloat16).T, ((0, 0), (0, LANES - 4)))
    shard1 = jnp.concatenate([attend_in.astype(jnp.bfloat16), norm_rows], axis=1)
    column1 = over_rep(lay, shard1)
    rows = inputs.shape[1]
    memory = rows - segments.shape[1]
    pad = -rows % 32
    attend_out_, expand_, contract_, inputs_, cotangent_, segments_ = after(
        [attend_out, expand, contract, inputs, cotangent, segments], [shard1]
    )
    labels = jnp.concatenate(
        [jnp.full((memory,), -1, jnp.int32), segments_[0], jnp.full((pad,), -2, jnp.int32)]
    )
    labels = jnp.broadcast_to(labels[:, None], (labels.shape[0], LANES))
    x = jnp.pad(inputs_[0], ((0, pad), (0, 0)))
    dy = jnp.pad(cotangent_[0], ((0, pad), (0, 0)))
    deep = [contract_[j * own : (j + 1) * own] for j in range(4)]
    shard2 = jnp.concatenate([part.astype(jnp.bfloat16) for part in (attend_out_, expand_, *deep)], axis=1)
    x, dy, labels, shard2 = after([x, dy, labels, shard2], column1[1:])
    column2 = over_rep(lay, shard2)
    blocks1 = over_plane(lay, column_of(column1))
    blocks2 = over_plane(lay, column_of(after(column2, blocks1)))
    pieces1 = over_core(lay, blocks1)
    *pieces1, x, labels = after([*pieces1, x, labels], blocks2[:1])
    qx, kx, vx, mixed, gains = attend(x, labels, pieces1)
    pieces2 = over_core(lay, after(blocks2, [mixed]))
    deep_pieces = []
    if not plain:
        first = depth + hidden
        for piece in pieces2:
            part = piece[:, first:].reshape(lay.rep, own, 4, depth).transpose(0, 2, 1, 3)
            deep_pieces.append(part.reshape(-1, depth))
    outputs, dox, middle_grad, keep2, send2, second_norms, *deep_out = feed(
        lay.rep, x, mixed, dy, gains, pieces2, deep_pieces
    )
    if not plain:
        keep2, send2 = [
            jnp.concatenate(
                [
                    wide[:, :, : depth + hidden],
                    part.reshape(lay.plane, lay.rep, 4, own, depth).transpose(0, 1, 3, 2, 4).reshape(lay.plane, -1, 4 * depth),
                ],
                axis=2,
            )
            for wide, part in zip((keep2, send2), deep_out)
        ]
    own2, *low2 = chip_sum(keep2, lay.to_core(send2))
    got2 = [lay.to_plane(part, m) for m, part in enumerate(low2, 1)]
    (dox,) = after([dox], low2)
    packed = attend_back(qx, kx, vx, dox)
    own2, *got2 = after([own2, *got2], [packed])
    own2, *low2 = plane_sum(own2, got2, lay.rep)
    got2 = [lay.to_rep(part, k) for k, part in enumerate(low2, 1)]
    (packed_,) = after([packed], low2)
    keep1, send1 = project_back(x, packed_, gains, lay.plane, lay.rep * own)
    own1, *low1 = chip_sum(keep1, lay.to_core(send1))
    got1 = [lay.to_plane(part, m) for m, part in enumerate(low1, 1)]
    (packed_,) = after([packed], low1)
    input_gradient, first_norms = input_back(x, packed_, gains, middle_grad, pieces1)
    norm_grads = jnp.concatenate([first_norms[:2], second_norms[:2]], axis=0)
    norm_grads = jnp.sum(exchange(lay, norm_grads.reshape(4, count, -1).transpose(1, 0, 2)), axis=0)
    own2, *got2 = after([own2, *got2], [first_norms])
    spans = [[(0, own, (0, depth))], [(0, own, (depth, depth + hidden))]]
    spans.append([(j * own, own, (depth + hidden + j * depth, depth + hidden + (j + 1) * depth)) for j in range(4)])
    momenta2, variances2, directions2, sums2 = moments(
        spans, (1, 2, 3), [own2, *got2], jnp.zeros((8, LANES), jnp.float32), masters[1:4],
        (moment_out, moment_expand, moment_contract), (square_out, square_expand, square_contract),
    )
    own1, *got1 = after([own1, *got1], [sums2])
    own1, *low1 = plane_sum(own1, got1, lay.rep)
    got1 = [lay.to_rep(part, k) for k, part in enumerate(low1, 1)]
    momenta1, variances1, directions1, sums1 = moments(
        [[(0, own, (0, width))], [(0, 4, None)]], (0, 4), [own1, *got1], norm_grads, (attend_in, layer_norms),
        (moment_in, moment_norms), (square_in, square_norms),
    )
    sums = exchange(lay, jnp.broadcast_to((sums1 + sums2)[None], (count, 1, LANES)))
    directions = (directions1[0], *directions2, directions1[1])
    updated, trust_table = update(sums[:, 0], masters, directions)
    outputs = outputs[None, :rows]
    input_gradient = input_gradient[None, :rows]
    momenta = (momenta1[0], *momenta2, momenta1[1])
    variances = (variances1[0], *variances2, variances1[1])
    return (outputs, input_gradient, *updated, *momenta, *variances, trust_table)


def solution(mesh):
    placed = (
        P(("dp", "rep"), None, None),
        P(("dp", "rep"), None),
        P(("dp", "rep"), None, None),
        P(("dp", "rep"), None),
        P(("dp", "rep"), None),
        P(("dp", "rep"), None),
        P(("dp", "rep"), None),
        P(None, ("dp", "rep")),
        P(("dp", "rep"), None),
        P(("dp", "rep"), None),
        P(("dp", "rep"), None),
        P(("dp", "rep"), None),
        P(None, ("dp", "rep")),
        P(("dp", "rep"), None),
        P(("dp", "rep"), None),
        P(("dp", "rep"), None),
        P(("dp", "rep"), None),
        P(None, ("dp", "rep")),
    )
    return jax.shard_map(
        partial(body, Layout(mesh)),
        mesh=mesh,
        in_specs=placed,
        out_specs=(
            P(("dp", "rep"), None, None),
            P(("dp", "rep"), None, None),
            P(("dp", "rep"), None),
            P(("dp", "rep"), None),
            P(("dp", "rep"), None),
            P(("dp", "rep"), None),
            P(None, ("dp", "rep")),
            P(("dp", "rep"), None),
            P(("dp", "rep"), None),
            P(("dp", "rep"), None),
            P(("dp", "rep"), None),
            P(None, ("dp", "rep")),
            P(("dp", "rep"), None),
            P(("dp", "rep"), None),
            P(("dp", "rep"), None),
            P(("dp", "rep"), None),
            P(None, ("dp", "rep")),
            P(),
        ),
        check_vma=False,
    )
```

```python
from functools import partial
import math

import jax
import jax.numpy as jnp
from jax import lax
from jax.experimental import pallas as pl
from jax.experimental.pallas import tpu as pltpu
from jax.sharding import PartitionSpec as P

HEADS = 8
HEAD_DIM = 64


EPSILON = 1e-05
ADAM_EPSILON = 1e-06
DECAY = 0.01
RATE = 0.5
BETA = 0.5
LANES = 128
HALF = 64
BIG = 1e30
FEATS = 4
TILE = 256
THIN = 32
CHUNK = 352
VMEM = pltpu.MemorySpace.VMEM


def params(mebibytes):
    return pltpu.CompilerParams(vmem_limit_bytes=mebibytes * 1024 * 1024)


def dot(a, b, ca, cb):
    return lax.dot_general(a, b, (((ca,), (cb,)), ((), ())), preferred_element_type=jnp.float32)


def normalize(values):
    center = values - jnp.mean(values, axis=-1, keepdims=True)
    scale = lax.rsqrt(jnp.mean(center * center, axis=-1, keepdims=True) + EPSILON)
    return center * scale, scale


def core_index():
    return lax.rem(lax.axis_index("dp"), 2)


def plane_index():
    return lax.div(lax.axis_index("dp"), 2)


def block_at(m, other, rows):
    core = core_index()
    side = 1 - core if other else core
    return pl.multiple_of((2 * (plane_index() ^ m) + side) * rows, rows)


def assemble(pieces, full_ref, columns):
    plane = len(pieces) // 2
    for i, piece in enumerate(pieces):
        at = block_at(i % plane, i >= plane, piece.shape[0])
        full_ref[pl.ds(at, piece.shape[0]), :] = piece[:, columns]


def assemble_deep(pieces, full_ref, first, reps):
    plane = len(pieces) // 2
    width = full_ref.shape[1]
    for i, piece in enumerate(pieces):
        rows = piece.shape[0] // reps
        at = block_at(i % plane, i >= plane, 4 * piece.shape[0])
        for z in range(reps):
            for j in range(4):
                source = piece[z * rows : (z + 1) * rows, first + j * width : first + (j + 1) * width]
                full_ref[pl.ds(at + (4 * z + j) * rows, rows), :] = source


def split_rows(full_ref, keep_ref, send_ref, lanes):
    plane, rows, _ = keep_ref.shape
    core = core_index()
    for p in range(plane):
        at = pl.multiple_of((2 * p + core) * rows, rows)
        keep_ref[p, :, lanes] = full_ref[pl.ds(at, rows), :].astype(keep_ref.dtype)
        at = pl.multiple_of((2 * p + 1 - core) * rows, rows)
        send_ref[p, :, lanes] = full_ref[pl.ds(at, rows), :].astype(jnp.bfloat16)


def split_deep(full_ref, keep_ref, send_ref, first, reps):
    plane, rows, _ = keep_ref.shape
    width = full_ref.shape[1]
    core = core_index()
    each = rows // reps
    for p in range(plane):
        for side, target in ((core, keep_ref), (1 - core, send_ref)):
            base = pl.multiple_of((2 * p + side) * 4 * rows, 4 * rows)
            for z in range(reps):
                for j in range(4):
                    source = full_ref[pl.ds(base + (4 * z + j) * each, each), :]
                    columns = slice(first + j * width, first + (j + 1) * width)
                    target[p, z * each : (z + 1) * each, columns] = source.astype(target.dtype)


def row_chunks(rows, size):
    return [(at, min(size, rows - at)) for at in range(0, rows, size)]


def windows(rows):
    half = (rows - THIN) // 2
    span = half + THIN
    spans = [(at, TILE, 0, span) for at in range(0, half, TILE)]
    spans.append((half, THIN, 0, rows))
    return spans + [(at, TILE, half, span) for at in range(span, rows, TILE)]


def arrange_kernel(inputs, cotangent, segments, x, dy, labels, begin, room):
    tokens = segments.shape[1]
    half = tokens // 2
    memory = inputs.shape[0] - tokens
    segment = segments[...].astype(jnp.float32)
    ahead = pltpu.roll(jnp.broadcast_to(segment, (8, tokens)), tokens - half + 1, 1)[:1]
    lane = lax.broadcasted_iota(jnp.int32, (1, tokens), 1)
    fits = (segment == ahead) & (lane <= half)
    start = jnp.sum(jnp.where(fits, lane.astype(jnp.float32), 0.0), axis=1, keepdims=True)
    begin[...] = jnp.broadcast_to(start, begin.shape)
    row = lax.broadcasted_iota(jnp.int32, (half, LANES), 0).astype(jnp.float32)
    early = row < start
    thin = lax.broadcasted_iota(jnp.int32, (THIN, LANES), 0) < memory
    for source, target in ((inputs, x), (cotangent, dy)):
        for at in range(0, inputs.shape[1], LANES):
            columns = slice(at, at + LANES)
            room[: inputs.shape[0]] = source[:, columns].astype(jnp.float32)
            left, right = room[memory : memory + half], room[memory + half : memory + tokens]
            target[:half, columns] = jnp.where(early, right, left).astype(target.dtype)
            target[half : half + THIN, columns] = jnp.where(thin, room[:THIN], 0.0).astype(target.dtype)
            target[half + THIN :, columns] = jnp.where(early, left, right).astype(target.dtype)
    left = jnp.transpose(jnp.broadcast_to(segment[:, :half], (LANES, half)))
    right = jnp.transpose(jnp.broadcast_to(segment[:, half:], (LANES, half)))
    labels[:half] = jnp.where(early, right, left).astype(jnp.int32)
    labels[half : half + THIN] = jnp.where(thin, -1, -2)
    labels[half + THIN :] = jnp.where(early, left, right).astype(jnp.int32)


def arrange(inputs, cotangent, segments):
    width = inputs.shape[1]
    rows = segments.shape[1] + THIN
    return pl.pallas_call(
        arrange_kernel,
        out_shape=(
            jax.ShapeDtypeStruct((rows, width), inputs.dtype),
            jax.ShapeDtypeStruct((rows, width), inputs.dtype),
            jax.ShapeDtypeStruct((rows, LANES), jnp.int32),
            jax.ShapeDtypeStruct((8, LANES), jnp.float32),
        ),
        in_specs=[pl.BlockSpec(memory_space=VMEM)] * 3,
        out_specs=[pl.BlockSpec(memory_space=VMEM)] * 4,
        scratch_shapes=[pltpu.VMEM((rows, LANES), jnp.float32)],
        compiler_params=params(8),
        name="arrange",
    )(inputs, cotangent, segments)


def arrange_back_kernel(begin, first, second, first_out, second_out, room):
    rows = first_out.shape[0]
    half = (first.shape[0] - THIN) // 2
    memory = rows - 2 * half
    row = lax.broadcasted_iota(jnp.int32, (half, LANES), 0).astype(jnp.float32)
    early = row < begin[:1]
    for source, target in ((first, first_out), (second, second_out)):
        for at in range(0, first.shape[1], LANES):
            columns = slice(at, at + LANES)
            left = source[:half, columns].astype(jnp.float32)
            right = source[half + THIN :, columns].astype(jnp.float32)
            room[:THIN] = source[half : half + THIN, columns].astype(jnp.float32)
            room[memory : memory + half] = jnp.where(early, right, left)
            room[memory + half : rows] = jnp.where(early, left, right)
            target[:, columns] = room[:rows].astype(target.dtype)


def arrange_back(begin, first, second, rows):
    width = first.shape[1]
    return pl.pallas_call(
        arrange_back_kernel,
        out_shape=[jax.ShapeDtypeStruct((rows, width), first.dtype)] * 2,
        in_specs=[pl.BlockSpec(memory_space=VMEM)] * 3,
        out_specs=[pl.BlockSpec(memory_space=VMEM)] * 2,
        scratch_shapes=[pltpu.VMEM((first.shape[0], LANES), jnp.float32)],
        compiler_params=params(8),
        name="arrange_back",
    )(begin, first, second)


def attend_kernel(count, x, labels, *refs):
    pieces = refs[:count]
    qx, kx, vx, mixed, gains, weight, qs = refs[count:]
    rows = x.shape[0]
    width = mixed.shape[1]
    assemble(pieces, weight, slice(None))
    gains[...] = jnp.transpose(weight[:, 3 * width :].astype(jnp.float32))[:8]
    gain, bias = gains[0:1], gains[1:2]

    def one_chunk(i, carry):
        span = pl.ds(pl.multiple_of(i * CHUNK, CHUNK), CHUNK)
        normed, _ = normalize(x[span].astype(jnp.float32))
        first = (normed * gain + bias).astype(jnp.bfloat16)
        lane = lax.broadcasted_iota(jnp.int32, (CHUNK, LANES), 1)
        low = lane < HALF
        feature = lane % HALF
        label = labels[span]
        blocked = ((feature < FEATS) & (label >= 0) & (feature != label)) | (feature == FEATS)
        query_side = jnp.where(blocked, -BIG, 0.0)
        marked = ((feature < FEATS) & (feature == label)) | ((feature == FEATS) & (label == -2))
        key_side = jnp.where(marked | (feature > FEATS), 1.0, 0.0)
        sides = (query_side, key_side, jnp.ones_like(key_side))
        for kind, target in enumerate((qs, kx, vx)):
            whole = dot(first, weight[:, kind * width : (kind + 1) * width], 1, 0)
            whole = whole.astype(jnp.bfloat16).astype(jnp.float32)
            for pair in range(width // LANES):
                part = whole[:, pair * LANES : (pair + 1) * LANES]
                if kind == 0:
                    part = part * (1.0 / math.sqrt(HEAD_DIM))
                at = 2 * pair * LANES
                target[span, at : at + LANES] = jnp.where(low, part, sides[kind]).astype(jnp.bfloat16)
                target[span, at + LANES : at + 2 * LANES] = jnp.where(low, sides[kind], part).astype(jnp.bfloat16)
        return carry

    lax.fori_loop(0, rows // CHUNK, one_chunk, 0)

    def one_pair(pair, carry):
        columns = pl.ds(pl.multiple_of(pair * LANES, LANES), LANES)
        for at, size, key_at, key_size in windows(rows):
            span = pl.ds(at, size)
            seen = pl.ds(key_at, key_size)
            lane = lax.broadcasted_iota(jnp.int32, (size, LANES), 1)
            low = lane < HALF
            feature = lane % HALF
            got = []
            for side in range(2):
                head = pl.ds(pl.multiple_of((2 * pair + side) * LANES, LANES), LANES)
                queries = qs[span, head]
                scores = dot(queries, kx[seen, head], 1, 1)
                highest = jnp.max(scores, axis=1, keepdims=True)
                raised = jnp.exp(scores - highest).astype(jnp.bfloat16)
                found = dot(raised, vx[seen, head], 1, 0)
                total = -(highest + jnp.log(found))
                first = total.astype(jnp.bfloat16).astype(jnp.float32)
                second = (total - first).astype(jnp.bfloat16).astype(jnp.float32)
                third = total - first - second
                values = jnp.where(feature == 5, first, jnp.where(feature == 6, second, third))
                place = (feature > FEATS) & (feature < 8) & (low if side else ~low)
                qx[span, head] = jnp.where(place, values, queries.astype(jnp.float32)).astype(jnp.bfloat16)
                got.append(found)
            over = pltpu.roll(jnp.where(low, got[1], got[0]), HALF, 1)
            mixed[span, columns] = (jnp.where(low, got[0], got[1]) / over).astype(jnp.bfloat16)
        return carry

    lax.fori_loop(0, width // LANES, one_pair, 0)


def attend(x, labels, pieces):
    rows, width = x.shape
    wide = jax.ShapeDtypeStruct((rows, 2 * width), jnp.bfloat16)
    depth = len(pieces) * pieces[0].shape[0]
    return pl.pallas_call(
        partial(attend_kernel, len(pieces)),
        out_shape=(
            wide,
            wide,
            wide,
            jax.ShapeDtypeStruct((rows, width), jnp.bfloat16),
            jax.ShapeDtypeStruct((8, width), jnp.float32),
        ),
        in_specs=[pl.BlockSpec(memory_space=VMEM)] * (2 + len(pieces)),
        out_specs=[pl.BlockSpec(memory_space=VMEM)] * 5,
        scratch_shapes=[
            pltpu.VMEM((depth, pieces[0].shape[1]), jnp.bfloat16),
            pltpu.VMEM((rows, 2 * width), jnp.bfloat16),
        ],
        compiler_params=params(16),
        name="attend",
    )(x, labels, *pieces)


def attend_back_kernel(qx, kx, vx, dox, packed, total):
    rows = qx.shape[0]
    width = packed.shape[1] // 3

    def one_pair(pair, carry):
        heads = [pl.ds(pl.multiple_of((2 * pair + side) * LANES, LANES), LANES) for side in range(2)]
        spots = [pl.ds(pl.multiple_of(kind * width + pair * LANES, LANES), LANES) for kind in range(3)]
        total[...] = jnp.zeros_like(total)
        for at, size, query_at, query_size in windows(rows):
            span = pl.ds(at, size)
            seen = pl.ds(query_at, query_size)
            low = lax.broadcasted_iota(jnp.int32, (size, LANES), 1) < HALF
            got = []
            for side in range(2):
                head = heads[side]
                keys = kx[span, head]
                queries = qx[seen, head]
                upstream = dox[seen, head]
                attention = jnp.exp(dot(keys, queries, 1, 1))
                grad = dot(vx[span, head], upstream, 1, 1)
                scores = (attention * grad).astype(jnp.bfloat16)
                got.append((dot(scores, queries, 1, 0), dot(attention.astype(jnp.bfloat16), upstream, 1, 0)))
                total[side, seen] += dot(scores, keys, 0, 0)
            packed[span, spots[1]] = jnp.where(low, got[0][0], got[1][0]).astype(jnp.bfloat16)
            packed[span, spots[2]] = jnp.where(low, got[0][1], got[1][1]).astype(jnp.bfloat16)
        low = lax.broadcasted_iota(jnp.int32, (rows, LANES), 1) < HALF
        packed[:, spots[0]] = (jnp.where(low, total[0], total[1]) * (1.0 / math.sqrt(HEAD_DIM))).astype(jnp.bfloat16)
        return carry

    lax.fori_loop(0, width // LANES, one_pair, 0)


def attend_back(qx, kx, vx, dox):
    rows, wide = qx.shape
    return pl.pallas_call(
        attend_back_kernel,
        out_shape=jax.ShapeDtypeStruct((rows, 3 * wide // 2), jnp.bfloat16),
        in_specs=[pl.BlockSpec(memory_space=VMEM)] * 4,
        out_specs=pl.BlockSpec(memory_space=VMEM),
        scratch_shapes=[pltpu.VMEM((2, rows, LANES), jnp.float32)],
        compiler_params=params(16),
        name="attend_back",
    )(qx, kx, vx, dox)


def norm_back(grad, normed, scale, gain):
    scaled = grad * gain
    return scale * (
        scaled
        - jnp.mean(scaled, axis=-1, keepdims=True)
        - normed * jnp.mean(scaled * normed, axis=-1, keepdims=True)
    )


def feed_kernel(reps, count, deep_count, x, mixed, dy, gains, *refs):
    pieces = refs[:count]
    deep_pieces = refs[count : count + deep_count]
    outputs, dox, middle_grad, keep2, send2, norm_grads, *deep_out = refs[count + deep_count : -7]
    wide, contract, active, hidden_grad, second, middle_low, block = refs[-7:]
    rows, width = x.shape
    hidden = contract.shape[0]
    wide_part = slice(0, width + hidden)
    assemble(pieces, wide, wide_part)
    if deep_count:
        assemble(deep_pieces, contract, slice(None))
    else:
        assemble_deep(pieces, contract, width + hidden, reps)
    gain, bias = gains[2:3], gains[3:4]
    zero = jnp.zeros((1, width), jnp.float32)

    def one_chunk(i, carry):
        gain_sum, bias_sum = carry
        span = pl.ds(pl.multiple_of(i * CHUNK, CHUNK), CHUNK)
        middle = x[span].astype(jnp.float32) + dot(mixed[span], wide[:, :width], 1, 0)
        normed, scale = normalize(middle)
        low = (normed * gain + bias).astype(jnp.bfloat16)
        second[span] = low
        result = middle
        back = jnp.zeros_like(middle)
        for start in range(0, hidden, 512):
            part = slice(start, start + 512)
            from_expand = wide[:, width + start : width + start + 512]
            up = dot(low, from_expand, 1, 0)
            square = up * up
            bend = jnp.tanh(0.7978845608028654 * up * (1.0 + 0.044715 * square))
            half = 0.5 * (1.0 + bend)
            act = (up * half).astype(jnp.bfloat16)
            active[span, part] = act
            slope = half + 0.5 * up * (1.0 - bend * bend) * (0.7978845608028654 * (1.0 + 3 * 0.044715 * square))
            down = (dot(dy[span], contract[part], 1, 1) * slope).astype(jnp.bfloat16)
            hidden_grad[span, part] = down
            result = result + dot(act, contract[part], 1, 0)
            back = back + dot(down, from_expand, 1, 1)
        outputs[span] = result.astype(jnp.bfloat16)
        gain_sum = gain_sum + jnp.sum(back * normed, axis=0, keepdims=True)
        bias_sum = bias_sum + jnp.sum(back, axis=0, keepdims=True)
        grad = dy[span].astype(jnp.float32) + norm_back(back, normed, scale, gain)
        middle_grad[span] = grad
        grad_low = grad.astype(jnp.bfloat16)
        middle_low[span] = grad_low
        mixed_grad = dot(grad_low, wide[:, :width], 1, 1).astype(jnp.bfloat16).astype(jnp.float32)
        lane = lax.broadcasted_iota(jnp.int32, (CHUNK, LANES), 1)
        left = lane < HALF
        feature = lane % HALF
        for pair in range(width // LANES):
            columns = slice(pair * LANES, (pair + 1) * LANES)
            piece = mixed_grad[:, columns]
            product = piece * mixed[span, columns].astype(jnp.float32)
            for side in range(2):
                mine = left if side == 0 else ~left
                delta = -jnp.sum(jnp.where(mine, product, 0.0), axis=1, keepdims=True)
                one = delta.astype(jnp.bfloat16).astype(jnp.float32)
                two = (delta - one).astype(jnp.bfloat16).astype(jnp.float32)
                three = delta - one - two
                extra = jnp.where(feature == 0, one, jnp.where(feature == 1, two, jnp.where(feature == 2, three, 0.0)))
                head = (2 * pair + side) * LANES
                dox[span, head : head + LANES] = jnp.where(mine, piece, extra).astype(jnp.bfloat16)
        return gain_sum, bias_sum

    gain_sum, bias_sum = lax.fori_loop(0, rows // CHUNK, one_chunk, (zero, zero))
    norm_grads[...] = jnp.concatenate([gain_sum, bias_sum, jnp.zeros((6, width), jnp.float32)], axis=0)
    plane = keep2.shape[0]
    deep = hidden // (2 * plane)
    each = 512 // (2 * deep)

    def one_block(i, carry):
        columns = pl.ds(pl.multiple_of(i * 512, 512), 512)
        block[...] = dot(active[:, columns], dy[...], 0, 0)
        planes = pl.ds(i * each, each)
        if deep_count:
            split_rows(block, deep_out[0].at[planes], deep_out[1].at[planes], slice(0, width))
        else:
            split_deep(block, keep2.at[planes], send2.at[planes], width + hidden, reps)
        block[...] = dot(second[...], hidden_grad[:, columns], 0, 0)
        split_rows(block, keep2, send2, pl.ds(pl.multiple_of(width + i * 512, 512), 512))
        return carry

    lax.fori_loop(0, hidden // 512, one_block, 0)
    block[...] = dot(mixed[...], middle_low[...], 0, 0)
    split_rows(block, keep2, send2, slice(0, width))


def feed(reps, x, mixed, dy, gains, pieces, deep_pieces):
    rows, width = x.shape
    plane = len(pieces) // 2
    deep = pieces[0].shape[0]
    columns = pieces[0].shape[1]
    hidden = 4 * width
    out_shape = [
        jax.ShapeDtypeStruct((rows, width), jnp.bfloat16),
        jax.ShapeDtypeStruct((rows, 2 * width), jnp.bfloat16),
        jax.ShapeDtypeStruct((rows, width), jnp.float32),
        jax.ShapeDtypeStruct((plane, deep, columns), jnp.bfloat16),
        jax.ShapeDtypeStruct((plane, deep, columns), jnp.bfloat16),
        jax.ShapeDtypeStruct((8, width), jnp.float32),
    ]
    if deep_pieces:
        out_shape.append(jax.ShapeDtypeStruct((plane, 4 * deep, width), jnp.bfloat16))
        out_shape.append(jax.ShapeDtypeStruct((plane, 4 * deep, width), jnp.bfloat16))
    return pl.pallas_call(
        partial(feed_kernel, reps, len(pieces), len(deep_pieces)),
        out_shape=out_shape,
        in_specs=[pl.BlockSpec(memory_space=VMEM)] * (4 + len(pieces) + len(deep_pieces)),
        out_specs=[pl.BlockSpec(memory_space=VMEM)] * len(out_shape),
        scratch_shapes=[
            pltpu.VMEM((width, width + hidden), jnp.bfloat16),
            pltpu.VMEM((hidden, width), jnp.bfloat16),
            pltpu.VMEM((rows, hidden), jnp.bfloat16),
            pltpu.VMEM((rows, hidden), jnp.bfloat16),
            pltpu.VMEM((rows, width), jnp.bfloat16),
            pltpu.VMEM((rows, width), jnp.bfloat16),
            pltpu.VMEM((width, 512), jnp.float32),
        ],
        compiler_params=params(30),
        name="feed",
    )(x, mixed, dy, gains, *pieces, *deep_pieces)


def project_back_kernel(x, packed, gains, first_norms, second_norms, keep, send, first, block):
    rows, width = x.shape
    gain, bias = gains[0:1], gains[1:2]

    def one_chunk(i, carry):
        span = pl.ds(pl.multiple_of(i * CHUNK, CHUNK), CHUNK)
        normed, _ = normalize(x[span].astype(jnp.float32))
        first[span] = (normed * gain + bias).astype(jnp.bfloat16)
        return carry

    lax.fori_loop(0, rows // CHUNK, one_chunk, 0)

    def one_block(i, carry):
        columns = pl.ds(pl.multiple_of(i * 512, 512), 512)
        block[...] = dot(first[...], packed[:, columns], 0, 0)
        split_rows(block, keep, send, columns)
        return carry

    lax.fori_loop(0, packed.shape[1] // 512, one_block, 0)
    fill = jnp.zeros((LANES - 4, width), jnp.float32)
    norms = jnp.concatenate([first_norms[:2], second_norms[:2], fill], axis=0)
    block[:, :LANES] = jnp.transpose(norms)
    split_rows(block.at[:, :LANES], keep, send, slice(packed.shape[1], packed.shape[1] + LANES))


def project_back(x, packed, gains, first_norms, second_norms, plane, deep):
    rows, width = x.shape
    shape = (plane, deep, packed.shape[1] + LANES)
    return pl.pallas_call(
        project_back_kernel,
        out_shape=(jax.ShapeDtypeStruct(shape, jnp.bfloat16), jax.ShapeDtypeStruct(shape, jnp.bfloat16)),
        in_specs=[pl.BlockSpec(memory_space=VMEM)] * 5,
        out_specs=[pl.BlockSpec(memory_space=VMEM)] * 2,
        scratch_shapes=[pltpu.VMEM((rows, width), jnp.bfloat16), pltpu.VMEM((width, 512), jnp.float32)],
        compiler_params=params(10),
        name="project_back",
    )(x, packed, gains, first_norms, second_norms)


def input_back_kernel(x, packed, gains, middle_grad, *refs):
    pieces = refs[:-3]
    grad_in, norm_grads, weight = refs[-3:]
    rows, width = x.shape
    assemble(pieces, weight, slice(None))
    gain = gains[0:1]
    zero = jnp.zeros((1, width), jnp.float32)

    def one_chunk(i, carry):
        gain_sum, bias_sum = carry
        span = pl.ds(pl.multiple_of(i * CHUNK, CHUNK), CHUNK)
        normed, scale = normalize(x[span].astype(jnp.float32))
        back = dot(packed[span], weight[:, : 3 * width], 1, 1)
        grad_in[span] = (middle_grad[span] + norm_back(back, normed, scale, gain)).astype(jnp.bfloat16)
        gain_sum = gain_sum + jnp.sum(back * normed, axis=0, keepdims=True)
        return gain_sum, bias_sum + jnp.sum(back, axis=0, keepdims=True)

    gain_sum, bias_sum = lax.fori_loop(0, rows // CHUNK, one_chunk, (zero, zero))
    norm_grads[...] = jnp.concatenate([gain_sum, bias_sum, jnp.zeros((6, width), jnp.float32)], axis=0)


def input_back(x, packed, gains, middle_grad, pieces):
    rows, width = x.shape
    return pl.pallas_call(
        input_back_kernel,
        out_shape=(jax.ShapeDtypeStruct((rows, width), jnp.bfloat16), jax.ShapeDtypeStruct((8, width), jnp.float32)),
        in_specs=[pl.BlockSpec(memory_space=VMEM)] * (4 + len(pieces)),
        out_specs=[pl.BlockSpec(memory_space=VMEM)] * 2,
        scratch_shapes=[pltpu.VMEM((width, pieces[0].shape[1]), jnp.bfloat16)],
        compiler_params=params(10),
        name="input_back",
    )(x, packed, gains, middle_grad, *pieces)


def column_kernel(*refs):
    reps = len(refs) - 1
    out = refs[-1]
    z = lax.axis_index("rep")
    rows = refs[0].shape[0]
    got = [ref[...].astype(jnp.float32) for ref in refs[:-1]]
    parts = []
    for j in range(reps):
        part = got[0]
        for k in range(1, reps):
            part = jnp.where(lax.rem(z + reps - k, reps) == j, got[k], part)
        parts.append(part)
    out[...] = jnp.concatenate(parts, axis=0).astype(out.dtype)


def column_of(shards):
    rows, cols = shards[0].shape
    reps = len(shards)
    return pl.pallas_call(
        column_kernel,
        out_shape=jax.ShapeDtypeStruct((reps * rows, cols), shards[0].dtype),
        in_specs=[pl.BlockSpec(memory_space=VMEM)] * reps,
        out_specs=pl.BlockSpec(memory_space=VMEM),
        compiler_params=params(4),
        name="column",
    )(*shards)


def chip_sum_kernel(keep, got, own, *low):
    p = plane_index()
    own[...] = keep[p].astype(jnp.float32) + got[p].astype(jnp.float32)
    for m, ref in enumerate(low, 1):
        ref[...] = (keep[p ^ m].astype(jnp.float32) + got[p ^ m].astype(jnp.float32)).astype(jnp.bfloat16)


def chip_sum(keep, got):
    plane, rows, cols = keep.shape
    block = cols if cols < 2048 else 1536
    part = pl.BlockSpec((rows, block), lambda i: (0, i))
    whole = pl.BlockSpec((plane, rows, block), lambda i: (0, 0, i))
    return pl.pallas_call(
        chip_sum_kernel,
        grid=(cols // block,),
        out_shape=[jax.ShapeDtypeStruct((rows, cols), jnp.float32)]
        + [jax.ShapeDtypeStruct((rows, cols), jnp.bfloat16)] * (plane - 1),
        in_specs=[whole, whole],
        out_specs=[part] * plane,
        compiler_params=params(12),
        name="chip_sum",
    )(keep, got)


def plane_sum_kernel(own, *refs):
    plane = sum(1 for ref in refs if ref.shape == own.shape) + 1
    got, out, low = refs[: plane - 1], refs[plane - 1], refs[plane:]
    reps = len(low) + 1
    rows = out.shape[0]
    z = lax.axis_index("rep")
    total = own[...]
    for ref in got:
        total = total + ref[...].astype(jnp.float32)
    for k, ref in enumerate((out, *low)):
        part = total[:rows]
        for j in range(1, reps):
            part = jnp.where(lax.rem(z + k, reps) == j, total[j * rows : (j + 1) * rows], part)
        ref[...] = part.astype(ref.dtype)


def plane_sum(own, got, reps):
    rows, cols = own.shape
    block = cols if cols < 2048 else 1536
    part = pl.BlockSpec((rows, block), lambda i: (0, i))
    small = pl.BlockSpec((rows // reps, block), lambda i: (0, i))
    return pl.pallas_call(
        plane_sum_kernel,
        grid=(cols // block,),
        out_shape=[jax.ShapeDtypeStruct((rows // reps, cols), jnp.float32)]
        + [jax.ShapeDtypeStruct((rows // reps, cols), jnp.bfloat16)] * (reps - 1),
        in_specs=[part] * (1 + len(got)),
        out_specs=[small] * reps,
        compiler_params=params(10),
        name="plane_sum",
    )(own, *got)


def full_sum(value):
    return jnp.sum(jnp.sum(value, axis=1, keepdims=True), axis=0, keepdims=True)


def turned(columns):
    rows, count = columns.shape
    same = lax.broadcasted_iota(jnp.int32, (rows, rows), 0) == lax.broadcasted_iota(jnp.int32, (rows, rows), 1)
    line = lax.broadcasted_iota(jnp.int32, (count, rows), 0)
    out = jnp.zeros((count, rows), jnp.float32)
    for j in range(count):
        row = jnp.sum(jnp.where(same, columns[:, j : j + 1], 0.0), axis=0, keepdims=True)
        out = jnp.where(line == j, row, out)
    return out


def moments_kernel(pieces_of, first_index, reps, *refs):
    n = len(pieces_of)
    grads, arrays = refs[:reps], refs[reps:]
    total = grads[0][...]
    for ref in grads[1:]:
        total = total + ref[...].astype(jnp.float32)
    weights, firsts, seconds = arrays[:n], arrays[n : 2 * n], arrays[2 * n : 3 * n]
    momenta, variances, directions = arrays[3 * n : 4 * n], arrays[4 * n : 5 * n], arrays[5 * n : 6 * n]
    sums = arrays[6 * n]
    lane = lax.broadcasted_iota(jnp.int32, (1, LANES), 1)
    row = jnp.zeros((1, LANES), jnp.float32)
    for i, parts in enumerate(pieces_of):
        weight_sum = jnp.zeros((1, 1), jnp.float32)
        step_sum = jnp.zeros((1, 1), jnp.float32)
        for at, size, columns in parts:
            rows = slice(at, at + size)
            gradient = total[:, columns[0] : columns[1]]
            if len(columns) > 2:
                gradient = turned(gradient)
            weight = weights[i][rows]
            momentum = BETA * firsts[i][rows] + (1.0 - BETA) * gradient
            variance = BETA * seconds[i][rows] + (1.0 - BETA) * gradient * gradient
            direction = momentum / (jnp.sqrt(variance) + ADAM_EPSILON) + DECAY * weight
            momenta[i][rows] = momentum
            variances[i][rows] = variance
            directions[i][rows] = direction
            weight_sum = weight_sum + full_sum(weight * weight)
            step_sum = step_sum + full_sum(direction * direction)
        row = jnp.where(lane == first_index[i], weight_sum, row)
        row = jnp.where(lane == 5 + first_index[i], step_sum, row)
    sums[...] = row


def moments(pieces_of, first_index, grads, weights, firsts, seconds):
    arrays = [*grads, *weights, *firsts, *seconds]
    shapes = [jax.ShapeDtypeStruct(weight.shape, jnp.float32) for weight in weights]
    outs = pl.pallas_call(
        partial(moments_kernel, pieces_of, first_index, len(grads)),
        out_shape=shapes * 3 + [jax.ShapeDtypeStruct((1, LANES), jnp.float32)],
        in_specs=[pl.BlockSpec(memory_space=VMEM)] * len(arrays),
        out_specs=[pl.BlockSpec(memory_space=VMEM)] * (3 * len(weights) + 1),
        compiler_params=params(8),
        name="moments",
    )(*arrays)
    n = len(weights)
    return outs[:n], outs[n : 2 * n], outs[2 * n : 3 * n], outs[3 * n]


def update_kernel(n, sums, *refs):
    weights, directions, updated, table = refs[:n], refs[n : 2 * n], refs[2 * n : 3 * n], refs[3 * n]
    norms = jnp.sqrt(jnp.sum(sums[...], axis=0, keepdims=True))
    row = lax.broadcasted_iota(jnp.int32, table.shape, 0)
    lane = lax.broadcasted_iota(jnp.int32, table.shape, 1)
    out = jnp.zeros(table.shape, jnp.float32)
    for i in range(n):
        weight_norm = norms[:, i : i + 1]
        step_norm = norms[:, 5 + i : 6 + i]
        ratio = weight_norm / step_norm
        updated[i][...] = weights[i][...] - RATE * ratio * directions[i][...]
        column = jnp.where(row == 0, weight_norm, jnp.where(row == 1, step_norm, ratio))
        out = jnp.where(lane == i, column, out)
    table[...] = out


def update(sums, weights, directions):
    n = len(weights)
    outs = pl.pallas_call(
        partial(update_kernel, n),
        out_shape=[jax.ShapeDtypeStruct(weight.shape, jnp.float32) for weight in weights]
        + [jax.ShapeDtypeStruct((8, LANES), jnp.float32)],
        in_specs=[pl.BlockSpec(memory_space=VMEM)] * (1 + 2 * n),
        out_specs=[pl.BlockSpec(memory_space=VMEM)] * (n + 1),
        compiler_params=params(6),
        name="update",
    )(sums, *weights, *directions)
    return outs[:n], outs[n][:3, :n]


AXES = ("dp", "rep")


class Layout:
    def __init__(self, mesh):
        self.dp = mesh.shape["dp"]
        self.rep = mesh.shape["rep"]
        self.plane = self.dp // 2

    def permute(self, value, move):
        pairs = []
        for p in range(self.plane):
            for c in range(2):
                for z in range(self.rep):
                    q, d, w = move(p, c, z)
                    pairs.append(((p * 2 + c) * self.rep + z, (q * 2 + d) * self.rep + w))
        return lax.ppermute(value, AXES, pairs)

    def to_core(self, value):
        return self.permute(value, lambda p, c, z: (p, 1 - c, z))

    def to_plane(self, value, m):
        return self.permute(value, lambda p, c, z: (p ^ m, c, z))

    def to_rep(self, value, k):
        return self.permute(value, lambda p, c, z: (p, c, (z + k) % self.rep))

    def place(self):
        dp = lax.axis_index("dp")
        return dp // 2, dp % 2, lax.axis_index("rep")


def over_rep(lay, shard):
    return [shard] + [lay.to_rep(shard, k) for k in range(1, lay.rep)]


def over_plane(lay, column):
    return [column] + [lay.to_plane(column, m) for m in range(1, lay.plane)]


def over_core(lay, blocks):
    return blocks + [lay.to_core(block) for block in blocks]


def after(values, others):
    count = len(values)
    return list(lax.optimization_barrier((*values, *others))[:count])


def exchange(lay, value):
    return lax.all_to_all(value, AXES, 0, 0)


def body(
    lay,
    inputs,
    segments,
    cotangent,
    attend_in,
    attend_out,
    expand,
    contract,
    layer_norms,
    moment_in,
    moment_out,
    moment_expand,
    moment_contract,
    moment_norms,
    square_in,
    square_out,
    square_expand,
    square_contract,
    square_norms,
):
    masters = (attend_in, attend_out, expand, contract, layer_norms)
    width = attend_in.shape[1]
    depth = attend_out.shape[1]
    hidden = expand.shape[1]
    own = attend_in.shape[0]
    count = lay.dp * lay.rep
    plain = own % 16 == 0
    norm_rows = jnp.pad(layer_norms.astype(jnp.bfloat16).T, ((0, 0), (0, LANES - 4)))
    shard1 = jnp.concatenate([attend_in.astype(jnp.bfloat16), norm_rows], axis=1)
    column1 = over_rep(lay, shard1)
    rows = inputs.shape[1]
    attend_out_, expand_, contract_ = after([attend_out, expand, contract], [shard1])
    deep = [contract_[j * own : (j + 1) * own] for j in range(4)]
    shard2 = jnp.concatenate([part.astype(jnp.bfloat16) for part in (attend_out_, expand_, *deep)], axis=1)
    (shard2,) = after([shard2], column1[1:])
    column2 = over_rep(lay, shard2)
    inputs_, cotangent_, segments_ = after([inputs[0], cotangent[0], segments], [shard1])
    x, dy, labels, begin = arrange(inputs_, cotangent_, segments_)
    blocks1 = over_plane(lay, column_of(after(column1, [x])))
    blocks2 = over_plane(lay, column_of(after(column2, blocks1)))
    pieces1 = over_core(lay, blocks1)
    *pieces1, x, labels = after([*pieces1, x, labels], blocks2[:1])
    qx, kx, vx, mixed, gains = attend(x, labels, pieces1)
    pieces2 = over_core(lay, after(blocks2, [mixed]))
    deep_pieces = []
    if not plain:
        first = depth + hidden
        for piece in pieces2:
            part = piece[:, first:].reshape(lay.rep, own, 4, depth).transpose(0, 2, 1, 3)
            deep_pieces.append(part.reshape(-1, depth))
    outputs, dox, middle_grad, keep2, send2, second_norms, *deep_out = feed(
        lay.rep, x, mixed, dy, gains, pieces2, deep_pieces
    )
    if not plain:
        keep2, send2 = [
            jnp.concatenate(
                [
                    wide[:, :, : depth + hidden],
                    part.reshape(lay.plane, lay.rep, 4, own, depth).transpose(0, 1, 3, 2, 4).reshape(lay.plane, -1, 4 * depth),
                ],
                axis=2,
            )
            for wide, part in zip((keep2, send2), deep_out)
        ]
    own2, *low2 = chip_sum(keep2, lay.to_core(send2))
    got2 = [lay.to_plane(part, m) for m, part in enumerate(low2, 1)]
    (dox,) = after([dox], low2)
    packed = attend_back(qx, kx, vx, dox)
    input_gradient, first_norms = input_back(x, packed, gains, middle_grad, pieces1)
    own2, *got2 = after([own2, *got2], [first_norms])
    own2, *low2 = plane_sum(own2, got2, lay.rep)
    got2 = [lay.to_rep(part, k) for k, part in enumerate(low2, 1)]
    (packed_,) = after([packed], low2)
    keep1, send1 = project_back(x, packed_, gains, first_norms, second_norms, lay.plane, lay.rep * own)
    own1, *low1 = chip_sum(keep1, lay.to_core(send1))
    got1 = [lay.to_plane(part, m) for m, part in enumerate(low1, 1)]
    outputs, input_gradient = after([outputs, input_gradient], low1)
    outputs, input_gradient = arrange_back(begin, outputs, input_gradient, rows)
    spans = [[(0, own, (0, depth))], [(0, own, (depth, depth + hidden))]]
    spans.append([(j * own, own, (depth + hidden + j * depth, depth + hidden + (j + 1) * depth)) for j in range(4)])
    momenta2, variances2, directions2, sums2 = moments(
        spans, (1, 2, 3), [own2, *got2], masters[1:4],
        (moment_out, moment_expand, moment_contract), (square_out, square_expand, square_contract),
    )
    own1, *got1 = after([own1, *got1], [sums2])
    own1, *low1 = plane_sum(own1, got1, lay.rep)
    got1 = [lay.to_rep(part, k) for k, part in enumerate(low1, 1)]
    momenta1, variances1, directions1, sums1 = moments(
        [[(0, own, (0, width))], [(0, 4, (width, width + 4, True))]], (0, 4), [own1, *got1], (attend_in, layer_norms),
        (moment_in, moment_norms), (square_in, square_norms),
    )
    sums = exchange(lay, jnp.broadcast_to((sums1 + sums2)[None], (count, 1, LANES)))
    directions = (directions1[0], *directions2, directions1[1])
    updated, trust_table = update(sums[:, 0], masters, directions)
    momenta = (momenta1[0], *momenta2, momenta1[1])
    variances = (variances1[0], *variances2, variances1[1])
    return (outputs[None], input_gradient[None], *updated, *momenta, *variances, trust_table)


def solution(mesh):
    placed = (
        P(("dp", "rep"), None, None),
        P(("dp", "rep"), None),
        P(("dp", "rep"), None, None),
        P(("dp", "rep"), None),
        P(("dp", "rep"), None),
        P(("dp", "rep"), None),
        P(("dp", "rep"), None),
        P(None, ("dp", "rep")),
        P(("dp", "rep"), None),
        P(("dp", "rep"), None),
        P(("dp", "rep"), None),
        P(("dp", "rep"), None),
        P(None, ("dp", "rep")),
        P(("dp", "rep"), None),
        P(("dp", "rep"), None),
        P(("dp", "rep"), None),
        P(("dp", "rep"), None),
        P(None, ("dp", "rep")),
    )
    return jax.shard_map(
        partial(body, Layout(mesh)),
        mesh=mesh,
        in_specs=placed,
        out_specs=(
            P(("dp", "rep"), None, None),
            P(("dp", "rep"), None, None),
            P(("dp", "rep"), None),
            P(("dp", "rep"), None),
            P(("dp", "rep"), None),
            P(("dp", "rep"), None),
            P(None, ("dp", "rep")),
            P(("dp", "rep"), None),
            P(("dp", "rep"), None),
            P(("dp", "rep"), None),
            P(("dp", "rep"), None),
            P(None, ("dp", "rep")),
            P(("dp", "rep"), None),
            P(("dp", "rep"), None),
            P(("dp", "rep"), None),
            P(("dp", "rep"), None),
            P(None, ("dp", "rep")),
            P(),
        ),
        check_vma=False,
    )
```

```python
from functools import partial
import math

import jax
import jax.numpy as jnp
from jax import lax
from jax.experimental import pallas as pl
from jax.experimental.pallas import tpu as pltpu
from jax.sharding import PartitionSpec as P

HEADS = 8
HEAD_DIM = 64


EPSILON = 1e-05
ADAM_EPSILON = 1e-06
DECAY = 0.01
RATE = 0.5
BETA = 0.5
LANES = 128
HALF = 64
BIG = 1e30
FEATS = 4
TILE = 256
THIN = 32
CHUNK = 352
VMEM = pltpu.MemorySpace.VMEM
AXES = ("dp", "rep")


def params(mebibytes):
    return pltpu.CompilerParams(vmem_limit_bytes=mebibytes * 1024 * 1024)


def dot(a, b, ca, cb):
    return lax.dot_general(a, b, (((ca,), (cb,)), ((), ())), preferred_element_type=jnp.float32)


def normalize(values):
    center = values - jnp.mean(values, axis=-1, keepdims=True)
    scale = lax.rsqrt(jnp.mean(center * center, axis=-1, keepdims=True) + EPSILON)
    return center * scale, scale


class Layout:
    def __init__(self, mesh):
        self.dp = mesh.shape["dp"]
        self.rep = mesh.shape["rep"]
        self.plane = self.dp // 2
        self.mixed = self.plane == self.rep

    def pairs(self, move):
        pairs = []
        for p in range(self.plane):
            for c in range(2):
                for z in range(self.rep):
                    q, d, w = move(p, c, z)
                    pairs.append(((p * 2 + c) * self.rep + z, (q * 2 + d) * self.rep + w))
        return pairs

    def over(self, value, i, first):
        def move(p, c, z):
            along_z = (first == (c == 0)) if self.mixed else first
            return (p, c, (z + i) % self.rep) if along_z else (p ^ i, c, z)

        return lax.ppermute(value, AXES, self.pairs(move))

    def to_core(self, value):
        return lax.ppermute(value, AXES, self.pairs(lambda p, c, z: (p, 1 - c, z)))

    def core(self):
        return lax.rem(lax.axis_index("dp"), 2)

    def partner(self, side, i, first, sign):
        along_z = lax.rem(lax.axis_index("rep") + (sign * i) % self.rep, self.rep)
        in_plane = lax.div(lax.axis_index("dp"), 2) ^ i
        if not self.mixed:
            return along_z if first else in_plane
        return jnp.where(side == 0, along_z, in_plane) if first else jnp.where(side == 0, in_plane, along_z)

    def device(self, side, second, first):
        plain = (2 * second + side) * self.rep + first
        return jnp.where(side == 0, plain, (2 * first + side) * self.rep + second) if self.mixed else plain


def row_blocks(lay, side, second, rows):
    firsts = lay.rep
    if lay.mixed:
        return [(j * rows, pl.multiple_of(lay.device(side, second, j) * rows, rows), rows) for j in range(firsts)]
    return [(0, pl.multiple_of(lay.device(side, second, 0) * rows, firsts * rows), firsts * rows)]


def assemble(lay, pieces, full_ref, columns):
    count = len(pieces) // 2
    for i, piece in enumerate(pieces):
        side = lay.core() if i < count else 1 - lay.core()
        second = lay.partner(side, i % count, False, -1)
        for at, to, rows in row_blocks(lay, side, second, piece.shape[0] // lay.rep):
            full_ref[pl.ds(to, rows), :] = piece[at : at + rows, columns]


def assemble_deep(lay, pieces, full_ref, first):
    count = len(pieces) // 2
    width = full_ref.shape[1]
    for i, piece in enumerate(pieces):
        side = lay.core() if i < count else 1 - lay.core()
        second = lay.partner(side, i % count, False, -1)
        rows = piece.shape[0] // lay.rep
        for z in range(lay.rep):
            to = pl.multiple_of(lay.device(side, second, z) * 4 * rows, 4 * rows)
            for j in range(4):
                source = piece[z * rows : (z + 1) * rows, first + j * width : first + (j + 1) * width]
                full_ref[pl.ds(to + j * rows, rows), :] = source


def split_rows(lay, full_ref, keep_ref, send_ref, lanes):
    for target, side in ((keep_ref, lay.core()), (send_ref, 1 - lay.core())):
        for second in range(target.shape[0]):
            for at, source, rows in row_blocks(lay, side, second, target.shape[1] // lay.rep):
                target[second, at : at + rows, lanes] = full_ref[pl.ds(source, rows), :].astype(target.dtype)


def split_deep(lay, full_ref, keep_ref, send_ref, first):
    width = full_ref.shape[1]
    rows = keep_ref.shape[1] // lay.rep
    for target, side in ((keep_ref, lay.core()), (send_ref, 1 - lay.core())):
        for second in range(target.shape[0]):
            for z in range(lay.rep):
                source = pl.multiple_of(lay.device(side, second, z) * 4 * rows, 4 * rows)
                for j in range(4):
                    part = full_ref[pl.ds(source + j * rows, rows), :]
                    columns = slice(first + j * width, first + (j + 1) * width)
                    target[second, z * rows : (z + 1) * rows, columns] = part.astype(target.dtype)


def row_chunks(rows, size):
    return [(at, min(size, rows - at)) for at in range(0, rows, size)]


def windows(rows):
    half = (rows - THIN) // 2
    span = half + THIN
    spans = [(at, TILE, 0, span) for at in range(0, half, TILE)]
    spans.append((half, THIN, 0, rows))
    return spans + [(at, TILE, half, span) for at in range(span, rows, TILE)]


def arrange_kernel(inputs, cotangent, segments, x, dy, labels, begin, room):
    tokens = segments.shape[1]
    half = tokens // 2
    memory = inputs.shape[0] - tokens
    segment = segments[...].astype(jnp.float32)
    ahead = pltpu.roll(jnp.broadcast_to(segment, (8, tokens)), tokens - half + 1, 1)[:1]
    lane = lax.broadcasted_iota(jnp.int32, (1, tokens), 1)
    fits = (segment == ahead) & (lane <= half)
    start = jnp.sum(jnp.where(fits, lane.astype(jnp.float32), 0.0), axis=1, keepdims=True)
    begin[...] = jnp.broadcast_to(start, begin.shape)
    row = lax.broadcasted_iota(jnp.int32, (half, LANES), 0).astype(jnp.float32)
    early = row < start
    thin = lax.broadcasted_iota(jnp.int32, (THIN, LANES), 0) < memory
    for source, target in ((inputs, x), (cotangent, dy)):
        for at in range(0, inputs.shape[1], LANES):
            columns = slice(at, at + LANES)
            room[: inputs.shape[0]] = source[:, columns].astype(jnp.float32)
            left, right = room[memory : memory + half], room[memory + half : memory + tokens]
            target[:half, columns] = jnp.where(early, right, left).astype(target.dtype)
            target[half : half + THIN, columns] = jnp.where(thin, room[:THIN], 0.0).astype(target.dtype)
            target[half + THIN :, columns] = jnp.where(early, left, right).astype(target.dtype)
    left = jnp.transpose(jnp.broadcast_to(segment[:, :half], (LANES, half)))
    right = jnp.transpose(jnp.broadcast_to(segment[:, half:], (LANES, half)))
    labels[:half] = jnp.where(early, right, left).astype(jnp.int32)
    labels[half : half + THIN] = jnp.where(thin, -1, -2)
    labels[half + THIN :] = jnp.where(early, left, right).astype(jnp.int32)


def arrange(inputs, cotangent, segments):
    width = inputs.shape[1]
    rows = segments.shape[1] + THIN
    return pl.pallas_call(
        arrange_kernel,
        out_shape=(
            jax.ShapeDtypeStruct((rows, width), inputs.dtype),
            jax.ShapeDtypeStruct((rows, width), inputs.dtype),
            jax.ShapeDtypeStruct((rows, LANES), jnp.int32),
            jax.ShapeDtypeStruct((8, LANES), jnp.float32),
        ),
        in_specs=[pl.BlockSpec(memory_space=VMEM)] * 3,
        out_specs=[pl.BlockSpec(memory_space=VMEM)] * 4,
        scratch_shapes=[pltpu.VMEM((rows, LANES), jnp.float32)],
        compiler_params=params(8),
        name="arrange",
    )(inputs, cotangent, segments)


def arrange_back_kernel(begin, first, second, first_out, second_out, room):
    rows = first_out.shape[0]
    half = (first.shape[0] - THIN) // 2
    memory = rows - 2 * half
    row = lax.broadcasted_iota(jnp.int32, (half, LANES), 0).astype(jnp.float32)
    early = row < begin[:1]
    for source, target in ((first, first_out), (second, second_out)):
        for at in range(0, first.shape[1], LANES):
            columns = slice(at, at + LANES)
            left = source[:half, columns].astype(jnp.float32)
            right = source[half + THIN :, columns].astype(jnp.float32)
            room[:THIN] = source[half : half + THIN, columns].astype(jnp.float32)
            room[memory : memory + half] = jnp.where(early, right, left)
            room[memory + half : rows] = jnp.where(early, left, right)
            target[:, columns] = room[:rows].astype(target.dtype)


def arrange_back(begin, first, second, rows):
    width = first.shape[1]
    return pl.pallas_call(
        arrange_back_kernel,
        out_shape=[jax.ShapeDtypeStruct((rows, width), first.dtype)] * 2,
        in_specs=[pl.BlockSpec(memory_space=VMEM)] * 3,
        out_specs=[pl.BlockSpec(memory_space=VMEM)] * 2,
        scratch_shapes=[pltpu.VMEM((first.shape[0], LANES), jnp.float32)],
        compiler_params=params(8),
        name="arrange_back",
    )(begin, first, second)


def attend_kernel(lay, count, x, labels, *refs):
    pieces = refs[:count]
    qx, kx, vx, mixed, gains, weight, qs = refs[count:]
    rows = x.shape[0]
    width = mixed.shape[1]
    assemble(lay, pieces, weight, slice(None))
    gains[...] = jnp.transpose(weight[:, 3 * width :].astype(jnp.float32))[:8]
    gain, bias = gains[0:1], gains[1:2]

    def one_chunk(i, carry):
        span = pl.ds(pl.multiple_of(i * CHUNK, CHUNK), CHUNK)
        normed, _ = normalize(x[span].astype(jnp.float32))
        first = (normed * gain + bias).astype(jnp.bfloat16)
        lane = lax.broadcasted_iota(jnp.int32, (CHUNK, LANES), 1)
        low = lane < HALF
        feature = lane % HALF
        label = labels[span]
        blocked = ((feature < FEATS) & (label >= 0) & (feature != label)) | (feature == FEATS)
        query_side = jnp.where(blocked, -BIG, 0.0)
        marked = ((feature < FEATS) & (feature == label)) | ((feature == FEATS) & (label == -2))
        key_side = jnp.where(marked | (feature > FEATS), 1.0, 0.0)
        sides = (query_side, key_side, jnp.ones_like(key_side))
        for kind, target in enumerate((qs, kx, vx)):
            whole = dot(first, weight[:, kind * width : (kind + 1) * width], 1, 0)
            whole = whole.astype(jnp.bfloat16).astype(jnp.float32)
            for pair in range(width // LANES):
                part = whole[:, pair * LANES : (pair + 1) * LANES]
                if kind == 0:
                    part = part * (1.0 / math.sqrt(HEAD_DIM))
                at = 2 * pair * LANES
                target[span, at : at + LANES] = jnp.where(low, part, sides[kind]).astype(jnp.bfloat16)
                target[span, at + LANES : at + 2 * LANES] = jnp.where(low, sides[kind], part).astype(jnp.bfloat16)
        return carry

    lax.fori_loop(0, rows // CHUNK, one_chunk, 0)

    def one_pair(pair, carry):
        columns = pl.ds(pl.multiple_of(pair * LANES, LANES), LANES)
        for at, size, key_at, key_size in windows(rows):
            span = pl.ds(at, size)
            seen = pl.ds(key_at, key_size)
            lane = lax.broadcasted_iota(jnp.int32, (size, LANES), 1)
            low = lane < HALF
            feature = lane % HALF
            got = []
            for side in range(2):
                head = pl.ds(pl.multiple_of((2 * pair + side) * LANES, LANES), LANES)
                queries = qs[span, head]
                scores = dot(queries, kx[seen, head], 1, 1)
                highest = jnp.max(scores, axis=1, keepdims=True)
                raised = jnp.exp(scores - highest).astype(jnp.bfloat16)
                found = dot(raised, vx[seen, head], 1, 0)
                total = -(highest + jnp.log(found))
                first = total.astype(jnp.bfloat16).astype(jnp.float32)
                second = (total - first).astype(jnp.bfloat16).astype(jnp.float32)
                third = total - first - second
                values = jnp.where(feature == 5, first, jnp.where(feature == 6, second, third))
                place = (feature > FEATS) & (feature < 8) & (low if side else ~low)
                qx[span, head] = jnp.where(place, values, queries.astype(jnp.float32)).astype(jnp.bfloat16)
                got.append(found)
            over = pltpu.roll(jnp.where(low, got[1], got[0]), HALF, 1)
            mixed[span, columns] = (jnp.where(low, got[0], got[1]) / over).astype(jnp.bfloat16)
        return carry

    lax.fori_loop(0, width // LANES, one_pair, 0)


def attend(lay, x, labels, pieces):
    rows, width = x.shape
    wide = jax.ShapeDtypeStruct((rows, 2 * width), jnp.bfloat16)
    depth = len(pieces) * pieces[0].shape[0]
    return pl.pallas_call(
        partial(attend_kernel, lay, len(pieces)),
        out_shape=(
            wide,
            wide,
            wide,
            jax.ShapeDtypeStruct((rows, width), jnp.bfloat16),
            jax.ShapeDtypeStruct((8, width), jnp.float32),
        ),
        in_specs=[pl.BlockSpec(memory_space=VMEM)] * (2 + len(pieces)),
        out_specs=[pl.BlockSpec(memory_space=VMEM)] * 5,
        scratch_shapes=[
            pltpu.VMEM((depth, pieces[0].shape[1]), jnp.bfloat16),
            pltpu.VMEM((rows, 2 * width), jnp.bfloat16),
        ],
        compiler_params=params(16),
        name="attend",
    )(x, labels, *pieces)


def attend_back_kernel(qx, kx, vx, dox, packed, total):
    rows = qx.shape[0]
    width = packed.shape[1] // 3

    def one_pair(pair, carry):
        heads = [pl.ds(pl.multiple_of((2 * pair + side) * LANES, LANES), LANES) for side in range(2)]
        spots = [pl.ds(pl.multiple_of(kind * width + pair * LANES, LANES), LANES) for kind in range(3)]
        total[...] = jnp.zeros_like(total)
        for at, size, query_at, query_size in windows(rows):
            span = pl.ds(at, size)
            seen = pl.ds(query_at, query_size)
            low = lax.broadcasted_iota(jnp.int32, (size, LANES), 1) < HALF
            got = []
            for side in range(2):
                head = heads[side]
                keys = kx[span, head]
                queries = qx[seen, head]
                upstream = dox[seen, head]
                attention = jnp.exp(dot(keys, queries, 1, 1))
                grad = dot(vx[span, head], upstream, 1, 1)
                scores = (attention * grad).astype(jnp.bfloat16)
                got.append((dot(scores, queries, 1, 0), dot(attention.astype(jnp.bfloat16), upstream, 1, 0)))
                total[side, seen] += dot(scores, keys, 0, 0)
            packed[span, spots[1]] = jnp.where(low, got[0][0], got[1][0]).astype(jnp.bfloat16)
            packed[span, spots[2]] = jnp.where(low, got[0][1], got[1][1]).astype(jnp.bfloat16)
        low = lax.broadcasted_iota(jnp.int32, (rows, LANES), 1) < HALF
        packed[:, spots[0]] = (jnp.where(low, total[0], total[1]) * (1.0 / math.sqrt(HEAD_DIM))).astype(jnp.bfloat16)
        return carry

    lax.fori_loop(0, width // LANES, one_pair, 0)


def attend_back(qx, kx, vx, dox):
    rows, wide = qx.shape
    return pl.pallas_call(
        attend_back_kernel,
        out_shape=jax.ShapeDtypeStruct((rows, 3 * wide // 2), jnp.bfloat16),
        in_specs=[pl.BlockSpec(memory_space=VMEM)] * 4,
        out_specs=pl.BlockSpec(memory_space=VMEM),
        scratch_shapes=[pltpu.VMEM((2, rows, LANES), jnp.float32)],
        compiler_params=params(16),
        name="attend_back",
    )(qx, kx, vx, dox)


def norm_back(grad, normed, scale, gain):
    scaled = grad * gain
    return scale * (
        scaled
        - jnp.mean(scaled, axis=-1, keepdims=True)
        - normed * jnp.mean(scaled * normed, axis=-1, keepdims=True)
    )


def feed_kernel(lay, count, deep_count, x, mixed, dy, gains, *refs):
    pieces = refs[:count]
    deep_pieces = refs[count : count + deep_count]
    outputs, dox, middle_grad, keep2, send2, norm_grads, *deep_out = refs[count + deep_count : -8]
    wide, contract, active, hidden_grad, second, middle_low, block, deep_block = refs[-8:]
    rows, width = x.shape
    hidden = contract.shape[0]
    wide_part = slice(0, width + hidden)
    assemble(lay, pieces, wide, wide_part)
    if deep_count:
        assemble(lay, deep_pieces, contract, slice(None))
    else:
        assemble_deep(lay, pieces, contract, width + hidden)
    gain, bias = gains[2:3], gains[3:4]
    zero = jnp.zeros((1, width), jnp.float32)

    def one_chunk(i, carry):
        gain_sum, bias_sum = carry
        span = pl.ds(pl.multiple_of(i * CHUNK, CHUNK), CHUNK)
        middle = x[span].astype(jnp.float32) + dot(mixed[span], wide[:, :width], 1, 0)
        normed, scale = normalize(middle)
        low = (normed * gain + bias).astype(jnp.bfloat16)
        second[span] = low
        result = middle
        back = jnp.zeros_like(middle)
        for start in range(0, hidden, 512):
            part = slice(start, start + 512)
            from_expand = wide[:, width + start : width + start + 512]
            up = dot(low, from_expand, 1, 0)
            square = up * up
            bend = jnp.tanh(0.7978845608028654 * up * (1.0 + 0.044715 * square))
            half = 0.5 * (1.0 + bend)
            act = (up * half).astype(jnp.bfloat16)
            active[span, part] = act
            slope = half + 0.5 * up * (1.0 - bend * bend) * (0.7978845608028654 * (1.0 + 3 * 0.044715 * square))
            down = (dot(dy[span], contract[part], 1, 1) * slope).astype(jnp.bfloat16)
            hidden_grad[span, part] = down
            result = result + dot(act, contract[part], 1, 0)
            back = back + dot(down, from_expand, 1, 1)
        outputs[span] = result.astype(jnp.bfloat16)
        gain_sum = gain_sum + jnp.sum(back * normed, axis=0, keepdims=True)
        bias_sum = bias_sum + jnp.sum(back, axis=0, keepdims=True)
        grad = dy[span].astype(jnp.float32) + norm_back(back, normed, scale, gain)
        middle_grad[span] = grad
        grad_low = grad.astype(jnp.bfloat16)
        middle_low[span] = grad_low
        mixed_grad = dot(grad_low, wide[:, :width], 1, 1).astype(jnp.bfloat16).astype(jnp.float32)
        lane = lax.broadcasted_iota(jnp.int32, (CHUNK, LANES), 1)
        left = lane < HALF
        feature = lane % HALF
        for pair in range(width // LANES):
            columns = slice(pair * LANES, (pair + 1) * LANES)
            piece = mixed_grad[:, columns]
            product = piece * mixed[span, columns].astype(jnp.float32)
            for side in range(2):
                mine = left if side == 0 else ~left
                delta = -jnp.sum(jnp.where(mine, product, 0.0), axis=1, keepdims=True)
                one = delta.astype(jnp.bfloat16).astype(jnp.float32)
                two = (delta - one).astype(jnp.bfloat16).astype(jnp.float32)
                three = delta - one - two
                extra = jnp.where(feature == 0, one, jnp.where(feature == 1, two, jnp.where(feature == 2, three, 0.0)))
                head = (2 * pair + side) * LANES
                dox[span, head : head + LANES] = jnp.where(mine, piece, extra).astype(jnp.bfloat16)
        return gain_sum, bias_sum

    gain_sum, bias_sum = lax.fori_loop(0, rows // CHUNK, one_chunk, (zero, zero))
    norm_grads[...] = jnp.concatenate([gain_sum, bias_sum, jnp.zeros((6, width), jnp.float32)], axis=0)

    def one_block(i, carry):
        columns = pl.ds(pl.multiple_of(i * 512, 512), 512)
        deep_block[columns] = dot(active[:, columns], dy[...], 0, 0)
        block[...] = dot(second[...], hidden_grad[:, columns], 0, 0)
        split_rows(lay, block, keep2, send2, pl.ds(pl.multiple_of(width + i * 512, 512), 512))
        return carry

    lax.fori_loop(0, hidden // 512, one_block, 0)
    if deep_count:
        split_rows(lay, deep_block, *deep_out, slice(0, width))
    else:
        split_deep(lay, deep_block, keep2, send2, width + hidden)
    block[...] = dot(mixed[...], middle_low[...], 0, 0)
    split_rows(lay, block, keep2, send2, slice(0, width))


def feed(lay, x, mixed, dy, gains, pieces, deep_pieces):
    rows, width = x.shape
    plane = len(pieces) // 2
    deep = pieces[0].shape[0]
    columns = pieces[0].shape[1]
    hidden = 4 * width
    out_shape = [
        jax.ShapeDtypeStruct((rows, width), jnp.bfloat16),
        jax.ShapeDtypeStruct((rows, 2 * width), jnp.bfloat16),
        jax.ShapeDtypeStruct((rows, width), jnp.float32),
        jax.ShapeDtypeStruct((plane, deep, columns), jnp.bfloat16),
        jax.ShapeDtypeStruct((plane, deep, columns), jnp.bfloat16),
        jax.ShapeDtypeStruct((8, width), jnp.float32),
    ]
    if deep_pieces:
        out_shape.append(jax.ShapeDtypeStruct((plane, 4 * deep, width), jnp.bfloat16))
        out_shape.append(jax.ShapeDtypeStruct((plane, 4 * deep, width), jnp.bfloat16))
    return pl.pallas_call(
        partial(feed_kernel, lay, len(pieces), len(deep_pieces)),
        out_shape=out_shape,
        in_specs=[pl.BlockSpec(memory_space=VMEM)] * (4 + len(pieces) + len(deep_pieces)),
        out_specs=[pl.BlockSpec(memory_space=VMEM)] * len(out_shape),
        scratch_shapes=[
            pltpu.VMEM((width, width + hidden), jnp.bfloat16),
            pltpu.VMEM((hidden, width), jnp.bfloat16),
            pltpu.VMEM((rows, hidden), jnp.bfloat16),
            pltpu.VMEM((rows, hidden), jnp.bfloat16),
            pltpu.VMEM((rows, width), jnp.bfloat16),
            pltpu.VMEM((rows, width), jnp.bfloat16),
            pltpu.VMEM((width, 512), jnp.float32),
            pltpu.VMEM((hidden, width), jnp.float32),
        ],
        compiler_params=params(30),
        name="feed",
    )(x, mixed, dy, gains, *pieces, *deep_pieces)


def project_back_kernel(lay, x, packed, gains, first_norms, second_norms, keep, send, first, block):
    rows, width = x.shape
    gain, bias = gains[0:1], gains[1:2]

    def one_chunk(i, carry):
        span = pl.ds(pl.multiple_of(i * CHUNK, CHUNK), CHUNK)
        normed, _ = normalize(x[span].astype(jnp.float32))
        first[span] = (normed * gain + bias).astype(jnp.bfloat16)
        return carry

    lax.fori_loop(0, rows // CHUNK, one_chunk, 0)

    def one_block(i, carry):
        columns = pl.ds(pl.multiple_of(i * 512, 512), 512)
        block[...] = dot(first[...], packed[:, columns], 0, 0)
        split_rows(lay, block, keep, send, columns)
        return carry

    lax.fori_loop(0, packed.shape[1] // 512, one_block, 0)
    fill = jnp.zeros((LANES - 4, width), jnp.float32)
    norms = jnp.concatenate([first_norms[:2], second_norms[:2], fill], axis=0)
    block[:, :LANES] = jnp.transpose(norms)
    split_rows(lay, block.at[:, :LANES], keep, send, slice(packed.shape[1], packed.shape[1] + LANES))


def project_back(lay, x, packed, gains, first_norms, second_norms, own):
    rows, width = x.shape
    shape = (lay.plane, lay.rep * own, packed.shape[1] + LANES)
    return pl.pallas_call(
        partial(project_back_kernel, lay),
        out_shape=(jax.ShapeDtypeStruct(shape, jnp.bfloat16), jax.ShapeDtypeStruct(shape, jnp.bfloat16)),
        in_specs=[pl.BlockSpec(memory_space=VMEM)] * 5,
        out_specs=[pl.BlockSpec(memory_space=VMEM)] * 2,
        scratch_shapes=[pltpu.VMEM((rows, width), jnp.bfloat16), pltpu.VMEM((width, 512), jnp.float32)],
        compiler_params=params(10),
        name="project_back",
    )(x, packed, gains, first_norms, second_norms)


def input_back_kernel(lay, x, packed, gains, middle_grad, *refs):
    pieces = refs[:-3]
    grad_in, norm_grads, weight = refs[-3:]
    rows, width = x.shape
    assemble(lay, pieces, weight, slice(None))
    gain = gains[0:1]
    zero = jnp.zeros((1, width), jnp.float32)

    def one_chunk(i, carry):
        gain_sum, bias_sum = carry
        span = pl.ds(pl.multiple_of(i * CHUNK, CHUNK), CHUNK)
        normed, scale = normalize(x[span].astype(jnp.float32))
        back = dot(packed[span], weight[:, : 3 * width], 1, 1)
        grad_in[span] = (middle_grad[span] + norm_back(back, normed, scale, gain)).astype(jnp.bfloat16)
        gain_sum = gain_sum + jnp.sum(back * normed, axis=0, keepdims=True)
        return gain_sum, bias_sum + jnp.sum(back, axis=0, keepdims=True)

    gain_sum, bias_sum = lax.fori_loop(0, rows // CHUNK, one_chunk, (zero, zero))
    norm_grads[...] = jnp.concatenate([gain_sum, bias_sum, jnp.zeros((6, width), jnp.float32)], axis=0)


def input_back(lay, x, packed, gains, middle_grad, pieces):
    rows, width = x.shape
    return pl.pallas_call(
        partial(input_back_kernel, lay),
        out_shape=(jax.ShapeDtypeStruct((rows, width), jnp.bfloat16), jax.ShapeDtypeStruct((8, width), jnp.float32)),
        in_specs=[pl.BlockSpec(memory_space=VMEM)] * (4 + len(pieces)),
        out_specs=[pl.BlockSpec(memory_space=VMEM)] * 2,
        scratch_shapes=[pltpu.VMEM((width, pieces[0].shape[1]), jnp.bfloat16)],
        compiler_params=params(10),
        name="input_back",
    )(x, packed, gains, middle_grad, *pieces)


def column_kernel(lay, *refs):
    out = refs[-1]
    got = [ref[...].astype(jnp.float32) for ref in refs[:-1]]
    parts = []
    for j in range(len(got)):
        part = got[0]
        for i in range(1, len(got)):
            part = jnp.where(lay.partner(lay.core(), i, True, -1) == j, got[i], part)
        parts.append(part)
    out[...] = jnp.concatenate(parts, axis=0).astype(out.dtype)


def column_of(lay, shards):
    rows, cols = shards[0].shape
    return pl.pallas_call(
        partial(column_kernel, lay),
        out_shape=jax.ShapeDtypeStruct((len(shards) * rows, cols), shards[0].dtype),
        in_specs=[pl.BlockSpec(memory_space=VMEM)] * len(shards),
        out_specs=pl.BlockSpec(memory_space=VMEM),
        compiler_params=params(4),
        name="column",
    )(*shards)


def chip_sum_kernel(lay, keep, got, *outs):
    for i, ref in enumerate(outs):
        at = lay.partner(lay.core(), i, False, 1)
        ref[...] = (keep[at].astype(jnp.float32) + got[at].astype(jnp.float32)).astype(ref.dtype)


def chip_sum(lay, keep, got):
    plane, rows, cols = keep.shape
    block = cols if cols < 2048 else 1536
    part = pl.BlockSpec((rows, block), lambda i: (0, i))
    whole = pl.BlockSpec((plane, rows, block), lambda i: (0, 0, i))
    return pl.pallas_call(
        partial(chip_sum_kernel, lay),
        grid=(cols // block,),
        out_shape=[jax.ShapeDtypeStruct((rows, cols), jnp.float32)]
        + [jax.ShapeDtypeStruct((rows, cols), jnp.bfloat16)] * (plane - 1),
        in_specs=[whole, whole],
        out_specs=[part] * plane,
        compiler_params=params(12),
        name="chip_sum",
    )(keep, got)


def plane_sum_kernel(lay, own, *refs):
    got, outs = refs[: lay.plane - 1], refs[lay.plane - 1 :]
    rows = outs[0].shape[0]
    total = own[...]
    for ref in got:
        total = total + ref[...].astype(jnp.float32)
    for i, ref in enumerate(outs):
        at = lay.partner(lay.core(), i, True, 1)
        part = total[:rows]
        for j in range(1, lay.rep):
            part = jnp.where(at == j, total[j * rows : (j + 1) * rows], part)
        ref[...] = part.astype(ref.dtype)


def plane_sum(lay, own, got):
    rows, cols = own.shape
    reps = lay.rep
    block = cols if cols < 2048 else 1536
    part = pl.BlockSpec((rows, block), lambda i: (0, i))
    small = pl.BlockSpec((rows // reps, block), lambda i: (0, i))
    return pl.pallas_call(
        partial(plane_sum_kernel, lay),
        grid=(cols // block,),
        out_shape=[jax.ShapeDtypeStruct((rows // reps, cols), jnp.float32)]
        + [jax.ShapeDtypeStruct((rows // reps, cols), jnp.bfloat16)] * (reps - 1),
        in_specs=[part] * (1 + len(got)),
        out_specs=[small] * reps,
        compiler_params=params(10),
        name="plane_sum",
    )(own, *got)


def full_sum(value):
    return jnp.sum(jnp.sum(value, axis=1, keepdims=True), axis=0, keepdims=True)


def turned(columns):
    rows, count = columns.shape
    same = lax.broadcasted_iota(jnp.int32, (rows, rows), 0) == lax.broadcasted_iota(jnp.int32, (rows, rows), 1)
    line = lax.broadcasted_iota(jnp.int32, (count, rows), 0)
    out = jnp.zeros((count, rows), jnp.float32)
    for j in range(count):
        row = jnp.sum(jnp.where(same, columns[:, j : j + 1], 0.0), axis=0, keepdims=True)
        out = jnp.where(line == j, row, out)
    return out


def moments_kernel(pieces_of, first_index, reps, *refs):
    n = len(pieces_of)
    grads, arrays = refs[:reps], refs[reps:]
    total = grads[0][...]
    for ref in grads[1:]:
        total = total + ref[...].astype(jnp.float32)
    weights, firsts, seconds = arrays[:n], arrays[n : 2 * n], arrays[2 * n : 3 * n]
    momenta, variances, directions = arrays[3 * n : 4 * n], arrays[4 * n : 5 * n], arrays[5 * n : 6 * n]
    sums = arrays[6 * n]
    lane = lax.broadcasted_iota(jnp.int32, (1, LANES), 1)
    row = jnp.zeros((1, LANES), jnp.float32)
    for i, parts in enumerate(pieces_of):
        weight_sum = jnp.zeros((1, 1), jnp.float32)
        step_sum = jnp.zeros((1, 1), jnp.float32)
        for at, size, columns in parts:
            rows = slice(at, at + size)
            gradient = total[:, columns[0] : columns[1]]
            if len(columns) > 2:
                gradient = turned(gradient)
            weight = weights[i][rows]
            momentum = BETA * firsts[i][rows] + (1.0 - BETA) * gradient
            variance = BETA * seconds[i][rows] + (1.0 - BETA) * gradient * gradient
            direction = momentum / (jnp.sqrt(variance) + ADAM_EPSILON) + DECAY * weight
            momenta[i][rows] = momentum
            variances[i][rows] = variance
            directions[i][rows] = direction
            weight_sum = weight_sum + full_sum(weight * weight)
            step_sum = step_sum + full_sum(direction * direction)
        row = jnp.where(lane == first_index[i], weight_sum, row)
        row = jnp.where(lane == 5 + first_index[i], step_sum, row)
    sums[...] = row


def moments(pieces_of, first_index, grads, weights, firsts, seconds):
    arrays = [*grads, *weights, *firsts, *seconds]
    shapes = [jax.ShapeDtypeStruct(weight.shape, jnp.float32) for weight in weights]
    outs = pl.pallas_call(
        partial(moments_kernel, pieces_of, first_index, len(grads)),
        out_shape=shapes * 3 + [jax.ShapeDtypeStruct((1, LANES), jnp.float32)],
        in_specs=[pl.BlockSpec(memory_space=VMEM)] * len(arrays),
        out_specs=[pl.BlockSpec(memory_space=VMEM)] * (3 * len(weights) + 1),
        compiler_params=params(8),
        name="moments",
    )(*arrays)
    n = len(weights)
    return outs[:n], outs[n : 2 * n], outs[2 * n : 3 * n], outs[3 * n]


def update_kernel(n, sums, *refs):
    weights, directions, updated, table = refs[:n], refs[n : 2 * n], refs[2 * n : 3 * n], refs[3 * n]
    norms = jnp.sqrt(jnp.sum(sums[...], axis=0, keepdims=True))
    row = lax.broadcasted_iota(jnp.int32, table.shape, 0)
    lane = lax.broadcasted_iota(jnp.int32, table.shape, 1)
    out = jnp.zeros(table.shape, jnp.float32)
    for i in range(n):
        weight_norm = norms[:, i : i + 1]
        step_norm = norms[:, 5 + i : 6 + i]
        ratio = weight_norm / step_norm
        updated[i][...] = weights[i][...] - RATE * ratio * directions[i][...]
        column = jnp.where(row == 0, weight_norm, jnp.where(row == 1, step_norm, ratio))
        out = jnp.where(lane == i, column, out)
    table[...] = out


def update(sums, weights, directions):
    n = len(weights)
    outs = pl.pallas_call(
        partial(update_kernel, n),
        out_shape=[jax.ShapeDtypeStruct(weight.shape, jnp.float32) for weight in weights]
        + [jax.ShapeDtypeStruct((8, LANES), jnp.float32)],
        in_specs=[pl.BlockSpec(memory_space=VMEM)] * (1 + 2 * n),
        out_specs=[pl.BlockSpec(memory_space=VMEM)] * (n + 1),
        compiler_params=params(6),
        name="update",
    )(sums, *weights, *directions)
    return outs[:n], outs[n][:3, :n]


def over(lay, value, first):
    return [value] + [lay.over(value, i, first) for i in range(1, lay.rep if first else lay.plane)]


def send_over(lay, parts, first):
    return [lay.over(part, i, first) for i, part in enumerate(parts, 1)]


def over_core(lay, blocks):
    return blocks + [lay.to_core(block) for block in blocks]


def after(values, others):
    count = len(values)
    return list(lax.optimization_barrier((*values, *others))[:count])


def exchange(lay, value):
    return lax.all_to_all(value, AXES, 0, 0)


def body(
    lay,
    inputs,
    segments,
    cotangent,
    attend_in,
    attend_out,
    expand,
    contract,
    layer_norms,
    moment_in,
    moment_out,
    moment_expand,
    moment_contract,
    moment_norms,
    square_in,
    square_out,
    square_expand,
    square_contract,
    square_norms,
):
    masters = (attend_in, attend_out, expand, contract, layer_norms)
    width = attend_in.shape[1]
    depth = attend_out.shape[1]
    hidden = expand.shape[1]
    own = attend_in.shape[0]
    count = lay.dp * lay.rep
    plain = own % 16 == 0
    norm_rows = jnp.pad(layer_norms.astype(jnp.bfloat16).T, ((0, 0), (0, LANES - 4)))
    shard1 = jnp.concatenate([attend_in.astype(jnp.bfloat16), norm_rows], axis=1)
    column1 = over(lay, shard1, True)
    rows = inputs.shape[1]
    attend_out_, expand_, contract_ = after([attend_out, expand, contract], [shard1])
    deep = [contract_[j * own : (j + 1) * own] for j in range(4)]
    shard2 = jnp.concatenate([part.astype(jnp.bfloat16) for part in (attend_out_, expand_, *deep)], axis=1)
    (shard2,) = after([shard2], column1[1:])
    column2 = over(lay, shard2, True)
    (segments_,) = after([segments], [shard1])
    x, dy, labels, begin = arrange(inputs[0], cotangent[0], segments_)
    blocks1 = over(lay, column_of(lay, after(column1, [x])), False)
    blocks2 = over(lay, column_of(lay, after(column2, blocks1)), False)
    pieces1 = over_core(lay, blocks1)
    *pieces1, x, labels = after([*pieces1, x, labels], blocks2[:1])
    qx, kx, vx, mixed, gains = attend(lay, x, labels, pieces1)
    pieces2 = over_core(lay, after(blocks2, [mixed]))
    deep_pieces = []
    if not plain:
        first = depth + hidden
        for piece in pieces2:
            part = piece[:, first:].reshape(lay.rep, own, 4, depth).transpose(0, 2, 1, 3)
            deep_pieces.append(part.reshape(-1, depth))
    outputs, dox, middle_grad, keep2, send2, second_norms, *deep_out = feed(
        lay, x, mixed, dy, gains, pieces2, deep_pieces
    )
    if not plain:
        keep2, send2 = [
            jnp.concatenate(
                [
                    wide[:, :, : depth + hidden],
                    part.reshape(lay.plane, lay.rep, 4, own, depth).transpose(0, 1, 3, 2, 4).reshape(lay.plane, -1, 4 * depth),
                ],
                axis=2,
            )
            for wide, part in zip((keep2, send2), deep_out)
        ]
    own2, *low2 = chip_sum(lay, keep2, lay.to_core(send2))
    got2 = send_over(lay, low2, False)
    (dox,) = after([dox], low2)
    packed = attend_back(qx, kx, vx, dox)
    input_gradient, first_norms = input_back(lay, x, packed, gains, middle_grad, pieces1)
    own2, *got2 = after([own2, *got2], [first_norms])
    own2, *low2 = plane_sum(lay, own2, got2)
    got2 = send_over(lay, low2, True)
    (packed_,) = after([packed], low2)
    keep1, send1 = project_back(lay, x, packed_, gains, first_norms, second_norms, own)
    own1, *low1 = chip_sum(lay, keep1, lay.to_core(send1))
    got1 = send_over(lay, low1, False)
    outputs, input_gradient = after([outputs, input_gradient], low1)
    outputs, input_gradient = arrange_back(begin, outputs, input_gradient, rows)
    spans = [[(0, own, (0, depth))], [(0, own, (depth, depth + hidden))]]
    spans.append([(j * own, own, (depth + hidden + j * depth, depth + hidden + (j + 1) * depth)) for j in range(4)])
    momenta2, variances2, directions2, sums2 = moments(
        spans, (1, 2, 3), [own2, *got2], masters[1:4],
        (moment_out, moment_expand, moment_contract), (square_out, square_expand, square_contract),
    )
    own1, *low1 = plane_sum(lay, own1, got1)
    got1 = send_over(lay, low1, True)
    momenta1, variances1, directions1, sums1 = moments(
        [[(0, own, (0, width))], [(0, 4, (width, width + 4, True))]], (0, 4), [own1, *got1], (attend_in, layer_norms),
        (moment_in, moment_norms), (square_in, square_norms),
    )
    sums = exchange(lay, jnp.broadcast_to((sums1 + sums2)[None], (count, 1, LANES)))
    directions = (directions1[0], *directions2, directions1[1])
    updated, trust_table = update(sums[:, 0], masters, directions)
    momenta = (momenta1[0], *momenta2, momenta1[1])
    variances = (variances1[0], *variances2, variances1[1])
    return (outputs[None], input_gradient[None], *updated, *momenta, *variances, trust_table)


def solution(mesh):
    placed = (
        P(("dp", "rep"), None, None),
        P(("dp", "rep"), None),
        P(("dp", "rep"), None, None),
        P(("dp", "rep"), None),
        P(("dp", "rep"), None),
        P(("dp", "rep"), None),
        P(("dp", "rep"), None),
        P(None, ("dp", "rep")),
        P(("dp", "rep"), None),
        P(("dp", "rep"), None),
        P(("dp", "rep"), None),
        P(("dp", "rep"), None),
        P(None, ("dp", "rep")),
        P(("dp", "rep"), None),
        P(("dp", "rep"), None),
        P(("dp", "rep"), None),
        P(("dp", "rep"), None),
        P(None, ("dp", "rep")),
    )
    return jax.shard_map(
        partial(body, Layout(mesh)),
        mesh=mesh,
        in_specs=placed,
        out_specs=(
            P(("dp", "rep"), None, None),
            P(("dp", "rep"), None, None),
            P(("dp", "rep"), None),
            P(("dp", "rep"), None),
            P(("dp", "rep"), None),
            P(("dp", "rep"), None),
            P(None, ("dp", "rep")),
            P(("dp", "rep"), None),
            P(("dp", "rep"), None),
            P(("dp", "rep"), None),
            P(("dp", "rep"), None),
            P(None, ("dp", "rep")),
            P(("dp", "rep"), None),
            P(("dp", "rep"), None),
            P(("dp", "rep"), None),
            P(("dp", "rep"), None),
            P(None, ("dp", "rep")),
            P(),
        ),
        check_vma=False,
    )
```

```python
from functools import partial
import math

import jax
import jax.numpy as jnp
from jax import lax
from jax.experimental import pallas as pl
from jax.experimental.pallas import tpu as pltpu
from jax.sharding import PartitionSpec as P

HEADS = 8
HEAD_DIM = 64


EPSILON = 1e-05
ADAM_EPSILON = 1e-06
DECAY = 0.01
RATE = 0.5
BETA = 0.5
LANES = 128
HALF = 64
BIG = 1e30
FEATS = 4
TILE = 256
THIN = 32
CHUNK = 352
DEEP_CHUNK = 528
VMEM = pltpu.MemorySpace.VMEM
AXES = ("dp", "rep")


def params(mebibytes):
    return pltpu.CompilerParams(vmem_limit_bytes=mebibytes * 1024 * 1024)


def dot(a, b, ca, cb):
    return lax.dot_general(a, b, (((ca,), (cb,)), ((), ())), preferred_element_type=jnp.float32)


def normalize(values):
    center = values - jnp.mean(values, axis=-1, keepdims=True)
    scale = lax.rsqrt(jnp.mean(center * center, axis=-1, keepdims=True) + EPSILON)
    return center * scale, scale


class Layout:
    def __init__(self, mesh, mixed):
        self.dp = mesh.shape["dp"]
        self.rep = mesh.shape["rep"]
        self.plane = self.dp // 2
        self.mixed = mixed and self.plane == self.rep

    def pairs(self, move):
        pairs = []
        for p in range(self.plane):
            for c in range(2):
                for z in range(self.rep):
                    q, d, w = move(p, c, z)
                    pairs.append(((p * 2 + c) * self.rep + z, (q * 2 + d) * self.rep + w))
        return pairs

    def over(self, value, i, first):
        def move(p, c, z):
            along_z = (first == (c == 0)) if self.mixed else first
            return (p, c, (z + i) % self.rep) if along_z else (p ^ i, c, z)

        return lax.ppermute(value, AXES, self.pairs(move))

    def to_core(self, value):
        return lax.ppermute(value, AXES, self.pairs(lambda p, c, z: (p, 1 - c, z)))

    def core(self):
        return lax.rem(lax.axis_index("dp"), 2)

    def partner(self, side, i, first, sign):
        along_z = lax.rem(lax.axis_index("rep") + (sign * i) % self.rep, self.rep)
        in_plane = lax.div(lax.axis_index("dp"), 2) ^ i
        if not self.mixed:
            return along_z if first else in_plane
        return jnp.where(side == 0, along_z, in_plane) if first else jnp.where(side == 0, in_plane, along_z)

    def device(self, side, second, first):
        plain = (2 * second + side) * self.rep + first
        return jnp.where(side == 0, plain, (2 * first + side) * self.rep + second) if self.mixed else plain


def row_blocks(lay, side, second, rows):
    firsts = lay.rep
    if lay.mixed:
        return [(j * rows, pl.multiple_of(lay.device(side, second, j) * rows, rows), rows) for j in range(firsts)]
    return [(0, pl.multiple_of(lay.device(side, second, 0) * rows, firsts * rows), firsts * rows)]


def assemble(lay, pieces, full_ref, columns):
    count = len(pieces) // 2
    for i, piece in enumerate(pieces):
        side = lay.core() if i < count else 1 - lay.core()
        second = lay.partner(side, i % count, False, -1)
        for at, to, rows in row_blocks(lay, side, second, piece.shape[0] // lay.rep):
            full_ref[pl.ds(to, rows), :] = piece[at : at + rows, columns]


def assemble_deep(lay, pieces, full_ref, first):
    count = len(pieces) // 2
    width = full_ref.shape[1]
    for i, piece in enumerate(pieces):
        side = lay.core() if i < count else 1 - lay.core()
        second = lay.partner(side, i % count, False, -1)
        rows = piece.shape[0] // lay.rep
        for z in range(lay.rep):
            to = pl.multiple_of(lay.device(side, second, z) * 4 * rows, 4 * rows)
            for j in range(4):
                source = piece[z * rows : (z + 1) * rows, first + j * width : first + (j + 1) * width]
                full_ref[pl.ds(to + j * rows, rows), :] = source


def split_rows(lay, full_ref, keep_ref, send_ref, lanes):
    for target, side in ((keep_ref, lay.core()), (send_ref, 1 - lay.core())):
        for second in range(target.shape[0]):
            for at, source, rows in row_blocks(lay, side, second, target.shape[1] // lay.rep):
                target[second, at : at + rows, lanes] = full_ref[pl.ds(source, rows), :].astype(target.dtype)


def split_deep(lay, full_ref, keep_ref, send_ref, first):
    width = full_ref.shape[1]
    rows = keep_ref.shape[1] // lay.rep
    for target, side in ((keep_ref, lay.core()), (send_ref, 1 - lay.core())):
        for second in range(target.shape[0]):
            for z in range(lay.rep):
                source = pl.multiple_of(lay.device(side, second, z) * 4 * rows, 4 * rows)
                for j in range(4):
                    part = full_ref[pl.ds(source + j * rows, rows), :]
                    columns = slice(first + j * width, first + (j + 1) * width)
                    target[second, z * rows : (z + 1) * rows, columns] = part.astype(target.dtype)


def row_chunks(rows, size):
    return [(at, min(size, rows - at)) for at in range(0, rows, size)]


def windows(rows):
    half = (rows - THIN) // 2
    span = half + THIN
    spans = [(at, TILE, 0, span) for at in range(0, half, TILE)]
    spans.append((half, THIN, 0, rows))
    return spans + [(at, TILE, half, span) for at in range(span, rows, TILE)]


def arrange_kernel(inputs, cotangent, segments, x, dy, labels, begin, room):
    tokens = segments.shape[1]
    half = tokens // 2
    memory = inputs.shape[0] - tokens
    segment = segments[...].astype(jnp.float32)
    ahead = pltpu.roll(jnp.broadcast_to(segment, (8, tokens)), tokens - half + 1, 1)[:1]
    lane = lax.broadcasted_iota(jnp.int32, (1, tokens), 1)
    fits = (segment == ahead) & (lane <= half)
    start = jnp.sum(jnp.where(fits, lane.astype(jnp.float32), 0.0), axis=1, keepdims=True)
    begin[...] = jnp.broadcast_to(start, begin.shape)
    row = lax.broadcasted_iota(jnp.int32, (half, LANES), 0).astype(jnp.float32)
    early = row < start
    thin = lax.broadcasted_iota(jnp.int32, (THIN, LANES), 0) < memory
    for source, target in ((inputs, x), (cotangent, dy)):
        for at in range(0, inputs.shape[1], LANES):
            columns = slice(at, at + LANES)
            room[: inputs.shape[0]] = source[:, columns].astype(jnp.float32)
            left, right = room[memory : memory + half], room[memory + half : memory + tokens]
            target[:half, columns] = jnp.where(early, right, left).astype(target.dtype)
            target[half : half + THIN, columns] = jnp.where(thin, room[:THIN], 0.0).astype(target.dtype)
            target[half + THIN :, columns] = jnp.where(early, left, right).astype(target.dtype)
    left = jnp.transpose(jnp.broadcast_to(segment[:, :half], (LANES, half)))
    right = jnp.transpose(jnp.broadcast_to(segment[:, half:], (LANES, half)))
    labels[:half] = jnp.where(early, right, left).astype(jnp.int32)
    labels[half : half + THIN] = jnp.where(thin, -1, -2)
    labels[half + THIN :] = jnp.where(early, left, right).astype(jnp.int32)


def arrange(inputs, cotangent, segments):
    width = inputs.shape[1]
    rows = segments.shape[1] + THIN
    return pl.pallas_call(
        arrange_kernel,
        out_shape=(
            jax.ShapeDtypeStruct((rows, width), inputs.dtype),
            jax.ShapeDtypeStruct((rows, width), inputs.dtype),
            jax.ShapeDtypeStruct((rows, LANES), jnp.int32),
            jax.ShapeDtypeStruct((8, LANES), jnp.float32),
        ),
        in_specs=[pl.BlockSpec(memory_space=VMEM)] * 3,
        out_specs=[pl.BlockSpec(memory_space=VMEM)] * 4,
        scratch_shapes=[pltpu.VMEM((rows, LANES), jnp.float32)],
        compiler_params=params(8),
        name="arrange",
    )(inputs, cotangent, segments)


def finish_kernel(begin, middle, active, contract, grad_in, outputs, grad_out, room):
    rows = outputs.shape[0]
    half = (middle.shape[0] - THIN) // 2
    memory = rows - 2 * half
    wide = room.shape[1]
    row = lax.broadcasted_iota(jnp.int32, (half, wide), 0).astype(jnp.float32)
    early = row < begin[:1, :1]

    def place(value, target, columns):
        left, right = value[:half], value[half + THIN :]
        room[:THIN] = value[half : half + THIN]
        room[memory : memory + half] = jnp.where(early, right, left)
        room[memory + half : rows] = jnp.where(early, left, right)
        target[:, columns] = room[:rows].astype(target.dtype)

    for at in range(0, middle.shape[1], wide):
        columns = slice(at, at + wide)
        place(middle[:, columns] + dot(active[...], contract[:, columns], 1, 0), outputs, columns)
        place(grad_in[:, columns].astype(jnp.float32), grad_out, columns)


def finish(begin, middle, active, contract, grad_in, rows):
    width = middle.shape[1]
    return pl.pallas_call(
        finish_kernel,
        out_shape=[jax.ShapeDtypeStruct((rows, width), grad_in.dtype)] * 2,
        in_specs=[pl.BlockSpec(memory_space=VMEM)] * 5,
        out_specs=[pl.BlockSpec(memory_space=VMEM)] * 2,
        scratch_shapes=[pltpu.VMEM((middle.shape[0], 256), jnp.float32)],
        compiler_params=params(10),
        name="finish",
    )(begin, middle, active, contract, grad_in)


def attend_kernel(lay, count, x, labels, *refs):
    pieces = refs[:count]
    qx, kx, vx, mixed, gains, weight, qs = refs[count:]
    rows = x.shape[0]
    width = mixed.shape[1]
    assemble(lay, pieces, weight, slice(None))
    gains[...] = jnp.transpose(weight[:, 3 * width :].astype(jnp.float32))[:8]
    gain, bias = gains[0:1], gains[1:2]

    def one_chunk(i, carry):
        span = pl.ds(pl.multiple_of(i * CHUNK, CHUNK), CHUNK)
        normed, _ = normalize(x[span].astype(jnp.float32))
        first = (normed * gain + bias).astype(jnp.bfloat16)
        lane = lax.broadcasted_iota(jnp.int32, (CHUNK, LANES), 1)
        low = lane < HALF
        feature = lane % HALF
        label = labels[span]
        blocked = ((feature < FEATS) & (label >= 0) & (feature != label)) | (feature == FEATS)
        query_side = jnp.where(blocked, -BIG, 0.0)
        marked = ((feature < FEATS) & (feature == label)) | ((feature == FEATS) & (label == -2))
        key_side = jnp.where(marked | (feature > FEATS), 1.0, 0.0)
        sides = (query_side, key_side, jnp.ones_like(key_side))
        for kind, target in enumerate((qs, kx, vx)):
            whole = dot(first, weight[:, kind * width : (kind + 1) * width], 1, 0)
            whole = whole.astype(jnp.bfloat16).astype(jnp.float32)
            for pair in range(width // LANES):
                part = whole[:, pair * LANES : (pair + 1) * LANES]
                if kind == 0:
                    part = part * (1.0 / math.sqrt(HEAD_DIM))
                at = 2 * pair * LANES
                target[span, at : at + LANES] = jnp.where(low, part, sides[kind]).astype(jnp.bfloat16)
                target[span, at + LANES : at + 2 * LANES] = jnp.where(low, sides[kind], part).astype(jnp.bfloat16)
        return carry

    lax.fori_loop(0, rows // CHUNK, one_chunk, 0)

    def one_pair(pair, carry):
        columns = pl.ds(pl.multiple_of(pair * LANES, LANES), LANES)
        for at, size, key_at, key_size in windows(rows):
            span = pl.ds(at, size)
            seen = pl.ds(key_at, key_size)
            lane = lax.broadcasted_iota(jnp.int32, (size, LANES), 1)
            low = lane < HALF
            feature = lane % HALF
            got = []
            for side in range(2):
                head = pl.ds(pl.multiple_of((2 * pair + side) * LANES, LANES), LANES)
                queries = qs[span, head]
                scores = dot(queries, kx[seen, head], 1, 1)
                highest = jnp.max(scores, axis=1, keepdims=True)
                raised = jnp.exp(scores - highest).astype(jnp.bfloat16)
                found = dot(raised, vx[seen, head], 1, 0)
                total = -(highest + jnp.log(found))
                first = total.astype(jnp.bfloat16).astype(jnp.float32)
                second = (total - first).astype(jnp.bfloat16).astype(jnp.float32)
                third = total - first - second
                values = jnp.where(feature == 5, first, jnp.where(feature == 6, second, third))
                place = (feature > FEATS) & (feature < 8) & (low if side else ~low)
                qx[span, head] = jnp.where(place, values, queries.astype(jnp.float32)).astype(jnp.bfloat16)
                got.append(found)
            over = pltpu.roll(jnp.where(low, got[1], got[0]), HALF, 1)
            mixed[span, columns] = (jnp.where(low, got[0], got[1]) / over).astype(jnp.bfloat16)
        return carry

    lax.fori_loop(0, width // LANES, one_pair, 0)


def attend(lay, x, labels, pieces):
    rows, width = x.shape
    wide = jax.ShapeDtypeStruct((rows, 2 * width), jnp.bfloat16)
    depth = len(pieces) * pieces[0].shape[0]
    return pl.pallas_call(
        partial(attend_kernel, lay, len(pieces)),
        out_shape=(
            wide,
            wide,
            wide,
            jax.ShapeDtypeStruct((rows, width), jnp.bfloat16),
            jax.ShapeDtypeStruct((8, width), jnp.float32),
        ),
        in_specs=[pl.BlockSpec(memory_space=VMEM)] * (2 + len(pieces)),
        out_specs=[pl.BlockSpec(memory_space=VMEM)] * 5,
        scratch_shapes=[
            pltpu.VMEM((depth, pieces[0].shape[1]), jnp.bfloat16),
            pltpu.VMEM((rows, 2 * width), jnp.bfloat16),
        ],
        compiler_params=params(16),
        name="attend",
    )(x, labels, *pieces)


def attend_back_kernel(qx, kx, vx, dox, packed, total):
    rows = qx.shape[0]
    width = packed.shape[1] // 3

    def one_pair(pair, carry):
        heads = [pl.ds(pl.multiple_of((2 * pair + side) * LANES, LANES), LANES) for side in range(2)]
        spots = [pl.ds(pl.multiple_of(kind * width + pair * LANES, LANES), LANES) for kind in range(3)]
        total[...] = jnp.zeros_like(total)
        for at, size, query_at, query_size in windows(rows):
            span = pl.ds(at, size)
            seen = pl.ds(query_at, query_size)
            low = lax.broadcasted_iota(jnp.int32, (size, LANES), 1) < HALF
            got = []
            for side in range(2):
                head = heads[side]
                keys = kx[span, head]
                queries = qx[seen, head]
                upstream = dox[seen, head]
                attention = jnp.exp(dot(keys, queries, 1, 1))
                grad = dot(vx[span, head], upstream, 1, 1)
                scores = (attention * grad).astype(jnp.bfloat16)
                got.append((dot(scores, queries, 1, 0), dot(attention.astype(jnp.bfloat16), upstream, 1, 0)))
                total[side, seen] += dot(scores, keys, 0, 0)
            packed[span, spots[1]] = jnp.where(low, got[0][0], got[1][0]).astype(jnp.bfloat16)
            packed[span, spots[2]] = jnp.where(low, got[0][1], got[1][1]).astype(jnp.bfloat16)
        low = lax.broadcasted_iota(jnp.int32, (rows, LANES), 1) < HALF
        packed[:, spots[0]] = (jnp.where(low, total[0], total[1]) * (1.0 / math.sqrt(HEAD_DIM))).astype(jnp.bfloat16)
        return carry

    lax.fori_loop(0, width // LANES, one_pair, 0)


def attend_back(qx, kx, vx, dox):
    rows, wide = qx.shape
    return pl.pallas_call(
        attend_back_kernel,
        out_shape=jax.ShapeDtypeStruct((rows, 3 * wide // 2), jnp.bfloat16),
        in_specs=[pl.BlockSpec(memory_space=VMEM)] * 4,
        out_specs=pl.BlockSpec(memory_space=VMEM),
        scratch_shapes=[pltpu.VMEM((2, rows, LANES), jnp.float32)],
        compiler_params=params(16),
        name="attend_back",
    )(qx, kx, vx, dox)


def norm_back(grad, normed, scale, gain):
    scaled = grad * gain
    return scale * (
        scaled
        - jnp.mean(scaled, axis=-1, keepdims=True)
        - normed * jnp.mean(scaled * normed, axis=-1, keepdims=True)
    )


def feed_kernel(lay, count, deep_count, x, mixed, dy, gains, *refs):
    pieces = refs[:count]
    deep_pieces = refs[count : count + deep_count]
    outs = refs[count + deep_count : -5]
    middle, middle_grad, middle_low, active, contract, out_weight, keep2, send2, norm_grads, *deep_out = outs
    wide, hidden_grad, second, block, deep_block = refs[-5:]
    rows, width = x.shape
    hidden = contract.shape[0]
    assemble(lay, pieces, wide, slice(0, width + hidden))
    if deep_count:
        assemble(lay, deep_pieces, contract, slice(None))
    else:
        assemble_deep(lay, pieces, contract, width + hidden)
    out_weight[...] = wide[:, :width]
    gain, bias = gains[2:3], gains[3:4]
    zero = jnp.zeros((1, width), jnp.float32)

    def one_chunk(i, carry):
        gain_sum, bias_sum = carry
        span = pl.ds(pl.multiple_of(i * DEEP_CHUNK, DEEP_CHUNK), DEEP_CHUNK)
        start = x[span].astype(jnp.float32) + dot(mixed[span], wide[:, :width], 1, 0)
        middle[span] = start
        normed, scale = normalize(start)
        low = (normed * gain + bias).astype(jnp.bfloat16)
        second[span] = low
        for start in range(0, hidden, 512):
            part = slice(start, start + 512)
            up = dot(low, wide[:, width + start : width + start + 512], 1, 0)
            square = up * up
            bend = jnp.tanh(0.7978845608028654 * up * (1.0 + 0.044715 * square))
            half = 0.5 * (1.0 + bend)
            active[span, part] = (up * half).astype(jnp.bfloat16)
            slope = half + 0.5 * up * (1.0 - bend * bend) * (0.7978845608028654 * (1.0 + 3 * 0.044715 * square))
            hidden_grad[span, part] = (dot(dy[span], contract[part], 1, 1) * slope).astype(jnp.bfloat16)
        back = dot(hidden_grad[span], wide[:, width:], 1, 1)
        gain_sum = gain_sum + jnp.sum(back * normed, axis=0, keepdims=True)
        bias_sum = bias_sum + jnp.sum(back, axis=0, keepdims=True)
        grad = dy[span].astype(jnp.float32) + norm_back(back, normed, scale, gain)
        middle_grad[span] = grad
        middle_low[span] = grad.astype(jnp.bfloat16)
        return gain_sum, bias_sum

    gain_sum, bias_sum = lax.fori_loop(0, rows // DEEP_CHUNK, one_chunk, (zero, zero))
    norm_grads[...] = jnp.concatenate([gain_sum, bias_sum, jnp.zeros((6, width), jnp.float32)], axis=0)

    def one_block(i, carry):
        columns = pl.ds(pl.multiple_of(i * 512, 512), 512)
        deep_block[columns] = dot(active[:, columns], dy[...], 0, 0)
        block[...] = dot(second[...], hidden_grad[:, columns], 0, 0)
        split_rows(lay, block, keep2, send2, pl.ds(pl.multiple_of(width + i * 512, 512), 512))
        return carry

    lax.fori_loop(0, hidden // 512, one_block, 0)
    if deep_count:
        split_rows(lay, deep_block, *deep_out, slice(0, width))
    else:
        split_deep(lay, deep_block, keep2, send2, width + hidden)
    block[...] = dot(mixed[...], middle_low[...], 0, 0)
    split_rows(lay, block, keep2, send2, slice(0, width))


def feed(lay, x, mixed, dy, gains, pieces, deep_pieces):
    rows, width = x.shape
    plane = len(pieces) // 2
    deep = pieces[0].shape[0]
    columns = pieces[0].shape[1]
    hidden = 4 * width
    out_shape = [
        jax.ShapeDtypeStruct((rows, width), jnp.float32),
        jax.ShapeDtypeStruct((rows, width), jnp.float32),
        jax.ShapeDtypeStruct((rows, width), jnp.bfloat16),
        jax.ShapeDtypeStruct((rows, hidden), jnp.bfloat16),
        jax.ShapeDtypeStruct((hidden, width), jnp.bfloat16),
        jax.ShapeDtypeStruct((width, width), jnp.bfloat16),
        jax.ShapeDtypeStruct((plane, deep, columns), jnp.bfloat16),
        jax.ShapeDtypeStruct((plane, deep, columns), jnp.bfloat16),
        jax.ShapeDtypeStruct((8, width), jnp.float32),
    ]
    if deep_pieces:
        out_shape.append(jax.ShapeDtypeStruct((plane, 4 * deep, width), jnp.bfloat16))
        out_shape.append(jax.ShapeDtypeStruct((plane, 4 * deep, width), jnp.bfloat16))
    return pl.pallas_call(
        partial(feed_kernel, lay, len(pieces), len(deep_pieces)),
        out_shape=out_shape,
        in_specs=[pl.BlockSpec(memory_space=VMEM)] * (4 + len(pieces) + len(deep_pieces)),
        out_specs=[pl.BlockSpec(memory_space=VMEM)] * len(out_shape),
        scratch_shapes=[
            pltpu.VMEM((width, width + hidden), jnp.bfloat16),
            pltpu.VMEM((rows, hidden), jnp.bfloat16),
            pltpu.VMEM((rows, width), jnp.bfloat16),
            pltpu.VMEM((width, 512), jnp.float32),
            pltpu.VMEM((hidden, width), jnp.float32),
        ],
        compiler_params=params(26),
        name="feed",
    )(x, mixed, dy, gains, *pieces, *deep_pieces)


def mixed_back_kernel(middle_low, mixed, out_weight, dox):
    rows, width = mixed.shape

    def one_chunk(i, carry):
        span = pl.ds(pl.multiple_of(i * DEEP_CHUNK, DEEP_CHUNK), DEEP_CHUNK)
        mixed_grad = dot(middle_low[span], out_weight[...], 1, 1).astype(jnp.bfloat16).astype(jnp.float32)
        lane = lax.broadcasted_iota(jnp.int32, (DEEP_CHUNK, LANES), 1)
        left = lane < HALF
        feature = lane % HALF
        for pair in range(width // LANES):
            columns = slice(pair * LANES, (pair + 1) * LANES)
            piece = mixed_grad[:, columns]
            product = piece * mixed[span, columns].astype(jnp.float32)
            for side in range(2):
                mine = left if side == 0 else ~left
                delta = -jnp.sum(jnp.where(mine, product, 0.0), axis=1, keepdims=True)
                one = delta.astype(jnp.bfloat16).astype(jnp.float32)
                two = (delta - one).astype(jnp.bfloat16).astype(jnp.float32)
                three = delta - one - two
                extra = jnp.where(feature == 0, one, jnp.where(feature == 1, two, jnp.where(feature == 2, three, 0.0)))
                head = (2 * pair + side) * LANES
                dox[span, head : head + LANES] = jnp.where(mine, piece, extra).astype(jnp.bfloat16)
        return carry

    lax.fori_loop(0, rows // DEEP_CHUNK, one_chunk, 0)


def mixed_back(middle_low, mixed, out_weight):
    rows, width = mixed.shape
    return pl.pallas_call(
        mixed_back_kernel,
        out_shape=jax.ShapeDtypeStruct((rows, 2 * width), jnp.bfloat16),
        in_specs=[pl.BlockSpec(memory_space=VMEM)] * 3,
        out_specs=pl.BlockSpec(memory_space=VMEM),
        compiler_params=params(10),
        name="mixed_back",
    )(middle_low, mixed, out_weight)


def project_back_kernel(lay, x, packed, gains, first_norms, second_norms, keep, send, first, block):
    rows, width = x.shape
    gain, bias = gains[0:1], gains[1:2]

    def one_chunk(i, carry):
        span = pl.ds(pl.multiple_of(i * CHUNK, CHUNK), CHUNK)
        normed, _ = normalize(x[span].astype(jnp.float32))
        first[span] = (normed * gain + bias).astype(jnp.bfloat16)
        return carry

    lax.fori_loop(0, rows // CHUNK, one_chunk, 0)

    def one_block(i, carry):
        columns = pl.ds(pl.multiple_of(i * 512, 512), 512)
        block[...] = dot(first[...], packed[:, columns], 0, 0)
        split_rows(lay, block, keep, send, columns)
        return carry

    lax.fori_loop(0, packed.shape[1] // 512, one_block, 0)
    fill = jnp.zeros((LANES - 4, width), jnp.float32)
    norms = jnp.concatenate([first_norms[:2], second_norms[:2], fill], axis=0)
    block[:, :LANES] = jnp.transpose(norms)
    split_rows(lay, block.at[:, :LANES], keep, send, slice(packed.shape[1], packed.shape[1] + LANES))


def project_back(lay, x, packed, gains, first_norms, second_norms, own):
    rows, width = x.shape
    shape = (lay.plane, lay.rep * own, packed.shape[1] + LANES)
    return pl.pallas_call(
        partial(project_back_kernel, lay),
        out_shape=(jax.ShapeDtypeStruct(shape, jnp.bfloat16), jax.ShapeDtypeStruct(shape, jnp.bfloat16)),
        in_specs=[pl.BlockSpec(memory_space=VMEM)] * 5,
        out_specs=[pl.BlockSpec(memory_space=VMEM)] * 2,
        scratch_shapes=[pltpu.VMEM((rows, width), jnp.bfloat16), pltpu.VMEM((width, 512), jnp.float32)],
        compiler_params=params(10),
        name="project_back",
    )(x, packed, gains, first_norms, second_norms)


def input_back_kernel(lay, x, packed, gains, middle_grad, *refs):
    pieces = refs[:-3]
    grad_in, norm_grads, weight = refs[-3:]
    rows, width = x.shape
    assemble(lay, pieces, weight, slice(None))
    gain = gains[0:1]
    zero = jnp.zeros((1, width), jnp.float32)

    def one_chunk(i, carry):
        gain_sum, bias_sum = carry
        span = pl.ds(pl.multiple_of(i * CHUNK, CHUNK), CHUNK)
        normed, scale = normalize(x[span].astype(jnp.float32))
        back = dot(packed[span], weight[:, : 3 * width], 1, 1)
        grad_in[span] = (middle_grad[span] + norm_back(back, normed, scale, gain)).astype(jnp.bfloat16)
        gain_sum = gain_sum + jnp.sum(back * normed, axis=0, keepdims=True)
        return gain_sum, bias_sum + jnp.sum(back, axis=0, keepdims=True)

    gain_sum, bias_sum = lax.fori_loop(0, rows // CHUNK, one_chunk, (zero, zero))
    norm_grads[...] = jnp.concatenate([gain_sum, bias_sum, jnp.zeros((6, width), jnp.float32)], axis=0)


def input_back(lay, x, packed, gains, middle_grad, pieces):
    rows, width = x.shape
    return pl.pallas_call(
        partial(input_back_kernel, lay),
        out_shape=(jax.ShapeDtypeStruct((rows, width), jnp.bfloat16), jax.ShapeDtypeStruct((8, width), jnp.float32)),
        in_specs=[pl.BlockSpec(memory_space=VMEM)] * (4 + len(pieces)),
        out_specs=[pl.BlockSpec(memory_space=VMEM)] * 2,
        scratch_shapes=[pltpu.VMEM((width, pieces[0].shape[1]), jnp.bfloat16)],
        compiler_params=params(10),
        name="input_back",
    )(x, packed, gains, middle_grad, *pieces)


def column_kernel(lay, *refs):
    out = refs[-1]
    got = [ref[...].astype(jnp.float32) for ref in refs[:-1]]
    parts = []
    for j in range(len(got)):
        part = got[0]
        for i in range(1, len(got)):
            part = jnp.where(lay.partner(lay.core(), i, True, -1) == j, got[i], part)
        parts.append(part)
    out[...] = jnp.concatenate(parts, axis=0).astype(out.dtype)


def column_of(lay, shards):
    rows, cols = shards[0].shape
    return pl.pallas_call(
        partial(column_kernel, lay),
        out_shape=jax.ShapeDtypeStruct((len(shards) * rows, cols), shards[0].dtype),
        in_specs=[pl.BlockSpec(memory_space=VMEM)] * len(shards),
        out_specs=pl.BlockSpec(memory_space=VMEM),
        compiler_params=params(4),
        name="column",
    )(*shards)


def chip_sum_kernel(lay, keep, got, *outs):
    for i, ref in enumerate(outs):
        at = lay.partner(lay.core(), i, False, 1)
        ref[...] = (keep[at].astype(jnp.float32) + got[at].astype(jnp.float32)).astype(ref.dtype)


def chip_sum(lay, keep, got):
    plane, rows, cols = keep.shape
    block = cols if cols < 2048 else 1536
    part = pl.BlockSpec((rows, block), lambda i: (0, i))
    whole = pl.BlockSpec((plane, rows, block), lambda i: (0, 0, i))
    return pl.pallas_call(
        partial(chip_sum_kernel, lay),
        grid=(cols // block,),
        out_shape=[jax.ShapeDtypeStruct((rows, cols), jnp.float32)]
        + [jax.ShapeDtypeStruct((rows, cols), jnp.bfloat16)] * (plane - 1),
        in_specs=[whole, whole],
        out_specs=[part] * plane,
        compiler_params=params(12),
        name="chip_sum",
    )(keep, got)


def plane_sum_kernel(lay, own, *refs):
    got, outs = refs[: lay.plane - 1], refs[lay.plane - 1 :]
    rows = outs[0].shape[0]
    total = own[...]
    for ref in got:
        total = total + ref[...].astype(jnp.float32)
    for i, ref in enumerate(outs):
        at = lay.partner(lay.core(), i, True, 1)
        part = total[:rows]
        for j in range(1, lay.rep):
            part = jnp.where(at == j, total[j * rows : (j + 1) * rows], part)
        ref[...] = part.astype(ref.dtype)


def plane_sum(lay, own, got):
    rows, cols = own.shape
    reps = lay.rep
    block = cols if cols < 2048 else 1536
    part = pl.BlockSpec((rows, block), lambda i: (0, i))
    small = pl.BlockSpec((rows // reps, block), lambda i: (0, i))
    return pl.pallas_call(
        partial(plane_sum_kernel, lay),
        grid=(cols // block,),
        out_shape=[jax.ShapeDtypeStruct((rows // reps, cols), jnp.float32)]
        + [jax.ShapeDtypeStruct((rows // reps, cols), jnp.bfloat16)] * (reps - 1),
        in_specs=[part] * (1 + len(got)),
        out_specs=[small] * reps,
        compiler_params=params(10),
        name="plane_sum",
    )(own, *got)


def full_sum(value):
    return jnp.sum(jnp.sum(value, axis=1, keepdims=True), axis=0, keepdims=True)


def turned(columns):
    rows, count = columns.shape
    same = lax.broadcasted_iota(jnp.int32, (rows, rows), 0) == lax.broadcasted_iota(jnp.int32, (rows, rows), 1)
    line = lax.broadcasted_iota(jnp.int32, (count, rows), 0)
    out = jnp.zeros((count, rows), jnp.float32)
    for j in range(count):
        row = jnp.sum(jnp.where(same, columns[:, j : j + 1], 0.0), axis=0, keepdims=True)
        out = jnp.where(line == j, row, out)
    return out


def moments_kernel(pieces_of, first_index, reps, more, *refs):
    n = len(pieces_of)
    grads, others, arrays = refs[:reps], refs[reps : reps + more], refs[reps + more :]
    total = grads[0][...]
    for ref in grads[1:]:
        total = total + ref[...].astype(jnp.float32)
    weights, firsts, seconds = arrays[:n], arrays[n : 2 * n], arrays[2 * n : 3 * n]
    momenta, variances, directions = arrays[3 * n : 4 * n], arrays[4 * n : 5 * n], arrays[5 * n : 6 * n]
    sums = arrays[6 * n]
    lane = lax.broadcasted_iota(jnp.int32, (1, LANES), 1)
    row = others[0][0] if more else jnp.zeros((1, LANES), jnp.float32)
    for i, parts in enumerate(pieces_of):
        weight_sum = jnp.zeros((1, 1), jnp.float32)
        step_sum = jnp.zeros((1, 1), jnp.float32)
        for at, size, columns in parts:
            rows = slice(at, at + size)
            gradient = total[:, columns[0] : columns[1]]
            if len(columns) > 2:
                gradient = turned(gradient)
            weight = weights[i][rows]
            momentum = BETA * firsts[i][rows] + (1.0 - BETA) * gradient
            variance = BETA * seconds[i][rows] + (1.0 - BETA) * gradient * gradient
            direction = momentum / (jnp.sqrt(variance) + ADAM_EPSILON) + DECAY * weight
            momenta[i][rows] = momentum
            variances[i][rows] = variance
            directions[i][rows] = direction
            weight_sum = weight_sum + full_sum(weight * weight)
            step_sum = step_sum + full_sum(direction * direction)
        row = jnp.where(lane == first_index[i], weight_sum, row)
        row = jnp.where(lane == 5 + first_index[i], step_sum, row)
    sums[...] = jnp.broadcast_to(row, sums.shape)


def moments(pieces_of, first_index, grads, others, copies, weights, firsts, seconds):
    arrays = [*grads, *others, *weights, *firsts, *seconds]
    shapes = [jax.ShapeDtypeStruct(weight.shape, jnp.float32) for weight in weights]
    outs = pl.pallas_call(
        partial(moments_kernel, pieces_of, first_index, len(grads), len(others)),
        out_shape=shapes * 3 + [jax.ShapeDtypeStruct((copies, 1, LANES), jnp.float32)],
        in_specs=[pl.BlockSpec(memory_space=VMEM)] * len(arrays),
        out_specs=[pl.BlockSpec(memory_space=VMEM)] * (3 * len(weights) + 1),
        compiler_params=params(8),
        name="moments",
    )(*arrays)
    n = len(weights)
    return outs[:n], outs[n : 2 * n], outs[2 * n : 3 * n], outs[3 * n]


def update_kernel(n, sums, *refs):
    weights, directions, updated, table = refs[:n], refs[n : 2 * n], refs[2 * n : 3 * n], refs[3 * n]
    norms = jnp.sqrt(jnp.sum(sums[...], axis=0))
    row = lax.broadcasted_iota(jnp.int32, table.shape, 0)
    lane = lax.broadcasted_iota(jnp.int32, table.shape, 1)
    out = jnp.zeros(table.shape, jnp.float32)
    for i in range(n):
        weight_norm = norms[:, i : i + 1]
        step_norm = norms[:, 5 + i : 6 + i]
        ratio = weight_norm / step_norm
        updated[i][...] = weights[i][...] - RATE * ratio * directions[i][...]
        column = jnp.where(row == 0, weight_norm, jnp.where(row == 1, step_norm, ratio))
        out = jnp.where(lane == i, column, out)
    table[...] = out


def update(sums, weights, directions):
    n = len(weights)
    outs = pl.pallas_call(
        partial(update_kernel, n),
        out_shape=[jax.ShapeDtypeStruct(weight.shape, jnp.float32) for weight in weights]
        + [jax.ShapeDtypeStruct((3, n), jnp.float32)],
        in_specs=[pl.BlockSpec(memory_space=VMEM)] * (1 + 2 * n),
        out_specs=[pl.BlockSpec(memory_space=VMEM)] * (n + 1),
        compiler_params=params(6),
        name="update",
    )(sums, *weights, *directions)
    return outs[:n], outs[n]


def over(lay, value, first):
    return [value] + [lay.over(value, i, first) for i in range(1, lay.rep if first else lay.plane)]


def send_over(lay, parts, first):
    return [lay.over(part, i, first) for i, part in enumerate(parts, 1)]


def over_core(lay, blocks):
    return blocks + [lay.to_core(block) for block in blocks]


def after(values, others):
    count = len(values)
    return list(lax.optimization_barrier((*values, *others))[:count])


def exchange(lay, value):
    return lax.all_to_all(value, AXES, 0, 0)


def body(
    lay,
    inputs,
    segments,
    cotangent,
    attend_in,
    attend_out,
    expand,
    contract,
    layer_norms,
    moment_in,
    moment_out,
    moment_expand,
    moment_contract,
    moment_norms,
    square_in,
    square_out,
    square_expand,
    square_contract,
    square_norms,
):
    plain, twin = lay
    lay = plain
    masters = (attend_in, attend_out, expand, contract, layer_norms)
    width = attend_in.shape[1]
    depth = attend_out.shape[1]
    hidden = expand.shape[1]
    own = attend_in.shape[0]
    count = lay.dp * lay.rep
    whole_tiles = own % 16 == 0
    norm_rows = jnp.pad(layer_norms.astype(jnp.bfloat16).T, ((0, 0), (0, LANES - 4)))
    shard1 = jnp.concatenate([attend_in.astype(jnp.bfloat16), norm_rows], axis=1)
    column1 = over(plain, shard1, True)
    rows = inputs.shape[1]
    attend_out_, expand_, contract_ = after([attend_out, expand, contract], [shard1])
    deep = [contract_[j * own : (j + 1) * own] for j in range(4)]
    shard2 = jnp.concatenate([part.astype(jnp.bfloat16) for part in (attend_out_, expand_, *deep)], axis=1)
    (shard2,) = after([shard2], column1[1:])
    column2 = over(twin, shard2, True)
    blocks1 = over(plain, column_of(plain, column1), False)
    (segments_,) = after([segments], blocks1[:1])
    x, dy, labels, begin = arrange(inputs[0], cotangent[0], segments_)
    blocks2 = over(twin, column_of(twin, after(column2, [*blocks1, x])), False)
    pieces1 = over_core(lay, blocks1)
    *pieces1, x, labels = after([*pieces1, x, labels], blocks2[:1])
    qx, kx, vx, mixed, gains = attend(plain, x, labels, pieces1)
    near = lay.to_core(blocks2[0])
    blocks2[1:] = after(blocks2[1:], [mixed])
    pieces2 = [*blocks2, near, *[lay.to_core(block) for block in blocks2[1:]]]
    deep_pieces = []
    if not whole_tiles:
        first = depth + hidden
        for piece in pieces2:
            part = piece[:, first:].reshape(lay.rep, own, 4, depth).transpose(0, 2, 1, 3)
            deep_pieces.append(part.reshape(-1, depth))
    middle, middle_grad, middle_low, active, contract_all, out_weight, keep2, send2, second_norms, *deep_out = feed(
        twin, x, mixed, dy, gains, pieces2, deep_pieces
    )
    if not whole_tiles:
        keep2, send2 = [
            jnp.concatenate(
                [
                    wide[:, :, : depth + hidden],
                    part.reshape(lay.plane, lay.rep, 4, own, depth).transpose(0, 1, 3, 2, 4).reshape(lay.plane, -1, 4 * depth),
                ],
                axis=2,
            )
            for wide, part in zip((keep2, send2), deep_out)
        ]
    chip2 = lay.to_core(send2)
    dox = mixed_back(middle_low, mixed, out_weight)
    keep2, chip2 = after([keep2, chip2], [dox])
    own2, *low2 = chip_sum(twin, keep2, chip2)
    got2 = send_over(twin, low2, False)
    (dox,) = after([dox], low2)
    packed = attend_back(qx, kx, vx, dox)
    input_gradient, first_norms = input_back(plain, x, packed, gains, middle_grad, pieces1)
    keep1, send1 = project_back(plain, x, packed, gains, first_norms, second_norms, own)
    own2, *got2 = after([own2, *got2], [send1])
    own2, *low2 = plane_sum(twin, own2, got2)
    got2 = send_over(twin, low2, True)
    (send1,) = after([send1], low2[:1])
    own1, *low1 = chip_sum(plain, keep1, lay.to_core(send1))
    got1 = send_over(plain, low1, False)
    spans = [[(0, own, (0, depth))], [(0, own, (depth, depth + hidden))]]
    spans.append([(j * own, own, (depth + hidden + j * depth, depth + hidden + (j + 1) * depth)) for j in range(4)])
    momenta2, variances2, directions2, sums2 = moments(
        spans, (1, 2, 3), [own2, *got2], [], 1, masters[1:4],
        (moment_out, moment_expand, moment_contract), (square_out, square_expand, square_contract),
    )
    own1, *low1 = plane_sum(plain, own1, got1)
    got1 = send_over(plain, low1, True)
    momenta1, variances1, directions1, sums1 = moments(
        [[(0, own, (0, width))], [(0, 4, (width, width + 4, True))]], (0, 4), [own1, *got1], [sums2], count, (attend_in, layer_norms),
        (moment_in, moment_norms), (square_in, square_norms),
    )
    sums = exchange(lay, sums1)
    (middle,) = after([middle], [sums1])
    outputs, input_gradient = finish(begin, middle, active, contract_all, input_gradient, rows)
    directions = (directions1[0], *directions2, directions1[1])
    updated, trust_table = update(sums, masters, directions)
    momenta = (momenta1[0], *momenta2, momenta1[1])
    variances = (variances1[0], *variances2, variances1[1])
    return (outputs[None], input_gradient[None], *updated, *momenta, *variances, trust_table)


def solution(mesh):
    placed = (
        P(("dp", "rep"), None, None),
        P(("dp", "rep"), None),
        P(("dp", "rep"), None, None),
        P(("dp", "rep"), None),
        P(("dp", "rep"), None),
        P(("dp", "rep"), None),
        P(("dp", "rep"), None),
        P(None, ("dp", "rep")),
        P(("dp", "rep"), None),
        P(("dp", "rep"), None),
        P(("dp", "rep"), None),
        P(("dp", "rep"), None),
        P(None, ("dp", "rep")),
        P(("dp", "rep"), None),
        P(("dp", "rep"), None),
        P(("dp", "rep"), None),
        P(("dp", "rep"), None),
        P(None, ("dp", "rep")),
    )
    return jax.shard_map(
        partial(body, (Layout(mesh, False), Layout(mesh, True))),
        mesh=mesh,
        in_specs=placed,
        out_specs=(
            P(("dp", "rep"), None, None),
            P(("dp", "rep"), None, None),
            P(("dp", "rep"), None),
            P(("dp", "rep"), None),
            P(("dp", "rep"), None),
            P(("dp", "rep"), None),
            P(None, ("dp", "rep")),
            P(("dp", "rep"), None),
            P(("dp", "rep"), None),
            P(("dp", "rep"), None),
            P(("dp", "rep"), None),
            P(None, ("dp", "rep")),
            P(("dp", "rep"), None),
            P(("dp", "rep"), None),
            P(("dp", "rep"), None),
            P(("dp", "rep"), None),
            P(None, ("dp", "rep")),
            P(),
        ),
        check_vma=False,
    )
```

```python
from functools import partial
import math

import jax
import jax.numpy as jnp
from jax import lax
from jax.experimental import pallas as pl
from jax.experimental.pallas import tpu as pltpu
from jax.sharding import PartitionSpec as P

HEADS = 8
HEAD_DIM = 64


EPSILON = 1e-05
ADAM_EPSILON = 1e-06
DECAY = 0.01
RATE = 0.5
BETA = 0.5
LANES = 128
HALF = 64
BIG = 1e30
FEATS = 4
TILE = 256
THIN = 32
CHUNK = 352
DEEP_CHUNK = 528
VMEM = pltpu.MemorySpace.VMEM
AXES = ("dp", "rep")


def params(mebibytes):
    return pltpu.CompilerParams(vmem_limit_bytes=mebibytes * 1024 * 1024)


def dot(a, b, ca, cb):
    return lax.dot_general(a, b, (((ca,), (cb,)), ((), ())), preferred_element_type=jnp.float32)


def normalize(values):
    center = values - jnp.mean(values, axis=-1, keepdims=True)
    scale = lax.rsqrt(jnp.mean(center * center, axis=-1, keepdims=True) + EPSILON)
    return center * scale, scale


class Layout:
    def __init__(self, mesh, mixed):
        self.dp = mesh.shape["dp"]
        self.rep = mesh.shape["rep"]
        self.plane = self.dp // 2
        self.mixed = mixed and self.plane == self.rep

    def pairs(self, move):
        pairs = []
        for p in range(self.plane):
            for c in range(2):
                for z in range(self.rep):
                    q, d, w = move(p, c, z)
                    pairs.append(((p * 2 + c) * self.rep + z, (q * 2 + d) * self.rep + w))
        return pairs

    def over(self, value, i, first):
        def move(p, c, z):
            along_z = (first == (c == 0)) if self.mixed else first
            return (p, c, (z + i) % self.rep) if along_z else (p ^ i, c, z)

        return lax.ppermute(value, AXES, self.pairs(move))

    def to_core(self, value):
        return lax.ppermute(value, AXES, self.pairs(lambda p, c, z: (p, 1 - c, z)))

    def core(self):
        return lax.rem(lax.axis_index("dp"), 2)

    def partner(self, side, i, first, sign):
        along_z = lax.rem(lax.axis_index("rep") + (sign * i) % self.rep, self.rep)
        in_plane = lax.div(lax.axis_index("dp"), 2) ^ i
        if not self.mixed:
            return along_z if first else in_plane
        return jnp.where(side == 0, along_z, in_plane) if first else jnp.where(side == 0, in_plane, along_z)

    def device(self, side, second, first):
        plain = (2 * second + side) * self.rep + first
        return jnp.where(side == 0, plain, (2 * first + side) * self.rep + second) if self.mixed else plain


def row_blocks(lay, side, second, rows):
    firsts = lay.rep
    if lay.mixed:
        return [(j * rows, pl.multiple_of(lay.device(side, second, j) * rows, rows), rows) for j in range(firsts)]
    return [(0, pl.multiple_of(lay.device(side, second, 0) * rows, firsts * rows), firsts * rows)]


def assemble(lay, pieces, full_ref, columns):
    count = len(pieces) // 2
    for i, piece in enumerate(pieces):
        side = lay.core() if i < count else 1 - lay.core()
        second = lay.partner(side, i % count, False, -1)
        for at, to, rows in row_blocks(lay, side, second, piece.shape[0] // lay.rep):
            full_ref[pl.ds(to, rows), :] = piece[at : at + rows, columns]


def assemble_deep(lay, pieces, full_ref, first):
    count = len(pieces) // 2
    width = full_ref.shape[1]
    for i, piece in enumerate(pieces):
        side = lay.core() if i < count else 1 - lay.core()
        second = lay.partner(side, i % count, False, -1)
        rows = piece.shape[0] // lay.rep
        for z in range(lay.rep):
            to = pl.multiple_of(lay.device(side, second, z) * 4 * rows, 4 * rows)
            for j in range(4):
                source = piece[z * rows : (z + 1) * rows, first + j * width : first + (j + 1) * width]
                full_ref[pl.ds(to + j * rows, rows), :] = source


def split_rows(lay, full_ref, keep_ref, send_ref, lanes):
    for target, side in ((keep_ref, lay.core()), (send_ref, 1 - lay.core())):
        for second in range(target.shape[0]):
            for at, source, rows in row_blocks(lay, side, second, target.shape[1] // lay.rep):
                target[second, at : at + rows, lanes] = full_ref[pl.ds(source, rows), :].astype(target.dtype)


def split_deep(lay, full_ref, keep_ref, send_ref, first):
    width = full_ref.shape[1]
    rows = keep_ref.shape[1] // lay.rep
    for target, side in ((keep_ref, lay.core()), (send_ref, 1 - lay.core())):
        for second in range(target.shape[0]):
            for z in range(lay.rep):
                source = pl.multiple_of(lay.device(side, second, z) * 4 * rows, 4 * rows)
                for j in range(4):
                    part = full_ref[pl.ds(source + j * rows, rows), :]
                    columns = slice(first + j * width, first + (j + 1) * width)
                    target[second, z * rows : (z + 1) * rows, columns] = part.astype(target.dtype)


def row_chunks(rows, size):
    return [(at, min(size, rows - at)) for at in range(0, rows, size)]


def windows(rows):
    half = (rows - THIN) // 2
    span = half + THIN
    spans = [(at, TILE, 0, span) for at in range(0, half, TILE)]
    spans.append((half, THIN, 0, rows))
    return spans + [(at, TILE, half, span) for at in range(span, rows, TILE)]


def arrange_kernel(inputs, cotangent, segments, x, dy, labels, begin, room):
    tokens = segments.shape[1]
    half = tokens // 2
    memory = inputs.shape[0] - tokens
    segment = segments[...].astype(jnp.float32)
    ahead = pltpu.roll(jnp.broadcast_to(segment, (8, tokens)), tokens - half + 1, 1)[:1]
    lane = lax.broadcasted_iota(jnp.int32, (1, tokens), 1)
    fits = (segment == ahead) & (lane <= half)
    start = jnp.sum(jnp.where(fits, lane.astype(jnp.float32), 0.0), axis=1, keepdims=True)
    begin[...] = jnp.broadcast_to(start, begin.shape)
    row = lax.broadcasted_iota(jnp.int32, (half, LANES), 0).astype(jnp.float32)
    early = row < start
    thin = lax.broadcasted_iota(jnp.int32, (THIN, LANES), 0) < memory
    for source, target in ((inputs, x), (cotangent, dy)):
        for at in range(0, inputs.shape[1], LANES):
            columns = slice(at, at + LANES)
            room[: inputs.shape[0]] = source[:, columns].astype(jnp.float32)
            left, right = room[memory : memory + half], room[memory + half : memory + tokens]
            target[:half, columns] = jnp.where(early, right, left).astype(target.dtype)
            target[half : half + THIN, columns] = jnp.where(thin, room[:THIN], 0.0).astype(target.dtype)
            target[half + THIN :, columns] = jnp.where(early, left, right).astype(target.dtype)
    left = jnp.transpose(jnp.broadcast_to(segment[:, :half], (LANES, half)))
    right = jnp.transpose(jnp.broadcast_to(segment[:, half:], (LANES, half)))
    labels[:half] = jnp.where(early, right, left).astype(jnp.int32)
    labels[half : half + THIN] = jnp.where(thin, -1, -2)
    labels[half + THIN :] = jnp.where(early, left, right).astype(jnp.int32)


def arrange(inputs, cotangent, segments):
    width = inputs.shape[1]
    rows = segments.shape[1] + THIN
    return pl.pallas_call(
        arrange_kernel,
        out_shape=(
            jax.ShapeDtypeStruct((rows, width), inputs.dtype),
            jax.ShapeDtypeStruct((rows, width), inputs.dtype),
            jax.ShapeDtypeStruct((rows, LANES), jnp.int32),
            jax.ShapeDtypeStruct((8, LANES), jnp.float32),
        ),
        in_specs=[pl.BlockSpec(memory_space=VMEM)] * 3,
        out_specs=[pl.BlockSpec(memory_space=VMEM)] * 4,
        scratch_shapes=[pltpu.VMEM((rows, LANES), jnp.float32)],
        compiler_params=params(8),
        name="arrange",
    )(inputs, cotangent, segments)


def finish_kernel(begin, middle, active, contract, grad_in, outputs, grad_out, room):
    rows = outputs.shape[0]
    half = (middle.shape[0] - THIN) // 2
    memory = rows - 2 * half
    wide = room.shape[1]
    row = lax.broadcasted_iota(jnp.int32, (half, wide), 0).astype(jnp.float32)
    early = row < begin[:1, :1]

    def place(value, target, columns):
        left, right = value[:half], value[half + THIN :]
        room[:THIN] = value[half : half + THIN]
        room[memory : memory + half] = jnp.where(early, right, left)
        room[memory + half : rows] = jnp.where(early, left, right)
        target[:, columns] = room[:rows].astype(target.dtype)

    for at in range(0, middle.shape[1], wide):
        columns = slice(at, at + wide)
        place(middle[:, columns] + dot(active[...], contract[:, columns], 1, 0), outputs, columns)
        place(grad_in[:, columns].astype(jnp.float32), grad_out, columns)


def finish(begin, middle, active, contract, grad_in, rows):
    width = middle.shape[1]
    return pl.pallas_call(
        finish_kernel,
        out_shape=[jax.ShapeDtypeStruct((rows, width), grad_in.dtype)] * 2,
        in_specs=[pl.BlockSpec(memory_space=VMEM)] * 5,
        out_specs=[pl.BlockSpec(memory_space=VMEM)] * 2,
        scratch_shapes=[pltpu.VMEM((middle.shape[0], 256), jnp.float32)],
        compiler_params=params(10),
        name="finish",
    )(begin, middle, active, contract, grad_in)


def attend_kernel(lay, count, x, labels, *refs):
    pieces = refs[:count]
    qx, kx, vx, mixed, gains, weight, qs = refs[count:]
    rows = x.shape[0]
    width = mixed.shape[1]
    assemble(lay, pieces, weight, slice(None))
    gains[...] = jnp.transpose(weight[:, 3 * width :].astype(jnp.float32))[:8]
    gain, bias = gains[0:1], gains[1:2]

    def one_chunk(i, carry):
        span = pl.ds(pl.multiple_of(i * CHUNK, CHUNK), CHUNK)
        normed, _ = normalize(x[span].astype(jnp.float32))
        first = (normed * gain + bias).astype(jnp.bfloat16)
        lane = lax.broadcasted_iota(jnp.int32, (CHUNK, LANES), 1)
        low = lane < HALF
        feature = lane % HALF
        label = labels[span]
        blocked = ((feature < FEATS) & (label >= 0) & (feature != label)) | (feature == FEATS)
        query_side = jnp.where(blocked, -BIG, 0.0)
        marked = ((feature < FEATS) & (feature == label)) | ((feature == FEATS) & (label == -2))
        key_side = jnp.where(marked | (feature > FEATS), 1.0, 0.0)
        sides = (query_side, key_side, jnp.ones_like(key_side))
        for kind, target in enumerate((qs, kx, vx)):
            whole = dot(first, weight[:, kind * width : (kind + 1) * width], 1, 0)
            whole = whole.astype(jnp.bfloat16).astype(jnp.float32)
            for pair in range(width // LANES):
                part = whole[:, pair * LANES : (pair + 1) * LANES]
                if kind == 0:
                    part = part * (1.0 / math.sqrt(HEAD_DIM))
                at = 2 * pair * LANES
                target[span, at : at + LANES] = jnp.where(low, part, sides[kind]).astype(jnp.bfloat16)
                target[span, at + LANES : at + 2 * LANES] = jnp.where(low, sides[kind], part).astype(jnp.bfloat16)
        return carry

    lax.fori_loop(0, rows // CHUNK, one_chunk, 0)

    def one_pair(pair, carry):
        columns = pl.ds(pl.multiple_of(pair * LANES, LANES), LANES)
        for at, size, key_at, key_size in windows(rows):
            span = pl.ds(at, size)
            seen = pl.ds(key_at, key_size)
            lane = lax.broadcasted_iota(jnp.int32, (size, LANES), 1)
            low = lane < HALF
            feature = lane % HALF
            got = []
            for side in range(2):
                head = pl.ds(pl.multiple_of((2 * pair + side) * LANES, LANES), LANES)
                queries = qs[span, head]
                scores = dot(queries, kx[seen, head], 1, 1)
                highest = jnp.max(scores, axis=1, keepdims=True)
                raised = jnp.exp(scores - highest).astype(jnp.bfloat16)
                found = dot(raised, vx[seen, head], 1, 0)
                total = -(highest + jnp.log(found))
                first = total.astype(jnp.bfloat16).astype(jnp.float32)
                second = (total - first).astype(jnp.bfloat16).astype(jnp.float32)
                third = total - first - second
                values = jnp.where(feature == 5, first, jnp.where(feature == 6, second, third))
                place = (feature > FEATS) & (feature < 8) & (low if side else ~low)
                qx[span, head] = jnp.where(place, values, queries.astype(jnp.float32)).astype(jnp.bfloat16)
                got.append(found)
            over = pltpu.roll(jnp.where(low, got[1], got[0]), HALF, 1)
            mixed[span, columns] = (jnp.where(low, got[0], got[1]) / over).astype(jnp.bfloat16)
        return carry

    lax.fori_loop(0, width // LANES, one_pair, 0)


def attend(lay, x, labels, pieces):
    rows, width = x.shape
    wide = jax.ShapeDtypeStruct((rows, 2 * width), jnp.bfloat16)
    depth = len(pieces) * pieces[0].shape[0]
    return pl.pallas_call(
        partial(attend_kernel, lay, len(pieces)),
        out_shape=(
            wide,
            wide,
            wide,
            jax.ShapeDtypeStruct((rows, width), jnp.bfloat16),
            jax.ShapeDtypeStruct((8, width), jnp.float32),
        ),
        in_specs=[pl.BlockSpec(memory_space=VMEM)] * (2 + len(pieces)),
        out_specs=[pl.BlockSpec(memory_space=VMEM)] * 5,
        scratch_shapes=[
            pltpu.VMEM((depth, pieces[0].shape[1]), jnp.bfloat16),
            pltpu.VMEM((rows, 2 * width), jnp.bfloat16),
        ],
        compiler_params=params(16),
        name="attend",
    )(x, labels, *pieces)


def attend_back_kernel(qx, kx, vx, dox, packed, total):
    rows = qx.shape[0]
    width = packed.shape[1] // 3

    def one_pair(pair, carry):
        heads = [pl.ds(pl.multiple_of((2 * pair + side) * LANES, LANES), LANES) for side in range(2)]
        spots = [pl.ds(pl.multiple_of(kind * width + pair * LANES, LANES), LANES) for kind in range(3)]
        total[...] = jnp.zeros_like(total)
        for at, size, query_at, query_size in windows(rows):
            span = pl.ds(at, size)
            seen = pl.ds(query_at, query_size)
            low = lax.broadcasted_iota(jnp.int32, (size, LANES), 1) < HALF
            got = []
            for side in range(2):
                head = heads[side]
                keys = kx[span, head]
                queries = qx[seen, head]
                upstream = dox[seen, head]
                attention = jnp.exp(dot(keys, queries, 1, 1))
                grad = dot(vx[span, head], upstream, 1, 1)
                scores = (attention * grad).astype(jnp.bfloat16)
                got.append((dot(scores, queries, 1, 0), dot(attention.astype(jnp.bfloat16), upstream, 1, 0)))
                total[side, seen] += dot(scores, keys, 0, 0)
            packed[span, spots[1]] = jnp.where(low, got[0][0], got[1][0]).astype(jnp.bfloat16)
            packed[span, spots[2]] = jnp.where(low, got[0][1], got[1][1]).astype(jnp.bfloat16)
        low = lax.broadcasted_iota(jnp.int32, (rows, LANES), 1) < HALF
        packed[:, spots[0]] = (jnp.where(low, total[0], total[1]) * (1.0 / math.sqrt(HEAD_DIM))).astype(jnp.bfloat16)
        return carry

    lax.fori_loop(0, width // LANES, one_pair, 0)


def attend_back(qx, kx, vx, dox):
    rows, wide = qx.shape
    return pl.pallas_call(
        attend_back_kernel,
        out_shape=jax.ShapeDtypeStruct((rows, 3 * wide // 2), jnp.bfloat16),
        in_specs=[pl.BlockSpec(memory_space=VMEM)] * 4,
        out_specs=pl.BlockSpec(memory_space=VMEM),
        scratch_shapes=[pltpu.VMEM((2, rows, LANES), jnp.float32)],
        compiler_params=params(16),
        name="attend_back",
    )(qx, kx, vx, dox)


def norm_back(grad, normed, scale, gain):
    scaled = grad * gain
    return scale * (
        scaled
        - jnp.mean(scaled, axis=-1, keepdims=True)
        - normed * jnp.mean(scaled * normed, axis=-1, keepdims=True)
    )


def feed_kernel(lay, count, deep_count, x, mixed, dy, gains, *refs):
    pieces = refs[:count]
    deep_pieces = refs[count : count + deep_count]
    outs = refs[count + deep_count : -5]
    middle, middle_grad, middle_low, active, contract, out_weight, keep2, send2, norm_grads, *deep_out = outs
    wide, hidden_grad, second, block, deep_block = refs[-5:]
    rows, width = x.shape
    hidden = contract.shape[0]
    assemble(lay, pieces, wide, slice(0, width + hidden))
    if deep_count:
        assemble(lay, deep_pieces, contract, slice(None))
    else:
        assemble_deep(lay, pieces, contract, width + hidden)
    out_weight[...] = wide[:, :width]
    gain, bias = gains[2:3], gains[3:4]
    zero = jnp.zeros((1, width), jnp.float32)

    def one_chunk(i, carry):
        gain_sum, bias_sum = carry
        span = pl.ds(pl.multiple_of(i * DEEP_CHUNK, DEEP_CHUNK), DEEP_CHUNK)
        start = x[span].astype(jnp.float32) + dot(mixed[span], wide[:, :width], 1, 0)
        middle[span] = start
        normed, scale = normalize(start)
        low = (normed * gain + bias).astype(jnp.bfloat16)
        second[span] = low
        for start in range(0, hidden, 512):
            part = slice(start, start + 512)
            up = dot(low, wide[:, width + start : width + start + 512], 1, 0)
            square = up * up
            bend = jnp.tanh(0.7978845608028654 * up * (1.0 + 0.044715 * square))
            half = 0.5 * (1.0 + bend)
            active[span, part] = (up * half).astype(jnp.bfloat16)
            slope = half + 0.5 * up * (1.0 - bend * bend) * (0.7978845608028654 * (1.0 + 3 * 0.044715 * square))
            hidden_grad[span, part] = (dot(dy[span], contract[part], 1, 1) * slope).astype(jnp.bfloat16)
        back = dot(hidden_grad[span], wide[:, width:], 1, 1)
        gain_sum = gain_sum + jnp.sum(back * normed, axis=0, keepdims=True)
        bias_sum = bias_sum + jnp.sum(back, axis=0, keepdims=True)
        grad = dy[span].astype(jnp.float32) + norm_back(back, normed, scale, gain)
        middle_grad[span] = grad
        middle_low[span] = grad.astype(jnp.bfloat16)
        return gain_sum, bias_sum

    gain_sum, bias_sum = lax.fori_loop(0, rows // DEEP_CHUNK, one_chunk, (zero, zero))
    norm_grads[...] = jnp.concatenate([gain_sum, bias_sum, jnp.zeros((6, width), jnp.float32)], axis=0)

    def one_block(i, carry):
        columns = pl.ds(pl.multiple_of(i * 512, 512), 512)
        deep_block[columns] = dot(active[:, columns], dy[...], 0, 0)
        block[...] = dot(second[...], hidden_grad[:, columns], 0, 0)
        split_rows(lay, block, keep2, send2, pl.ds(pl.multiple_of(width + i * 512, 512), 512))
        return carry

    lax.fori_loop(0, hidden // 512, one_block, 0)
    if deep_count:
        split_rows(lay, deep_block, *deep_out, slice(0, width))
    else:
        split_deep(lay, deep_block, keep2, send2, width + hidden)
    block[...] = dot(mixed[...], middle_low[...], 0, 0)
    split_rows(lay, block, keep2, send2, slice(0, width))


def feed(lay, x, mixed, dy, gains, pieces, deep_pieces):
    rows, width = x.shape
    plane = len(pieces) // 2
    deep = pieces[0].shape[0]
    columns = pieces[0].shape[1]
    hidden = 4 * width
    out_shape = [
        jax.ShapeDtypeStruct((rows, width), jnp.float32),
        jax.ShapeDtypeStruct((rows, width), jnp.float32),
        jax.ShapeDtypeStruct((rows, width), jnp.bfloat16),
        jax.ShapeDtypeStruct((rows, hidden), jnp.bfloat16),
        jax.ShapeDtypeStruct((hidden, width), jnp.bfloat16),
        jax.ShapeDtypeStruct((width, width), jnp.bfloat16),
        jax.ShapeDtypeStruct((plane, deep, columns), jnp.bfloat16),
        jax.ShapeDtypeStruct((plane, deep, columns), jnp.bfloat16),
        jax.ShapeDtypeStruct((8, width), jnp.float32),
    ]
    if deep_pieces:
        out_shape.append(jax.ShapeDtypeStruct((plane, 4 * deep, width), jnp.bfloat16))
        out_shape.append(jax.ShapeDtypeStruct((plane, 4 * deep, width), jnp.bfloat16))
    return pl.pallas_call(
        partial(feed_kernel, lay, len(pieces), len(deep_pieces)),
        out_shape=out_shape,
        in_specs=[pl.BlockSpec(memory_space=VMEM)] * (4 + len(pieces) + len(deep_pieces)),
        out_specs=[pl.BlockSpec(memory_space=VMEM)] * len(out_shape),
        scratch_shapes=[
            pltpu.VMEM((width, width + hidden), jnp.bfloat16),
            pltpu.VMEM((rows, hidden), jnp.bfloat16),
            pltpu.VMEM((rows, width), jnp.bfloat16),
            pltpu.VMEM((width, 512), jnp.float32),
            pltpu.VMEM((hidden, width), jnp.float32),
        ],
        compiler_params=params(26),
        name="feed",
    )(x, mixed, dy, gains, *pieces, *deep_pieces)


def mixed_back_kernel(middle_low, mixed, out_weight, dox):
    rows, width = mixed.shape

    def one_chunk(i, carry):
        span = pl.ds(pl.multiple_of(i * DEEP_CHUNK, DEEP_CHUNK), DEEP_CHUNK)
        mixed_grad = dot(middle_low[span], out_weight[...], 1, 1).astype(jnp.bfloat16).astype(jnp.float32)
        lane = lax.broadcasted_iota(jnp.int32, (DEEP_CHUNK, LANES), 1)
        left = lane < HALF
        feature = lane % HALF
        for pair in range(width // LANES):
            columns = slice(pair * LANES, (pair + 1) * LANES)
            piece = mixed_grad[:, columns]
            product = piece * mixed[span, columns].astype(jnp.float32)
            for side in range(2):
                mine = left if side == 0 else ~left
                delta = -jnp.sum(jnp.where(mine, product, 0.0), axis=1, keepdims=True)
                one = delta.astype(jnp.bfloat16).astype(jnp.float32)
                two = (delta - one).astype(jnp.bfloat16).astype(jnp.float32)
                three = delta - one - two
                extra = jnp.where(feature == 0, one, jnp.where(feature == 1, two, jnp.where(feature == 2, three, 0.0)))
                head = (2 * pair + side) * LANES
                dox[span, head : head + LANES] = jnp.where(mine, piece, extra).astype(jnp.bfloat16)
        return carry

    lax.fori_loop(0, rows // DEEP_CHUNK, one_chunk, 0)


def mixed_back(middle_low, mixed, out_weight):
    rows, width = mixed.shape
    return pl.pallas_call(
        mixed_back_kernel,
        out_shape=jax.ShapeDtypeStruct((rows, 2 * width), jnp.bfloat16),
        in_specs=[pl.BlockSpec(memory_space=VMEM)] * 3,
        out_specs=pl.BlockSpec(memory_space=VMEM),
        compiler_params=params(10),
        name="mixed_back",
    )(middle_low, mixed, out_weight)


def project_back_kernel(lay, x, packed, gains, first_norms, second_norms, keep, send, first, block):
    rows, width = x.shape
    gain, bias = gains[0:1], gains[1:2]

    def one_chunk(i, carry):
        span = pl.ds(pl.multiple_of(i * CHUNK, CHUNK), CHUNK)
        normed, _ = normalize(x[span].astype(jnp.float32))
        first[span] = (normed * gain + bias).astype(jnp.bfloat16)
        return carry

    lax.fori_loop(0, rows // CHUNK, one_chunk, 0)

    def one_block(i, carry):
        columns = pl.ds(pl.multiple_of(i * 512, 512), 512)
        block[...] = dot(first[...], packed[:, columns], 0, 0)
        split_rows(lay, block, keep, send, columns)
        return carry

    lax.fori_loop(0, packed.shape[1] // 512, one_block, 0)
    fill = jnp.zeros((LANES - 4, width), jnp.float32)
    norms = jnp.concatenate([first_norms[:2], second_norms[:2], fill], axis=0)
    block[:, :LANES] = jnp.transpose(norms)
    split_rows(lay, block.at[:, :LANES], keep, send, slice(packed.shape[1], packed.shape[1] + LANES))


def project_back(lay, x, packed, gains, first_norms, second_norms, own):
    rows, width = x.shape
    shape = (lay.plane, lay.rep * own, packed.shape[1] + LANES)
    return pl.pallas_call(
        partial(project_back_kernel, lay),
        out_shape=(jax.ShapeDtypeStruct(shape, jnp.bfloat16), jax.ShapeDtypeStruct(shape, jnp.bfloat16)),
        in_specs=[pl.BlockSpec(memory_space=VMEM)] * 5,
        out_specs=[pl.BlockSpec(memory_space=VMEM)] * 2,
        scratch_shapes=[pltpu.VMEM((rows, width), jnp.bfloat16), pltpu.VMEM((width, 512), jnp.float32)],
        compiler_params=params(10),
        name="project_back",
    )(x, packed, gains, first_norms, second_norms)


def input_back_kernel(lay, x, packed, gains, middle_grad, *refs):
    pieces = refs[:-3]
    grad_in, norm_grads, weight = refs[-3:]
    rows, width = x.shape
    assemble(lay, pieces, weight, slice(None))
    gain = gains[0:1]
    zero = jnp.zeros((1, width), jnp.float32)

    def one_chunk(i, carry):
        gain_sum, bias_sum = carry
        span = pl.ds(pl.multiple_of(i * CHUNK, CHUNK), CHUNK)
        normed, scale = normalize(x[span].astype(jnp.float32))
        back = dot(packed[span], weight[:, : 3 * width], 1, 1)
        grad_in[span] = (middle_grad[span] + norm_back(back, normed, scale, gain)).astype(jnp.bfloat16)
        gain_sum = gain_sum + jnp.sum(back * normed, axis=0, keepdims=True)
        return gain_sum, bias_sum + jnp.sum(back, axis=0, keepdims=True)

    gain_sum, bias_sum = lax.fori_loop(0, rows // CHUNK, one_chunk, (zero, zero))
    norm_grads[...] = jnp.concatenate([gain_sum, bias_sum, jnp.zeros((6, width), jnp.float32)], axis=0)


def input_back(lay, x, packed, gains, middle_grad, pieces):
    rows, width = x.shape
    return pl.pallas_call(
        partial(input_back_kernel, lay),
        out_shape=(jax.ShapeDtypeStruct((rows, width), jnp.bfloat16), jax.ShapeDtypeStruct((8, width), jnp.float32)),
        in_specs=[pl.BlockSpec(memory_space=VMEM)] * (4 + len(pieces)),
        out_specs=[pl.BlockSpec(memory_space=VMEM)] * 2,
        scratch_shapes=[pltpu.VMEM((width, pieces[0].shape[1]), jnp.bfloat16)],
        compiler_params=params(10),
        name="input_back",
    )(x, packed, gains, middle_grad, *pieces)


def column_kernel(lay, *refs):
    out = refs[-1]
    got = [ref[...].astype(jnp.float32) for ref in refs[:-1]]
    parts = []
    for j in range(len(got)):
        part = got[0]
        for i in range(1, len(got)):
            part = jnp.where(lay.partner(lay.core(), i, True, -1) == j, got[i], part)
        parts.append(part)
    out[...] = jnp.concatenate(parts, axis=0).astype(out.dtype)


def column_of(lay, shards):
    rows, cols = shards[0].shape
    return pl.pallas_call(
        partial(column_kernel, lay),
        out_shape=jax.ShapeDtypeStruct((len(shards) * rows, cols), shards[0].dtype),
        in_specs=[pl.BlockSpec(memory_space=VMEM)] * len(shards),
        out_specs=pl.BlockSpec(memory_space=VMEM),
        compiler_params=params(4),
        name="column",
    )(*shards)


def chip_sum_kernel(lay, keep, got, *outs):
    for i, ref in enumerate(outs):
        at = lay.partner(lay.core(), i, False, 1)
        ref[...] = (keep[at].astype(jnp.float32) + got[at].astype(jnp.float32)).astype(ref.dtype)


def chip_sum(lay, keep, got):
    plane, rows, cols = keep.shape
    block = cols if cols < 2048 else 1536
    part = pl.BlockSpec((rows, block), lambda i: (0, i))
    whole = pl.BlockSpec((plane, rows, block), lambda i: (0, 0, i))
    return pl.pallas_call(
        partial(chip_sum_kernel, lay),
        grid=(cols // block,),
        out_shape=[jax.ShapeDtypeStruct((rows, cols), jnp.float32)]
        + [jax.ShapeDtypeStruct((rows, cols), jnp.bfloat16)] * (plane - 1),
        in_specs=[whole, whole],
        out_specs=[part] * plane,
        compiler_params=params(12),
        name="chip_sum",
    )(keep, got)


def plane_sum_kernel(lay, own, *refs):
    got, outs = refs[: lay.plane - 1], refs[lay.plane - 1 :]
    rows = outs[0].shape[0]
    total = own[...]
    for ref in got:
        total = total + ref[...].astype(jnp.float32)
    for i, ref in enumerate(outs):
        at = lay.partner(lay.core(), i, True, 1)
        part = total[:rows]
        for j in range(1, lay.rep):
            part = jnp.where(at == j, total[j * rows : (j + 1) * rows], part)
        ref[...] = part.astype(ref.dtype)


def plane_sum(lay, own, got):
    rows, cols = own.shape
    reps = lay.rep
    block = cols if cols < 2048 else 1536
    part = pl.BlockSpec((rows, block), lambda i: (0, i))
    small = pl.BlockSpec((rows // reps, block), lambda i: (0, i))
    return pl.pallas_call(
        partial(plane_sum_kernel, lay),
        grid=(cols // block,),
        out_shape=[jax.ShapeDtypeStruct((rows // reps, cols), jnp.float32)]
        + [jax.ShapeDtypeStruct((rows // reps, cols), jnp.bfloat16)] * (reps - 1),
        in_specs=[part] * (1 + len(got)),
        out_specs=[small] * reps,
        compiler_params=params(10),
        name="plane_sum",
    )(own, *got)


def full_sum(value):
    return jnp.sum(jnp.sum(value, axis=1, keepdims=True), axis=0, keepdims=True)


def turned(columns):
    rows, count = columns.shape
    same = lax.broadcasted_iota(jnp.int32, (rows, rows), 0) == lax.broadcasted_iota(jnp.int32, (rows, rows), 1)
    line = lax.broadcasted_iota(jnp.int32, (count, rows), 0)
    out = jnp.zeros((count, rows), jnp.float32)
    for j in range(count):
        row = jnp.sum(jnp.where(same, columns[:, j : j + 1], 0.0), axis=0, keepdims=True)
        out = jnp.where(line == j, row, out)
    return out


def moments_kernel(pieces_of, first_index, reps, more, *refs):
    n = len(pieces_of)
    grads, others, arrays = refs[:reps], refs[reps : reps + more], refs[reps + more :]
    total = grads[0][...]
    for ref in grads[1:]:
        total = total + ref[...].astype(jnp.float32)
    weights, firsts, seconds = arrays[:n], arrays[n : 2 * n], arrays[2 * n : 3 * n]
    momenta, variances, directions = arrays[3 * n : 4 * n], arrays[4 * n : 5 * n], arrays[5 * n : 6 * n]
    sums = arrays[6 * n]
    lane = lax.broadcasted_iota(jnp.int32, (1, LANES), 1)
    row = others[0][0] if more else jnp.zeros((1, LANES), jnp.float32)
    for i, parts in enumerate(pieces_of):
        weight_sum = jnp.zeros((1, 1), jnp.float32)
        step_sum = jnp.zeros((1, 1), jnp.float32)
        for at, size, columns in parts:
            rows = slice(at, at + size)
            gradient = total[:, columns[0] : columns[1]]
            if len(columns) > 2:
                gradient = turned(gradient)
            weight = weights[i][rows]
            momentum = BETA * firsts[i][rows] + (1.0 - BETA) * gradient
            variance = BETA * seconds[i][rows] + (1.0 - BETA) * gradient * gradient
            direction = momentum / (jnp.sqrt(variance) + ADAM_EPSILON) + DECAY * weight
            momenta[i][rows] = momentum
            variances[i][rows] = variance
            directions[i][rows] = direction
            weight_sum = weight_sum + full_sum(weight * weight)
            step_sum = step_sum + full_sum(direction * direction)
        row = jnp.where(lane == first_index[i], weight_sum, row)
        row = jnp.where(lane == 5 + first_index[i], step_sum, row)
    sums[...] = jnp.broadcast_to(row, sums.shape)


def moments(pieces_of, first_index, grads, others, copies, weights, firsts, seconds):
    arrays = [*grads, *others, *weights, *firsts, *seconds]
    shapes = [jax.ShapeDtypeStruct(weight.shape, jnp.float32) for weight in weights]
    outs = pl.pallas_call(
        partial(moments_kernel, pieces_of, first_index, len(grads), len(others)),
        out_shape=shapes * 3 + [jax.ShapeDtypeStruct((copies, 1, LANES), jnp.float32)],
        in_specs=[pl.BlockSpec(memory_space=VMEM)] * len(arrays),
        out_specs=[pl.BlockSpec(memory_space=VMEM)] * (3 * len(weights) + 1),
        compiler_params=params(8),
        name="moments",
    )(*arrays)
    n = len(weights)
    return outs[:n], outs[n : 2 * n], outs[2 * n : 3 * n], outs[3 * n]


def update_kernel(n, sums, *refs):
    weights, directions, updated, table = refs[:n], refs[n : 2 * n], refs[2 * n : 3 * n], refs[3 * n]
    norms = jnp.sqrt(jnp.sum(sums[...], axis=0))
    row = lax.broadcasted_iota(jnp.int32, table.shape, 0)
    lane = lax.broadcasted_iota(jnp.int32, table.shape, 1)
    out = jnp.zeros(table.shape, jnp.float32)
    for i in range(n):
        weight_norm = norms[:, i : i + 1]
        step_norm = norms[:, 5 + i : 6 + i]
        ratio = weight_norm / step_norm
        updated[i][...] = weights[i][...] - RATE * ratio * directions[i][...]
        column = jnp.where(row == 0, weight_norm, jnp.where(row == 1, step_norm, ratio))
        out = jnp.where(lane == i, column, out)
    table[...] = out


def update(sums, weights, directions):
    n = len(weights)
    outs = pl.pallas_call(
        partial(update_kernel, n),
        out_shape=[jax.ShapeDtypeStruct(weight.shape, jnp.float32) for weight in weights]
        + [jax.ShapeDtypeStruct((3, n), jnp.float32)],
        in_specs=[pl.BlockSpec(memory_space=VMEM)] * (1 + 2 * n),
        out_specs=[pl.BlockSpec(memory_space=VMEM)] * (n + 1),
        compiler_params=params(6),
        name="update",
    )(sums, *weights, *directions)
    return outs[:n], outs[n]


def over(lay, value, first):
    return [value] + [lay.over(value, i, first) for i in range(1, lay.rep if first else lay.plane)]


def send_over(lay, parts, first):
    return [lay.over(part, i, first) for i, part in enumerate(parts, 1)]


def over_core(lay, blocks):
    return blocks + [lay.to_core(block) for block in blocks]


def after(values, others):
    count = len(values)
    return list(lax.optimization_barrier((*values, *others))[:count])


def exchange(lay, value):
    return lax.all_to_all(value, AXES, 0, 0)


def body(
    lay,
    inputs,
    segments,
    cotangent,
    attend_in,
    attend_out,
    expand,
    contract,
    layer_norms,
    moment_in,
    moment_out,
    moment_expand,
    moment_contract,
    moment_norms,
    square_in,
    square_out,
    square_expand,
    square_contract,
    square_norms,
):
    plain, twin = lay
    lay = plain
    masters = (attend_in, attend_out, expand, contract, layer_norms)
    width = attend_in.shape[1]
    depth = attend_out.shape[1]
    hidden = expand.shape[1]
    own = attend_in.shape[0]
    count = lay.dp * lay.rep
    whole_tiles = own % 16 == 0
    norm_rows = jnp.pad(layer_norms.astype(jnp.bfloat16).T, ((0, 0), (0, LANES - 4)))
    shard1 = jnp.concatenate([attend_in.astype(jnp.bfloat16), norm_rows], axis=1)
    column1 = over(plain, shard1, True)
    rows = inputs.shape[1]
    attend_out_, expand_, contract_ = after([attend_out, expand, contract], [shard1])
    deep = [contract_[j * own : (j + 1) * own] for j in range(4)]
    shard2 = jnp.concatenate([part.astype(jnp.bfloat16) for part in (attend_out_, expand_, *deep)], axis=1)
    (shard2,) = after([shard2], column1[1:])
    column2 = over(twin, shard2, True)
    blocks1 = over(plain, column_of(plain, column1), False)
    (segments_,) = after([segments], blocks1[:1])
    x, dy, labels, begin = arrange(inputs[0], cotangent[0], segments_)
    blocks2 = over(twin, column_of(twin, after(column2, [*blocks1, x])), False)
    pieces1 = over_core(lay, blocks1)
    *pieces1, x, labels = after([*pieces1, x, labels], blocks2[:1])
    qx, kx, vx, mixed, gains = attend(plain, x, labels, pieces1)
    near = lay.to_core(blocks2[0])
    blocks2[1:] = after(blocks2[1:], [mixed])
    pieces2 = [*blocks2, near, *[lay.to_core(block) for block in blocks2[1:]]]
    deep_pieces = []
    if not whole_tiles:
        first = depth + hidden
        for piece in pieces2:
            part = piece[:, first:].reshape(lay.rep, own, 4, depth).transpose(0, 2, 1, 3)
            deep_pieces.append(part.reshape(-1, depth))
    middle, middle_grad, middle_low, active, contract_all, out_weight, keep2, send2, second_norms, *deep_out = feed(
        twin, x, mixed, dy, gains, pieces2, deep_pieces
    )
    if not whole_tiles:
        keep2, send2 = [
            jnp.concatenate(
                [
                    wide[:, :, : depth + hidden],
                    part.reshape(lay.plane, lay.rep, 4, own, depth).transpose(0, 1, 3, 2, 4).reshape(lay.plane, -1, 4 * depth),
                ],
                axis=2,
            )
            for wide, part in zip((keep2, send2), deep_out)
        ]
    chip2 = lay.to_core(send2)
    dox = mixed_back(middle_low, mixed, out_weight)
    keep2, chip2 = after([keep2, chip2], [dox])
    own2, *low2 = chip_sum(twin, keep2, chip2)
    got2 = send_over(twin, low2, False)
    (dox,) = after([dox], low2)
    packed = attend_back(qx, kx, vx, dox)
    input_gradient, first_norms = input_back(plain, x, packed, gains, middle_grad, pieces1)
    keep1, send1 = project_back(plain, x, packed, gains, first_norms, second_norms, own)
    own2, *got2 = after([own2, *got2], [send1])
    own2, *low2 = plane_sum(twin, own2, got2)
    got2 = send_over(twin, low2, True)
    (send1,) = after([send1], low2[:1])
    own1, *low1 = chip_sum(plain, keep1, lay.to_core(send1))
    got1 = send_over(plain, low1, False)
    (middle,) = after([middle], low1)
    outputs, input_gradient = finish(begin, middle, active, contract_all, input_gradient, rows)
    own1, *got1 = after([own1, *got1], [outputs])
    spans = [[(0, own, (0, depth))], [(0, own, (depth, depth + hidden))]]
    spans.append([(j * own, own, (depth + hidden + j * depth, depth + hidden + (j + 1) * depth)) for j in range(4)])
    momenta2, variances2, directions2, sums2 = moments(
        spans, (1, 2, 3), [own2, *got2], [], 1, masters[1:4],
        (moment_out, moment_expand, moment_contract), (square_out, square_expand, square_contract),
    )
    own1, *low1 = plane_sum(plain, own1, got1)
    got1 = send_over(plain, low1, True)
    momenta1, variances1, directions1, sums1 = moments(
        [[(0, own, (0, width))], [(0, 4, (width, width + 4, True))]], (0, 4), [own1, *got1], [sums2], count, (attend_in, layer_norms),
        (moment_in, moment_norms), (square_in, square_norms),
    )
    sums = exchange(lay, sums1)
    directions = (directions1[0], *directions2, directions1[1])
    updated, trust_table = update(sums, masters, directions)
    momenta = (momenta1[0], *momenta2, momenta1[1])
    variances = (variances1[0], *variances2, variances1[1])
    return (outputs[None], input_gradient[None], *updated, *momenta, *variances, trust_table)


def solution(mesh):
    placed = (
        P(("dp", "rep"), None, None),
        P(("dp", "rep"), None),
        P(("dp", "rep"), None, None),
        P(("dp", "rep"), None),
        P(("dp", "rep"), None),
        P(("dp", "rep"), None),
        P(("dp", "rep"), None),
        P(None, ("dp", "rep")),
        P(("dp", "rep"), None),
        P(("dp", "rep"), None),
        P(("dp", "rep"), None),
        P(("dp", "rep"), None),
        P(None, ("dp", "rep")),
        P(("dp", "rep"), None),
        P(("dp", "rep"), None),
        P(("dp", "rep"), None),
        P(("dp", "rep"), None),
        P(None, ("dp", "rep")),
    )
    return jax.shard_map(
        partial(body, (Layout(mesh, False), Layout(mesh, True))),
        mesh=mesh,
        in_specs=placed,
        out_specs=(
            P(("dp", "rep"), None, None),
            P(("dp", "rep"), None, None),
            P(("dp", "rep"), None),
            P(("dp", "rep"), None),
            P(("dp", "rep"), None),
            P(("dp", "rep"), None),
            P(None, ("dp", "rep")),
            P(("dp", "rep"), None),
            P(("dp", "rep"), None),
            P(("dp", "rep"), None),
            P(("dp", "rep"), None),
            P(None, ("dp", "rep")),
            P(("dp", "rep"), None),
            P(("dp", "rep"), None),
            P(("dp", "rep"), None),
            P(("dp", "rep"), None),
            P(None, ("dp", "rep")),
            P(),
        ),
        check_vma=False,
    )
```

```python
from functools import partial
import math

import jax
import jax.numpy as jnp
from jax import lax
from jax.experimental import pallas as pl
from jax.experimental.pallas import tpu as pltpu
from jax.sharding import PartitionSpec as P

HEADS = 8
HEAD_DIM = 64


EPSILON = 1e-05
ADAM_EPSILON = 1e-06
DECAY = 0.01
RATE = 0.5
BETA = 0.5
LANES = 128
HALF = 64
BIG = 1e30
FEATS = 4
TILE = 256
THIN = 32
CHUNK = 352
DEEP_CHUNK = 528
GELU_ONE = 0.7978845608028654
GELU_CUBE = 0.044715 * GELU_ONE
VMEM = pltpu.MemorySpace.VMEM
AXES = ("dp", "rep")


def params(mebibytes):
    return pltpu.CompilerParams(vmem_limit_bytes=mebibytes * 1024 * 1024)


def dot(a, b, ca, cb):
    return lax.dot_general(a, b, (((ca,), (cb,)), ((), ())), preferred_element_type=jnp.float32)


def normalize(values):
    center = values - jnp.mean(values, axis=-1, keepdims=True)
    scale = lax.rsqrt(jnp.mean(center * center, axis=-1, keepdims=True) + EPSILON)
    return center * scale, scale


class Layout:
    def __init__(self, mesh, mixed):
        self.dp = mesh.shape["dp"]
        self.rep = mesh.shape["rep"]
        self.plane = self.dp // 2
        self.mixed = mixed and self.plane == self.rep

    def pairs(self, move):
        pairs = []
        for p in range(self.plane):
            for c in range(2):
                for z in range(self.rep):
                    q, d, w = move(p, c, z)
                    pairs.append(((p * 2 + c) * self.rep + z, (q * 2 + d) * self.rep + w))
        return pairs

    def over(self, value, i, first):
        def move(p, c, z):
            along_z = (first == (c == 0)) if self.mixed else first
            return (p, c, (z + i) % self.rep) if along_z else (p ^ i, c, z)

        return lax.ppermute(value, AXES, self.pairs(move))

    def to_core(self, value):
        return lax.ppermute(value, AXES, self.pairs(lambda p, c, z: (p, 1 - c, z)))

    def core(self):
        return lax.rem(lax.axis_index("dp"), 2)

    def partner(self, side, i, first, sign):
        along_z = lax.rem(lax.axis_index("rep") + (sign * i) % self.rep, self.rep)
        in_plane = lax.div(lax.axis_index("dp"), 2) ^ i
        if not self.mixed:
            return along_z if first else in_plane
        return jnp.where(side == 0, along_z, in_plane) if first else jnp.where(side == 0, in_plane, along_z)

    def device(self, side, second, first):
        plain = (2 * second + side) * self.rep + first
        return jnp.where(side == 0, plain, (2 * first + side) * self.rep + second) if self.mixed else plain


def row_blocks(lay, side, second, rows):
    firsts = lay.rep
    if lay.mixed:
        return [(j * rows, pl.multiple_of(lay.device(side, second, j) * rows, rows), rows) for j in range(firsts)]
    return [(0, pl.multiple_of(lay.device(side, second, 0) * rows, firsts * rows), firsts * rows)]


def assemble(lay, pieces, full_ref, columns):
    count = len(pieces) // 2
    for i, piece in enumerate(pieces):
        side = lay.core() if i < count else 1 - lay.core()
        second = lay.partner(side, i % count, False, -1)
        for at, to, rows in row_blocks(lay, side, second, piece.shape[0] // lay.rep):
            full_ref[pl.ds(to, rows), :] = piece[at : at + rows, columns]


def assemble_deep(lay, pieces, full_ref, first):
    count = len(pieces) // 2
    width = full_ref.shape[1]
    for i, piece in enumerate(pieces):
        side = lay.core() if i < count else 1 - lay.core()
        second = lay.partner(side, i % count, False, -1)
        rows = piece.shape[0] // lay.rep
        for z in range(lay.rep):
            to = pl.multiple_of(lay.device(side, second, z) * 4 * rows, 4 * rows)
            for j in range(4):
                source = piece[z * rows : (z + 1) * rows, first + j * width : first + (j + 1) * width]
                full_ref[pl.ds(to + j * rows, rows), :] = source


def split_rows(lay, full_ref, keep_ref, send_ref, lanes):
    for target, side in ((keep_ref, lay.core()), (send_ref, 1 - lay.core())):
        for second in range(target.shape[0]):
            for at, source, rows in row_blocks(lay, side, second, target.shape[1] // lay.rep):
                target[second, at : at + rows, lanes] = full_ref[pl.ds(source, rows), :].astype(target.dtype)


def split_deep(lay, full_ref, keep_ref, send_ref, first):
    width = full_ref.shape[1]
    rows = keep_ref.shape[1] // lay.rep
    for target, side in ((keep_ref, lay.core()), (send_ref, 1 - lay.core())):
        for second in range(target.shape[0]):
            for z in range(lay.rep):
                source = pl.multiple_of(lay.device(side, second, z) * 4 * rows, 4 * rows)
                for j in range(4):
                    part = full_ref[pl.ds(source + j * rows, rows), :]
                    columns = slice(first + j * width, first + (j + 1) * width)
                    target[second, z * rows : (z + 1) * rows, columns] = part.astype(target.dtype)


def row_chunks(rows, size):
    return [(at, min(size, rows - at)) for at in range(0, rows, size)]


def windows(rows):
    half = (rows - THIN) // 2
    span = half + THIN
    spans = [(at, TILE, 0, span) for at in range(0, half, TILE)]
    spans.append((half, THIN, 0, rows))
    return spans + [(at, TILE, half, span) for at in range(span, rows, TILE)]


def arrange_kernel(inputs, cotangent, segments, x, dy, labels, begin, room):
    tokens = segments.shape[1]
    half = tokens // 2
    memory = inputs.shape[0] - tokens
    segment = segments[...].astype(jnp.float32)
    ahead = pltpu.roll(jnp.broadcast_to(segment, (8, tokens)), tokens - half + 1, 1)[:1]
    lane = lax.broadcasted_iota(jnp.int32, (1, tokens), 1)
    fits = (segment == ahead) & (lane <= half)
    start = jnp.sum(jnp.where(fits, lane.astype(jnp.float32), 0.0), axis=1, keepdims=True)
    begin[...] = jnp.broadcast_to(start, begin.shape)
    row = lax.broadcasted_iota(jnp.int32, (half, LANES), 0).astype(jnp.float32)
    early = row < start
    thin = lax.broadcasted_iota(jnp.int32, (THIN, LANES), 0) < memory
    for source, target in ((inputs, x), (cotangent, dy)):
        for at in range(0, inputs.shape[1], LANES):
            columns = slice(at, at + LANES)
            room[: inputs.shape[0]] = source[:, columns].astype(jnp.float32)
            left, right = room[memory : memory + half], room[memory + half : memory + tokens]
            target[:half, columns] = jnp.where(early, right, left).astype(target.dtype)
            target[half : half + THIN, columns] = jnp.where(thin, room[:THIN], 0.0).astype(target.dtype)
            target[half + THIN :, columns] = jnp.where(early, left, right).astype(target.dtype)
    left = jnp.transpose(jnp.broadcast_to(segment[:, :half], (LANES, half)))
    right = jnp.transpose(jnp.broadcast_to(segment[:, half:], (LANES, half)))
    labels[:half] = jnp.where(early, right, left).astype(jnp.int32)
    labels[half : half + THIN] = jnp.where(thin, -1, -2)
    labels[half + THIN :] = jnp.where(early, left, right).astype(jnp.int32)


def arrange(inputs, cotangent, segments):
    width = inputs.shape[1]
    rows = segments.shape[1] + THIN
    return pl.pallas_call(
        arrange_kernel,
        out_shape=(
            jax.ShapeDtypeStruct((rows, width), inputs.dtype),
            jax.ShapeDtypeStruct((rows, width), inputs.dtype),
            jax.ShapeDtypeStruct((rows, LANES), jnp.int32),
            jax.ShapeDtypeStruct((8, LANES), jnp.float32),
        ),
        in_specs=[pl.BlockSpec(memory_space=VMEM)] * 3,
        out_specs=[pl.BlockSpec(memory_space=VMEM)] * 4,
        scratch_shapes=[pltpu.VMEM((rows, LANES), jnp.float32)],
        compiler_params=params(8),
        name="arrange",
    )(inputs, cotangent, segments)


def finish_kernel(begin, middle, active, contract, grad_in, outputs, grad_out, room):
    rows = outputs.shape[0]
    half = (middle.shape[0] - THIN) // 2
    memory = rows - 2 * half
    wide = room.shape[1]
    row = lax.broadcasted_iota(jnp.int32, (half, wide), 0).astype(jnp.float32)
    early = row < begin[:1, :1]

    def place(value, target, columns):
        left, right = value[:half], value[half + THIN :]
        room[:THIN] = value[half : half + THIN]
        room[memory : memory + half] = jnp.where(early, right, left)
        room[memory + half : rows] = jnp.where(early, left, right)
        target[:, columns] = room[:rows].astype(target.dtype)

    for at in range(0, middle.shape[1], wide):
        columns = slice(at, at + wide)
        place(middle[:, columns] + dot(active[...], contract[:, columns], 1, 0), outputs, columns)
        place(grad_in[:, columns].astype(jnp.float32), grad_out, columns)


def finish(begin, middle, active, contract, grad_in, rows):
    width = middle.shape[1]
    return pl.pallas_call(
        finish_kernel,
        out_shape=[jax.ShapeDtypeStruct((rows, width), grad_in.dtype)] * 2,
        in_specs=[pl.BlockSpec(memory_space=VMEM)] * 5,
        out_specs=[pl.BlockSpec(memory_space=VMEM)] * 2,
        scratch_shapes=[pltpu.VMEM((middle.shape[0], 256), jnp.float32)],
        compiler_params=params(10),
        name="finish",
    )(begin, middle, active, contract, grad_in)


def attend_kernel(lay, count, x, labels, *refs):
    pieces = refs[:count]
    qx, kx, vx, mixed, gains, weight, qs = refs[count:]
    rows = x.shape[0]
    width = mixed.shape[1]
    assemble(lay, pieces, weight, slice(None))
    gains[...] = jnp.transpose(weight[:, 3 * width :].astype(jnp.float32))[:8]
    gain, bias = gains[0:1], gains[1:2]

    def one_chunk(i, carry):
        span = pl.ds(pl.multiple_of(i * CHUNK, CHUNK), CHUNK)
        normed, _ = normalize(x[span].astype(jnp.float32))
        first = (normed * gain + bias).astype(jnp.bfloat16)
        lane = lax.broadcasted_iota(jnp.int32, (CHUNK, LANES), 1)
        low = lane < HALF
        feature = lane % HALF
        label = labels[span]
        blocked = ((feature < FEATS) & (label >= 0) & (feature != label)) | (feature == FEATS)
        query_side = jnp.where(blocked, -BIG, 0.0)
        marked = ((feature < FEATS) & (feature == label)) | ((feature == FEATS) & (label == -2))
        key_side = jnp.where(marked | (feature > FEATS), 1.0, 0.0)
        sides = (query_side, key_side, jnp.ones_like(key_side))
        for kind, target in enumerate((qs, kx, vx)):
            whole = dot(first, weight[:, kind * width : (kind + 1) * width], 1, 0)
            whole = whole.astype(jnp.bfloat16).astype(jnp.float32)
            for pair in range(width // LANES):
                part = whole[:, pair * LANES : (pair + 1) * LANES]
                if kind == 0:
                    part = part * (1.0 / math.sqrt(HEAD_DIM))
                at = 2 * pair * LANES
                target[span, at : at + LANES] = jnp.where(low, part, sides[kind]).astype(jnp.bfloat16)
                target[span, at + LANES : at + 2 * LANES] = jnp.where(low, sides[kind], part).astype(jnp.bfloat16)
        return carry

    lax.fori_loop(0, rows // CHUNK, one_chunk, 0)

    def one_pair(pair, carry):
        columns = pl.ds(pl.multiple_of(pair * LANES, LANES), LANES)
        for at, size, key_at, key_size in windows(rows):
            span = pl.ds(at, size)
            seen = pl.ds(key_at, key_size)
            lane = lax.broadcasted_iota(jnp.int32, (size, LANES), 1)
            low = lane < HALF
            feature = lane % HALF
            got = []
            for side in range(2):
                head = pl.ds(pl.multiple_of((2 * pair + side) * LANES, LANES), LANES)
                queries = qs[span, head]
                scores = dot(queries, kx[seen, head], 1, 1)
                highest = jnp.max(scores, axis=1, keepdims=True)
                raised = jnp.exp(scores - highest).astype(jnp.bfloat16)
                found = dot(raised, vx[seen, head], 1, 0)
                total = -(highest + jnp.log(found))
                first = total.astype(jnp.bfloat16).astype(jnp.float32)
                second = (total - first).astype(jnp.bfloat16).astype(jnp.float32)
                third = total - first - second
                values = jnp.where(feature == 5, first, jnp.where(feature == 6, second, third))
                place = (feature > FEATS) & (feature < 8) & (low if side else ~low)
                qx[span, head] = jnp.where(place, values, queries.astype(jnp.float32)).astype(jnp.bfloat16)
                got.append(found)
            over = pltpu.roll(jnp.where(low, got[1], got[0]), HALF, 1)
            mixed[span, columns] = (jnp.where(low, got[0], got[1]) / over).astype(jnp.bfloat16)
        return carry

    lax.fori_loop(0, width // LANES, one_pair, 0)


def attend(lay, x, labels, pieces):
    rows, width = x.shape
    wide = jax.ShapeDtypeStruct((rows, 2 * width), jnp.bfloat16)
    depth = len(pieces) * pieces[0].shape[0]
    return pl.pallas_call(
        partial(attend_kernel, lay, len(pieces)),
        out_shape=(
            wide,
            wide,
            wide,
            jax.ShapeDtypeStruct((rows, width), jnp.bfloat16),
            jax.ShapeDtypeStruct((8, width), jnp.float32),
        ),
        in_specs=[pl.BlockSpec(memory_space=VMEM)] * (2 + len(pieces)),
        out_specs=[pl.BlockSpec(memory_space=VMEM)] * 5,
        scratch_shapes=[
            pltpu.VMEM((depth, pieces[0].shape[1]), jnp.bfloat16),
            pltpu.VMEM((rows, 2 * width), jnp.bfloat16),
        ],
        compiler_params=params(16),
        name="attend",
    )(x, labels, *pieces)


def attend_back_kernel(qx, kx, vx, dox, packed, total):
    rows = qx.shape[0]
    width = packed.shape[1] // 3

    def one_pair(pair, carry):
        heads = [pl.ds(pl.multiple_of((2 * pair + side) * LANES, LANES), LANES) for side in range(2)]
        spots = [pl.ds(pl.multiple_of(kind * width + pair * LANES, LANES), LANES) for kind in range(3)]
        total[...] = jnp.zeros_like(total)
        for at, size, query_at, query_size in windows(rows):
            span = pl.ds(at, size)
            seen = pl.ds(query_at, query_size)
            low = lax.broadcasted_iota(jnp.int32, (size, LANES), 1) < HALF
            got = []
            for side in range(2):
                head = heads[side]
                keys = kx[span, head]
                queries = qx[seen, head]
                upstream = dox[seen, head]
                attention = jnp.exp(dot(keys, queries, 1, 1))
                grad = dot(vx[span, head], upstream, 1, 1)
                scores = (attention * grad).astype(jnp.bfloat16)
                got.append((dot(scores, queries, 1, 0), dot(attention.astype(jnp.bfloat16), upstream, 1, 0)))
                total[side, seen] += dot(scores, keys, 0, 0)
            packed[span, spots[1]] = jnp.where(low, got[0][0], got[1][0]).astype(jnp.bfloat16)
            packed[span, spots[2]] = jnp.where(low, got[0][1], got[1][1]).astype(jnp.bfloat16)
        low = lax.broadcasted_iota(jnp.int32, (rows, LANES), 1) < HALF
        packed[:, spots[0]] = (jnp.where(low, total[0], total[1]) * (1.0 / math.sqrt(HEAD_DIM))).astype(jnp.bfloat16)
        return carry

    lax.fori_loop(0, width // LANES, one_pair, 0)


def attend_back(qx, kx, vx, dox):
    rows, wide = qx.shape
    return pl.pallas_call(
        attend_back_kernel,
        out_shape=jax.ShapeDtypeStruct((rows, 3 * wide // 2), jnp.bfloat16),
        in_specs=[pl.BlockSpec(memory_space=VMEM)] * 4,
        out_specs=pl.BlockSpec(memory_space=VMEM),
        scratch_shapes=[pltpu.VMEM((2, rows, LANES), jnp.float32)],
        compiler_params=params(16),
        name="attend_back",
    )(qx, kx, vx, dox)


def norm_back(grad, normed, scale, gain):
    scaled = grad * gain
    return scale * (
        scaled
        - jnp.mean(scaled, axis=-1, keepdims=True)
        - normed * jnp.mean(scaled * normed, axis=-1, keepdims=True)
    )


def feed_kernel(lay, count, deep_count, x, mixed, dy, gains, *refs):
    pieces = refs[:count]
    deep_pieces = refs[count : count + deep_count]
    outs = refs[count + deep_count : -5]
    middle, middle_grad, middle_low, active, contract, out_weight, keep2, send2, norm_grads, *deep_out = outs
    wide, hidden_grad, second, block, deep_block = refs[-5:]
    rows, width = x.shape
    hidden = contract.shape[0]
    assemble(lay, pieces, wide, slice(0, width + hidden))
    if deep_count:
        assemble(lay, deep_pieces, contract, slice(None))
    else:
        assemble_deep(lay, pieces, contract, width + hidden)
    out_weight[...] = wide[:, :width]
    gain, bias = gains[2:3], gains[3:4]
    zero = jnp.zeros((1, width), jnp.float32)

    def one_chunk(i, carry):
        gain_sum, bias_sum = carry
        span = pl.ds(pl.multiple_of(i * DEEP_CHUNK, DEEP_CHUNK), DEEP_CHUNK)
        start = x[span].astype(jnp.float32) + dot(mixed[span], wide[:, :width], 1, 0)
        middle[span] = start
        normed, scale = normalize(start)
        low = (normed * gain + bias).astype(jnp.bfloat16)
        second[span] = low
        for start in range(0, hidden, 512):
            part = slice(start, start + 512)
            up = dot(low, wide[:, width + start : width + start + 512], 1, 0)
            square = up * up
            half = 0.5 + 0.5 * jnp.tanh(up * (GELU_ONE + GELU_CUBE * square))
            active[span, part] = (up * half).astype(jnp.bfloat16)
            slope = half * (1.0 + (1.0 - half) * (up * (2.0 * GELU_ONE + 6.0 * GELU_CUBE * square)))
            hidden_grad[span, part] = (dot(dy[span], contract[part], 1, 1) * slope).astype(jnp.bfloat16)
        back = dot(hidden_grad[span], wide[:, width:], 1, 1)
        gain_sum = gain_sum + jnp.sum(back * normed, axis=0, keepdims=True)
        bias_sum = bias_sum + jnp.sum(back, axis=0, keepdims=True)
        grad = dy[span].astype(jnp.float32) + norm_back(back, normed, scale, gain)
        middle_grad[span] = grad
        middle_low[span] = grad.astype(jnp.bfloat16)
        return gain_sum, bias_sum

    gain_sum, bias_sum = lax.fori_loop(0, rows // DEEP_CHUNK, one_chunk, (zero, zero))
    norm_grads[...] = jnp.concatenate([gain_sum, bias_sum, jnp.zeros((6, width), jnp.float32)], axis=0)

    def one_block(i, carry):
        columns = pl.ds(pl.multiple_of(i * 512, 512), 512)
        deep_block[columns] = dot(active[:, columns], dy[...], 0, 0)
        block[...] = dot(second[...], hidden_grad[:, columns], 0, 0)
        split_rows(lay, block, keep2, send2, pl.ds(pl.multiple_of(width + i * 512, 512), 512))
        return carry

    lax.fori_loop(0, hidden // 512, one_block, 0)
    if deep_count:
        split_rows(lay, deep_block, *deep_out, slice(0, width))
    else:
        split_deep(lay, deep_block, keep2, send2, width + hidden)
    block[...] = dot(mixed[...], middle_low[...], 0, 0)
    split_rows(lay, block, keep2, send2, slice(0, width))


def feed(lay, x, mixed, dy, gains, pieces, deep_pieces):
    rows, width = x.shape
    plane = len(pieces) // 2
    deep = pieces[0].shape[0]
    columns = pieces[0].shape[1]
    hidden = 4 * width
    out_shape = [
        jax.ShapeDtypeStruct((rows, width), jnp.float32),
        jax.ShapeDtypeStruct((rows, width), jnp.float32),
        jax.ShapeDtypeStruct((rows, width), jnp.bfloat16),
        jax.ShapeDtypeStruct((rows, hidden), jnp.bfloat16),
        jax.ShapeDtypeStruct((hidden, width), jnp.bfloat16),
        jax.ShapeDtypeStruct((width, width), jnp.bfloat16),
        jax.ShapeDtypeStruct((plane, deep, columns), jnp.bfloat16),
        jax.ShapeDtypeStruct((plane, deep, columns), jnp.bfloat16),
        jax.ShapeDtypeStruct((8, width), jnp.float32),
    ]
    if deep_pieces:
        out_shape.append(jax.ShapeDtypeStruct((plane, 4 * deep, width), jnp.bfloat16))
        out_shape.append(jax.ShapeDtypeStruct((plane, 4 * deep, width), jnp.bfloat16))
    return pl.pallas_call(
        partial(feed_kernel, lay, len(pieces), len(deep_pieces)),
        out_shape=out_shape,
        in_specs=[pl.BlockSpec(memory_space=VMEM)] * (4 + len(pieces) + len(deep_pieces)),
        out_specs=[pl.BlockSpec(memory_space=VMEM)] * len(out_shape),
        scratch_shapes=[
            pltpu.VMEM((width, width + hidden), jnp.bfloat16),
            pltpu.VMEM((rows, hidden), jnp.bfloat16),
            pltpu.VMEM((rows, width), jnp.bfloat16),
            pltpu.VMEM((width, 512), jnp.float32),
            pltpu.VMEM((hidden, width), jnp.float32),
        ],
        compiler_params=params(26),
        name="feed",
    )(x, mixed, dy, gains, *pieces, *deep_pieces)


def mixed_back_kernel(middle_low, mixed, out_weight, dox):
    rows, width = mixed.shape

    def one_chunk(i, carry):
        span = pl.ds(pl.multiple_of(i * DEEP_CHUNK, DEEP_CHUNK), DEEP_CHUNK)
        mixed_grad = dot(middle_low[span], out_weight[...], 1, 1).astype(jnp.bfloat16).astype(jnp.float32)
        lane = lax.broadcasted_iota(jnp.int32, (DEEP_CHUNK, LANES), 1)
        left = lane < HALF
        feature = lane % HALF
        for pair in range(width // LANES):
            columns = slice(pair * LANES, (pair + 1) * LANES)
            piece = mixed_grad[:, columns]
            product = piece * mixed[span, columns].astype(jnp.float32)
            for side in range(2):
                mine = left if side == 0 else ~left
                delta = -jnp.sum(jnp.where(mine, product, 0.0), axis=1, keepdims=True)
                one = delta.astype(jnp.bfloat16).astype(jnp.float32)
                two = (delta - one).astype(jnp.bfloat16).astype(jnp.float32)
                three = delta - one - two
                extra = jnp.where(feature == 0, one, jnp.where(feature == 1, two, jnp.where(feature == 2, three, 0.0)))
                head = (2 * pair + side) * LANES
                dox[span, head : head + LANES] = jnp.where(mine, piece, extra).astype(jnp.bfloat16)
        return carry

    lax.fori_loop(0, rows // DEEP_CHUNK, one_chunk, 0)


def mixed_back(middle_low, mixed, out_weight):
    rows, width = mixed.shape
    return pl.pallas_call(
        mixed_back_kernel,
        out_shape=jax.ShapeDtypeStruct((rows, 2 * width), jnp.bfloat16),
        in_specs=[pl.BlockSpec(memory_space=VMEM)] * 3,
        out_specs=pl.BlockSpec(memory_space=VMEM),
        compiler_params=params(10),
        name="mixed_back",
    )(middle_low, mixed, out_weight)


def project_back_kernel(lay, x, packed, gains, first_norms, second_norms, keep, send, first, block):
    rows, width = x.shape
    gain, bias = gains[0:1], gains[1:2]

    def one_chunk(i, carry):
        span = pl.ds(pl.multiple_of(i * CHUNK, CHUNK), CHUNK)
        normed, _ = normalize(x[span].astype(jnp.float32))
        first[span] = (normed * gain + bias).astype(jnp.bfloat16)
        return carry

    lax.fori_loop(0, rows // CHUNK, one_chunk, 0)

    def one_block(i, carry):
        columns = pl.ds(pl.multiple_of(i * 512, 512), 512)
        block[...] = dot(first[...], packed[:, columns], 0, 0)
        split_rows(lay, block, keep, send, columns)
        return carry

    lax.fori_loop(0, packed.shape[1] // 512, one_block, 0)
    fill = jnp.zeros((LANES - 4, width), jnp.float32)
    norms = jnp.concatenate([first_norms[:2], second_norms[:2], fill], axis=0)
    block[:, :LANES] = jnp.transpose(norms)
    split_rows(lay, block.at[:, :LANES], keep, send, slice(packed.shape[1], packed.shape[1] + LANES))


def project_back(lay, x, packed, gains, first_norms, second_norms, own):
    rows, width = x.shape
    shape = (lay.plane, lay.rep * own, packed.shape[1] + LANES)
    return pl.pallas_call(
        partial(project_back_kernel, lay),
        out_shape=(jax.ShapeDtypeStruct(shape, jnp.bfloat16), jax.ShapeDtypeStruct(shape, jnp.bfloat16)),
        in_specs=[pl.BlockSpec(memory_space=VMEM)] * 5,
        out_specs=[pl.BlockSpec(memory_space=VMEM)] * 2,
        scratch_shapes=[pltpu.VMEM((rows, width), jnp.bfloat16), pltpu.VMEM((width, 512), jnp.float32)],
        compiler_params=params(10),
        name="project_back",
    )(x, packed, gains, first_norms, second_norms)


def input_back_kernel(lay, x, packed, gains, middle_grad, *refs):
    pieces = refs[:-3]
    grad_in, norm_grads, weight = refs[-3:]
    rows, width = x.shape
    assemble(lay, pieces, weight, slice(None))
    gain = gains[0:1]
    zero = jnp.zeros((1, width), jnp.float32)

    def one_chunk(i, carry):
        gain_sum, bias_sum = carry
        span = pl.ds(pl.multiple_of(i * CHUNK, CHUNK), CHUNK)
        normed, scale = normalize(x[span].astype(jnp.float32))
        back = dot(packed[span], weight[:, : 3 * width], 1, 1)
        grad_in[span] = (middle_grad[span] + norm_back(back, normed, scale, gain)).astype(jnp.bfloat16)
        gain_sum = gain_sum + jnp.sum(back * normed, axis=0, keepdims=True)
        return gain_sum, bias_sum + jnp.sum(back, axis=0, keepdims=True)

    gain_sum, bias_sum = lax.fori_loop(0, rows // CHUNK, one_chunk, (zero, zero))
    norm_grads[...] = jnp.concatenate([gain_sum, bias_sum, jnp.zeros((6, width), jnp.float32)], axis=0)


def input_back(lay, x, packed, gains, middle_grad, pieces):
    rows, width = x.shape
    return pl.pallas_call(
        partial(input_back_kernel, lay),
        out_shape=(jax.ShapeDtypeStruct((rows, width), jnp.bfloat16), jax.ShapeDtypeStruct((8, width), jnp.float32)),
        in_specs=[pl.BlockSpec(memory_space=VMEM)] * (4 + len(pieces)),
        out_specs=[pl.BlockSpec(memory_space=VMEM)] * 2,
        scratch_shapes=[pltpu.VMEM((width, pieces[0].shape[1]), jnp.bfloat16)],
        compiler_params=params(10),
        name="input_back",
    )(x, packed, gains, middle_grad, *pieces)


def pack_kernel(weight, norms, out):
    rows, width = weight.shape
    out[:, :width] = weight[...].astype(out.dtype)
    same = lax.broadcasted_iota(jnp.int32, (rows, rows), 0) == lax.broadcasted_iota(jnp.int32, (rows, rows), 1)
    lane = lax.broadcasted_iota(jnp.int32, (rows, LANES), 1)
    tile = jnp.zeros((rows, LANES), jnp.float32)
    for j in range(norms.shape[0]):
        column = jnp.sum(jnp.where(same, norms[j : j + 1, :], 0.0), axis=1, keepdims=True)
        tile = jnp.where(lane == j, column, tile)
    out[:, width:] = tile.astype(out.dtype)


def pack(weight, norms):
    rows, width = weight.shape
    return pl.pallas_call(
        pack_kernel,
        out_shape=jax.ShapeDtypeStruct((rows, width + LANES), jnp.bfloat16),
        in_specs=[pl.BlockSpec(memory_space=VMEM)] * 2,
        out_specs=pl.BlockSpec(memory_space=VMEM),
        compiler_params=params(4),
        name="pack",
    )(weight, norms)


def column_kernel(lay, *refs):
    out = refs[-1]
    got = [ref[...].astype(jnp.float32) for ref in refs[:-1]]
    parts = []
    for j in range(len(got)):
        part = got[0]
        for i in range(1, len(got)):
            part = jnp.where(lay.partner(lay.core(), i, True, -1) == j, got[i], part)
        parts.append(part)
    out[...] = jnp.concatenate(parts, axis=0).astype(out.dtype)


def column_of(lay, shards):
    rows, cols = shards[0].shape
    return pl.pallas_call(
        partial(column_kernel, lay),
        out_shape=jax.ShapeDtypeStruct((len(shards) * rows, cols), shards[0].dtype),
        in_specs=[pl.BlockSpec(memory_space=VMEM)] * len(shards),
        out_specs=pl.BlockSpec(memory_space=VMEM),
        compiler_params=params(4),
        name="column",
    )(*shards)


def chip_sum_kernel(lay, keep, got, *outs):
    for i, ref in enumerate(outs):
        at = lay.partner(lay.core(), i, False, 1)
        ref[...] = (keep[at].astype(jnp.float32) + got[at].astype(jnp.float32)).astype(ref.dtype)


def chip_sum(lay, keep, got):
    plane, rows, cols = keep.shape
    block = cols if cols < 2048 else 1536
    part = pl.BlockSpec((rows, block), lambda i: (0, i))
    whole = pl.BlockSpec((plane, rows, block), lambda i: (0, 0, i))
    return pl.pallas_call(
        partial(chip_sum_kernel, lay),
        grid=(cols // block,),
        out_shape=[jax.ShapeDtypeStruct((rows, cols), jnp.float32)]
        + [jax.ShapeDtypeStruct((rows, cols), jnp.bfloat16)] * (plane - 1),
        in_specs=[whole, whole],
        out_specs=[part] * plane,
        compiler_params=params(12),
        name="chip_sum",
    )(keep, got)


def plane_sum_kernel(lay, own, *refs):
    got, outs = refs[: lay.plane - 1], refs[lay.plane - 1 :]
    rows = outs[0].shape[0]
    total = own[...]
    for ref in got:
        total = total + ref[...].astype(jnp.float32)
    for i, ref in enumerate(outs):
        at = lay.partner(lay.core(), i, True, 1)
        part = total[:rows]
        for j in range(1, lay.rep):
            part = jnp.where(at == j, total[j * rows : (j + 1) * rows], part)
        ref[...] = part.astype(ref.dtype)


def plane_sum(lay, own, got):
    rows, cols = own.shape
    reps = lay.rep
    block = cols if cols < 2048 else 1536
    part = pl.BlockSpec((rows, block), lambda i: (0, i))
    small = pl.BlockSpec((rows // reps, block), lambda i: (0, i))
    return pl.pallas_call(
        partial(plane_sum_kernel, lay),
        grid=(cols // block,),
        out_shape=[jax.ShapeDtypeStruct((rows // reps, cols), jnp.float32)]
        + [jax.ShapeDtypeStruct((rows // reps, cols), jnp.bfloat16)] * (reps - 1),
        in_specs=[part] * (1 + len(got)),
        out_specs=[small] * reps,
        compiler_params=params(10),
        name="plane_sum",
    )(own, *got)


def full_sum(value):
    return jnp.sum(jnp.sum(value, axis=1, keepdims=True), axis=0, keepdims=True)


def turned(columns):
    rows, count = columns.shape
    same = lax.broadcasted_iota(jnp.int32, (rows, rows), 0) == lax.broadcasted_iota(jnp.int32, (rows, rows), 1)
    line = lax.broadcasted_iota(jnp.int32, (count, rows), 0)
    out = jnp.zeros((count, rows), jnp.float32)
    for j in range(count):
        row = jnp.sum(jnp.where(same, columns[:, j : j + 1], 0.0), axis=0, keepdims=True)
        out = jnp.where(line == j, row, out)
    return out


def moments_kernel(pieces_of, first_index, reps, more, *refs):
    n = len(pieces_of)
    grads, others, arrays = refs[:reps], refs[reps : reps + more], refs[reps + more :]
    total = grads[0][...]
    for ref in grads[1:]:
        total = total + ref[...].astype(jnp.float32)
    weights, firsts, seconds = arrays[:n], arrays[n : 2 * n], arrays[2 * n : 3 * n]
    momenta, variances, directions = arrays[3 * n : 4 * n], arrays[4 * n : 5 * n], arrays[5 * n : 6 * n]
    sums = arrays[6 * n]
    lane = lax.broadcasted_iota(jnp.int32, (1, LANES), 1)
    row = others[0][0] if more else jnp.zeros((1, LANES), jnp.float32)
    for i, parts in enumerate(pieces_of):
        weight_sum = jnp.zeros((1, 1), jnp.float32)
        step_sum = jnp.zeros((1, 1), jnp.float32)
        for at, size, columns in parts:
            rows = slice(at, at + size)
            gradient = total[:, columns[0] : columns[1]]
            if len(columns) > 2:
                gradient = turned(gradient)
            weight = weights[i][rows]
            momentum = BETA * firsts[i][rows] + (1.0 - BETA) * gradient
            variance = BETA * seconds[i][rows] + (1.0 - BETA) * gradient * gradient
            direction = momentum / (jnp.sqrt(variance) + ADAM_EPSILON) + DECAY * weight
            momenta[i][rows] = momentum
            variances[i][rows] = variance
            directions[i][rows] = direction
            weight_sum = weight_sum + full_sum(weight * weight)
            step_sum = step_sum + full_sum(direction * direction)
        row = jnp.where(lane == first_index[i], weight_sum, row)
        row = jnp.where(lane == 5 + first_index[i], step_sum, row)
    sums[...] = jnp.broadcast_to(row, sums.shape)


def moments(pieces_of, first_index, grads, others, copies, weights, firsts, seconds):
    arrays = [*grads, *others, *weights, *firsts, *seconds]
    shapes = [jax.ShapeDtypeStruct(weight.shape, jnp.float32) for weight in weights]
    outs = pl.pallas_call(
        partial(moments_kernel, pieces_of, first_index, len(grads), len(others)),
        out_shape=shapes * 3 + [jax.ShapeDtypeStruct((copies, 1, LANES), jnp.float32)],
        in_specs=[pl.BlockSpec(memory_space=VMEM)] * len(arrays),
        out_specs=[pl.BlockSpec(memory_space=VMEM)] * (3 * len(weights) + 1),
        compiler_params=params(8),
        name="moments",
    )(*arrays)
    n = len(weights)
    return outs[:n], outs[n : 2 * n], outs[2 * n : 3 * n], outs[3 * n]


def update_kernel(n, sums, *refs):
    weights, directions, updated, table = refs[:n], refs[n : 2 * n], refs[2 * n : 3 * n], refs[3 * n]
    norms = jnp.sqrt(jnp.sum(sums[...], axis=0))
    row = lax.broadcasted_iota(jnp.int32, table.shape, 0)
    lane = lax.broadcasted_iota(jnp.int32, table.shape, 1)
    out = jnp.zeros(table.shape, jnp.float32)
    for i in range(n):
        weight_norm = norms[:, i : i + 1]
        step_norm = norms[:, 5 + i : 6 + i]
        ratio = weight_norm / step_norm
        updated[i][...] = weights[i][...] - RATE * ratio * directions[i][...]
        column = jnp.where(row == 0, weight_norm, jnp.where(row == 1, step_norm, ratio))
        out = jnp.where(lane == i, column, out)
    table[...] = out


def update(sums, weights, directions):
    n = len(weights)
    outs = pl.pallas_call(
        partial(update_kernel, n),
        out_shape=[jax.ShapeDtypeStruct(weight.shape, jnp.float32) for weight in weights]
        + [jax.ShapeDtypeStruct((3, n), jnp.float32)],
        in_specs=[pl.BlockSpec(memory_space=VMEM)] * (1 + 2 * n),
        out_specs=[pl.BlockSpec(memory_space=VMEM)] * (n + 1),
        compiler_params=params(6),
        name="update",
    )(sums, *weights, *directions)
    return outs[:n], outs[n]


def over(lay, value, first):
    return [value] + [lay.over(value, i, first) for i in range(1, lay.rep if first else lay.plane)]


def send_over(lay, parts, first):
    return [lay.over(part, i, first) for i, part in enumerate(parts, 1)]


def over_core(lay, blocks):
    return blocks + [lay.to_core(block) for block in blocks]


def after(values, others):
    count = len(values)
    return list(lax.optimization_barrier((*values, *others))[:count])


def exchange(lay, value):
    return lax.all_to_all(value, AXES, 0, 0)


def body(
    lay,
    inputs,
    segments,
    cotangent,
    attend_in,
    attend_out,
    expand,
    contract,
    layer_norms,
    moment_in,
    moment_out,
    moment_expand,
    moment_contract,
    moment_norms,
    square_in,
    square_out,
    square_expand,
    square_contract,
    square_norms,
):
    plain, twin = lay
    lay = plain
    masters = (attend_in, attend_out, expand, contract, layer_norms)
    width = attend_in.shape[1]
    depth = attend_out.shape[1]
    hidden = expand.shape[1]
    own = attend_in.shape[0]
    count = lay.dp * lay.rep
    whole_tiles = own % 16 == 0
    shard1 = pack(attend_in, layer_norms)
    column1 = over(plain, shard1, True)
    rows = inputs.shape[1]
    attend_out_, expand_, contract_ = after([attend_out, expand, contract], [shard1])
    deep = [contract_[j * own : (j + 1) * own] for j in range(4)]
    shard2 = jnp.concatenate([part.astype(jnp.bfloat16) for part in (attend_out_, expand_, *deep)], axis=1)
    (shard2,) = after([shard2], column1[1:])
    column2 = over(twin, shard2, True)
    blocks1 = over(plain, column_of(plain, column1), False)
    (segments_,) = after([segments], blocks1[:1])
    x, dy, labels, begin = arrange(inputs[0], cotangent[0], segments_)
    blocks2 = over(twin, column_of(twin, after(column2, [*blocks1, x])), False)
    pieces1 = over_core(lay, blocks1)
    *pieces1, x, labels = after([*pieces1, x, labels], blocks2[:1])
    qx, kx, vx, mixed, gains = attend(plain, x, labels, pieces1)
    near = lay.to_core(blocks2[0])
    blocks2[1:] = after(blocks2[1:], [mixed])
    pieces2 = [*blocks2, near, *[lay.to_core(block) for block in blocks2[1:]]]
    deep_pieces = []
    if not whole_tiles:
        first = depth + hidden
        for piece in pieces2:
            part = piece[:, first:].reshape(lay.rep, own, 4, depth).transpose(0, 2, 1, 3)
            deep_pieces.append(part.reshape(-1, depth))
    middle, middle_grad, middle_low, active, contract_all, out_weight, keep2, send2, second_norms, *deep_out = feed(
        twin, x, mixed, dy, gains, pieces2, deep_pieces
    )
    if not whole_tiles:
        keep2, send2 = [
            jnp.concatenate(
                [
                    wide[:, :, : depth + hidden],
                    part.reshape(lay.plane, lay.rep, 4, own, depth).transpose(0, 1, 3, 2, 4).reshape(lay.plane, -1, 4 * depth),
                ],
                axis=2,
            )
            for wide, part in zip((keep2, send2), deep_out)
        ]
    chip2 = lay.to_core(send2)
    dox = mixed_back(middle_low, mixed, out_weight)
    keep2, chip2 = after([keep2, chip2], [dox])
    own2, *low2 = chip_sum(twin, keep2, chip2)
    got2 = send_over(twin, low2, False)
    (dox,) = after([dox], low2)
    packed = attend_back(qx, kx, vx, dox)
    input_gradient, first_norms = input_back(plain, x, packed, gains, middle_grad, pieces1)
    keep1, send1 = project_back(plain, x, packed, gains, first_norms, second_norms, own)
    own2, send1, *got2 = after([own2, send1, *got2], [])
    own2, *low2 = plane_sum(twin, own2, got2)
    got2 = send_over(twin, low2, True)
    own1, *low1 = chip_sum(plain, keep1, lay.to_core(send1))
    got1 = send_over(plain, low1, False)
    (middle,) = after([middle], low1)
    outputs, input_gradient = finish(begin, middle, active, contract_all, input_gradient, rows)
    own1, *got1 = after([own1, *got1], [outputs])
    spans = [[(0, own, (0, depth))], [(0, own, (depth, depth + hidden))]]
    spans.append([(j * own, own, (depth + hidden + j * depth, depth + hidden + (j + 1) * depth)) for j in range(4)])
    momenta2, variances2, directions2, sums2 = moments(
        spans, (1, 2, 3), [own2, *got2], [], 1, masters[1:4],
        (moment_out, moment_expand, moment_contract), (square_out, square_expand, square_contract),
    )
    own1, *low1 = plane_sum(plain, own1, got1)
    got1 = send_over(plain, low1, True)
    momenta1, variances1, directions1, sums1 = moments(
        [[(0, own, (0, width))], [(0, 4, (width, width + 4, True))]], (0, 4), [own1, *got1], [sums2], count, (attend_in, layer_norms),
        (moment_in, moment_norms), (square_in, square_norms),
    )
    sums = exchange(lay, sums1)
    directions = (directions1[0], *directions2, directions1[1])
    updated, trust_table = update(sums, masters, directions)
    momenta = (momenta1[0], *momenta2, momenta1[1])
    variances = (variances1[0], *variances2, variances1[1])
    return (outputs[None], input_gradient[None], *updated, *momenta, *variances, trust_table)


def solution(mesh):
    placed = (
        P(("dp", "rep"), None, None),
        P(("dp", "rep"), None),
        P(("dp", "rep"), None, None),
        P(("dp", "rep"), None),
        P(("dp", "rep"), None),
        P(("dp", "rep"), None),
        P(("dp", "rep"), None),
        P(None, ("dp", "rep")),
        P(("dp", "rep"), None),
        P(("dp", "rep"), None),
        P(("dp", "rep"), None),
        P(("dp", "rep"), None),
        P(None, ("dp", "rep")),
        P(("dp", "rep"), None),
        P(("dp", "rep"), None),
        P(("dp", "rep"), None),
        P(("dp", "rep"), None),
        P(None, ("dp", "rep")),
    )
    return jax.shard_map(
        partial(body, (Layout(mesh, False), Layout(mesh, True))),
        mesh=mesh,
        in_specs=placed,
        out_specs=(
            P(("dp", "rep"), None, None),
            P(("dp", "rep"), None, None),
            P(("dp", "rep"), None),
            P(("dp", "rep"), None),
            P(("dp", "rep"), None),
            P(("dp", "rep"), None),
            P(None, ("dp", "rep")),
            P(("dp", "rep"), None),
            P(("dp", "rep"), None),
            P(("dp", "rep"), None),
            P(("dp", "rep"), None),
            P(None, ("dp", "rep")),
            P(("dp", "rep"), None),
            P(("dp", "rep"), None),
            P(("dp", "rep"), None),
            P(("dp", "rep"), None),
            P(None, ("dp", "rep")),
            P(),
        ),
        check_vma=False,
    )
```

```python
from functools import partial
import math

import jax
import jax.numpy as jnp
from jax import lax
from jax.experimental import pallas as pl
from jax.experimental.pallas import tpu as pltpu
from jax.sharding import PartitionSpec as P

HEADS = 8
HEAD_DIM = 64


EPSILON = 1e-05
ADAM_EPSILON = 1e-06
DECAY = 0.01
RATE = 0.5
BETA = 0.5
LANES = 128
HALF = 64
BIG = 1e30
FEATS = 4
TILE = 256
THIN = 32
CHUNK = 352
DEEP_CHUNK = 528
GELU_ONE = 0.7978845608028654
GELU_CUBE = 0.044715 * GELU_ONE
VMEM = pltpu.MemorySpace.VMEM
AXES = ("dp", "rep")


def params(mebibytes):
    return pltpu.CompilerParams(vmem_limit_bytes=mebibytes * 1024 * 1024)


def dot(a, b, ca, cb):
    return lax.dot_general(a, b, (((ca,), (cb,)), ((), ())), preferred_element_type=jnp.float32)


def normalize(values):
    center = values - jnp.mean(values, axis=-1, keepdims=True)
    scale = lax.rsqrt(jnp.mean(center * center, axis=-1, keepdims=True) + EPSILON)
    return center * scale, scale


class Layout:
    def __init__(self, mesh, mixed):
        self.dp = mesh.shape["dp"]
        self.rep = mesh.shape["rep"]
        self.plane = self.dp // 2
        self.mixed = mixed and self.plane == self.rep

    def pairs(self, move):
        pairs = []
        for p in range(self.plane):
            for c in range(2):
                for z in range(self.rep):
                    q, d, w = move(p, c, z)
                    pairs.append(((p * 2 + c) * self.rep + z, (q * 2 + d) * self.rep + w))
        return pairs

    def over(self, value, i, first):
        def move(p, c, z):
            along_z = (first == (c == 0)) if self.mixed else first
            return (p, c, (z + i) % self.rep) if along_z else (p ^ i, c, z)

        return lax.ppermute(value, AXES, self.pairs(move))

    def to_core(self, value):
        return lax.ppermute(value, AXES, self.pairs(lambda p, c, z: (p, 1 - c, z)))

    def core(self):
        return lax.rem(lax.axis_index("dp"), 2)

    def partner(self, side, i, first, sign):
        along_z = lax.rem(lax.axis_index("rep") + (sign * i) % self.rep, self.rep)
        in_plane = lax.div(lax.axis_index("dp"), 2) ^ i
        if not self.mixed:
            return along_z if first else in_plane
        return jnp.where(side == 0, along_z, in_plane) if first else jnp.where(side == 0, in_plane, along_z)

    def device(self, side, second, first):
        plain = (2 * second + side) * self.rep + first
        return jnp.where(side == 0, plain, (2 * first + side) * self.rep + second) if self.mixed else plain


def row_blocks(lay, side, second, rows):
    firsts = lay.rep
    if lay.mixed:
        return [(j * rows, pl.multiple_of(lay.device(side, second, j) * rows, rows), rows) for j in range(firsts)]
    return [(0, pl.multiple_of(lay.device(side, second, 0) * rows, firsts * rows), firsts * rows)]


def assemble(lay, pieces, full_ref, columns):
    count = len(pieces) // 2
    for i, piece in enumerate(pieces):
        side = lay.core() if i < count else 1 - lay.core()
        second = lay.partner(side, i % count, False, -1)
        for at, to, rows in row_blocks(lay, side, second, piece.shape[0] // lay.rep):
            full_ref[pl.ds(to, rows), :] = piece[at : at + rows, columns]


def assemble_deep(lay, pieces, full_ref, first):
    count = len(pieces) // 2
    width = full_ref.shape[1]
    for i, piece in enumerate(pieces):
        side = lay.core() if i < count else 1 - lay.core()
        second = lay.partner(side, i % count, False, -1)
        rows = piece.shape[0] // lay.rep
        for z in range(lay.rep):
            to = pl.multiple_of(lay.device(side, second, z) * 4 * rows, 4 * rows)
            for j in range(4):
                source = piece[z * rows : (z + 1) * rows, first + j * width : first + (j + 1) * width]
                full_ref[pl.ds(to + j * rows, rows), :] = source


def split_rows(lay, full_ref, keep_ref, send_ref, lanes):
    for target, side in ((keep_ref, lay.core()), (send_ref, 1 - lay.core())):
        for second in range(target.shape[0]):
            for at, source, rows in row_blocks(lay, side, second, target.shape[1] // lay.rep):
                target[second, at : at + rows, lanes] = full_ref[pl.ds(source, rows), :].astype(target.dtype)


def split_deep(lay, full_ref, keep_ref, send_ref, first):
    width = full_ref.shape[1]
    rows = keep_ref.shape[1] // lay.rep
    for target, side in ((keep_ref, lay.core()), (send_ref, 1 - lay.core())):
        for second in range(target.shape[0]):
            for z in range(lay.rep):
                source = pl.multiple_of(lay.device(side, second, z) * 4 * rows, 4 * rows)
                for j in range(4):
                    part = full_ref[pl.ds(source + j * rows, rows), :]
                    columns = slice(first + j * width, first + (j + 1) * width)
                    target[second, z * rows : (z + 1) * rows, columns] = part.astype(target.dtype)


def row_chunks(rows, size):
    return [(at, min(size, rows - at)) for at in range(0, rows, size)]


def windows(rows):
    half = (rows - THIN) // 2
    span = half + THIN
    spans = [(at, TILE, 0, span) for at in range(0, half, TILE)]
    spans.append((half, THIN, 0, rows))
    return spans + [(at, TILE, half, span) for at in range(span, rows, TILE)]


def arrange_kernel(inputs, cotangent, segments, x, dy, labels, begin, room):
    tokens = segments.shape[1]
    half = tokens // 2
    memory = inputs.shape[0] - tokens
    segment = segments[...].astype(jnp.float32)
    ahead = pltpu.roll(jnp.broadcast_to(segment, (8, tokens)), tokens - half + 1, 1)[:1]
    lane = lax.broadcasted_iota(jnp.int32, (1, tokens), 1)
    fits = (segment == ahead) & (lane <= half)
    start = jnp.sum(jnp.where(fits, lane.astype(jnp.float32), 0.0), axis=1, keepdims=True)
    begin[...] = jnp.broadcast_to(start, begin.shape)
    row = lax.broadcasted_iota(jnp.int32, (half, LANES), 0).astype(jnp.float32)
    early = row < start
    thin = lax.broadcasted_iota(jnp.int32, (THIN, LANES), 0) < memory
    for source, target in ((inputs, x), (cotangent, dy)):
        for at in range(0, inputs.shape[1], LANES):
            columns = slice(at, at + LANES)
            room[: inputs.shape[0]] = source[:, columns].astype(jnp.float32)
            left, right = room[memory : memory + half], room[memory + half : memory + tokens]
            target[:half, columns] = jnp.where(early, right, left).astype(target.dtype)
            target[half : half + THIN, columns] = jnp.where(thin, room[:THIN], 0.0).astype(target.dtype)
            target[half + THIN :, columns] = jnp.where(early, left, right).astype(target.dtype)
    left = jnp.transpose(jnp.broadcast_to(segment[:, :half], (LANES, half)))
    right = jnp.transpose(jnp.broadcast_to(segment[:, half:], (LANES, half)))
    labels[:half] = jnp.where(early, right, left).astype(jnp.int32)
    labels[half : half + THIN] = jnp.where(thin, -1, -2)
    labels[half + THIN :] = jnp.where(early, left, right).astype(jnp.int32)


def arrange(inputs, cotangent, segments):
    width = inputs.shape[1]
    rows = segments.shape[1] + THIN
    return pl.pallas_call(
        arrange_kernel,
        out_shape=(
            jax.ShapeDtypeStruct((rows, width), inputs.dtype),
            jax.ShapeDtypeStruct((rows, width), inputs.dtype),
            jax.ShapeDtypeStruct((rows, LANES), jnp.int32),
            jax.ShapeDtypeStruct((8, LANES), jnp.float32),
        ),
        in_specs=[pl.BlockSpec(memory_space=VMEM)] * 3,
        out_specs=[pl.BlockSpec(memory_space=VMEM)] * 4,
        scratch_shapes=[pltpu.VMEM((rows, LANES), jnp.float32)],
        compiler_params=params(8),
        name="arrange",
    )(inputs, cotangent, segments)


def finish_kernel(begin, middle, active, contract, grad_in, outputs, grad_out, room):
    rows = outputs.shape[0]
    half = (middle.shape[0] - THIN) // 2
    memory = rows - 2 * half
    wide = room.shape[1]
    row = lax.broadcasted_iota(jnp.int32, (half, wide), 0).astype(jnp.float32)
    early = row < begin[:1, :1]

    def place(value, target, columns):
        left, right = value[:half], value[half + THIN :]
        room[:THIN] = value[half : half + THIN]
        room[memory : memory + half] = jnp.where(early, right, left)
        room[memory + half : rows] = jnp.where(early, left, right)
        target[:, columns] = room[:rows].astype(target.dtype)

    for at in range(0, middle.shape[1], wide):
        columns = slice(at, at + wide)
        place(middle[:, columns] + dot(active[...], contract[:, columns], 1, 0), outputs, columns)
        place(grad_in[:, columns].astype(jnp.float32), grad_out, columns)


def finish(begin, middle, active, contract, grad_in, rows):
    width = middle.shape[1]
    return pl.pallas_call(
        finish_kernel,
        out_shape=[jax.ShapeDtypeStruct((rows, width), grad_in.dtype)] * 2,
        in_specs=[pl.BlockSpec(memory_space=VMEM)] * 5,
        out_specs=[pl.BlockSpec(memory_space=VMEM)] * 2,
        scratch_shapes=[pltpu.VMEM((middle.shape[0], 256), jnp.float32)],
        compiler_params=params(10),
        name="finish",
    )(begin, middle, active, contract, grad_in)


def attend_kernel(lay, count, x, labels, *refs):
    pieces = refs[:count]
    qx, kx, vx, mixed, gains, weight, qs = refs[count:]
    rows = x.shape[0]
    width = mixed.shape[1]
    assemble(lay, pieces, weight, slice(None))
    gains[...] = jnp.transpose(weight[:, 3 * width :].astype(jnp.float32))[:8]
    gain, bias = gains[0:1], gains[1:2]

    def one_chunk(i, carry):
        span = pl.ds(pl.multiple_of(i * CHUNK, CHUNK), CHUNK)
        normed, _ = normalize(x[span].astype(jnp.float32))
        first = (normed * gain + bias).astype(jnp.bfloat16)
        lane = lax.broadcasted_iota(jnp.int32, (CHUNK, LANES), 1)
        low = lane < HALF
        feature = lane % HALF
        label = labels[span]
        blocked = ((feature < FEATS) & (label >= 0) & (feature != label)) | (feature == FEATS)
        query_side = jnp.where(blocked, -BIG, 0.0)
        marked = ((feature < FEATS) & (feature == label)) | ((feature == FEATS) & (label == -2))
        key_side = jnp.where(marked | (feature > FEATS), 1.0, 0.0)
        sides = (query_side, key_side, jnp.ones_like(key_side))
        for kind, target in enumerate((qs, kx, vx)):
            whole = dot(first, weight[:, kind * width : (kind + 1) * width], 1, 0)
            whole = whole.astype(jnp.bfloat16).astype(jnp.float32)
            for pair in range(width // LANES):
                part = whole[:, pair * LANES : (pair + 1) * LANES]
                if kind == 0:
                    part = part * (1.0 / math.sqrt(HEAD_DIM))
                at = 2 * pair * LANES
                target[span, at : at + LANES] = jnp.where(low, part, sides[kind]).astype(jnp.bfloat16)
                target[span, at + LANES : at + 2 * LANES] = jnp.where(low, sides[kind], part).astype(jnp.bfloat16)
        return carry

    lax.fori_loop(0, rows // CHUNK, one_chunk, 0)

    def one_pair(pair, carry):
        columns = pl.ds(pl.multiple_of(pair * LANES, LANES), LANES)
        for at, size, key_at, key_size in windows(rows):
            span = pl.ds(at, size)
            seen = pl.ds(key_at, key_size)
            lane = lax.broadcasted_iota(jnp.int32, (size, LANES), 1)
            low = lane < HALF
            feature = lane % HALF
            got = []
            for side in range(2):
                head = pl.ds(pl.multiple_of((2 * pair + side) * LANES, LANES), LANES)
                queries = qs[span, head]
                scores = dot(queries, kx[seen, head], 1, 1)
                highest = jnp.max(scores, axis=1, keepdims=True)
                raised = jnp.exp(scores - highest).astype(jnp.bfloat16)
                found = dot(raised, vx[seen, head], 1, 0)
                total = -(highest + jnp.log(found))
                first = total.astype(jnp.bfloat16).astype(jnp.float32)
                second = (total - first).astype(jnp.bfloat16).astype(jnp.float32)
                third = total - first - second
                values = jnp.where(feature == 5, first, jnp.where(feature == 6, second, third))
                place = (feature > FEATS) & (feature < 8) & (low if side else ~low)
                qx[span, head] = jnp.where(place, values, queries.astype(jnp.float32)).astype(jnp.bfloat16)
                got.append(found)
            over = pltpu.roll(jnp.where(low, got[1], got[0]), HALF, 1)
            mixed[span, columns] = (jnp.where(low, got[0], got[1]) / over).astype(jnp.bfloat16)
        return carry

    lax.fori_loop(0, width // LANES, one_pair, 0)


def attend(lay, x, labels, pieces):
    rows, width = x.shape
    wide = jax.ShapeDtypeStruct((rows, 2 * width), jnp.bfloat16)
    depth = len(pieces) * pieces[0].shape[0]
    return pl.pallas_call(
        partial(attend_kernel, lay, len(pieces)),
        out_shape=(
            wide,
            wide,
            wide,
            jax.ShapeDtypeStruct((rows, width), jnp.bfloat16),
            jax.ShapeDtypeStruct((8, width), jnp.float32),
        ),
        in_specs=[pl.BlockSpec(memory_space=VMEM)] * (2 + len(pieces)),
        out_specs=[pl.BlockSpec(memory_space=VMEM)] * 5,
        scratch_shapes=[
            pltpu.VMEM((depth, pieces[0].shape[1]), jnp.bfloat16),
            pltpu.VMEM((rows, 2 * width), jnp.bfloat16),
        ],
        compiler_params=params(16),
        name="attend",
    )(x, labels, *pieces)


def attend_back_kernel(qx, kx, vx, dox, packed, total):
    rows = qx.shape[0]
    width = packed.shape[1] // 3

    def one_pair(pair, carry):
        heads = [pl.ds(pl.multiple_of((2 * pair + side) * LANES, LANES), LANES) for side in range(2)]
        spots = [pl.ds(pl.multiple_of(kind * width + pair * LANES, LANES), LANES) for kind in range(3)]
        total[...] = jnp.zeros_like(total)
        for at, size, query_at, query_size in windows(rows):
            span = pl.ds(at, size)
            seen = pl.ds(query_at, query_size)
            low = lax.broadcasted_iota(jnp.int32, (size, LANES), 1) < HALF
            got = []
            for side in range(2):
                head = heads[side]
                keys = kx[span, head]
                queries = qx[seen, head]
                upstream = dox[seen, head]
                attention = jnp.exp(dot(keys, queries, 1, 1))
                grad = dot(vx[span, head], upstream, 1, 1)
                scores = (attention * grad).astype(jnp.bfloat16)
                got.append((dot(scores, queries, 1, 0), dot(attention.astype(jnp.bfloat16), upstream, 1, 0)))
                total[side, seen] += dot(scores, keys, 0, 0)
            packed[span, spots[1]] = jnp.where(low, got[0][0], got[1][0]).astype(jnp.bfloat16)
            packed[span, spots[2]] = jnp.where(low, got[0][1], got[1][1]).astype(jnp.bfloat16)
        low = lax.broadcasted_iota(jnp.int32, (rows, LANES), 1) < HALF
        packed[:, spots[0]] = (jnp.where(low, total[0], total[1]) * (1.0 / math.sqrt(HEAD_DIM))).astype(jnp.bfloat16)
        return carry

    lax.fori_loop(0, width // LANES, one_pair, 0)


def attend_back(qx, kx, vx, dox):
    rows, wide = qx.shape
    return pl.pallas_call(
        attend_back_kernel,
        out_shape=jax.ShapeDtypeStruct((rows, 3 * wide // 2), jnp.bfloat16),
        in_specs=[pl.BlockSpec(memory_space=VMEM)] * 4,
        out_specs=pl.BlockSpec(memory_space=VMEM),
        scratch_shapes=[pltpu.VMEM((2, rows, LANES), jnp.float32)],
        compiler_params=params(16),
        name="attend_back",
    )(qx, kx, vx, dox)


def norm_back(grad, normed, scale, gain):
    scaled = grad * gain
    return scale * (
        scaled
        - jnp.mean(scaled, axis=-1, keepdims=True)
        - normed * jnp.mean(scaled * normed, axis=-1, keepdims=True)
    )


def feed_kernel(lay, count, deep_count, x, mixed, dy, gains, *refs):
    pieces = refs[:count]
    deep_pieces = refs[count : count + deep_count]
    outs = refs[count + deep_count : -5]
    middle, middle_grad, middle_low, active, contract, out_weight, keep2, send2, norm_grads, *deep_out = outs
    wide, hidden_grad, second, block, deep_block = refs[-5:]
    rows, width = x.shape
    hidden = contract.shape[0]
    assemble(lay, pieces, wide, slice(0, width + hidden))
    if deep_count:
        assemble(lay, deep_pieces, contract, slice(None))
    else:
        assemble_deep(lay, pieces, contract, width + hidden)
    out_weight[...] = wide[:, :width]
    gain, bias = gains[2:3], gains[3:4]
    zero = jnp.zeros((1, width), jnp.float32)

    def one_chunk(i, carry):
        gain_sum, bias_sum = carry
        span = pl.ds(pl.multiple_of(i * DEEP_CHUNK, DEEP_CHUNK), DEEP_CHUNK)
        start = x[span].astype(jnp.float32) + dot(mixed[span], wide[:, :width], 1, 0)
        middle[span] = start
        normed, scale = normalize(start)
        low = (normed * gain + bias).astype(jnp.bfloat16)
        second[span] = low
        for start in range(0, hidden, 512):
            part = slice(start, start + 512)
            up = dot(low, wide[:, width + start : width + start + 512], 1, 0)
            square = up * up
            half = 0.5 + 0.5 * jnp.tanh(up * (GELU_ONE + GELU_CUBE * square))
            active[span, part] = (up * half).astype(jnp.bfloat16)
            slope = half + (half * (1.0 - half) * up) * (2.0 * GELU_ONE + 6.0 * GELU_CUBE * square)
            hidden_grad[span, part] = (dot(dy[span], contract[part], 1, 1) * slope).astype(jnp.bfloat16)
        back = dot(hidden_grad[span], wide[:, width:], 1, 1)
        gain_sum = gain_sum + jnp.sum(back * normed, axis=0, keepdims=True)
        bias_sum = bias_sum + jnp.sum(back, axis=0, keepdims=True)
        grad = dy[span].astype(jnp.float32) + norm_back(back, normed, scale, gain)
        middle_grad[span] = grad
        middle_low[span] = grad.astype(jnp.bfloat16)
        return gain_sum, bias_sum

    gain_sum, bias_sum = lax.fori_loop(0, rows // DEEP_CHUNK, one_chunk, (zero, zero))
    norm_grads[...] = jnp.concatenate([gain_sum, bias_sum, jnp.zeros((6, width), jnp.float32)], axis=0)

    def one_block(i, carry):
        columns = pl.ds(pl.multiple_of(i * 512, 512), 512)
        deep_block[columns] = dot(active[:, columns], dy[...], 0, 0)
        block[...] = dot(second[...], hidden_grad[:, columns], 0, 0)
        split_rows(lay, block, keep2, send2, pl.ds(pl.multiple_of(width + i * 512, 512), 512))
        return carry

    lax.fori_loop(0, hidden // 512, one_block, 0)
    if deep_count:
        split_rows(lay, deep_block, *deep_out, slice(0, width))
    else:
        split_deep(lay, deep_block, keep2, send2, width + hidden)
    block[...] = dot(mixed[...], middle_low[...], 0, 0)
    split_rows(lay, block, keep2, send2, slice(0, width))


def feed(lay, x, mixed, dy, gains, pieces, deep_pieces):
    rows, width = x.shape
    plane = len(pieces) // 2
    deep = pieces[0].shape[0]
    columns = pieces[0].shape[1]
    hidden = 4 * width
    out_shape = [
        jax.ShapeDtypeStruct((rows, width), jnp.float32),
        jax.ShapeDtypeStruct((rows, width), jnp.float32),
        jax.ShapeDtypeStruct((rows, width), jnp.bfloat16),
        jax.ShapeDtypeStruct((rows, hidden), jnp.bfloat16),
        jax.ShapeDtypeStruct((hidden, width), jnp.bfloat16),
        jax.ShapeDtypeStruct((width, width), jnp.bfloat16),
        jax.ShapeDtypeStruct((plane, deep, columns), jnp.bfloat16),
        jax.ShapeDtypeStruct((plane, deep, columns), jnp.bfloat16),
        jax.ShapeDtypeStruct((8, width), jnp.float32),
    ]
    if deep_pieces:
        out_shape.append(jax.ShapeDtypeStruct((plane, 4 * deep, width), jnp.bfloat16))
        out_shape.append(jax.ShapeDtypeStruct((plane, 4 * deep, width), jnp.bfloat16))
    return pl.pallas_call(
        partial(feed_kernel, lay, len(pieces), len(deep_pieces)),
        out_shape=out_shape,
        in_specs=[pl.BlockSpec(memory_space=VMEM)] * (4 + len(pieces) + len(deep_pieces)),
        out_specs=[pl.BlockSpec(memory_space=VMEM)] * len(out_shape),
        scratch_shapes=[
            pltpu.VMEM((width, width + hidden), jnp.bfloat16),
            pltpu.VMEM((rows, hidden), jnp.bfloat16),
            pltpu.VMEM((rows, width), jnp.bfloat16),
            pltpu.VMEM((width, 512), jnp.float32),
            pltpu.VMEM((hidden, width), jnp.float32),
        ],
        compiler_params=params(26),
        name="feed",
    )(x, mixed, dy, gains, *pieces, *deep_pieces)


def mixed_back_kernel(middle_low, mixed, out_weight, dox):
    rows, width = mixed.shape

    def one_chunk(i, carry):
        span = pl.ds(pl.multiple_of(i * DEEP_CHUNK, DEEP_CHUNK), DEEP_CHUNK)
        mixed_grad = dot(middle_low[span], out_weight[...], 1, 1).astype(jnp.bfloat16).astype(jnp.float32)
        lane = lax.broadcasted_iota(jnp.int32, (DEEP_CHUNK, LANES), 1)
        left = lane < HALF
        feature = lane % HALF
        for pair in range(width // LANES):
            columns = slice(pair * LANES, (pair + 1) * LANES)
            piece = mixed_grad[:, columns]
            product = piece * mixed[span, columns].astype(jnp.float32)
            for side in range(2):
                mine = left if side == 0 else ~left
                delta = -jnp.sum(jnp.where(mine, product, 0.0), axis=1, keepdims=True)
                one = delta.astype(jnp.bfloat16).astype(jnp.float32)
                two = (delta - one).astype(jnp.bfloat16).astype(jnp.float32)
                three = delta - one - two
                extra = jnp.where(feature == 0, one, jnp.where(feature == 1, two, jnp.where(feature == 2, three, 0.0)))
                head = (2 * pair + side) * LANES
                dox[span, head : head + LANES] = jnp.where(mine, piece, extra).astype(jnp.bfloat16)
        return carry

    lax.fori_loop(0, rows // DEEP_CHUNK, one_chunk, 0)


def mixed_back(middle_low, mixed, out_weight):
    rows, width = mixed.shape
    return pl.pallas_call(
        mixed_back_kernel,
        out_shape=jax.ShapeDtypeStruct((rows, 2 * width), jnp.bfloat16),
        in_specs=[pl.BlockSpec(memory_space=VMEM)] * 3,
        out_specs=pl.BlockSpec(memory_space=VMEM),
        compiler_params=params(10),
        name="mixed_back",
    )(middle_low, mixed, out_weight)


def project_back_kernel(lay, x, packed, gains, first_norms, second_norms, keep, send, first, block):
    rows, width = x.shape
    gain, bias = gains[0:1], gains[1:2]

    def one_chunk(i, carry):
        span = pl.ds(pl.multiple_of(i * CHUNK, CHUNK), CHUNK)
        normed, _ = normalize(x[span].astype(jnp.float32))
        first[span] = (normed * gain + bias).astype(jnp.bfloat16)
        return carry

    lax.fori_loop(0, rows // CHUNK, one_chunk, 0)

    def one_block(i, carry):
        columns = pl.ds(pl.multiple_of(i * 512, 512), 512)
        block[...] = dot(first[...], packed[:, columns], 0, 0)
        split_rows(lay, block, keep, send, columns)
        return carry

    lax.fori_loop(0, packed.shape[1] // 512, one_block, 0)
    fill = jnp.zeros((LANES - 4, width), jnp.float32)
    norms = jnp.concatenate([first_norms[:2], second_norms[:2], fill], axis=0)
    block[:, :LANES] = jnp.transpose(norms)
    split_rows(lay, block.at[:, :LANES], keep, send, slice(packed.shape[1], packed.shape[1] + LANES))


def project_back(lay, x, packed, gains, first_norms, second_norms, own):
    rows, width = x.shape
    shape = (lay.plane, lay.rep * own, packed.shape[1] + LANES)
    return pl.pallas_call(
        partial(project_back_kernel, lay),
        out_shape=(jax.ShapeDtypeStruct(shape, jnp.bfloat16), jax.ShapeDtypeStruct(shape, jnp.bfloat16)),
        in_specs=[pl.BlockSpec(memory_space=VMEM)] * 5,
        out_specs=[pl.BlockSpec(memory_space=VMEM)] * 2,
        scratch_shapes=[pltpu.VMEM((rows, width), jnp.bfloat16), pltpu.VMEM((width, 512), jnp.float32)],
        compiler_params=params(10),
        name="project_back",
    )(x, packed, gains, first_norms, second_norms)


def input_back_kernel(lay, x, packed, gains, middle_grad, *refs):
    pieces = refs[:-3]
    grad_in, norm_grads, weight = refs[-3:]
    rows, width = x.shape
    assemble(lay, pieces, weight, slice(None))
    gain = gains[0:1]
    zero = jnp.zeros((1, width), jnp.float32)

    def one_chunk(i, carry):
        gain_sum, bias_sum = carry
        span = pl.ds(pl.multiple_of(i * CHUNK, CHUNK), CHUNK)
        normed, scale = normalize(x[span].astype(jnp.float32))
        back = dot(packed[span], weight[:, : 3 * width], 1, 1)
        grad_in[span] = (middle_grad[span] + norm_back(back, normed, scale, gain)).astype(jnp.bfloat16)
        gain_sum = gain_sum + jnp.sum(back * normed, axis=0, keepdims=True)
        return gain_sum, bias_sum + jnp.sum(back, axis=0, keepdims=True)

    gain_sum, bias_sum = lax.fori_loop(0, rows // CHUNK, one_chunk, (zero, zero))
    norm_grads[...] = jnp.concatenate([gain_sum, bias_sum, jnp.zeros((6, width), jnp.float32)], axis=0)


def input_back(lay, x, packed, gains, middle_grad, pieces):
    rows, width = x.shape
    return pl.pallas_call(
        partial(input_back_kernel, lay),
        out_shape=(jax.ShapeDtypeStruct((rows, width), jnp.bfloat16), jax.ShapeDtypeStruct((8, width), jnp.float32)),
        in_specs=[pl.BlockSpec(memory_space=VMEM)] * (4 + len(pieces)),
        out_specs=[pl.BlockSpec(memory_space=VMEM)] * 2,
        scratch_shapes=[pltpu.VMEM((width, pieces[0].shape[1]), jnp.bfloat16)],
        compiler_params=params(10),
        name="input_back",
    )(x, packed, gains, middle_grad, *pieces)


def pack_kernel(weight, norms, out, weight_here, norms_here, done):
    copies = [
        pltpu.make_async_copy(norms, norms_here, done.at[0]),
        pltpu.make_async_copy(weight, weight_here, done.at[1]),
    ]
    for copy in copies:
        copy.start()
    rows, width = weight_here.shape
    same = lax.broadcasted_iota(jnp.int32, (rows, rows), 0) == lax.broadcasted_iota(jnp.int32, (rows, rows), 1)
    lane = lax.broadcasted_iota(jnp.int32, (rows, LANES), 1)
    tile = jnp.zeros((rows, LANES), jnp.float32)
    copies[0].wait()
    for j in range(norms_here.shape[0]):
        column = jnp.sum(jnp.where(same, norms_here[j : j + 1, :], 0.0), axis=1, keepdims=True)
        tile = jnp.where(lane == j, column, tile)
    out[:, width:] = tile.astype(out.dtype)
    copies[1].wait()
    out[:, :width] = weight_here[...].astype(out.dtype)


def pack(weight, norms):
    rows, width = weight.shape
    return pl.pallas_call(
        pack_kernel,
        out_shape=jax.ShapeDtypeStruct((rows, width + LANES), jnp.bfloat16),
        in_specs=[pl.BlockSpec(memory_space=pltpu.MemorySpace.HBM)] * 2,
        out_specs=pl.BlockSpec(memory_space=VMEM),
        scratch_shapes=[
            pltpu.VMEM(weight.shape, weight.dtype),
            pltpu.VMEM(norms.shape, norms.dtype),
            pltpu.SemaphoreType.DMA((2,)),
        ],
        compiler_params=params(4),
        name="pack",
    )(weight, norms)


def column_kernel(lay, *refs):
    out = refs[-1]
    got = [ref[...].astype(jnp.float32) for ref in refs[:-1]]
    parts = []
    for j in range(len(got)):
        part = got[0]
        for i in range(1, len(got)):
            part = jnp.where(lay.partner(lay.core(), i, True, -1) == j, got[i], part)
        parts.append(part)
    out[...] = jnp.concatenate(parts, axis=0).astype(out.dtype)


def column_of(lay, shards):
    rows, cols = shards[0].shape
    return pl.pallas_call(
        partial(column_kernel, lay),
        out_shape=jax.ShapeDtypeStruct((len(shards) * rows, cols), shards[0].dtype),
        in_specs=[pl.BlockSpec(memory_space=VMEM)] * len(shards),
        out_specs=pl.BlockSpec(memory_space=VMEM),
        compiler_params=params(4),
        name="column",
    )(*shards)


def chip_sum_kernel(lay, keep, got, *outs):
    for i, ref in enumerate(outs):
        at = lay.partner(lay.core(), i, False, 1)
        ref[...] = (keep[at].astype(jnp.float32) + got[at].astype(jnp.float32)).astype(ref.dtype)


def chip_sum(lay, keep, got):
    plane, rows, cols = keep.shape
    return pl.pallas_call(
        partial(chip_sum_kernel, lay),
        out_shape=[jax.ShapeDtypeStruct((rows, cols), jnp.float32)]
        + [jax.ShapeDtypeStruct((rows, cols), jnp.bfloat16)] * (plane - 1),
        in_specs=[pl.BlockSpec(memory_space=VMEM)] * 2,
        out_specs=[pl.BlockSpec(memory_space=VMEM)] * plane,
        compiler_params=params(14),
        name="chip_sum",
    )(keep, got)


def plane_sum_kernel(lay, own, *refs):
    got, outs = refs[: lay.plane - 1], refs[lay.plane - 1 :]
    rows = outs[0].shape[0]
    total = own[...]
    for ref in got:
        total = total + ref[...].astype(jnp.float32)
    for i, ref in enumerate(outs):
        at = lay.partner(lay.core(), i, True, 1)
        part = total[:rows]
        for j in range(1, lay.rep):
            part = jnp.where(at == j, total[j * rows : (j + 1) * rows], part)
        ref[...] = part.astype(ref.dtype)


def plane_sum(lay, own, got):
    rows, cols = own.shape
    reps = lay.rep
    return pl.pallas_call(
        partial(plane_sum_kernel, lay),
        out_shape=[jax.ShapeDtypeStruct((rows // reps, cols), jnp.float32)]
        + [jax.ShapeDtypeStruct((rows // reps, cols), jnp.bfloat16)] * (reps - 1),
        in_specs=[pl.BlockSpec(memory_space=VMEM)] * (1 + len(got)),
        out_specs=[pl.BlockSpec(memory_space=VMEM)] * reps,
        compiler_params=params(10),
        name="plane_sum",
    )(own, *got)


def full_sum(value):
    return jnp.sum(jnp.sum(value, axis=1, keepdims=True), axis=0, keepdims=True)


def turned(columns):
    rows, count = columns.shape
    same = lax.broadcasted_iota(jnp.int32, (rows, rows), 0) == lax.broadcasted_iota(jnp.int32, (rows, rows), 1)
    line = lax.broadcasted_iota(jnp.int32, (count, rows), 0)
    out = jnp.zeros((count, rows), jnp.float32)
    for j in range(count):
        row = jnp.sum(jnp.where(same, columns[:, j : j + 1], 0.0), axis=0, keepdims=True)
        out = jnp.where(line == j, row, out)
    return out


def moments_kernel(pieces_of, first_index, reps, more, *refs):
    n = len(pieces_of)
    grads, others, arrays = refs[:reps], refs[reps : reps + more], refs[reps + more :]
    total = grads[0][...]
    for ref in grads[1:]:
        total = total + ref[...].astype(jnp.float32)
    weights, firsts, seconds = arrays[:n], arrays[n : 2 * n], arrays[2 * n : 3 * n]
    momenta, variances, directions = arrays[3 * n : 4 * n], arrays[4 * n : 5 * n], arrays[5 * n : 6 * n]
    sums = arrays[6 * n]
    lane = lax.broadcasted_iota(jnp.int32, (1, LANES), 1)
    row = others[0][0] if more else jnp.zeros((1, LANES), jnp.float32)
    for i, parts in enumerate(pieces_of):
        weight_sum = jnp.zeros((1, 1), jnp.float32)
        step_sum = jnp.zeros((1, 1), jnp.float32)
        for at, size, columns in parts:
            rows = slice(at, at + size)
            gradient = total[:, columns[0] : columns[1]]
            if len(columns) > 2:
                gradient = turned(gradient)
            weight = weights[i][rows]
            momentum = BETA * firsts[i][rows] + (1.0 - BETA) * gradient
            variance = BETA * seconds[i][rows] + (1.0 - BETA) * gradient * gradient
            direction = momentum / (jnp.sqrt(variance) + ADAM_EPSILON) + DECAY * weight
            momenta[i][rows] = momentum
            variances[i][rows] = variance
            directions[i][rows] = direction
            weight_sum = weight_sum + full_sum(weight * weight)
            step_sum = step_sum + full_sum(direction * direction)
        row = jnp.where(lane == first_index[i], weight_sum, row)
        row = jnp.where(lane == 5 + first_index[i], step_sum, row)
    sums[...] = jnp.broadcast_to(row, sums.shape)


def moments(pieces_of, first_index, grads, others, copies, weights, firsts, seconds):
    arrays = [*grads, *others, *weights, *firsts, *seconds]
    shapes = [jax.ShapeDtypeStruct(weight.shape, jnp.float32) for weight in weights]
    outs = pl.pallas_call(
        partial(moments_kernel, pieces_of, first_index, len(grads), len(others)),
        out_shape=shapes * 3 + [jax.ShapeDtypeStruct((copies, 1, LANES), jnp.float32)],
        in_specs=[pl.BlockSpec(memory_space=VMEM)] * len(arrays),
        out_specs=[pl.BlockSpec(memory_space=VMEM)] * (3 * len(weights) + 1),
        compiler_params=params(8),
        name="moments",
    )(*arrays)
    n = len(weights)
    return outs[:n], outs[n : 2 * n], outs[2 * n : 3 * n], outs[3 * n]


def update_kernel(n, sums, *refs):
    weights, directions, updated, table = refs[:n], refs[n : 2 * n], refs[2 * n : 3 * n], refs[3 * n]
    norms = jnp.sqrt(jnp.sum(sums[...], axis=0))
    row = lax.broadcasted_iota(jnp.int32, table.shape, 0)
    lane = lax.broadcasted_iota(jnp.int32, table.shape, 1)
    out = jnp.zeros(table.shape, jnp.float32)
    for i in range(n):
        weight_norm = norms[:, i : i + 1]
        step_norm = norms[:, 5 + i : 6 + i]
        ratio = weight_norm / step_norm
        updated[i][...] = weights[i][...] - RATE * ratio * directions[i][...]
        column = jnp.where(row == 0, weight_norm, jnp.where(row == 1, step_norm, ratio))
        out = jnp.where(lane == i, column, out)
    table[...] = out


def update(sums, weights, directions):
    n = len(weights)
    outs = pl.pallas_call(
        partial(update_kernel, n),
        out_shape=[jax.ShapeDtypeStruct(weight.shape, jnp.float32) for weight in weights]
        + [jax.ShapeDtypeStruct((3, n), jnp.float32)],
        in_specs=[pl.BlockSpec(memory_space=VMEM)] * (1 + 2 * n),
        out_specs=[pl.BlockSpec(memory_space=VMEM)] * (n + 1),
        compiler_params=params(6),
        name="update",
    )(sums, *weights, *directions)
    return outs[:n], outs[n]


def over(lay, value, first):
    return [value] + [lay.over(value, i, first) for i in range(1, lay.rep if first else lay.plane)]


def send_over(lay, parts, first):
    return [lay.over(part, i, first) for i, part in enumerate(parts, 1)]


def over_core(lay, blocks):
    return blocks + [lay.to_core(block) for block in blocks]


def after(values, others):
    count = len(values)
    return list(lax.optimization_barrier((*values, *others))[:count])


def exchange(lay, value):
    return lax.all_to_all(value, AXES, 0, 0)


def body(
    lay,
    inputs,
    segments,
    cotangent,
    attend_in,
    attend_out,
    expand,
    contract,
    layer_norms,
    moment_in,
    moment_out,
    moment_expand,
    moment_contract,
    moment_norms,
    square_in,
    square_out,
    square_expand,
    square_contract,
    square_norms,
):
    plain, twin = lay
    lay = plain
    masters = (attend_in, attend_out, expand, contract, layer_norms)
    width = attend_in.shape[1]
    depth = attend_out.shape[1]
    hidden = expand.shape[1]
    own = attend_in.shape[0]
    count = lay.dp * lay.rep
    whole_tiles = own % 16 == 0
    shard1 = pack(attend_in, layer_norms)
    column1 = over(plain, shard1, True)
    rows = inputs.shape[1]
    attend_out_, expand_, contract_ = after([attend_out, expand, contract], [shard1])
    deep = [contract_[j * own : (j + 1) * own] for j in range(4)]
    shard2 = jnp.concatenate([part.astype(jnp.bfloat16) for part in (attend_out_, expand_, *deep)], axis=1)
    (shard2,) = after([shard2], column1[1:])
    column2 = over(twin, shard2, True)
    blocks1 = over(plain, column_of(plain, column1), False)
    (segments_,) = after([segments], blocks1[:1])
    x, dy, labels, begin = arrange(inputs[0], cotangent[0], segments_)
    blocks2 = over(twin, column_of(twin, after(column2, [*blocks1, x])), False)
    pieces1 = over_core(lay, blocks1)
    *pieces1, x, labels = after([*pieces1, x, labels], blocks2[:1])
    qx, kx, vx, mixed, gains = attend(plain, x, labels, pieces1)
    near = lay.to_core(blocks2[0])
    blocks2[1:] = after(blocks2[1:], [mixed])
    pieces2 = [*blocks2, near, *[lay.to_core(block) for block in blocks2[1:]]]
    deep_pieces = []
    if not whole_tiles:
        first = depth + hidden
        for piece in pieces2:
            part = piece[:, first:].reshape(lay.rep, own, 4, depth).transpose(0, 2, 1, 3)
            deep_pieces.append(part.reshape(-1, depth))
    middle, middle_grad, middle_low, active, contract_all, out_weight, keep2, send2, second_norms, *deep_out = feed(
        twin, x, mixed, dy, gains, pieces2, deep_pieces
    )
    if not whole_tiles:
        keep2, send2 = [
            jnp.concatenate(
                [
                    wide[:, :, : depth + hidden],
                    part.reshape(lay.plane, lay.rep, 4, own, depth).transpose(0, 1, 3, 2, 4).reshape(lay.plane, -1, 4 * depth),
                ],
                axis=2,
            )
            for wide, part in zip((keep2, send2), deep_out)
        ]
    chip2 = lay.to_core(send2)
    dox = mixed_back(middle_low, mixed, out_weight)
    keep2, chip2 = after([keep2, chip2], [dox])
    own2, *low2 = chip_sum(twin, keep2, chip2)
    got2 = send_over(twin, low2, False)
    (dox,) = after([dox], low2)
    packed = attend_back(qx, kx, vx, dox)
    input_gradient, first_norms = input_back(plain, x, packed, gains, middle_grad, pieces1)
    keep1, send1 = project_back(plain, x, packed, gains, first_norms, second_norms, own)
    own2, send1, *got2 = after([own2, send1, *got2], [])
    own2, *low2 = plane_sum(twin, own2, got2)
    got2 = send_over(twin, low2, True)
    own1, *low1 = chip_sum(plain, keep1, lay.to_core(send1))
    got1 = send_over(plain, low1, False)
    (middle,) = after([middle], low1)
    outputs, input_gradient = finish(begin, middle, active, contract_all, input_gradient, rows)
    own1, *got1 = after([own1, *got1], [outputs])
    spans = [[(0, own, (0, depth))], [(0, own, (depth, depth + hidden))]]
    spans.append([(j * own, own, (depth + hidden + j * depth, depth + hidden + (j + 1) * depth)) for j in range(4)])
    momenta2, variances2, directions2, sums2 = moments(
        spans, (1, 2, 3), [own2, *got2], [], 1, masters[1:4],
        (moment_out, moment_expand, moment_contract), (square_out, square_expand, square_contract),
    )
    own1, *low1 = plane_sum(plain, own1, got1)
    got1 = send_over(plain, low1, True)
    momenta1, variances1, directions1, sums1 = moments(
        [[(0, own, (0, width))], [(0, 4, (width, width + 4, True))]], (0, 4), [own1, *got1], [sums2], count, (attend_in, layer_norms),
        (moment_in, moment_norms), (square_in, square_norms),
    )
    sums = exchange(lay, sums1)
    directions = (directions1[0], *directions2, directions1[1])
    updated, trust_table = update(sums, masters, directions)
    momenta = (momenta1[0], *momenta2, momenta1[1])
    variances = (variances1[0], *variances2, variances1[1])
    return (outputs[None], input_gradient[None], *updated, *momenta, *variances, trust_table)


def solution(mesh):
    placed = (
        P(("dp", "rep"), None, None),
        P(("dp", "rep"), None),
        P(("dp", "rep"), None, None),
        P(("dp", "rep"), None),
        P(("dp", "rep"), None),
        P(("dp", "rep"), None),
        P(("dp", "rep"), None),
        P(None, ("dp", "rep")),
        P(("dp", "rep"), None),
        P(("dp", "rep"), None),
        P(("dp", "rep"), None),
        P(("dp", "rep"), None),
        P(None, ("dp", "rep")),
        P(("dp", "rep"), None),
        P(("dp", "rep"), None),
        P(("dp", "rep"), None),
        P(("dp", "rep"), None),
        P(None, ("dp", "rep")),
    )
    return jax.shard_map(
        partial(body, (Layout(mesh, False), Layout(mesh, True))),
        mesh=mesh,
        in_specs=placed,
        out_specs=(
            P(("dp", "rep"), None, None),
            P(("dp", "rep"), None, None),
            P(("dp", "rep"), None),
            P(("dp", "rep"), None),
            P(("dp", "rep"), None),
            P(("dp", "rep"), None),
            P(None, ("dp", "rep")),
            P(("dp", "rep"), None),
            P(("dp", "rep"), None),
            P(("dp", "rep"), None),
            P(("dp", "rep"), None),
            P(None, ("dp", "rep")),
            P(("dp", "rep"), None),
            P(("dp", "rep"), None),
            P(("dp", "rep"), None),
            P(("dp", "rep"), None),
            P(None, ("dp", "rep")),
            P(),
        ),
        check_vma=False,
    )
```

```python
from functools import partial
import math

import jax
import jax.numpy as jnp
from jax import lax
from jax.experimental import pallas as pl
from jax.experimental.pallas import tpu as pltpu
from jax.sharding import PartitionSpec as P

HEADS = 8
HEAD_DIM = 64


EPSILON = 1e-05
ADAM_EPSILON = 1e-06
DECAY = 0.01
RATE = 0.5
BETA = 0.5
LANES = 128
HALF = 64
BIG = 1e30
FEATS = 4
TILE = 256
THIN = 32
CHUNK = 352
DEEP_CHUNK = 528
GELU_ONE = 0.7978845608028654
GELU_CUBE = 0.044715 * GELU_ONE
VMEM = pltpu.MemorySpace.VMEM
AXES = ("dp", "rep")


def params(mebibytes):
    return pltpu.CompilerParams(vmem_limit_bytes=mebibytes * 1024 * 1024)


def dot(a, b, ca, cb):
    return lax.dot_general(a, b, (((ca,), (cb,)), ((), ())), preferred_element_type=jnp.float32)


def normalize(values):
    center = values - jnp.mean(values, axis=-1, keepdims=True)
    scale = lax.rsqrt(jnp.mean(center * center, axis=-1, keepdims=True) + EPSILON)
    return center * scale, scale


class Layout:
    def __init__(self, mesh, mixed):
        self.dp = mesh.shape["dp"]
        self.rep = mesh.shape["rep"]
        self.plane = self.dp // 2
        self.mixed = mixed and self.plane == self.rep

    def pairs(self, move):
        pairs = []
        for p in range(self.plane):
            for c in range(2):
                for z in range(self.rep):
                    q, d, w = move(p, c, z)
                    pairs.append(((p * 2 + c) * self.rep + z, (q * 2 + d) * self.rep + w))
        return pairs

    def over(self, value, i, first):
        def move(p, c, z):
            along_z = (first == (c == 0)) if self.mixed else first
            return (p, c, (z + i) % self.rep) if along_z else (p ^ i, c, z)

        return lax.ppermute(value, AXES, self.pairs(move))

    def to_core(self, value):
        return lax.ppermute(value, AXES, self.pairs(lambda p, c, z: (p, 1 - c, z)))

    def core(self):
        return lax.rem(lax.axis_index("dp"), 2)

    def partner(self, side, i, first, sign):
        along_z = lax.rem(lax.axis_index("rep") + (sign * i) % self.rep, self.rep)
        in_plane = lax.div(lax.axis_index("dp"), 2) ^ i
        if not self.mixed:
            return along_z if first else in_plane
        return jnp.where(side == 0, along_z, in_plane) if first else jnp.where(side == 0, in_plane, along_z)

    def device(self, side, second, first):
        plain = (2 * second + side) * self.rep + first
        return jnp.where(side == 0, plain, (2 * first + side) * self.rep + second) if self.mixed else plain


def row_blocks(lay, side, second, rows):
    firsts = lay.rep
    if lay.mixed:
        return [(j * rows, pl.multiple_of(lay.device(side, second, j) * rows, rows), rows) for j in range(firsts)]
    return [(0, pl.multiple_of(lay.device(side, second, 0) * rows, firsts * rows), firsts * rows)]


def assemble(lay, pieces, full_ref, columns):
    count = len(pieces) // 2
    for i, piece in enumerate(pieces):
        side = lay.core() if i < count else 1 - lay.core()
        second = lay.partner(side, i % count, False, -1)
        for at, to, rows in row_blocks(lay, side, second, piece.shape[0] // lay.rep):
            full_ref[pl.ds(to, rows), :] = piece[at : at + rows, columns]


def assemble_deep(lay, pieces, full_ref, first):
    count = len(pieces) // 2
    width = full_ref.shape[1]
    for i, piece in enumerate(pieces):
        side = lay.core() if i < count else 1 - lay.core()
        second = lay.partner(side, i % count, False, -1)
        rows = piece.shape[0] // lay.rep
        for z in range(lay.rep):
            to = pl.multiple_of(lay.device(side, second, z) * 4 * rows, 4 * rows)
            for j in range(4):
                source = piece[z * rows : (z + 1) * rows, first + j * width : first + (j + 1) * width]
                full_ref[pl.ds(to + j * rows, rows), :] = source


def split_rows(lay, full_ref, keep_ref, send_ref, lanes):
    for target, side in ((keep_ref, lay.core()), (send_ref, 1 - lay.core())):
        for second in range(target.shape[0]):
            for at, source, rows in row_blocks(lay, side, second, target.shape[1] // lay.rep):
                target[second, at : at + rows, lanes] = full_ref[pl.ds(source, rows), :].astype(target.dtype)


def split_deep(lay, full_ref, keep_ref, send_ref, first):
    width = full_ref.shape[1]
    rows = keep_ref.shape[1] // lay.rep
    for target, side in ((keep_ref, lay.core()), (send_ref, 1 - lay.core())):
        for second in range(target.shape[0]):
            for z in range(lay.rep):
                source = pl.multiple_of(lay.device(side, second, z) * 4 * rows, 4 * rows)
                for j in range(4):
                    part = full_ref[pl.ds(source + j * rows, rows), :]
                    columns = slice(first + j * width, first + (j + 1) * width)
                    target[second, z * rows : (z + 1) * rows, columns] = part.astype(target.dtype)


def row_chunks(rows, size):
    return [(at, min(size, rows - at)) for at in range(0, rows, size)]


def windows(rows):
    half = (rows - THIN) // 2
    span = half + THIN
    spans = [(at, TILE, 0, span) for at in range(0, half, TILE)]
    spans.append((half, THIN, 0, rows))
    return spans + [(at, TILE, half, span) for at in range(span, rows, TILE)]


def arrange_kernel(inputs, cotangent, segments, x, dy, labels, begin, room):
    tokens = segments.shape[1]
    half = tokens // 2
    memory = inputs.shape[0] - tokens
    segment = segments[...].astype(jnp.float32)
    ahead = pltpu.roll(jnp.broadcast_to(segment, (8, tokens)), tokens - half + 1, 1)[:1]
    lane = lax.broadcasted_iota(jnp.int32, (1, tokens), 1)
    fits = (segment == ahead) & (lane <= half)
    start = jnp.sum(jnp.where(fits, lane.astype(jnp.float32), 0.0), axis=1, keepdims=True)
    begin[...] = jnp.broadcast_to(start, begin.shape)
    row = lax.broadcasted_iota(jnp.int32, (half, LANES), 0).astype(jnp.float32)
    early = row < start
    thin = lax.broadcasted_iota(jnp.int32, (THIN, LANES), 0) < memory
    for source, target in ((inputs, x), (cotangent, dy)):
        for at in range(0, inputs.shape[1], LANES):
            columns = slice(at, at + LANES)
            room[: inputs.shape[0]] = source[:, columns].astype(jnp.float32)
            left, right = room[memory : memory + half], room[memory + half : memory + tokens]
            target[:half, columns] = jnp.where(early, right, left).astype(target.dtype)
            target[half : half + THIN, columns] = jnp.where(thin, room[:THIN], 0.0).astype(target.dtype)
            target[half + THIN :, columns] = jnp.where(early, left, right).astype(target.dtype)
    left = jnp.transpose(jnp.broadcast_to(segment[:, :half], (LANES, half)))
    right = jnp.transpose(jnp.broadcast_to(segment[:, half:], (LANES, half)))
    labels[:half] = jnp.where(early, right, left).astype(jnp.int32)
    labels[half : half + THIN] = jnp.where(thin, -1, -2)
    labels[half + THIN :] = jnp.where(early, left, right).astype(jnp.int32)


def arrange(inputs, cotangent, segments):
    width = inputs.shape[1]
    rows = segments.shape[1] + THIN
    return pl.pallas_call(
        arrange_kernel,
        out_shape=(
            jax.ShapeDtypeStruct((rows, width), inputs.dtype),
            jax.ShapeDtypeStruct((rows, width), inputs.dtype),
            jax.ShapeDtypeStruct((rows, LANES), jnp.int32),
            jax.ShapeDtypeStruct((8, LANES), jnp.float32),
        ),
        in_specs=[pl.BlockSpec(memory_space=VMEM)] * 3,
        out_specs=[pl.BlockSpec(memory_space=VMEM)] * 4,
        scratch_shapes=[pltpu.VMEM((rows, LANES), jnp.float32)],
        compiler_params=params(8),
        name="arrange",
    )(inputs, cotangent, segments)


def finish_kernel(begin, middle, active, contract, grad_in, outputs, grad_out, room):
    rows = outputs.shape[0]
    half = (middle.shape[0] - THIN) // 2
    memory = rows - 2 * half
    wide = room.shape[1]
    row = lax.broadcasted_iota(jnp.int32, (half, wide), 0).astype(jnp.float32)
    early = row < begin[:1, :1]

    def place(value, target, columns):
        left, right = value[:half], value[half + THIN :]
        room[:THIN] = value[half : half + THIN]
        room[memory : memory + half] = jnp.where(early, right, left)
        room[memory + half : rows] = jnp.where(early, left, right)
        target[:, columns] = room[:rows].astype(target.dtype)

    for at in range(0, middle.shape[1], wide):
        columns = slice(at, at + wide)
        place(middle[:, columns] + dot(active[...], contract[:, columns], 1, 0), outputs, columns)
        place(grad_in[:, columns].astype(jnp.float32), grad_out, columns)


def finish(begin, middle, active, contract, grad_in, rows):
    width = middle.shape[1]
    return pl.pallas_call(
        finish_kernel,
        out_shape=[jax.ShapeDtypeStruct((rows, width), grad_in.dtype)] * 2,
        in_specs=[pl.BlockSpec(memory_space=VMEM)] * 5,
        out_specs=[pl.BlockSpec(memory_space=VMEM)] * 2,
        scratch_shapes=[pltpu.VMEM((middle.shape[0], 256), jnp.float32)],
        compiler_params=params(10),
        name="finish",
    )(begin, middle, active, contract, grad_in)


def attend_kernel(lay, count, x, labels, *refs):
    pieces = refs[:count]
    qx, kx, vx, mixed, gains, weight, qs = refs[count:]
    rows = x.shape[0]
    width = mixed.shape[1]
    assemble(lay, pieces, weight, slice(None))
    gains[...] = jnp.transpose(weight[:, 3 * width :].astype(jnp.float32))[:8]
    gain, bias = gains[0:1], gains[1:2]

    def one_chunk(i, carry):
        span = pl.ds(pl.multiple_of(i * CHUNK, CHUNK), CHUNK)
        normed, _ = normalize(x[span].astype(jnp.float32))
        first = (normed * gain + bias).astype(jnp.bfloat16)
        lane = lax.broadcasted_iota(jnp.int32, (CHUNK, LANES), 1)
        low = lane < HALF
        feature = lane % HALF
        label = labels[span]
        blocked = ((feature < FEATS) & (label >= 0) & (feature != label)) | (feature == FEATS)
        query_side = jnp.where(blocked, -BIG, 0.0)
        marked = ((feature < FEATS) & (feature == label)) | ((feature == FEATS) & (label == -2))
        key_side = jnp.where(marked | (feature > FEATS), 1.0, 0.0)
        sides = (query_side, key_side, jnp.ones_like(key_side))
        for kind, target in enumerate((qs, kx, vx)):
            whole = dot(first, weight[:, kind * width : (kind + 1) * width], 1, 0)
            whole = whole.astype(jnp.bfloat16).astype(jnp.float32)
            for pair in range(width // LANES):
                part = whole[:, pair * LANES : (pair + 1) * LANES]
                if kind == 0:
                    part = part * (1.0 / math.sqrt(HEAD_DIM))
                at = 2 * pair * LANES
                target[span, at : at + LANES] = jnp.where(low, part, sides[kind]).astype(jnp.bfloat16)
                target[span, at + LANES : at + 2 * LANES] = jnp.where(low, sides[kind], part).astype(jnp.bfloat16)
        return carry

    lax.fori_loop(0, rows // CHUNK, one_chunk, 0)

    def one_pair(pair, carry):
        columns = pl.ds(pl.multiple_of(pair * LANES, LANES), LANES)
        for at, size, key_at, key_size in windows(rows):
            span = pl.ds(at, size)
            seen = pl.ds(key_at, key_size)
            lane = lax.broadcasted_iota(jnp.int32, (size, LANES), 1)
            low = lane < HALF
            feature = lane % HALF
            got = []
            for side in range(2):
                head = pl.ds(pl.multiple_of((2 * pair + side) * LANES, LANES), LANES)
                queries = qs[span, head]
                scores = dot(queries, kx[seen, head], 1, 1)
                highest = jnp.max(scores, axis=1, keepdims=True)
                raised = jnp.exp(scores - highest).astype(jnp.bfloat16)
                found = dot(raised, vx[seen, head], 1, 0)
                total = -(highest + jnp.log(found))
                first = total.astype(jnp.bfloat16).astype(jnp.float32)
                second = (total - first).astype(jnp.bfloat16).astype(jnp.float32)
                third = total - first - second
                values = jnp.where(feature == 5, first, jnp.where(feature == 6, second, third))
                place = (feature > FEATS) & (feature < 8) & (low if side else ~low)
                qx[span, head] = jnp.where(place, values, queries.astype(jnp.float32)).astype(jnp.bfloat16)
                got.append(found)
            over = pltpu.roll(jnp.where(low, got[1], got[0]), HALF, 1)
            mixed[span, columns] = (jnp.where(low, got[0], got[1]) / over).astype(jnp.bfloat16)
        return carry

    lax.fori_loop(0, width // LANES, one_pair, 0)


def attend(lay, x, labels, pieces):
    rows, width = x.shape
    wide = jax.ShapeDtypeStruct((rows, 2 * width), jnp.bfloat16)
    depth = len(pieces) * pieces[0].shape[0]
    return pl.pallas_call(
        partial(attend_kernel, lay, len(pieces)),
        out_shape=(
            wide,
            wide,
            wide,
            jax.ShapeDtypeStruct((rows, width), jnp.bfloat16),
            jax.ShapeDtypeStruct((8, width), jnp.float32),
        ),
        in_specs=[pl.BlockSpec(memory_space=VMEM)] * (2 + len(pieces)),
        out_specs=[pl.BlockSpec(memory_space=VMEM)] * 5,
        scratch_shapes=[
            pltpu.VMEM((depth, pieces[0].shape[1]), jnp.bfloat16),
            pltpu.VMEM((rows, 2 * width), jnp.bfloat16),
        ],
        compiler_params=params(16),
        name="attend",
    )(x, labels, *pieces)


def attend_back_kernel(qx, kx, vx, dox, packed, total):
    rows = qx.shape[0]
    width = packed.shape[1] // 3

    def one_pair(pair, carry):
        heads = [pl.ds(pl.multiple_of((2 * pair + side) * LANES, LANES), LANES) for side in range(2)]
        spots = [pl.ds(pl.multiple_of(kind * width + pair * LANES, LANES), LANES) for kind in range(3)]
        total[...] = jnp.zeros_like(total)
        for at, size, query_at, query_size in windows(rows):
            span = pl.ds(at, size)
            seen = pl.ds(query_at, query_size)
            low = lax.broadcasted_iota(jnp.int32, (size, LANES), 1) < HALF
            got = []
            for side in range(2):
                head = heads[side]
                keys = kx[span, head]
                queries = qx[seen, head]
                upstream = dox[seen, head]
                attention = jnp.exp(dot(keys, queries, 1, 1))
                grad = dot(vx[span, head], upstream, 1, 1)
                scores = (attention * grad).astype(jnp.bfloat16)
                got.append((dot(scores, queries, 1, 0), dot(attention.astype(jnp.bfloat16), upstream, 1, 0)))
                total[side, seen] += dot(scores, keys, 0, 0)
            packed[span, spots[1]] = jnp.where(low, got[0][0], got[1][0]).astype(jnp.bfloat16)
            packed[span, spots[2]] = jnp.where(low, got[0][1], got[1][1]).astype(jnp.bfloat16)
        low = lax.broadcasted_iota(jnp.int32, (rows, LANES), 1) < HALF
        packed[:, spots[0]] = (jnp.where(low, total[0], total[1]) * (1.0 / math.sqrt(HEAD_DIM))).astype(jnp.bfloat16)
        return carry

    lax.fori_loop(0, width // LANES, one_pair, 0)


def attend_back(qx, kx, vx, dox):
    rows, wide = qx.shape
    return pl.pallas_call(
        attend_back_kernel,
        out_shape=jax.ShapeDtypeStruct((rows, 3 * wide // 2), jnp.bfloat16),
        in_specs=[pl.BlockSpec(memory_space=VMEM)] * 4,
        out_specs=pl.BlockSpec(memory_space=VMEM),
        scratch_shapes=[pltpu.VMEM((2, rows, LANES), jnp.float32)],
        compiler_params=params(16),
        name="attend_back",
    )(qx, kx, vx, dox)


def norm_back(grad, normed, scale, gain):
    scaled = grad * gain
    return scale * (
        scaled
        - jnp.mean(scaled, axis=-1, keepdims=True)
        - normed * jnp.mean(scaled * normed, axis=-1, keepdims=True)
    )


def feed_kernel(lay, count, deep_count, x, mixed, dy, gains, *refs):
    pieces = refs[:count]
    deep_pieces = refs[count : count + deep_count]
    outs = refs[count + deep_count : -5]
    middle, middle_grad, middle_low, active, contract, out_weight, keep2, send2, norm_grads, *deep_out = outs
    wide, hidden_grad, second, block, deep_block = refs[-5:]
    rows, width = x.shape
    hidden = contract.shape[0]
    assemble(lay, pieces, wide, slice(0, width + hidden))
    if deep_count:
        assemble(lay, deep_pieces, contract, slice(None))
    else:
        assemble_deep(lay, pieces, contract, width + hidden)
    out_weight[...] = wide[:, :width]
    gain, bias = gains[2:3], gains[3:4]
    zero = jnp.zeros((1, width), jnp.float32)

    def one_chunk(i, carry):
        gain_sum, bias_sum = carry
        span = pl.ds(pl.multiple_of(i * DEEP_CHUNK, DEEP_CHUNK), DEEP_CHUNK)
        start = x[span].astype(jnp.float32) + dot(mixed[span], wide[:, :width], 1, 0)
        middle[span] = start
        normed, scale = normalize(start)
        low = (normed * gain + bias).astype(jnp.bfloat16)
        second[span] = low
        for start in range(0, hidden, 512):
            part = slice(start, start + 512)
            up = dot(low, wide[:, width + start : width + start + 512], 1, 0)
            square = up * up
            half = 0.5 + 0.5 * jnp.tanh(up * (GELU_ONE + GELU_CUBE * square))
            act = up * half
            active[span, part] = act.astype(jnp.bfloat16)
            slope = half + act * ((1.0 - half) * (2.0 * GELU_ONE + 6.0 * GELU_CUBE * square))
            hidden_grad[span, part] = (dot(dy[span], contract[part], 1, 1) * slope).astype(jnp.bfloat16)
        back = dot(hidden_grad[span], wide[:, width:], 1, 1)
        gain_sum = gain_sum + jnp.sum(back * normed, axis=0, keepdims=True)
        bias_sum = bias_sum + jnp.sum(back, axis=0, keepdims=True)
        grad = dy[span].astype(jnp.float32) + norm_back(back, normed, scale, gain)
        middle_grad[span] = grad
        middle_low[span] = grad.astype(jnp.bfloat16)
        return gain_sum, bias_sum

    gain_sum, bias_sum = lax.fori_loop(0, rows // DEEP_CHUNK, one_chunk, (zero, zero))
    norm_grads[...] = jnp.concatenate([gain_sum, bias_sum, jnp.zeros((6, width), jnp.float32)], axis=0)

    def one_block(i, carry):
        columns = pl.ds(pl.multiple_of(i * 512, 512), 512)
        deep_block[columns] = dot(active[:, columns], dy[...], 0, 0)
        block[...] = dot(second[...], hidden_grad[:, columns], 0, 0)
        split_rows(lay, block, keep2, send2, pl.ds(pl.multiple_of(width + i * 512, 512), 512))
        return carry

    lax.fori_loop(0, hidden // 512, one_block, 0)
    if deep_count:
        split_rows(lay, deep_block, *deep_out, slice(0, width))
    else:
        split_deep(lay, deep_block, keep2, send2, width + hidden)
    block[...] = dot(mixed[...], middle_low[...], 0, 0)
    split_rows(lay, block, keep2, send2, slice(0, width))


def feed(lay, x, mixed, dy, gains, pieces, deep_pieces):
    rows, width = x.shape
    plane = len(pieces) // 2
    deep = pieces[0].shape[0]
    columns = pieces[0].shape[1]
    hidden = 4 * width
    out_shape = [
        jax.ShapeDtypeStruct((rows, width), jnp.float32),
        jax.ShapeDtypeStruct((rows, width), jnp.float32),
        jax.ShapeDtypeStruct((rows, width), jnp.bfloat16),
        jax.ShapeDtypeStruct((rows, hidden), jnp.bfloat16),
        jax.ShapeDtypeStruct((hidden, width), jnp.bfloat16),
        jax.ShapeDtypeStruct((width, width), jnp.bfloat16),
        jax.ShapeDtypeStruct((plane, deep, columns), jnp.bfloat16),
        jax.ShapeDtypeStruct((plane, deep, columns), jnp.bfloat16),
        jax.ShapeDtypeStruct((8, width), jnp.float32),
    ]
    if deep_pieces:
        out_shape.append(jax.ShapeDtypeStruct((plane, 4 * deep, width), jnp.bfloat16))
        out_shape.append(jax.ShapeDtypeStruct((plane, 4 * deep, width), jnp.bfloat16))
    return pl.pallas_call(
        partial(feed_kernel, lay, len(pieces), len(deep_pieces)),
        out_shape=out_shape,
        in_specs=[pl.BlockSpec(memory_space=VMEM)] * (4 + len(pieces) + len(deep_pieces)),
        out_specs=[pl.BlockSpec(memory_space=VMEM)] * len(out_shape),
        scratch_shapes=[
            pltpu.VMEM((width, width + hidden), jnp.bfloat16),
            pltpu.VMEM((rows, hidden), jnp.bfloat16),
            pltpu.VMEM((rows, width), jnp.bfloat16),
            pltpu.VMEM((width, 512), jnp.float32),
            pltpu.VMEM((hidden, width), jnp.float32),
        ],
        compiler_params=params(26),
        name="feed",
    )(x, mixed, dy, gains, *pieces, *deep_pieces)


def mixed_back_kernel(middle_low, mixed, out_weight, dox):
    rows, width = mixed.shape

    def one_chunk(i, carry):
        span = pl.ds(pl.multiple_of(i * DEEP_CHUNK, DEEP_CHUNK), DEEP_CHUNK)
        mixed_grad = dot(middle_low[span], out_weight[...], 1, 1).astype(jnp.bfloat16).astype(jnp.float32)
        lane = lax.broadcasted_iota(jnp.int32, (DEEP_CHUNK, LANES), 1)
        left = lane < HALF
        feature = lane % HALF
        for pair in range(width // LANES):
            columns = slice(pair * LANES, (pair + 1) * LANES)
            piece = mixed_grad[:, columns]
            product = piece * mixed[span, columns].astype(jnp.float32)
            for side in range(2):
                mine = left if side == 0 else ~left
                delta = -jnp.sum(jnp.where(mine, product, 0.0), axis=1, keepdims=True)
                one = delta.astype(jnp.bfloat16).astype(jnp.float32)
                two = (delta - one).astype(jnp.bfloat16).astype(jnp.float32)
                three = delta - one - two
                extra = jnp.where(feature == 0, one, jnp.where(feature == 1, two, jnp.where(feature == 2, three, 0.0)))
                head = (2 * pair + side) * LANES
                dox[span, head : head + LANES] = jnp.where(mine, piece, extra).astype(jnp.bfloat16)
        return carry

    lax.fori_loop(0, rows // DEEP_CHUNK, one_chunk, 0)


def mixed_back(middle_low, mixed, out_weight):
    rows, width = mixed.shape
    return pl.pallas_call(
        mixed_back_kernel,
        out_shape=jax.ShapeDtypeStruct((rows, 2 * width), jnp.bfloat16),
        in_specs=[pl.BlockSpec(memory_space=VMEM)] * 3,
        out_specs=pl.BlockSpec(memory_space=VMEM),
        compiler_params=params(10),
        name="mixed_back",
    )(middle_low, mixed, out_weight)


def project_back_kernel(lay, x, packed, gains, first_norms, second_norms, keep, send, first, block):
    rows, width = x.shape
    gain, bias = gains[0:1], gains[1:2]

    def one_chunk(i, carry):
        span = pl.ds(pl.multiple_of(i * CHUNK, CHUNK), CHUNK)
        normed, _ = normalize(x[span].astype(jnp.float32))
        first[span] = (normed * gain + bias).astype(jnp.bfloat16)
        return carry

    lax.fori_loop(0, rows // CHUNK, one_chunk, 0)

    def one_block(i, carry):
        columns = pl.ds(pl.multiple_of(i * 512, 512), 512)
        block[...] = dot(first[...], packed[:, columns], 0, 0)
        split_rows(lay, block, keep, send, columns)
        return carry

    lax.fori_loop(0, packed.shape[1] // 512, one_block, 0)
    fill = jnp.zeros((LANES - 4, width), jnp.float32)
    norms = jnp.concatenate([first_norms[:2], second_norms[:2], fill], axis=0)
    block[:, :LANES] = jnp.transpose(norms)
    split_rows(lay, block.at[:, :LANES], keep, send, slice(packed.shape[1], packed.shape[1] + LANES))


def project_back(lay, x, packed, gains, first_norms, second_norms, own):
    rows, width = x.shape
    shape = (lay.plane, lay.rep * own, packed.shape[1] + LANES)
    return pl.pallas_call(
        partial(project_back_kernel, lay),
        out_shape=(jax.ShapeDtypeStruct(shape, jnp.bfloat16), jax.ShapeDtypeStruct(shape, jnp.bfloat16)),
        in_specs=[pl.BlockSpec(memory_space=VMEM)] * 5,
        out_specs=[pl.BlockSpec(memory_space=VMEM)] * 2,
        scratch_shapes=[pltpu.VMEM((rows, width), jnp.bfloat16), pltpu.VMEM((width, 512), jnp.float32)],
        compiler_params=params(10),
        name="project_back",
    )(x, packed, gains, first_norms, second_norms)


def input_back_kernel(lay, x, packed, gains, middle_grad, *refs):
    pieces = refs[:-3]
    grad_in, norm_grads, weight = refs[-3:]
    rows, width = x.shape
    assemble(lay, pieces, weight, slice(None))
    gain = gains[0:1]
    zero = jnp.zeros((1, width), jnp.float32)

    def one_chunk(i, carry):
        gain_sum, bias_sum = carry
        span = pl.ds(pl.multiple_of(i * CHUNK, CHUNK), CHUNK)
        normed, scale = normalize(x[span].astype(jnp.float32))
        back = dot(packed[span], weight[:, : 3 * width], 1, 1)
        grad_in[span] = (middle_grad[span] + norm_back(back, normed, scale, gain)).astype(jnp.bfloat16)
        gain_sum = gain_sum + jnp.sum(back * normed, axis=0, keepdims=True)
        return gain_sum, bias_sum + jnp.sum(back, axis=0, keepdims=True)

    gain_sum, bias_sum = lax.fori_loop(0, rows // CHUNK, one_chunk, (zero, zero))
    norm_grads[...] = jnp.concatenate([gain_sum, bias_sum, jnp.zeros((6, width), jnp.float32)], axis=0)


def input_back(lay, x, packed, gains, middle_grad, pieces):
    rows, width = x.shape
    return pl.pallas_call(
        partial(input_back_kernel, lay),
        out_shape=(jax.ShapeDtypeStruct((rows, width), jnp.bfloat16), jax.ShapeDtypeStruct((8, width), jnp.float32)),
        in_specs=[pl.BlockSpec(memory_space=VMEM)] * (4 + len(pieces)),
        out_specs=[pl.BlockSpec(memory_space=VMEM)] * 2,
        scratch_shapes=[pltpu.VMEM((width, pieces[0].shape[1]), jnp.bfloat16)],
        compiler_params=params(10),
        name="input_back",
    )(x, packed, gains, middle_grad, *pieces)


def pack_kernel(weight, norms, out, weight_here, norms_here, done):
    copies = [
        pltpu.make_async_copy(norms, norms_here, done.at[0]),
        pltpu.make_async_copy(weight, weight_here, done.at[1]),
    ]
    for copy in copies:
        copy.start()
    rows, width = weight_here.shape
    same = lax.broadcasted_iota(jnp.int32, (rows, rows), 0) == lax.broadcasted_iota(jnp.int32, (rows, rows), 1)
    lane = lax.broadcasted_iota(jnp.int32, (rows, LANES), 1)
    tile = jnp.zeros((rows, LANES), jnp.float32)
    copies[0].wait()
    for j in range(norms_here.shape[0]):
        column = jnp.sum(jnp.where(same, norms_here[j : j + 1, :], 0.0), axis=1, keepdims=True)
        tile = jnp.where(lane == j, column, tile)
    out[:, width:] = tile.astype(out.dtype)
    copies[1].wait()
    out[:, :width] = weight_here[...].astype(out.dtype)


def pack(weight, norms):
    rows, width = weight.shape
    return pl.pallas_call(
        pack_kernel,
        out_shape=jax.ShapeDtypeStruct((rows, width + LANES), jnp.bfloat16),
        in_specs=[pl.BlockSpec(memory_space=pltpu.MemorySpace.HBM)] * 2,
        out_specs=pl.BlockSpec(memory_space=VMEM),
        scratch_shapes=[
            pltpu.VMEM(weight.shape, weight.dtype),
            pltpu.VMEM(norms.shape, norms.dtype),
            pltpu.SemaphoreType.DMA((2,)),
        ],
        compiler_params=params(60),
        name="pack",
    )(weight, norms)


def column_kernel(lay, *refs):
    out = refs[-1]
    got = [ref[...].astype(jnp.float32) for ref in refs[:-1]]
    parts = []
    for j in range(len(got)):
        part = got[0]
        for i in range(1, len(got)):
            part = jnp.where(lay.partner(lay.core(), i, True, -1) == j, got[i], part)
        parts.append(part)
    out[...] = jnp.concatenate(parts, axis=0).astype(out.dtype)


def column_of(lay, shards):
    rows, cols = shards[0].shape
    return pl.pallas_call(
        partial(column_kernel, lay),
        out_shape=jax.ShapeDtypeStruct((len(shards) * rows, cols), shards[0].dtype),
        in_specs=[pl.BlockSpec(memory_space=VMEM)] * len(shards),
        out_specs=pl.BlockSpec(memory_space=VMEM),
        compiler_params=params(4),
        name="column",
    )(*shards)


def chip_sum_kernel(lay, keep, got, *outs):
    for i, ref in enumerate(outs):
        at = lay.partner(lay.core(), i, False, 1)
        ref[...] = (keep[at].astype(jnp.float32) + got[at].astype(jnp.float32)).astype(ref.dtype)


def chip_sum(lay, keep, got):
    plane, rows, cols = keep.shape
    return pl.pallas_call(
        partial(chip_sum_kernel, lay),
        out_shape=[jax.ShapeDtypeStruct((rows, cols), jnp.float32)]
        + [jax.ShapeDtypeStruct((rows, cols), jnp.bfloat16)] * (plane - 1),
        in_specs=[pl.BlockSpec(memory_space=VMEM)] * 2,
        out_specs=[pl.BlockSpec(memory_space=VMEM)] * plane,
        compiler_params=params(14),
        name="chip_sum",
    )(keep, got)


def plane_sum_kernel(lay, own, *refs):
    got, outs = refs[: lay.plane - 1], refs[lay.plane - 1 :]
    rows = outs[0].shape[0]
    total = own[...]
    for ref in got:
        total = total + ref[...].astype(jnp.float32)
    for i, ref in enumerate(outs):
        at = lay.partner(lay.core(), i, True, 1)
        part = total[:rows]
        for j in range(1, lay.rep):
            part = jnp.where(at == j, total[j * rows : (j + 1) * rows], part)
        ref[...] = part.astype(ref.dtype)


def plane_sum(lay, own, got):
    rows, cols = own.shape
    reps = lay.rep
    return pl.pallas_call(
        partial(plane_sum_kernel, lay),
        out_shape=[jax.ShapeDtypeStruct((rows // reps, cols), jnp.float32)]
        + [jax.ShapeDtypeStruct((rows // reps, cols), jnp.bfloat16)] * (reps - 1),
        in_specs=[pl.BlockSpec(memory_space=VMEM)] * (1 + len(got)),
        out_specs=[pl.BlockSpec(memory_space=VMEM)] * reps,
        compiler_params=params(10),
        name="plane_sum",
    )(own, *got)


def full_sum(value):
    return jnp.sum(jnp.sum(value, axis=1, keepdims=True), axis=0, keepdims=True)


def turned(columns):
    rows, count = columns.shape
    same = lax.broadcasted_iota(jnp.int32, (rows, rows), 0) == lax.broadcasted_iota(jnp.int32, (rows, rows), 1)
    line = lax.broadcasted_iota(jnp.int32, (count, rows), 0)
    out = jnp.zeros((count, rows), jnp.float32)
    for j in range(count):
        row = jnp.sum(jnp.where(same, columns[:, j : j + 1], 0.0), axis=0, keepdims=True)
        out = jnp.where(line == j, row, out)
    return out


def moments_kernel(pieces_of, first_index, reps, more, *refs):
    n = len(pieces_of)
    grads, others, arrays = refs[:reps], refs[reps : reps + more], refs[reps + more :]
    total = grads[0][...]
    for ref in grads[1:]:
        total = total + ref[...].astype(jnp.float32)
    weights, firsts, seconds = arrays[:n], arrays[n : 2 * n], arrays[2 * n : 3 * n]
    momenta, variances, directions = arrays[3 * n : 4 * n], arrays[4 * n : 5 * n], arrays[5 * n : 6 * n]
    sums = arrays[6 * n]
    lane = lax.broadcasted_iota(jnp.int32, (1, LANES), 1)
    row = others[0][0] if more else jnp.zeros((1, LANES), jnp.float32)
    for i, parts in enumerate(pieces_of):
        weight_sum = jnp.zeros((1, 1), jnp.float32)
        step_sum = jnp.zeros((1, 1), jnp.float32)
        for at, size, columns in parts:
            rows = slice(at, at + size)
            gradient = total[:, columns[0] : columns[1]]
            if len(columns) > 2:
                gradient = turned(gradient)
            weight = weights[i][rows]
            momentum = BETA * firsts[i][rows] + (1.0 - BETA) * gradient
            variance = BETA * seconds[i][rows] + (1.0 - BETA) * gradient * gradient
            direction = momentum / (jnp.sqrt(variance) + ADAM_EPSILON) + DECAY * weight
            momenta[i][rows] = momentum
            variances[i][rows] = variance
            directions[i][rows] = direction
            weight_sum = weight_sum + full_sum(weight * weight)
            step_sum = step_sum + full_sum(direction * direction)
        row = jnp.where(lane == first_index[i], weight_sum, row)
        row = jnp.where(lane == 5 + first_index[i], step_sum, row)
    sums[...] = jnp.broadcast_to(row, sums.shape)


def moments(pieces_of, first_index, grads, others, copies, weights, firsts, seconds):
    arrays = [*grads, *others, *weights, *firsts, *seconds]
    shapes = [jax.ShapeDtypeStruct(weight.shape, jnp.float32) for weight in weights]
    outs = pl.pallas_call(
        partial(moments_kernel, pieces_of, first_index, len(grads), len(others)),
        out_shape=shapes * 3 + [jax.ShapeDtypeStruct((copies, 1, LANES), jnp.float32)],
        in_specs=[pl.BlockSpec(memory_space=VMEM)] * len(arrays),
        out_specs=[pl.BlockSpec(memory_space=VMEM)] * (3 * len(weights) + 1),
        compiler_params=params(8),
        name="moments",
    )(*arrays)
    n = len(weights)
    return outs[:n], outs[n : 2 * n], outs[2 * n : 3 * n], outs[3 * n]


def update_kernel(n, sums, *refs):
    weights, directions, updated, table = refs[:n], refs[n : 2 * n], refs[2 * n : 3 * n], refs[3 * n]
    norms = jnp.sqrt(jnp.sum(sums[...], axis=0))
    row = lax.broadcasted_iota(jnp.int32, table.shape, 0)
    lane = lax.broadcasted_iota(jnp.int32, table.shape, 1)
    out = jnp.zeros(table.shape, jnp.float32)
    for i in range(n):
        weight_norm = norms[:, i : i + 1]
        step_norm = norms[:, 5 + i : 6 + i]
        ratio = weight_norm / step_norm
        updated[i][...] = weights[i][...] - RATE * ratio * directions[i][...]
        column = jnp.where(row == 0, weight_norm, jnp.where(row == 1, step_norm, ratio))
        out = jnp.where(lane == i, column, out)
    table[...] = out


def update(sums, weights, directions):
    n = len(weights)
    outs = pl.pallas_call(
        partial(update_kernel, n),
        out_shape=[jax.ShapeDtypeStruct(weight.shape, jnp.float32) for weight in weights]
        + [jax.ShapeDtypeStruct((3, n), jnp.float32)],
        in_specs=[pl.BlockSpec(memory_space=VMEM)] * (1 + 2 * n),
        out_specs=[pl.BlockSpec(memory_space=VMEM)] * (n + 1),
        compiler_params=params(6),
        name="update",
    )(sums, *weights, *directions)
    return outs[:n], outs[n]


def over(lay, value, first):
    return [value] + [lay.over(value, i, first) for i in range(1, lay.rep if first else lay.plane)]


def send_over(lay, parts, first):
    return [lay.over(part, i, first) for i, part in enumerate(parts, 1)]


def over_core(lay, blocks):
    return blocks + [lay.to_core(block) for block in blocks]


def after(values, others):
    count = len(values)
    return list(lax.optimization_barrier((*values, *others))[:count])


def exchange(lay, value):
    return lax.all_to_all(value, AXES, 0, 0)


def body(
    lay,
    inputs,
    segments,
    cotangent,
    attend_in,
    attend_out,
    expand,
    contract,
    layer_norms,
    moment_in,
    moment_out,
    moment_expand,
    moment_contract,
    moment_norms,
    square_in,
    square_out,
    square_expand,
    square_contract,
    square_norms,
):
    plain, twin = lay
    lay = plain
    masters = (attend_in, attend_out, expand, contract, layer_norms)
    width = attend_in.shape[1]
    depth = attend_out.shape[1]
    hidden = expand.shape[1]
    own = attend_in.shape[0]
    count = lay.dp * lay.rep
    whole_tiles = own % 16 == 0
    shard1 = pack(attend_in, layer_norms)
    column1 = over(plain, shard1, True)
    rows = inputs.shape[1]
    attend_out_, expand_, contract_ = after([attend_out, expand, contract], [shard1])
    deep = [contract_[j * own : (j + 1) * own] for j in range(4)]
    shard2 = jnp.concatenate([part.astype(jnp.bfloat16) for part in (attend_out_, expand_, *deep)], axis=1)
    (shard2,) = after([shard2], column1[1:])
    column2 = over(twin, shard2, True)
    blocks1 = over(plain, column_of(plain, column1), False)
    (segments_,) = after([segments], blocks1[:1])
    x, dy, labels, begin = arrange(inputs[0], cotangent[0], segments_)
    blocks2 = over(twin, column_of(twin, after(column2, [*blocks1, x])), False)
    pieces1 = over_core(lay, blocks1)
    *pieces1, x, labels = after([*pieces1, x, labels], blocks2[:1])
    qx, kx, vx, mixed, gains = attend(plain, x, labels, pieces1)
    near = lay.to_core(blocks2[0])
    blocks2[1:] = after(blocks2[1:], [mixed])
    pieces2 = [*blocks2, near, *[lay.to_core(block) for block in blocks2[1:]]]
    deep_pieces = []
    if not whole_tiles:
        first = depth + hidden
        for piece in pieces2:
            part = piece[:, first:].reshape(lay.rep, own, 4, depth).transpose(0, 2, 1, 3)
            deep_pieces.append(part.reshape(-1, depth))
    middle, middle_grad, middle_low, active, contract_all, out_weight, keep2, send2, second_norms, *deep_out = feed(
        twin, x, mixed, dy, gains, pieces2, deep_pieces
    )
    if not whole_tiles:
        keep2, send2 = [
            jnp.concatenate(
                [
                    wide[:, :, : depth + hidden],
                    part.reshape(lay.plane, lay.rep, 4, own, depth).transpose(0, 1, 3, 2, 4).reshape(lay.plane, -1, 4 * depth),
                ],
                axis=2,
            )
            for wide, part in zip((keep2, send2), deep_out)
        ]
    chip2 = lay.to_core(send2)
    dox = mixed_back(middle_low, mixed, out_weight)
    keep2, chip2 = after([keep2, chip2], [dox])
    own2, *low2 = chip_sum(twin, keep2, chip2)
    got2 = send_over(twin, low2, False)
    (dox,) = after([dox], low2)
    packed = attend_back(qx, kx, vx, dox)
    input_gradient, first_norms = input_back(plain, x, packed, gains, middle_grad, pieces1)
    keep1, send1 = project_back(plain, x, packed, gains, first_norms, second_norms, own)
    own2, send1, *got2 = after([own2, send1, *got2], [])
    own2, *low2 = plane_sum(twin, own2, got2)
    got2 = send_over(twin, low2, True)
    own1, *low1 = chip_sum(plain, keep1, lay.to_core(send1))
    got1 = send_over(plain, low1, False)
    (middle,) = after([middle], low1)
    outputs, input_gradient = finish(begin, middle, active, contract_all, input_gradient, rows)
    own1, *got1 = after([own1, *got1], [outputs])
    spans = [[(0, own, (0, depth))], [(0, own, (depth, depth + hidden))]]
    spans.append([(j * own, own, (depth + hidden + j * depth, depth + hidden + (j + 1) * depth)) for j in range(4)])
    momenta2, variances2, directions2, sums2 = moments(
        spans, (1, 2, 3), [own2, *got2], [], 1, masters[1:4],
        (moment_out, moment_expand, moment_contract), (square_out, square_expand, square_contract),
    )
    own1, *low1 = plane_sum(plain, own1, got1)
    got1 = send_over(plain, low1, True)
    momenta1, variances1, directions1, sums1 = moments(
        [[(0, own, (0, width))], [(0, 4, (width, width + 4, True))]], (0, 4), [own1, *got1], [sums2], count, (attend_in, layer_norms),
        (moment_in, moment_norms), (square_in, square_norms),
    )
    sums = exchange(lay, sums1)
    directions = (directions1[0], *directions2, directions1[1])
    updated, trust_table = update(sums, masters, directions)
    momenta = (momenta1[0], *momenta2, momenta1[1])
    variances = (variances1[0], *variances2, variances1[1])
    return (outputs[None], input_gradient[None], *updated, *momenta, *variances, trust_table)


def solution(mesh):
    placed = (
        P(("dp", "rep"), None, None),
        P(("dp", "rep"), None),
        P(("dp", "rep"), None, None),
        P(("dp", "rep"), None),
        P(("dp", "rep"), None),
        P(("dp", "rep"), None),
        P(("dp", "rep"), None),
        P(None, ("dp", "rep")),
        P(("dp", "rep"), None),
        P(("dp", "rep"), None),
        P(("dp", "rep"), None),
        P(("dp", "rep"), None),
        P(None, ("dp", "rep")),
        P(("dp", "rep"), None),
        P(("dp", "rep"), None),
        P(("dp", "rep"), None),
        P(("dp", "rep"), None),
        P(None, ("dp", "rep")),
    )
    return jax.shard_map(
        partial(body, (Layout(mesh, False), Layout(mesh, True))),
        mesh=mesh,
        in_specs=placed,
        out_specs=(
            P(("dp", "rep"), None, None),
            P(("dp", "rep"), None, None),
            P(("dp", "rep"), None),
            P(("dp", "rep"), None),
            P(("dp", "rep"), None),
            P(("dp", "rep"), None),
            P(None, ("dp", "rep")),
            P(("dp", "rep"), None),
            P(("dp", "rep"), None),
            P(("dp", "rep"), None),
            P(("dp", "rep"), None),
            P(None, ("dp", "rep")),
            P(("dp", "rep"), None),
            P(("dp", "rep"), None),
            P(("dp", "rep"), None),
            P(("dp", "rep"), None),
            P(None, ("dp", "rep")),
            P(),
        ),
        check_vma=False,
    )
```

```python
from functools import partial
import math

import jax
import jax.numpy as jnp
from jax import lax
from jax.experimental import pallas as pl
from jax.experimental.pallas import tpu as pltpu
from jax.sharding import PartitionSpec as P

HEADS = 8
HEAD_DIM = 64


EPSILON = 1e-05
ADAM_EPSILON = 1e-06
DECAY = 0.01
RATE = 0.5
BETA = 0.5
LANES = 128
HALF = 64
BIG = 1e30
FEATS = 4
TILE = 256
THIN = 32
CHUNK = 352
DEEP_CHUNK = 528
GELU_ONE = 0.7978845608028654
GELU_CUBE = 0.044715 * GELU_ONE
VMEM = pltpu.MemorySpace.VMEM
AXES = ("dp", "rep")


def params(mebibytes):
    return pltpu.CompilerParams(vmem_limit_bytes=mebibytes * 1024 * 1024)


def dot(a, b, ca, cb):
    return lax.dot_general(a, b, (((ca,), (cb,)), ((), ())), preferred_element_type=jnp.float32)


def normalize(values):
    center = values - jnp.mean(values, axis=-1, keepdims=True)
    scale = lax.rsqrt(jnp.mean(center * center, axis=-1, keepdims=True) + EPSILON)
    return center * scale, scale


class Layout:
    def __init__(self, mesh, mixed):
        self.dp = mesh.shape["dp"]
        self.rep = mesh.shape["rep"]
        self.plane = self.dp // 2
        self.mixed = mixed and self.plane == self.rep

    def pairs(self, move):
        pairs = []
        for p in range(self.plane):
            for c in range(2):
                for z in range(self.rep):
                    q, d, w = move(p, c, z)
                    pairs.append(((p * 2 + c) * self.rep + z, (q * 2 + d) * self.rep + w))
        return pairs

    def over(self, value, i, first):
        def move(p, c, z):
            along_z = (first == (c == 0)) if self.mixed else first
            return (p, c, (z + i) % self.rep) if along_z else (p ^ i, c, z)

        return lax.ppermute(value, AXES, self.pairs(move))

    def to_core(self, value):
        return lax.ppermute(value, AXES, self.pairs(lambda p, c, z: (p, 1 - c, z)))

    def core(self):
        return lax.rem(lax.axis_index("dp"), 2)

    def partner(self, side, i, first, sign):
        along_z = lax.rem(lax.axis_index("rep") + (sign * i) % self.rep, self.rep)
        in_plane = lax.div(lax.axis_index("dp"), 2) ^ i
        if not self.mixed:
            return along_z if first else in_plane
        return jnp.where(side == 0, along_z, in_plane) if first else jnp.where(side == 0, in_plane, along_z)

    def device(self, side, second, first):
        plain = (2 * second + side) * self.rep + first
        return jnp.where(side == 0, plain, (2 * first + side) * self.rep + second) if self.mixed else plain


def row_blocks(lay, side, second, rows):
    firsts = lay.rep
    if lay.mixed:
        return [(j * rows, pl.multiple_of(lay.device(side, second, j) * rows, rows), rows) for j in range(firsts)]
    return [(0, pl.multiple_of(lay.device(side, second, 0) * rows, firsts * rows), firsts * rows)]


def assemble(lay, pieces, full_ref, columns):
    count = len(pieces) // 2
    for i, piece in enumerate(pieces):
        side = lay.core() if i < count else 1 - lay.core()
        second = lay.partner(side, i % count, False, -1)
        for at, to, rows in row_blocks(lay, side, second, piece.shape[0] // lay.rep):
            full_ref[pl.ds(to, rows), :] = piece[at : at + rows, columns]


def assemble_deep(lay, pieces, full_ref, first):
    count = len(pieces) // 2
    width = full_ref.shape[1]
    for i, piece in enumerate(pieces):
        side = lay.core() if i < count else 1 - lay.core()
        second = lay.partner(side, i % count, False, -1)
        rows = piece.shape[0] // lay.rep
        for z in range(lay.rep):
            to = pl.multiple_of(lay.device(side, second, z) * 4 * rows, 4 * rows)
            for j in range(4):
                source = piece[z * rows : (z + 1) * rows, first + j * width : first + (j + 1) * width]
                full_ref[pl.ds(to + j * rows, rows), :] = source


def split_rows(lay, full_ref, keep_ref, send_ref, lanes):
    for target, side in ((keep_ref, lay.core()), (send_ref, 1 - lay.core())):
        for second in range(target.shape[0]):
            for at, source, rows in row_blocks(lay, side, second, target.shape[1] // lay.rep):
                target[second, at : at + rows, lanes] = full_ref[pl.ds(source, rows), :].astype(target.dtype)


def split_deep(lay, full_ref, keep_ref, send_ref, first):
    width = full_ref.shape[1]
    rows = keep_ref.shape[1] // lay.rep
    for target, side in ((keep_ref, lay.core()), (send_ref, 1 - lay.core())):
        for second in range(target.shape[0]):
            for z in range(lay.rep):
                source = pl.multiple_of(lay.device(side, second, z) * 4 * rows, 4 * rows)
                for j in range(4):
                    part = full_ref[pl.ds(source + j * rows, rows), :]
                    columns = slice(first + j * width, first + (j + 1) * width)
                    target[second, z * rows : (z + 1) * rows, columns] = part.astype(target.dtype)


def row_chunks(rows, size):
    return [(at, min(size, rows - at)) for at in range(0, rows, size)]


def windows(rows):
    half = (rows - THIN) // 2
    span = half + THIN
    spans = [(at, TILE, 0, span) for at in range(0, half, TILE)]
    spans.append((half, THIN, 0, rows))
    return spans + [(at, TILE, half, span) for at in range(span, rows, TILE)]


def arrange_kernel(inputs, cotangent, segments, x, dy, labels, begin, room):
    tokens = segments.shape[1]
    half = tokens // 2
    memory = inputs.shape[0] - tokens
    segment = segments[...].astype(jnp.float32)
    ahead = pltpu.roll(jnp.broadcast_to(segment, (8, tokens)), tokens - half + 1, 1)[:1]
    lane = lax.broadcasted_iota(jnp.int32, (1, tokens), 1)
    fits = (segment == ahead) & (lane <= half)
    start = jnp.sum(jnp.where(fits, lane.astype(jnp.float32), 0.0), axis=1, keepdims=True)
    begin[...] = jnp.broadcast_to(start, begin.shape)
    row = lax.broadcasted_iota(jnp.int32, (half, LANES), 0).astype(jnp.float32)
    early = row < start
    thin = lax.broadcasted_iota(jnp.int32, (THIN, LANES), 0) < memory
    for source, target in ((inputs, x), (cotangent, dy)):
        for at in range(0, inputs.shape[1], LANES):
            columns = slice(at, at + LANES)
            room[: inputs.shape[0]] = source[:, columns].astype(jnp.float32)
            left, right = room[memory : memory + half], room[memory + half : memory + tokens]
            target[:half, columns] = jnp.where(early, right, left).astype(target.dtype)
            target[half : half + THIN, columns] = jnp.where(thin, room[:THIN], 0.0).astype(target.dtype)
            target[half + THIN :, columns] = jnp.where(early, left, right).astype(target.dtype)
    left = jnp.transpose(jnp.broadcast_to(segment[:, :half], (LANES, half)))
    right = jnp.transpose(jnp.broadcast_to(segment[:, half:], (LANES, half)))
    labels[:half] = jnp.where(early, right, left).astype(jnp.int32)
    labels[half : half + THIN] = jnp.where(thin, -1, -2)
    labels[half + THIN :] = jnp.where(early, left, right).astype(jnp.int32)


def arrange(inputs, cotangent, segments):
    width = inputs.shape[1]
    rows = segments.shape[1] + THIN
    return pl.pallas_call(
        arrange_kernel,
        out_shape=(
            jax.ShapeDtypeStruct((rows, width), inputs.dtype),
            jax.ShapeDtypeStruct((rows, width), inputs.dtype),
            jax.ShapeDtypeStruct((rows, LANES), jnp.int32),
            jax.ShapeDtypeStruct((8, LANES), jnp.float32),
        ),
        in_specs=[pl.BlockSpec(memory_space=VMEM)] * 3,
        out_specs=[pl.BlockSpec(memory_space=VMEM)] * 4,
        scratch_shapes=[pltpu.VMEM((rows, LANES), jnp.float32)],
        compiler_params=params(8),
        name="arrange",
    )(inputs, cotangent, segments)


def finish_kernel(begin, middle, active, contract, grad_in, outputs, grad_out, room):
    rows = outputs.shape[0]
    half = (middle.shape[0] - THIN) // 2
    memory = rows - 2 * half
    wide = room.shape[1]
    row = lax.broadcasted_iota(jnp.int32, (half, wide), 0).astype(jnp.float32)
    early = row < begin[:1, :1]

    def place(value, target, columns):
        left, right = value[:half], value[half + THIN :]
        room[:THIN] = value[half : half + THIN]
        room[memory : memory + half] = jnp.where(early, right, left)
        room[memory + half : rows] = jnp.where(early, left, right)
        target[:, columns] = room[:rows].astype(target.dtype)

    for at in range(0, middle.shape[1], wide):
        columns = slice(at, at + wide)
        place(middle[:, columns] + dot(active[...], contract[:, columns], 1, 0), outputs, columns)
        place(grad_in[:, columns].astype(jnp.float32), grad_out, columns)


def finish(begin, middle, active, contract, grad_in, rows):
    width = middle.shape[1]
    return pl.pallas_call(
        finish_kernel,
        out_shape=[jax.ShapeDtypeStruct((rows, width), grad_in.dtype)] * 2,
        in_specs=[pl.BlockSpec(memory_space=VMEM)] * 5,
        out_specs=[pl.BlockSpec(memory_space=VMEM)] * 2,
        scratch_shapes=[pltpu.VMEM((middle.shape[0], 256), jnp.float32)],
        compiler_params=params(10),
        name="finish",
    )(begin, middle, active, contract, grad_in)


def attend_kernel(lay, count, x, labels, *refs):
    pieces = refs[:count]
    qx, kx, vx, mixed, gains, weight, qs = refs[count:]
    rows = x.shape[0]
    width = mixed.shape[1]
    assemble(lay, pieces, weight, slice(None))
    gains[...] = jnp.transpose(weight[:, 3 * width :].astype(jnp.float32))[:8]
    gain, bias = gains[0:1], gains[1:2]

    def one_chunk(i, carry):
        span = pl.ds(pl.multiple_of(i * CHUNK, CHUNK), CHUNK)
        normed, _ = normalize(x[span].astype(jnp.float32))
        first = (normed * gain + bias).astype(jnp.bfloat16)
        lane = lax.broadcasted_iota(jnp.int32, (CHUNK, LANES), 1)
        low = lane < HALF
        feature = lane % HALF
        label = labels[span]
        blocked = ((feature < FEATS) & (label >= 0) & (feature != label)) | (feature == FEATS)
        query_side = jnp.where(blocked, -BIG, 0.0)
        marked = ((feature < FEATS) & (feature == label)) | ((feature == FEATS) & (label == -2))
        key_side = jnp.where(marked | (feature > FEATS), 1.0, 0.0)
        sides = (query_side, key_side, jnp.ones_like(key_side))
        for kind, target in enumerate((qs, kx, vx)):
            whole = dot(first, weight[:, kind * width : (kind + 1) * width], 1, 0)
            whole = whole.astype(jnp.bfloat16).astype(jnp.float32)
            for pair in range(width // LANES):
                part = whole[:, pair * LANES : (pair + 1) * LANES]
                if kind == 0:
                    part = part * (1.0 / math.sqrt(HEAD_DIM))
                at = 2 * pair * LANES
                target[span, at : at + LANES] = jnp.where(low, part, sides[kind]).astype(jnp.bfloat16)
                target[span, at + LANES : at + 2 * LANES] = jnp.where(low, sides[kind], part).astype(jnp.bfloat16)
        return carry

    lax.fori_loop(0, rows // CHUNK, one_chunk, 0)

    def one_pair(pair, carry):
        columns = pl.ds(pl.multiple_of(pair * LANES, LANES), LANES)
        for at, size, key_at, key_size in windows(rows):
            span = pl.ds(at, size)
            seen = pl.ds(key_at, key_size)
            lane = lax.broadcasted_iota(jnp.int32, (size, LANES), 1)
            low = lane < HALF
            feature = lane % HALF
            got = []
            for side in range(2):
                head = pl.ds(pl.multiple_of((2 * pair + side) * LANES, LANES), LANES)
                queries = qs[span, head]
                scores = dot(queries, kx[seen, head], 1, 1)
                highest = jnp.max(scores, axis=1, keepdims=True)
                raised = jnp.exp(scores - highest).astype(jnp.bfloat16)
                found = dot(raised, vx[seen, head], 1, 0)
                total = -(highest + jnp.log(found))
                first = total.astype(jnp.bfloat16).astype(jnp.float32)
                second = (total - first).astype(jnp.bfloat16).astype(jnp.float32)
                third = total - first - second
                values = jnp.where(feature == 5, first, jnp.where(feature == 6, second, third))
                place = (feature > FEATS) & (feature < 8) & (low if side else ~low)
                qx[span, head] = jnp.where(place, values, queries.astype(jnp.float32)).astype(jnp.bfloat16)
                got.append(found)
            over = pltpu.roll(jnp.where(low, got[1], got[0]), HALF, 1)
            mixed[span, columns] = (jnp.where(low, got[0], got[1]) / over).astype(jnp.bfloat16)
        return carry

    lax.fori_loop(0, width // LANES, one_pair, 0)


def attend(lay, x, labels, pieces):
    rows, width = x.shape
    wide = jax.ShapeDtypeStruct((rows, 2 * width), jnp.bfloat16)
    depth = len(pieces) * pieces[0].shape[0]
    return pl.pallas_call(
        partial(attend_kernel, lay, len(pieces)),
        out_shape=(
            wide,
            wide,
            wide,
            jax.ShapeDtypeStruct((rows, width), jnp.bfloat16),
            jax.ShapeDtypeStruct((8, width), jnp.float32),
        ),
        in_specs=[pl.BlockSpec(memory_space=VMEM)] * (2 + len(pieces)),
        out_specs=[pl.BlockSpec(memory_space=VMEM)] * 5,
        scratch_shapes=[
            pltpu.VMEM((depth, pieces[0].shape[1]), jnp.bfloat16),
            pltpu.VMEM((rows, 2 * width), jnp.bfloat16),
        ],
        compiler_params=params(16),
        name="attend",
    )(x, labels, *pieces)


def attend_back_kernel(qx, kx, vx, dox, packed, total):
    rows = qx.shape[0]
    width = packed.shape[1] // 3

    def one_pair(pair, carry):
        heads = [pl.ds(pl.multiple_of((2 * pair + side) * LANES, LANES), LANES) for side in range(2)]
        spots = [pl.ds(pl.multiple_of(kind * width + pair * LANES, LANES), LANES) for kind in range(3)]
        total[...] = jnp.zeros_like(total)
        for at, size, query_at, query_size in windows(rows):
            span = pl.ds(at, size)
            seen = pl.ds(query_at, query_size)
            low = lax.broadcasted_iota(jnp.int32, (size, LANES), 1) < HALF
            got = []
            for side in range(2):
                head = heads[side]
                keys = kx[span, head]
                queries = qx[seen, head]
                upstream = dox[seen, head]
                attention = jnp.exp(dot(keys, queries, 1, 1))
                grad = dot(vx[span, head], upstream, 1, 1)
                scores = (attention * grad).astype(jnp.bfloat16)
                got.append((dot(scores, queries, 1, 0), dot(attention.astype(jnp.bfloat16), upstream, 1, 0)))
                total[side, seen] += dot(scores, keys, 0, 0)
            packed[span, spots[1]] = jnp.where(low, got[0][0], got[1][0]).astype(jnp.bfloat16)
            packed[span, spots[2]] = jnp.where(low, got[0][1], got[1][1]).astype(jnp.bfloat16)
        low = lax.broadcasted_iota(jnp.int32, (rows, LANES), 1) < HALF
        packed[:, spots[0]] = (jnp.where(low, total[0], total[1]) * (1.0 / math.sqrt(HEAD_DIM))).astype(jnp.bfloat16)
        return carry

    lax.fori_loop(0, width // LANES, one_pair, 0)


def attend_back(qx, kx, vx, dox):
    rows, wide = qx.shape
    return pl.pallas_call(
        attend_back_kernel,
        out_shape=jax.ShapeDtypeStruct((rows, 3 * wide // 2), jnp.bfloat16),
        in_specs=[pl.BlockSpec(memory_space=VMEM)] * 4,
        out_specs=pl.BlockSpec(memory_space=VMEM),
        scratch_shapes=[pltpu.VMEM((2, rows, LANES), jnp.float32)],
        compiler_params=params(16),
        name="attend_back",
    )(qx, kx, vx, dox)


def norm_back(grad, normed, scale, gain):
    scaled = grad * gain
    return scale * (
        scaled
        - jnp.mean(scaled, axis=-1, keepdims=True)
        - normed * jnp.mean(scaled * normed, axis=-1, keepdims=True)
    )


def feed_kernel(lay, count, deep_count, x, mixed, dy, gains, *refs):
    pieces = refs[:count]
    deep_pieces = refs[count : count + deep_count]
    outs = refs[count + deep_count : -5]
    middle, middle_grad, middle_low, active, contract, out_weight, keep2, send2, norm_grads, *deep_out = outs
    wide, hidden_grad, second, block, deep_block = refs[-5:]
    rows, width = x.shape
    hidden = contract.shape[0]
    assemble(lay, pieces, wide, slice(0, width + hidden))
    if deep_count:
        assemble(lay, deep_pieces, contract, slice(None))
    else:
        assemble_deep(lay, pieces, contract, width + hidden)
    out_weight[...] = wide[:, :width]
    gain, bias = gains[2:3], gains[3:4]
    zero = jnp.zeros((1, width), jnp.float32)

    def one_chunk(i, carry):
        gain_sum, bias_sum = carry
        span = pl.ds(pl.multiple_of(i * DEEP_CHUNK, DEEP_CHUNK), DEEP_CHUNK)
        start = x[span].astype(jnp.float32) + dot(mixed[span], wide[:, :width], 1, 0)
        middle[span] = start
        normed, scale = normalize(start)
        low = (normed * gain + bias).astype(jnp.bfloat16)
        second[span] = low
        for start in range(0, hidden, 512):
            part = slice(start, start + 512)
            up = dot(low, wide[:, width + start : width + start + 512], 1, 0)
            square = up * up
            half = 0.5 + 0.5 * jnp.tanh(up * (GELU_ONE + GELU_CUBE * square))
            act = up * half
            active[span, part] = act.astype(jnp.bfloat16)
            slope = half + act * ((1.0 - half) * (2.0 * GELU_ONE + 6.0 * GELU_CUBE * square))
            hidden_grad[span, part] = (dot(dy[span], contract[part], 1, 1) * slope).astype(jnp.bfloat16)
        back = dot(hidden_grad[span], wide[:, width:], 1, 1)
        gain_sum = gain_sum + jnp.sum(back * normed, axis=0, keepdims=True)
        bias_sum = bias_sum + jnp.sum(back, axis=0, keepdims=True)
        grad = dy[span].astype(jnp.float32) + norm_back(back, normed, scale, gain)
        middle_grad[span] = grad
        middle_low[span] = grad.astype(jnp.bfloat16)
        return gain_sum, bias_sum

    gain_sum, bias_sum = lax.fori_loop(0, rows // DEEP_CHUNK, one_chunk, (zero, zero))
    norm_grads[...] = jnp.concatenate([gain_sum, bias_sum, jnp.zeros((6, width), jnp.float32)], axis=0)

    def one_block(i, carry):
        columns = pl.ds(pl.multiple_of(i * 512, 512), 512)
        deep_block[columns] = dot(active[:, columns], dy[...], 0, 0)
        block[...] = dot(second[...], hidden_grad[:, columns], 0, 0)
        split_rows(lay, block, keep2, send2, pl.ds(pl.multiple_of(width + i * 512, 512), 512))
        return carry

    lax.fori_loop(0, hidden // 512, one_block, 0)
    if deep_count:
        split_rows(lay, deep_block, *deep_out, slice(0, width))
    else:
        split_deep(lay, deep_block, keep2, send2, width + hidden)
    block[...] = dot(mixed[...], middle_low[...], 0, 0)
    split_rows(lay, block, keep2, send2, slice(0, width))


def feed(lay, x, mixed, dy, gains, pieces, deep_pieces):
    rows, width = x.shape
    plane = len(pieces) // 2
    deep = pieces[0].shape[0]
    columns = pieces[0].shape[1]
    hidden = 4 * width
    out_shape = [
        jax.ShapeDtypeStruct((rows, width), jnp.float32),
        jax.ShapeDtypeStruct((rows, width), jnp.float32),
        jax.ShapeDtypeStruct((rows, width), jnp.bfloat16),
        jax.ShapeDtypeStruct((rows, hidden), jnp.bfloat16),
        jax.ShapeDtypeStruct((hidden, width), jnp.bfloat16),
        jax.ShapeDtypeStruct((width, width), jnp.bfloat16),
        jax.ShapeDtypeStruct((plane, deep, columns), jnp.bfloat16),
        jax.ShapeDtypeStruct((plane, deep, columns), jnp.bfloat16),
        jax.ShapeDtypeStruct((8, width), jnp.float32),
    ]
    if deep_pieces:
        out_shape.append(jax.ShapeDtypeStruct((plane, 4 * deep, width), jnp.bfloat16))
        out_shape.append(jax.ShapeDtypeStruct((plane, 4 * deep, width), jnp.bfloat16))
    return pl.pallas_call(
        partial(feed_kernel, lay, len(pieces), len(deep_pieces)),
        out_shape=out_shape,
        in_specs=[pl.BlockSpec(memory_space=VMEM)] * (4 + len(pieces) + len(deep_pieces)),
        out_specs=[pl.BlockSpec(memory_space=VMEM)] * len(out_shape),
        scratch_shapes=[
            pltpu.VMEM((width, width + hidden), jnp.bfloat16),
            pltpu.VMEM((rows, hidden), jnp.bfloat16),
            pltpu.VMEM((rows, width), jnp.bfloat16),
            pltpu.VMEM((width, 512), jnp.float32),
            pltpu.VMEM((hidden, width), jnp.float32),
        ],
        compiler_params=params(26),
        name="feed",
    )(x, mixed, dy, gains, *pieces, *deep_pieces)


def mixed_back_kernel(middle_low, mixed, out_weight, dox):
    rows, width = mixed.shape

    def one_chunk(i, carry):
        span = pl.ds(pl.multiple_of(i * DEEP_CHUNK, DEEP_CHUNK), DEEP_CHUNK)
        mixed_grad = dot(middle_low[span], out_weight[...], 1, 1).astype(jnp.bfloat16).astype(jnp.float32)
        lane = lax.broadcasted_iota(jnp.int32, (DEEP_CHUNK, LANES), 1)
        left = lane < HALF
        feature = lane % HALF
        for pair in range(width // LANES):
            columns = slice(pair * LANES, (pair + 1) * LANES)
            piece = mixed_grad[:, columns]
            product = piece * mixed[span, columns].astype(jnp.float32)
            for side in range(2):
                mine = left if side == 0 else ~left
                delta = -jnp.sum(jnp.where(mine, product, 0.0), axis=1, keepdims=True)
                one = delta.astype(jnp.bfloat16).astype(jnp.float32)
                two = (delta - one).astype(jnp.bfloat16).astype(jnp.float32)
                three = delta - one - two
                extra = jnp.where(feature == 0, one, jnp.where(feature == 1, two, jnp.where(feature == 2, three, 0.0)))
                head = (2 * pair + side) * LANES
                dox[span, head : head + LANES] = jnp.where(mine, piece, extra).astype(jnp.bfloat16)
        return carry

    lax.fori_loop(0, rows // DEEP_CHUNK, one_chunk, 0)


def mixed_back(middle_low, mixed, out_weight):
    rows, width = mixed.shape
    return pl.pallas_call(
        mixed_back_kernel,
        out_shape=jax.ShapeDtypeStruct((rows, 2 * width), jnp.bfloat16),
        in_specs=[pl.BlockSpec(memory_space=VMEM)] * 3,
        out_specs=pl.BlockSpec(memory_space=VMEM),
        compiler_params=params(10),
        name="mixed_back",
    )(middle_low, mixed, out_weight)


def project_back_kernel(lay, x, packed, gains, first_norms, second_norms, keep, send, first, block):
    rows, width = x.shape
    gain, bias = gains[0:1], gains[1:2]

    def one_chunk(i, carry):
        span = pl.ds(pl.multiple_of(i * CHUNK, CHUNK), CHUNK)
        normed, _ = normalize(x[span].astype(jnp.float32))
        first[span] = (normed * gain + bias).astype(jnp.bfloat16)
        return carry

    lax.fori_loop(0, rows // CHUNK, one_chunk, 0)

    def one_block(i, carry):
        columns = pl.ds(pl.multiple_of(i * 512, 512), 512)
        block[...] = dot(first[...], packed[:, columns], 0, 0)
        split_rows(lay, block, keep, send, columns)
        return carry

    lax.fori_loop(0, packed.shape[1] // 512, one_block, 0)
    fill = jnp.zeros((LANES - 4, width), jnp.float32)
    norms = jnp.concatenate([first_norms[:2], second_norms[:2], fill], axis=0)
    block[:, :LANES] = jnp.transpose(norms)
    split_rows(lay, block.at[:, :LANES], keep, send, slice(packed.shape[1], packed.shape[1] + LANES))


def project_back(lay, x, packed, gains, first_norms, second_norms, own):
    rows, width = x.shape
    shape = (lay.plane, lay.rep * own, packed.shape[1] + LANES)
    return pl.pallas_call(
        partial(project_back_kernel, lay),
        out_shape=(jax.ShapeDtypeStruct(shape, jnp.bfloat16), jax.ShapeDtypeStruct(shape, jnp.bfloat16)),
        in_specs=[pl.BlockSpec(memory_space=VMEM)] * 5,
        out_specs=[pl.BlockSpec(memory_space=VMEM)] * 2,
        scratch_shapes=[pltpu.VMEM((rows, width), jnp.bfloat16), pltpu.VMEM((width, 512), jnp.float32)],
        compiler_params=params(10),
        name="project_back",
    )(x, packed, gains, first_norms, second_norms)


def input_back_kernel(lay, x, packed, gains, middle_grad, *refs):
    pieces = refs[:-3]
    grad_in, norm_grads, weight = refs[-3:]
    rows, width = x.shape
    assemble(lay, pieces, weight, slice(None))
    gain = gains[0:1]
    zero = jnp.zeros((1, width), jnp.float32)

    def one_chunk(i, carry):
        gain_sum, bias_sum = carry
        span = pl.ds(pl.multiple_of(i * CHUNK, CHUNK), CHUNK)
        normed, scale = normalize(x[span].astype(jnp.float32))
        back = dot(packed[span], weight[:, : 3 * width], 1, 1)
        grad_in[span] = (middle_grad[span] + norm_back(back, normed, scale, gain)).astype(jnp.bfloat16)
        gain_sum = gain_sum + jnp.sum(back * normed, axis=0, keepdims=True)
        return gain_sum, bias_sum + jnp.sum(back, axis=0, keepdims=True)

    gain_sum, bias_sum = lax.fori_loop(0, rows // CHUNK, one_chunk, (zero, zero))
    norm_grads[...] = jnp.concatenate([gain_sum, bias_sum, jnp.zeros((6, width), jnp.float32)], axis=0)


def input_back(lay, x, packed, gains, middle_grad, pieces):
    rows, width = x.shape
    return pl.pallas_call(
        partial(input_back_kernel, lay),
        out_shape=(jax.ShapeDtypeStruct((rows, width), jnp.bfloat16), jax.ShapeDtypeStruct((8, width), jnp.float32)),
        in_specs=[pl.BlockSpec(memory_space=VMEM)] * (4 + len(pieces)),
        out_specs=[pl.BlockSpec(memory_space=VMEM)] * 2,
        scratch_shapes=[pltpu.VMEM((width, pieces[0].shape[1]), jnp.bfloat16)],
        compiler_params=params(10),
        name="input_back",
    )(x, packed, gains, middle_grad, *pieces)


def pack_kernel(*refs):
    count = 5
    sources, (first, second), here, done = refs[:count], refs[count : count + 2], refs[count + 2 : -1], refs[-1]
    copies = [pltpu.make_async_copy(source, local, done.at[i]) for i, (source, local) in enumerate(zip(sources, here))]
    for copy in copies:
        copy.start()
    norms, weight, out_weight, expand, contract = here
    rows, width = weight.shape
    depth, hidden = out_weight.shape[1], expand.shape[1]
    same = lax.broadcasted_iota(jnp.int32, (rows, rows), 0) == lax.broadcasted_iota(jnp.int32, (rows, rows), 1)
    lane = lax.broadcasted_iota(jnp.int32, (rows, LANES), 1)
    tile = jnp.zeros((rows, LANES), jnp.float32)
    copies[0].wait()
    for j in range(norms.shape[0]):
        column = jnp.sum(jnp.where(same, norms[j : j + 1, :], 0.0), axis=1, keepdims=True)
        tile = jnp.where(lane == j, column, tile)
    first[:, width:] = tile.astype(first.dtype)
    copies[1].wait()
    first[:, :width] = weight[...].astype(first.dtype)
    copies[2].wait()
    second[:, :depth] = out_weight[...].astype(second.dtype)
    copies[3].wait()
    second[:, depth : depth + hidden] = expand[...].astype(second.dtype)
    copies[4].wait()
    for j in range(4):
        at = depth + hidden + j * depth
        second[:, at : at + depth] = contract[j * rows : (j + 1) * rows].astype(second.dtype)


def pack(norms, weight, out_weight, expand, contract):
    rows, width = weight.shape
    sources = (norms, weight, out_weight, expand, contract)
    rest = out_weight.shape[1] + expand.shape[1] + 4 * contract.shape[1]
    return pl.pallas_call(
        pack_kernel,
        out_shape=(
            jax.ShapeDtypeStruct((rows, width + LANES), jnp.bfloat16),
            jax.ShapeDtypeStruct((rows, rest), jnp.bfloat16),
        ),
        in_specs=[pl.BlockSpec(memory_space=pltpu.MemorySpace.HBM)] * len(sources),
        out_specs=[pl.BlockSpec(memory_space=VMEM)] * 2,
        scratch_shapes=[pltpu.VMEM(source.shape, source.dtype) for source in sources]
        + [pltpu.SemaphoreType.DMA((len(sources),))],
        compiler_params=params(60),
        name="pack",
    )(*sources)


def column_kernel(lay, *refs):
    out = refs[-1]
    got = [ref[...].astype(jnp.float32) for ref in refs[:-1]]
    parts = []
    for j in range(len(got)):
        part = got[0]
        for i in range(1, len(got)):
            part = jnp.where(lay.partner(lay.core(), i, True, -1) == j, got[i], part)
        parts.append(part)
    out[...] = jnp.concatenate(parts, axis=0).astype(out.dtype)


def column_of(lay, shards):
    rows, cols = shards[0].shape
    return pl.pallas_call(
        partial(column_kernel, lay),
        out_shape=jax.ShapeDtypeStruct((len(shards) * rows, cols), shards[0].dtype),
        in_specs=[pl.BlockSpec(memory_space=VMEM)] * len(shards),
        out_specs=pl.BlockSpec(memory_space=VMEM),
        compiler_params=params(4),
        name="column",
    )(*shards)


def chip_sum_kernel(lay, keep, got, *outs):
    for i, ref in enumerate(outs):
        at = lay.partner(lay.core(), i, False, 1)
        ref[...] = (keep[at].astype(jnp.float32) + got[at].astype(jnp.float32)).astype(ref.dtype)


def chip_sum(lay, keep, got):
    plane, rows, cols = keep.shape
    return pl.pallas_call(
        partial(chip_sum_kernel, lay),
        out_shape=[jax.ShapeDtypeStruct((rows, cols), jnp.float32)]
        + [jax.ShapeDtypeStruct((rows, cols), jnp.bfloat16)] * (plane - 1),
        in_specs=[pl.BlockSpec(memory_space=VMEM)] * 2,
        out_specs=[pl.BlockSpec(memory_space=VMEM)] * plane,
        compiler_params=params(14),
        name="chip_sum",
    )(keep, got)


def plane_sum_kernel(lay, own, *refs):
    got, outs = refs[: lay.plane - 1], refs[lay.plane - 1 :]
    rows = outs[0].shape[0]
    total = own[...]
    for ref in got:
        total = total + ref[...].astype(jnp.float32)
    for i, ref in enumerate(outs):
        at = lay.partner(lay.core(), i, True, 1)
        part = total[:rows]
        for j in range(1, lay.rep):
            part = jnp.where(at == j, total[j * rows : (j + 1) * rows], part)
        ref[...] = part.astype(ref.dtype)


def plane_sum(lay, own, got):
    rows, cols = own.shape
    reps = lay.rep
    return pl.pallas_call(
        partial(plane_sum_kernel, lay),
        out_shape=[jax.ShapeDtypeStruct((rows // reps, cols), jnp.float32)]
        + [jax.ShapeDtypeStruct((rows // reps, cols), jnp.bfloat16)] * (reps - 1),
        in_specs=[pl.BlockSpec(memory_space=VMEM)] * (1 + len(got)),
        out_specs=[pl.BlockSpec(memory_space=VMEM)] * reps,
        compiler_params=params(10),
        name="plane_sum",
    )(own, *got)


def full_sum(value):
    return jnp.sum(jnp.sum(value, axis=1, keepdims=True), axis=0, keepdims=True)


def turned(columns):
    rows, count = columns.shape
    same = lax.broadcasted_iota(jnp.int32, (rows, rows), 0) == lax.broadcasted_iota(jnp.int32, (rows, rows), 1)
    line = lax.broadcasted_iota(jnp.int32, (count, rows), 0)
    out = jnp.zeros((count, rows), jnp.float32)
    for j in range(count):
        row = jnp.sum(jnp.where(same, columns[:, j : j + 1], 0.0), axis=0, keepdims=True)
        out = jnp.where(line == j, row, out)
    return out


def moments_kernel(pieces_of, first_index, reps, more, *refs):
    n = len(pieces_of)
    grads, others, arrays = refs[:reps], refs[reps : reps + more], refs[reps + more :]
    total = grads[0][...]
    for ref in grads[1:]:
        total = total + ref[...].astype(jnp.float32)
    weights, firsts, seconds = arrays[:n], arrays[n : 2 * n], arrays[2 * n : 3 * n]
    momenta, variances, directions = arrays[3 * n : 4 * n], arrays[4 * n : 5 * n], arrays[5 * n : 6 * n]
    sums = arrays[6 * n]
    lane = lax.broadcasted_iota(jnp.int32, (1, LANES), 1)
    row = others[0][0] if more else jnp.zeros((1, LANES), jnp.float32)
    for i, parts in enumerate(pieces_of):
        weight_sum = jnp.zeros((1, 1), jnp.float32)
        step_sum = jnp.zeros((1, 1), jnp.float32)
        for at, size, columns in parts:
            rows = slice(at, at + size)
            gradient = total[:, columns[0] : columns[1]]
            if len(columns) > 2:
                gradient = turned(gradient)
            weight = weights[i][rows]
            momentum = BETA * firsts[i][rows] + (1.0 - BETA) * gradient
            variance = BETA * seconds[i][rows] + (1.0 - BETA) * gradient * gradient
            direction = momentum / (jnp.sqrt(variance) + ADAM_EPSILON) + DECAY * weight
            momenta[i][rows] = momentum
            variances[i][rows] = variance
            directions[i][rows] = direction
            weight_sum = weight_sum + full_sum(weight * weight)
            step_sum = step_sum + full_sum(direction * direction)
        row = jnp.where(lane == first_index[i], weight_sum, row)
        row = jnp.where(lane == 5 + first_index[i], step_sum, row)
    sums[...] = jnp.broadcast_to(row, sums.shape)


def moments(pieces_of, first_index, grads, others, copies, weights, firsts, seconds):
    arrays = [*grads, *others, *weights, *firsts, *seconds]
    shapes = [jax.ShapeDtypeStruct(weight.shape, jnp.float32) for weight in weights]
    outs = pl.pallas_call(
        partial(moments_kernel, pieces_of, first_index, len(grads), len(others)),
        out_shape=shapes * 3 + [jax.ShapeDtypeStruct((copies, 1, LANES), jnp.float32)],
        in_specs=[pl.BlockSpec(memory_space=VMEM)] * len(arrays),
        out_specs=[pl.BlockSpec(memory_space=VMEM)] * (3 * len(weights) + 1),
        compiler_params=params(8),
        name="moments",
    )(*arrays)
    n = len(weights)
    return outs[:n], outs[n : 2 * n], outs[2 * n : 3 * n], outs[3 * n]


def update_kernel(n, sums, *refs):
    weights, directions, updated, table = refs[:n], refs[n : 2 * n], refs[2 * n : 3 * n], refs[3 * n]
    norms = jnp.sqrt(jnp.sum(sums[...], axis=0))
    row = lax.broadcasted_iota(jnp.int32, table.shape, 0)
    lane = lax.broadcasted_iota(jnp.int32, table.shape, 1)
    out = jnp.zeros(table.shape, jnp.float32)
    for i in range(n):
        weight_norm = norms[:, i : i + 1]
        step_norm = norms[:, 5 + i : 6 + i]
        ratio = weight_norm / step_norm
        updated[i][...] = weights[i][...] - RATE * ratio * directions[i][...]
        column = jnp.where(row == 0, weight_norm, jnp.where(row == 1, step_norm, ratio))
        out = jnp.where(lane == i, column, out)
    table[...] = out


def update(sums, weights, directions):
    n = len(weights)
    outs = pl.pallas_call(
        partial(update_kernel, n),
        out_shape=[jax.ShapeDtypeStruct(weight.shape, jnp.float32) for weight in weights]
        + [jax.ShapeDtypeStruct((3, n), jnp.float32)],
        in_specs=[pl.BlockSpec(memory_space=VMEM)] * (1 + 2 * n),
        out_specs=[pl.BlockSpec(memory_space=VMEM)] * (n + 1),
        compiler_params=params(6),
        name="update",
    )(sums, *weights, *directions)
    return outs[:n], outs[n]


def over(lay, value, first):
    return [value] + [lay.over(value, i, first) for i in range(1, lay.rep if first else lay.plane)]


def send_over(lay, parts, first):
    return [lay.over(part, i, first) for i, part in enumerate(parts, 1)]


def over_core(lay, blocks):
    return blocks + [lay.to_core(block) for block in blocks]


def after(values, others):
    count = len(values)
    return list(lax.optimization_barrier((*values, *others))[:count])


def exchange(lay, value):
    return lax.all_to_all(value, AXES, 0, 0)


def body(
    lay,
    inputs,
    segments,
    cotangent,
    attend_in,
    attend_out,
    expand,
    contract,
    layer_norms,
    moment_in,
    moment_out,
    moment_expand,
    moment_contract,
    moment_norms,
    square_in,
    square_out,
    square_expand,
    square_contract,
    square_norms,
):
    plain, twin = lay
    lay = plain
    masters = (attend_in, attend_out, expand, contract, layer_norms)
    width = attend_in.shape[1]
    depth = attend_out.shape[1]
    hidden = expand.shape[1]
    own = attend_in.shape[0]
    count = lay.dp * lay.rep
    whole_tiles = own % 16 == 0
    shard1, shard2 = pack(layer_norms, attend_in, attend_out, expand, contract)
    column1 = over(plain, shard1, True)
    rows = inputs.shape[1]
    (shard2,) = after([shard2], column1[1:])
    column2 = over(twin, shard2, True)
    blocks1 = over(plain, column_of(plain, column1), False)
    (segments_,) = after([segments], blocks1[:1])
    x, dy, labels, begin = arrange(inputs[0], cotangent[0], segments_)
    blocks2 = over(twin, column_of(twin, after(column2, [*blocks1, x])), False)
    pieces1 = over_core(lay, blocks1)
    *pieces1, x, labels = after([*pieces1, x, labels], blocks2[:1])
    qx, kx, vx, mixed, gains = attend(plain, x, labels, pieces1)
    near = lay.to_core(blocks2[0])
    blocks2[1:] = after(blocks2[1:], [mixed])
    pieces2 = [*blocks2, near, *[lay.to_core(block) for block in blocks2[1:]]]
    deep_pieces = []
    if not whole_tiles:
        first = depth + hidden
        for piece in pieces2:
            part = piece[:, first:].reshape(lay.rep, own, 4, depth).transpose(0, 2, 1, 3)
            deep_pieces.append(part.reshape(-1, depth))
    middle, middle_grad, middle_low, active, contract_all, out_weight, keep2, send2, second_norms, *deep_out = feed(
        twin, x, mixed, dy, gains, pieces2, deep_pieces
    )
    if not whole_tiles:
        keep2, send2 = [
            jnp.concatenate(
                [
                    wide[:, :, : depth + hidden],
                    part.reshape(lay.plane, lay.rep, 4, own, depth).transpose(0, 1, 3, 2, 4).reshape(lay.plane, -1, 4 * depth),
                ],
                axis=2,
            )
            for wide, part in zip((keep2, send2), deep_out)
        ]
    chip2 = lay.to_core(send2)
    dox = mixed_back(middle_low, mixed, out_weight)
    keep2, chip2 = after([keep2, chip2], [dox])
    own2, *low2 = chip_sum(twin, keep2, chip2)
    got2 = send_over(twin, low2, False)
    (dox,) = after([dox], low2)
    packed = attend_back(qx, kx, vx, dox)
    input_gradient, first_norms = input_back(plain, x, packed, gains, middle_grad, pieces1)
    keep1, send1 = project_back(plain, x, packed, gains, first_norms, second_norms, own)
    own2, send1, *got2 = after([own2, send1, *got2], [])
    own2, *low2 = plane_sum(twin, own2, got2)
    got2 = send_over(twin, low2, True)
    own1, *low1 = chip_sum(plain, keep1, lay.to_core(send1))
    got1 = send_over(plain, low1, False)
    (middle,) = after([middle], low1)
    outputs, input_gradient = finish(begin, middle, active, contract_all, input_gradient, rows)
    own1, *got1 = after([own1, *got1], [outputs])
    spans = [[(0, own, (0, depth))], [(0, own, (depth, depth + hidden))]]
    spans.append([(j * own, own, (depth + hidden + j * depth, depth + hidden + (j + 1) * depth)) for j in range(4)])
    momenta2, variances2, directions2, sums2 = moments(
        spans, (1, 2, 3), [own2, *got2], [], 1, masters[1:4],
        (moment_out, moment_expand, moment_contract), (square_out, square_expand, square_contract),
    )
    own1, *low1 = plane_sum(plain, own1, got1)
    got1 = send_over(plain, low1, True)
    momenta1, variances1, directions1, sums1 = moments(
        [[(0, own, (0, width))], [(0, 4, (width, width + 4, True))]], (0, 4), [own1, *got1], [sums2], count, (attend_in, layer_norms),
        (moment_in, moment_norms), (square_in, square_norms),
    )
    sums = exchange(lay, sums1)
    directions = (directions1[0], *directions2, directions1[1])
    updated, trust_table = update(sums, masters, directions)
    momenta = (momenta1[0], *momenta2, momenta1[1])
    variances = (variances1[0], *variances2, variances1[1])
    return (outputs[None], input_gradient[None], *updated, *momenta, *variances, trust_table)


def solution(mesh):
    placed = (
        P(("dp", "rep"), None, None),
        P(("dp", "rep"), None),
        P(("dp", "rep"), None, None),
        P(("dp", "rep"), None),
        P(("dp", "rep"), None),
        P(("dp", "rep"), None),
        P(("dp", "rep"), None),
        P(None, ("dp", "rep")),
        P(("dp", "rep"), None),
        P(("dp", "rep"), None),
        P(("dp", "rep"), None),
        P(("dp", "rep"), None),
        P(None, ("dp", "rep")),
        P(("dp", "rep"), None),
        P(("dp", "rep"), None),
        P(("dp", "rep"), None),
        P(("dp", "rep"), None),
        P(None, ("dp", "rep")),
    )
    return jax.shard_map(
        partial(body, (Layout(mesh, False), Layout(mesh, True))),
        mesh=mesh,
        in_specs=placed,
        out_specs=(
            P(("dp", "rep"), None, None),
            P(("dp", "rep"), None, None),
            P(("dp", "rep"), None),
            P(("dp", "rep"), None),
            P(("dp", "rep"), None),
            P(("dp", "rep"), None),
            P(None, ("dp", "rep")),
            P(("dp", "rep"), None),
            P(("dp", "rep"), None),
            P(("dp", "rep"), None),
            P(("dp", "rep"), None),
            P(None, ("dp", "rep")),
            P(("dp", "rep"), None),
            P(("dp", "rep"), None),
            P(("dp", "rep"), None),
            P(("dp", "rep"), None),
            P(None, ("dp", "rep")),
            P(),
        ),
        check_vma=False,
    )
```

```python
from functools import partial
import math

import jax
import jax.numpy as jnp
from jax import lax
from jax.experimental import pallas as pl
from jax.experimental.pallas import tpu as pltpu
from jax.sharding import PartitionSpec as P

HEADS = 8
HEAD_DIM = 64


EPSILON = 1e-05
ADAM_EPSILON = 1e-06
DECAY = 0.01
RATE = 0.5
BETA = 0.5
LANES = 128
HALF = 64
BIG = 1e30
FEATS = 4
TILE = 256
THIN = 32
CHUNK = 352
DEEP_CHUNK = 528
GELU_ONE = 0.7978845608028654
GELU_CUBE = 0.044715 * GELU_ONE
VMEM = pltpu.MemorySpace.VMEM
AXES = ("dp", "rep")


def params(mebibytes):
    return pltpu.CompilerParams(vmem_limit_bytes=mebibytes * 1024 * 1024)


def dot(a, b, ca, cb):
    return lax.dot_general(a, b, (((ca,), (cb,)), ((), ())), preferred_element_type=jnp.float32)


def normalize(values):
    center = values - jnp.mean(values, axis=-1, keepdims=True)
    scale = lax.rsqrt(jnp.mean(center * center, axis=-1, keepdims=True) + EPSILON)
    return center * scale, scale


class Layout:
    def __init__(self, mesh, mixed):
        self.dp = mesh.shape["dp"]
        self.rep = mesh.shape["rep"]
        self.plane = self.dp // 2
        self.mixed = mixed and self.plane == self.rep

    def pairs(self, move):
        pairs = []
        for p in range(self.plane):
            for c in range(2):
                for z in range(self.rep):
                    q, d, w = move(p, c, z)
                    pairs.append(((p * 2 + c) * self.rep + z, (q * 2 + d) * self.rep + w))
        return pairs

    def over(self, value, i, first):
        def move(p, c, z):
            along_z = (first == (c == 0)) if self.mixed else first
            return (p, c, (z + i) % self.rep) if along_z else (p ^ i, c, z)

        return lax.ppermute(value, AXES, self.pairs(move))

    def to_core(self, value):
        return lax.ppermute(value, AXES, self.pairs(lambda p, c, z: (p, 1 - c, z)))

    def core(self):
        return lax.rem(lax.axis_index("dp"), 2)

    def partner(self, side, i, first, sign):
        along_z = lax.rem(lax.axis_index("rep") + (sign * i) % self.rep, self.rep)
        in_plane = lax.div(lax.axis_index("dp"), 2) ^ i
        if not self.mixed:
            return along_z if first else in_plane
        return jnp.where(side == 0, along_z, in_plane) if first else jnp.where(side == 0, in_plane, along_z)

    def device(self, side, second, first):
        plain = (2 * second + side) * self.rep + first
        return jnp.where(side == 0, plain, (2 * first + side) * self.rep + second) if self.mixed else plain


def row_blocks(lay, side, second, rows):
    firsts = lay.rep
    if lay.mixed:
        return [(j * rows, pl.multiple_of(lay.device(side, second, j) * rows, rows), rows) for j in range(firsts)]
    return [(0, pl.multiple_of(lay.device(side, second, 0) * rows, firsts * rows), firsts * rows)]


def assemble(lay, pieces, full_ref, columns):
    count = len(pieces) // 2
    for i, piece in enumerate(pieces):
        side = lay.core() if i < count else 1 - lay.core()
        second = lay.partner(side, i % count, False, -1)
        for at, to, rows in row_blocks(lay, side, second, piece.shape[0] // lay.rep):
            full_ref[pl.ds(to, rows), :] = piece[at : at + rows, columns]


def assemble_deep(lay, pieces, full_ref, first):
    count = len(pieces) // 2
    width = full_ref.shape[1]
    for i, piece in enumerate(pieces):
        side = lay.core() if i < count else 1 - lay.core()
        second = lay.partner(side, i % count, False, -1)
        rows = piece.shape[0] // lay.rep
        for z in range(lay.rep):
            to = pl.multiple_of(lay.device(side, second, z) * 4 * rows, 4 * rows)
            for j in range(4):
                source = piece[z * rows : (z + 1) * rows, first + j * width : first + (j + 1) * width]
                full_ref[pl.ds(to + j * rows, rows), :] = source


def split_rows(lay, full_ref, keep_ref, send_ref, lanes):
    for target, side in ((keep_ref, lay.core()), (send_ref, 1 - lay.core())):
        for second in range(target.shape[0]):
            for at, source, rows in row_blocks(lay, side, second, target.shape[1] // lay.rep):
                target[second, at : at + rows, lanes] = full_ref[pl.ds(source, rows), :].astype(target.dtype)


def split_deep(lay, full_ref, keep_ref, send_ref, first):
    width = full_ref.shape[1]
    rows = keep_ref.shape[1] // lay.rep
    for target, side in ((keep_ref, lay.core()), (send_ref, 1 - lay.core())):
        for second in range(target.shape[0]):
            for z in range(lay.rep):
                source = pl.multiple_of(lay.device(side, second, z) * 4 * rows, 4 * rows)
                for j in range(4):
                    part = full_ref[pl.ds(source + j * rows, rows), :]
                    columns = slice(first + j * width, first + (j + 1) * width)
                    target[second, z * rows : (z + 1) * rows, columns] = part.astype(target.dtype)


def row_chunks(rows, size):
    return [(at, min(size, rows - at)) for at in range(0, rows, size)]


def windows(rows):
    half = (rows - THIN) // 2
    span = half + THIN
    spans = [(at, TILE, 0, span) for at in range(0, half, TILE)]
    spans.append((half, THIN, 0, rows))
    return spans + [(at, TILE, half, span) for at in range(span, rows, TILE)]


def arrange_kernel(inputs, cotangent, segments, x, dy, labels, begin, room):
    tokens = segments.shape[1]
    half = tokens // 2
    memory = inputs.shape[0] - tokens
    segment = segments[...].astype(jnp.float32)
    ahead = pltpu.roll(jnp.broadcast_to(segment, (8, tokens)), tokens - half + 1, 1)[:1]
    lane = lax.broadcasted_iota(jnp.int32, (1, tokens), 1)
    fits = (segment == ahead) & (lane <= half)
    start = jnp.sum(jnp.where(fits, lane.astype(jnp.float32), 0.0), axis=1, keepdims=True)
    begin[...] = jnp.broadcast_to(start, begin.shape)
    row = lax.broadcasted_iota(jnp.int32, (half, LANES), 0).astype(jnp.float32)
    early = row < start
    thin = lax.broadcasted_iota(jnp.int32, (THIN, LANES), 0) < memory
    for source, target in ((inputs, x), (cotangent, dy)):
        for at in range(0, inputs.shape[1], LANES):
            columns = slice(at, at + LANES)
            room[: inputs.shape[0]] = source[:, columns].astype(jnp.float32)
            left, right = room[memory : memory + half], room[memory + half : memory + tokens]
            target[:half, columns] = jnp.where(early, right, left).astype(target.dtype)
            target[half : half + THIN, columns] = jnp.where(thin, room[:THIN], 0.0).astype(target.dtype)
            target[half + THIN :, columns] = jnp.where(early, left, right).astype(target.dtype)
    left = jnp.transpose(jnp.broadcast_to(segment[:, :half], (LANES, half)))
    right = jnp.transpose(jnp.broadcast_to(segment[:, half:], (LANES, half)))
    labels[:half] = jnp.where(early, right, left).astype(jnp.int32)
    labels[half : half + THIN] = jnp.where(thin, -1, -2)
    labels[half + THIN :] = jnp.where(early, left, right).astype(jnp.int32)


def arrange(inputs, cotangent, segments):
    width = inputs.shape[1]
    rows = segments.shape[1] + THIN
    return pl.pallas_call(
        arrange_kernel,
        out_shape=(
            jax.ShapeDtypeStruct((rows, width), inputs.dtype),
            jax.ShapeDtypeStruct((rows, width), inputs.dtype),
            jax.ShapeDtypeStruct((rows, LANES), jnp.int32),
            jax.ShapeDtypeStruct((8, LANES), jnp.float32),
        ),
        in_specs=[pl.BlockSpec(memory_space=VMEM)] * 3,
        out_specs=[pl.BlockSpec(memory_space=VMEM)] * 4,
        scratch_shapes=[pltpu.VMEM((rows, LANES), jnp.float32)],
        compiler_params=params(8),
        name="arrange",
    )(inputs, cotangent, segments)


def finish_kernel(begin, middle, active, contract, grad_in, outputs, grad_out, room):
    rows = outputs.shape[0]
    half = (middle.shape[0] - THIN) // 2
    memory = rows - 2 * half
    wide = room.shape[1]
    row = lax.broadcasted_iota(jnp.int32, (half, wide), 0).astype(jnp.float32)
    early = row < begin[:1, :1]

    def place(value, target, columns):
        left, right = value[:half], value[half + THIN :]
        room[:THIN] = value[half : half + THIN]
        room[memory : memory + half] = jnp.where(early, right, left)
        room[memory + half : rows] = jnp.where(early, left, right)
        target[:, columns] = room[:rows].astype(target.dtype)

    for at in range(0, middle.shape[1], wide):
        columns = slice(at, at + wide)
        place(middle[:, columns] + dot(active[...], contract[:, columns], 1, 0), outputs, columns)
        place(grad_in[:, columns].astype(jnp.float32), grad_out, columns)


def finish(begin, middle, active, contract, grad_in, rows):
    width = middle.shape[1]
    return pl.pallas_call(
        finish_kernel,
        out_shape=[jax.ShapeDtypeStruct((rows, width), grad_in.dtype)] * 2,
        in_specs=[pl.BlockSpec(memory_space=VMEM)] * 5,
        out_specs=[pl.BlockSpec(memory_space=VMEM)] * 2,
        scratch_shapes=[pltpu.VMEM((middle.shape[0], 256), jnp.float32)],
        compiler_params=params(10),
        name="finish",
    )(begin, middle, active, contract, grad_in)


def attend_kernel(lay, count, x, labels, *refs):
    pieces = refs[:count]
    qx, kx, vx, mixed, gains, weight, qs = refs[count:]
    rows = x.shape[0]
    width = mixed.shape[1]
    assemble(lay, pieces, weight, slice(None))
    gains[...] = jnp.transpose(weight[:, 3 * width :].astype(jnp.float32))[:8]
    gain, bias = gains[0:1], gains[1:2]

    def one_chunk(i, carry):
        span = pl.ds(pl.multiple_of(i * CHUNK, CHUNK), CHUNK)
        normed, _ = normalize(x[span].astype(jnp.float32))
        first = (normed * gain + bias).astype(jnp.bfloat16)
        lane = lax.broadcasted_iota(jnp.int32, (CHUNK, LANES), 1)
        low = lane < HALF
        feature = lane % HALF
        label = labels[span]
        blocked = ((feature < FEATS) & (label >= 0) & (feature != label)) | (feature == FEATS)
        query_side = jnp.where(blocked, -BIG, 0.0)
        marked = ((feature < FEATS) & (feature == label)) | ((feature == FEATS) & (label == -2))
        key_side = jnp.where(marked | (feature > FEATS), 1.0, 0.0)
        sides = (query_side, key_side, jnp.ones_like(key_side))
        for kind, target in enumerate((qs, kx, vx)):
            whole = dot(first, weight[:, kind * width : (kind + 1) * width], 1, 0)
            whole = whole.astype(jnp.bfloat16).astype(jnp.float32)
            for pair in range(width // LANES):
                part = whole[:, pair * LANES : (pair + 1) * LANES]
                if kind == 0:
                    part = part * (1.0 / math.sqrt(HEAD_DIM))
                at = 2 * pair * LANES
                target[span, at : at + LANES] = jnp.where(low, part, sides[kind]).astype(jnp.bfloat16)
                target[span, at + LANES : at + 2 * LANES] = jnp.where(low, sides[kind], part).astype(jnp.bfloat16)
        return carry

    lax.fori_loop(0, rows // CHUNK, one_chunk, 0)

    def one_pair(pair, carry):
        columns = pl.ds(pl.multiple_of(pair * LANES, LANES), LANES)
        for at, size, key_at, key_size in windows(rows):
            span = pl.ds(at, size)
            seen = pl.ds(key_at, key_size)
            lane = lax.broadcasted_iota(jnp.int32, (size, LANES), 1)
            low = lane < HALF
            feature = lane % HALF
            got = []
            for side in range(2):
                head = pl.ds(pl.multiple_of((2 * pair + side) * LANES, LANES), LANES)
                queries = qs[span, head]
                scores = dot(queries, kx[seen, head], 1, 1)
                highest = jnp.max(scores, axis=1, keepdims=True)
                raised = jnp.exp(scores - highest).astype(jnp.bfloat16)
                found = dot(raised, vx[seen, head], 1, 0)
                total = -(highest + jnp.log(found))
                first = total.astype(jnp.bfloat16).astype(jnp.float32)
                second = (total - first).astype(jnp.bfloat16).astype(jnp.float32)
                third = total - first - second
                values = jnp.where(feature == 5, first, jnp.where(feature == 6, second, third))
                place = (feature > FEATS) & (feature < 8) & (low if side else ~low)
                qx[span, head] = jnp.where(place, values, queries.astype(jnp.float32)).astype(jnp.bfloat16)
                got.append(found)
            over = pltpu.roll(jnp.where(low, got[1], got[0]), HALF, 1)
            mixed[span, columns] = (jnp.where(low, got[0], got[1]) / over).astype(jnp.bfloat16)
        return carry

    lax.fori_loop(0, width // LANES, one_pair, 0)


def attend(lay, x, labels, pieces):
    rows, width = x.shape
    wide = jax.ShapeDtypeStruct((rows, 2 * width), jnp.bfloat16)
    depth = len(pieces) * pieces[0].shape[0]
    return pl.pallas_call(
        partial(attend_kernel, lay, len(pieces)),
        out_shape=(
            wide,
            wide,
            wide,
            jax.ShapeDtypeStruct((rows, width), jnp.bfloat16),
            jax.ShapeDtypeStruct((8, width), jnp.float32),
        ),
        in_specs=[pl.BlockSpec(memory_space=VMEM)] * (2 + len(pieces)),
        out_specs=[pl.BlockSpec(memory_space=VMEM)] * 5,
        scratch_shapes=[
            pltpu.VMEM((depth, pieces[0].shape[1]), jnp.bfloat16),
            pltpu.VMEM((rows, 2 * width), jnp.bfloat16),
        ],
        compiler_params=params(16),
        name="attend",
    )(x, labels, *pieces)


def attend_back_kernel(qx, kx, vx, dox, packed, total):
    rows = qx.shape[0]
    width = packed.shape[1] // 3

    def one_pair(pair, carry):
        heads = [pl.ds(pl.multiple_of((2 * pair + side) * LANES, LANES), LANES) for side in range(2)]
        spots = [pl.ds(pl.multiple_of(kind * width + pair * LANES, LANES), LANES) for kind in range(3)]
        total[...] = jnp.zeros_like(total)
        for at, size, query_at, query_size in windows(rows):
            span = pl.ds(at, size)
            seen = pl.ds(query_at, query_size)
            low = lax.broadcasted_iota(jnp.int32, (size, LANES), 1) < HALF
            got = []
            for side in range(2):
                head = heads[side]
                keys = kx[span, head]
                queries = qx[seen, head]
                upstream = dox[seen, head]
                attention = jnp.exp(dot(keys, queries, 1, 1))
                grad = dot(vx[span, head], upstream, 1, 1)
                scores = (attention * grad).astype(jnp.bfloat16)
                got.append((dot(scores, queries, 1, 0), dot(attention.astype(jnp.bfloat16), upstream, 1, 0)))
                total[side, seen] += dot(scores, keys, 0, 0)
            packed[span, spots[1]] = jnp.where(low, got[0][0], got[1][0]).astype(jnp.bfloat16)
            packed[span, spots[2]] = jnp.where(low, got[0][1], got[1][1]).astype(jnp.bfloat16)
        low = lax.broadcasted_iota(jnp.int32, (rows, LANES), 1) < HALF
        packed[:, spots[0]] = (jnp.where(low, total[0], total[1]) * (1.0 / math.sqrt(HEAD_DIM))).astype(jnp.bfloat16)
        return carry

    lax.fori_loop(0, width // LANES, one_pair, 0)


def attend_back(qx, kx, vx, dox):
    rows, wide = qx.shape
    return pl.pallas_call(
        attend_back_kernel,
        out_shape=jax.ShapeDtypeStruct((rows, 3 * wide // 2), jnp.bfloat16),
        in_specs=[pl.BlockSpec(memory_space=VMEM)] * 4,
        out_specs=pl.BlockSpec(memory_space=VMEM),
        scratch_shapes=[pltpu.VMEM((2, rows, LANES), jnp.float32)],
        compiler_params=params(16),
        name="attend_back",
    )(qx, kx, vx, dox)


def norm_back(grad, normed, scale, gain):
    scaled = grad * gain
    return scale * (
        scaled
        - jnp.mean(scaled, axis=-1, keepdims=True)
        - normed * jnp.mean(scaled * normed, axis=-1, keepdims=True)
    )


def feed_kernel(lay, count, deep_count, x, mixed, dy, gains, *refs):
    pieces = refs[:count]
    deep_pieces = refs[count : count + deep_count]
    outs = refs[count + deep_count : -5]
    middle, middle_grad, middle_low, active, contract, out_weight, keep2, send2, norm_grads, *deep_out = outs
    wide, hidden_grad, second, block, deep_block = refs[-5:]
    rows, width = x.shape
    hidden = contract.shape[0]
    assemble(lay, pieces, wide, slice(0, width + hidden))
    if deep_count:
        assemble(lay, deep_pieces, contract, slice(None))
    else:
        assemble_deep(lay, pieces, contract, width + hidden)
    out_weight[...] = wide[:, :width]
    gain, bias = gains[2:3], gains[3:4]
    zero = jnp.zeros((1, width), jnp.float32)

    def one_chunk(i, carry):
        gain_sum, bias_sum = carry
        span = pl.ds(pl.multiple_of(i * DEEP_CHUNK, DEEP_CHUNK), DEEP_CHUNK)
        start = x[span].astype(jnp.float32) + dot(mixed[span], wide[:, :width], 1, 0)
        middle[span] = start
        normed, scale = normalize(start)
        low = (normed * gain + bias).astype(jnp.bfloat16)
        second[span] = low
        for start in range(0, hidden, 512):
            part = slice(start, start + 512)
            up = dot(low, wide[:, width + start : width + start + 512], 1, 0)
            square = up * up
            half = 0.5 + 0.5 * jnp.tanh(up * (GELU_ONE + GELU_CUBE * square))
            act = up * half
            active[span, part] = act.astype(jnp.bfloat16)
            slope = half + act * ((1.0 - half) * (2.0 * GELU_ONE + 6.0 * GELU_CUBE * square))
            hidden_grad[span, part] = (dot(dy[span], contract[part], 1, 1) * slope).astype(jnp.bfloat16)
        back = dot(hidden_grad[span], wide[:, width:], 1, 1)
        gain_sum = gain_sum + jnp.sum(back * normed, axis=0, keepdims=True)
        bias_sum = bias_sum + jnp.sum(back, axis=0, keepdims=True)
        grad = dy[span].astype(jnp.float32) + norm_back(back, normed, scale, gain)
        middle_grad[span] = grad
        middle_low[span] = grad.astype(jnp.bfloat16)
        return gain_sum, bias_sum

    gain_sum, bias_sum = lax.fori_loop(0, rows // DEEP_CHUNK, one_chunk, (zero, zero))
    norm_grads[...] = jnp.concatenate([gain_sum, bias_sum, jnp.zeros((6, width), jnp.float32)], axis=0)

    def one_block(i, carry):
        columns = pl.ds(pl.multiple_of(i * 512, 512), 512)
        deep_block[columns] = dot(active[:, columns], dy[...], 0, 0)
        block[...] = dot(second[...], hidden_grad[:, columns], 0, 0)
        split_rows(lay, block, keep2, send2, pl.ds(pl.multiple_of(width + i * 512, 512), 512))
        return carry

    lax.fori_loop(0, hidden // 512, one_block, 0)
    if deep_count:
        split_rows(lay, deep_block, *deep_out, slice(0, width))
    else:
        split_deep(lay, deep_block, keep2, send2, width + hidden)
    block[...] = dot(mixed[...], middle_low[...], 0, 0)
    split_rows(lay, block, keep2, send2, slice(0, width))


def feed(lay, x, mixed, dy, gains, pieces, deep_pieces):
    rows, width = x.shape
    plane = len(pieces) // 2
    deep = pieces[0].shape[0]
    columns = pieces[0].shape[1]
    hidden = 4 * width
    out_shape = [
        jax.ShapeDtypeStruct((rows, width), jnp.float32),
        jax.ShapeDtypeStruct((rows, width), jnp.float32),
        jax.ShapeDtypeStruct((rows, width), jnp.bfloat16),
        jax.ShapeDtypeStruct((rows, hidden), jnp.bfloat16),
        jax.ShapeDtypeStruct((hidden, width), jnp.bfloat16),
        jax.ShapeDtypeStruct((width, width), jnp.bfloat16),
        jax.ShapeDtypeStruct((plane, deep, columns), jnp.bfloat16),
        jax.ShapeDtypeStruct((plane, deep, columns), jnp.bfloat16),
        jax.ShapeDtypeStruct((8, width), jnp.float32),
    ]
    if deep_pieces:
        out_shape.append(jax.ShapeDtypeStruct((plane, 4 * deep, width), jnp.bfloat16))
        out_shape.append(jax.ShapeDtypeStruct((plane, 4 * deep, width), jnp.bfloat16))
    return pl.pallas_call(
        partial(feed_kernel, lay, len(pieces), len(deep_pieces)),
        out_shape=out_shape,
        in_specs=[pl.BlockSpec(memory_space=VMEM)] * (4 + len(pieces) + len(deep_pieces)),
        out_specs=[pl.BlockSpec(memory_space=VMEM)] * len(out_shape),
        scratch_shapes=[
            pltpu.VMEM((width, width + hidden), jnp.bfloat16),
            pltpu.VMEM((rows, hidden), jnp.bfloat16),
            pltpu.VMEM((rows, width), jnp.bfloat16),
            pltpu.VMEM((width, 512), jnp.float32),
            pltpu.VMEM((hidden, width), jnp.float32),
        ],
        compiler_params=params(26),
        name="feed",
    )(x, mixed, dy, gains, *pieces, *deep_pieces)


def mixed_back_kernel(middle_low, mixed, out_weight, dox):
    rows, width = mixed.shape

    def one_chunk(i, carry):
        span = pl.ds(pl.multiple_of(i * DEEP_CHUNK, DEEP_CHUNK), DEEP_CHUNK)
        mixed_grad = dot(middle_low[span], out_weight[...], 1, 1).astype(jnp.bfloat16).astype(jnp.float32)
        lane = lax.broadcasted_iota(jnp.int32, (DEEP_CHUNK, LANES), 1)
        left = lane < HALF
        feature = lane % HALF
        for pair in range(width // LANES):
            columns = slice(pair * LANES, (pair + 1) * LANES)
            piece = mixed_grad[:, columns]
            product = piece * mixed[span, columns].astype(jnp.float32)
            for side in range(2):
                mine = left if side == 0 else ~left
                delta = -jnp.sum(jnp.where(mine, product, 0.0), axis=1, keepdims=True)
                one = delta.astype(jnp.bfloat16).astype(jnp.float32)
                two = (delta - one).astype(jnp.bfloat16).astype(jnp.float32)
                three = delta - one - two
                extra = jnp.where(feature == 0, one, jnp.where(feature == 1, two, jnp.where(feature == 2, three, 0.0)))
                head = (2 * pair + side) * LANES
                dox[span, head : head + LANES] = jnp.where(mine, piece, extra).astype(jnp.bfloat16)
        return carry

    lax.fori_loop(0, rows // DEEP_CHUNK, one_chunk, 0)


def mixed_back(middle_low, mixed, out_weight):
    rows, width = mixed.shape
    return pl.pallas_call(
        mixed_back_kernel,
        out_shape=jax.ShapeDtypeStruct((rows, 2 * width), jnp.bfloat16),
        in_specs=[pl.BlockSpec(memory_space=VMEM)] * 3,
        out_specs=pl.BlockSpec(memory_space=VMEM),
        compiler_params=params(10),
        name="mixed_back",
    )(middle_low, mixed, out_weight)


def project_back_kernel(lay, x, packed, gains, first_norms, second_norms, keep, send, first, block):
    rows, width = x.shape
    gain, bias = gains[0:1], gains[1:2]

    def one_chunk(i, carry):
        span = pl.ds(pl.multiple_of(i * CHUNK, CHUNK), CHUNK)
        normed, _ = normalize(x[span].astype(jnp.float32))
        first[span] = (normed * gain + bias).astype(jnp.bfloat16)
        return carry

    lax.fori_loop(0, rows // CHUNK, one_chunk, 0)

    def one_block(i, carry):
        columns = pl.ds(pl.multiple_of(i * 512, 512), 512)
        block[...] = dot(first[...], packed[:, columns], 0, 0)
        split_rows(lay, block, keep, send, columns)
        return carry

    lax.fori_loop(0, packed.shape[1] // 512, one_block, 0)
    fill = jnp.zeros((LANES - 4, width), jnp.float32)
    norms = jnp.concatenate([first_norms[:2], second_norms[:2], fill], axis=0)
    block[:, :LANES] = jnp.transpose(norms)
    split_rows(lay, block.at[:, :LANES], keep, send, slice(packed.shape[1], packed.shape[1] + LANES))


def project_back(lay, x, packed, gains, first_norms, second_norms, own):
    rows, width = x.shape
    shape = (lay.plane, lay.rep * own, packed.shape[1] + LANES)
    return pl.pallas_call(
        partial(project_back_kernel, lay),
        out_shape=(jax.ShapeDtypeStruct(shape, jnp.bfloat16), jax.ShapeDtypeStruct(shape, jnp.bfloat16)),
        in_specs=[pl.BlockSpec(memory_space=VMEM)] * 5,
        out_specs=[pl.BlockSpec(memory_space=VMEM)] * 2,
        scratch_shapes=[pltpu.VMEM((rows, width), jnp.bfloat16), pltpu.VMEM((width, 512), jnp.float32)],
        compiler_params=params(10),
        name="project_back",
    )(x, packed, gains, first_norms, second_norms)


def input_back_kernel(lay, x, packed, gains, middle_grad, *refs):
    pieces = refs[:-3]
    grad_in, norm_grads, weight = refs[-3:]
    rows, width = x.shape
    assemble(lay, pieces, weight, slice(None))
    gain = gains[0:1]
    zero = jnp.zeros((1, width), jnp.float32)

    def one_chunk(i, carry):
        gain_sum, bias_sum = carry
        span = pl.ds(pl.multiple_of(i * CHUNK, CHUNK), CHUNK)
        normed, scale = normalize(x[span].astype(jnp.float32))
        back = dot(packed[span], weight[:, : 3 * width], 1, 1)
        grad_in[span] = (middle_grad[span] + norm_back(back, normed, scale, gain)).astype(jnp.bfloat16)
        gain_sum = gain_sum + jnp.sum(back * normed, axis=0, keepdims=True)
        return gain_sum, bias_sum + jnp.sum(back, axis=0, keepdims=True)

    gain_sum, bias_sum = lax.fori_loop(0, rows // CHUNK, one_chunk, (zero, zero))
    norm_grads[...] = jnp.concatenate([gain_sum, bias_sum, jnp.zeros((6, width), jnp.float32)], axis=0)


def input_back(lay, x, packed, gains, middle_grad, pieces):
    rows, width = x.shape
    return pl.pallas_call(
        partial(input_back_kernel, lay),
        out_shape=(jax.ShapeDtypeStruct((rows, width), jnp.bfloat16), jax.ShapeDtypeStruct((8, width), jnp.float32)),
        in_specs=[pl.BlockSpec(memory_space=VMEM)] * (4 + len(pieces)),
        out_specs=[pl.BlockSpec(memory_space=VMEM)] * 2,
        scratch_shapes=[pltpu.VMEM((width, pieces[0].shape[1]), jnp.bfloat16)],
        compiler_params=params(10),
        name="input_back",
    )(x, packed, gains, middle_grad, *pieces)


def pack_kernel(weight, norms, out):
    rows, width = weight.shape
    out[:, :width] = weight[...].astype(out.dtype)
    same = lax.broadcasted_iota(jnp.int32, (rows, rows), 0) == lax.broadcasted_iota(jnp.int32, (rows, rows), 1)
    lane = lax.broadcasted_iota(jnp.int32, (rows, LANES), 1)
    tile = jnp.zeros((rows, LANES), jnp.float32)
    for j in range(norms.shape[0]):
        column = jnp.sum(jnp.where(same, norms[j : j + 1, :], 0.0), axis=1, keepdims=True)
        tile = jnp.where(lane == j, column, tile)
    out[:, width:] = tile.astype(out.dtype)


def pack(weight, norms):
    rows, width = weight.shape
    return pl.pallas_call(
        pack_kernel,
        out_shape=jax.ShapeDtypeStruct((rows, width + LANES), jnp.bfloat16),
        in_specs=[pl.BlockSpec(memory_space=VMEM)] * 2,
        out_specs=pl.BlockSpec(memory_space=VMEM),
        compiler_params=params(4),
        name="pack",
    )(weight, norms)


def column_kernel(lay, *refs):
    out = refs[-1]
    got = [ref[...].astype(jnp.float32) for ref in refs[:-1]]
    parts = []
    for j in range(len(got)):
        part = got[0]
        for i in range(1, len(got)):
            part = jnp.where(lay.partner(lay.core(), i, True, -1) == j, got[i], part)
        parts.append(part)
    out[...] = jnp.concatenate(parts, axis=0).astype(out.dtype)


def column_of(lay, shards):
    rows, cols = shards[0].shape
    return pl.pallas_call(
        partial(column_kernel, lay),
        out_shape=jax.ShapeDtypeStruct((len(shards) * rows, cols), shards[0].dtype),
        in_specs=[pl.BlockSpec(memory_space=VMEM)] * len(shards),
        out_specs=pl.BlockSpec(memory_space=VMEM),
        compiler_params=params(4),
        name="column",
    )(*shards)


def chip_sum_kernel(lay, keep, got, *outs):
    for i, ref in enumerate(outs):
        at = lay.partner(lay.core(), i, False, 1)
        ref[...] = (keep[at].astype(jnp.float32) + got[at].astype(jnp.float32)).astype(ref.dtype)


def chip_sum(lay, keep, got):
    plane, rows, cols = keep.shape
    return pl.pallas_call(
        partial(chip_sum_kernel, lay),
        out_shape=[jax.ShapeDtypeStruct((rows, cols), jnp.float32)]
        + [jax.ShapeDtypeStruct((rows, cols), jnp.bfloat16)] * (plane - 1),
        in_specs=[pl.BlockSpec(memory_space=VMEM)] * 2,
        out_specs=[pl.BlockSpec(memory_space=VMEM)] * plane,
        compiler_params=params(14),
        name="chip_sum",
    )(keep, got)


def plane_sum_kernel(lay, own, *refs):
    got, outs = refs[: lay.plane - 1], refs[lay.plane - 1 :]
    rows = outs[0].shape[0]
    total = own[...]
    for ref in got:
        total = total + ref[...].astype(jnp.float32)
    for i, ref in enumerate(outs):
        at = lay.partner(lay.core(), i, True, 1)
        part = total[:rows]
        for j in range(1, lay.rep):
            part = jnp.where(at == j, total[j * rows : (j + 1) * rows], part)
        ref[...] = part.astype(ref.dtype)


def plane_sum(lay, own, got):
    rows, cols = own.shape
    reps = lay.rep
    return pl.pallas_call(
        partial(plane_sum_kernel, lay),
        out_shape=[jax.ShapeDtypeStruct((rows // reps, cols), jnp.float32)]
        + [jax.ShapeDtypeStruct((rows // reps, cols), jnp.bfloat16)] * (reps - 1),
        in_specs=[pl.BlockSpec(memory_space=VMEM)] * (1 + len(got)),
        out_specs=[pl.BlockSpec(memory_space=VMEM)] * reps,
        compiler_params=params(10),
        name="plane_sum",
    )(own, *got)


def full_sum(value):
    return jnp.sum(jnp.sum(value, axis=1, keepdims=True), axis=0, keepdims=True)


def turned(columns):
    rows, count = columns.shape
    same = lax.broadcasted_iota(jnp.int32, (rows, rows), 0) == lax.broadcasted_iota(jnp.int32, (rows, rows), 1)
    line = lax.broadcasted_iota(jnp.int32, (count, rows), 0)
    out = jnp.zeros((count, rows), jnp.float32)
    for j in range(count):
        row = jnp.sum(jnp.where(same, columns[:, j : j + 1], 0.0), axis=0, keepdims=True)
        out = jnp.where(line == j, row, out)
    return out


def moments_kernel(pieces_of, first_index, reps, more, *refs):
    n = len(pieces_of)
    grads, others, arrays = refs[:reps], refs[reps : reps + more], refs[reps + more :]
    total = grads[0][...]
    for ref in grads[1:]:
        total = total + ref[...].astype(jnp.float32)
    weights, firsts, seconds = arrays[:n], arrays[n : 2 * n], arrays[2 * n : 3 * n]
    momenta, variances, directions = arrays[3 * n : 4 * n], arrays[4 * n : 5 * n], arrays[5 * n : 6 * n]
    sums = arrays[6 * n]
    lane = lax.broadcasted_iota(jnp.int32, (1, LANES), 1)
    row = others[0][0] if more else jnp.zeros((1, LANES), jnp.float32)
    for i, parts in enumerate(pieces_of):
        weight_sum = jnp.zeros((1, 1), jnp.float32)
        step_sum = jnp.zeros((1, 1), jnp.float32)
        for at, size, columns in parts:
            rows = slice(at, at + size)
            gradient = total[:, columns[0] : columns[1]]
            if len(columns) > 2:
                gradient = turned(gradient)
            weight = weights[i][rows]
            momentum = BETA * firsts[i][rows] + (1.0 - BETA) * gradient
            variance = BETA * seconds[i][rows] + (1.0 - BETA) * gradient * gradient
            direction = momentum / (jnp.sqrt(variance) + ADAM_EPSILON) + DECAY * weight
            momenta[i][rows] = momentum
            variances[i][rows] = variance
            directions[i][rows] = direction
            weight_sum = weight_sum + full_sum(weight * weight)
            step_sum = step_sum + full_sum(direction * direction)
        row = jnp.where(lane == first_index[i], weight_sum, row)
        row = jnp.where(lane == 5 + first_index[i], step_sum, row)
    sums[...] = jnp.broadcast_to(row, sums.shape)


def moments(pieces_of, first_index, grads, others, copies, weights, firsts, seconds):
    arrays = [*grads, *others, *weights, *firsts, *seconds]
    shapes = [jax.ShapeDtypeStruct(weight.shape, jnp.float32) for weight in weights]
    outs = pl.pallas_call(
        partial(moments_kernel, pieces_of, first_index, len(grads), len(others)),
        out_shape=shapes * 3 + [jax.ShapeDtypeStruct((copies, 1, LANES), jnp.float32)],
        in_specs=[pl.BlockSpec(memory_space=VMEM)] * len(arrays),
        out_specs=[pl.BlockSpec(memory_space=VMEM)] * (3 * len(weights) + 1),
        compiler_params=params(8),
        name="moments",
    )(*arrays)
    n = len(weights)
    return outs[:n], outs[n : 2 * n], outs[2 * n : 3 * n], outs[3 * n]


def update_kernel(n, sums, *refs):
    weights, directions, updated, table = refs[:n], refs[n : 2 * n], refs[2 * n : 3 * n], refs[3 * n]
    norms = jnp.sqrt(jnp.sum(sums[...], axis=0))
    row = lax.broadcasted_iota(jnp.int32, table.shape, 0)
    lane = lax.broadcasted_iota(jnp.int32, table.shape, 1)
    out = jnp.zeros(table.shape, jnp.float32)
    for i in range(n):
        weight_norm = norms[:, i : i + 1]
        step_norm = norms[:, 5 + i : 6 + i]
        ratio = weight_norm / step_norm
        updated[i][...] = weights[i][...] - RATE * ratio * directions[i][...]
        column = jnp.where(row == 0, weight_norm, jnp.where(row == 1, step_norm, ratio))
        out = jnp.where(lane == i, column, out)
    table[...] = out


def update(sums, weights, directions):
    n = len(weights)
    outs = pl.pallas_call(
        partial(update_kernel, n),
        out_shape=[jax.ShapeDtypeStruct(weight.shape, jnp.float32) for weight in weights]
        + [jax.ShapeDtypeStruct((3, n), jnp.float32)],
        in_specs=[pl.BlockSpec(memory_space=VMEM)] * (1 + 2 * n),
        out_specs=[pl.BlockSpec(memory_space=VMEM)] * (n + 1),
        compiler_params=params(6),
        name="update",
    )(sums, *weights, *directions)
    return outs[:n], outs[n]


def over(lay, value, first):
    return [value] + [lay.over(value, i, first) for i in range(1, lay.rep if first else lay.plane)]


def send_over(lay, parts, first):
    return [lay.over(part, i, first) for i, part in enumerate(parts, 1)]


def over_core(lay, blocks):
    return blocks + [lay.to_core(block) for block in blocks]


def after(values, others):
    count = len(values)
    return list(lax.optimization_barrier((*values, *others))[:count])


def exchange(lay, value):
    return lax.all_to_all(value, AXES, 0, 0)


def body(
    lay,
    inputs,
    segments,
    cotangent,
    attend_in,
    attend_out,
    expand,
    contract,
    layer_norms,
    moment_in,
    moment_out,
    moment_expand,
    moment_contract,
    moment_norms,
    square_in,
    square_out,
    square_expand,
    square_contract,
    square_norms,
):
    plain, twin = lay
    lay = plain
    masters = (attend_in, attend_out, expand, contract, layer_norms)
    width = attend_in.shape[1]
    depth = attend_out.shape[1]
    hidden = expand.shape[1]
    own = attend_in.shape[0]
    count = lay.dp * lay.rep
    whole_tiles = own % 16 == 0
    shard1 = pack(attend_in, layer_norms)
    column1 = over(plain, shard1, True)
    rows = inputs.shape[1]
    attend_out_, expand_, contract_ = after([attend_out, expand, contract], [shard1])
    deep = [contract_[j * own : (j + 1) * own] for j in range(4)]
    shard2 = jnp.concatenate([part.astype(jnp.bfloat16) for part in (attend_out_, expand_, *deep)], axis=1)
    (shard2,) = after([shard2], column1[1:])
    column2 = over(twin, shard2, True)
    blocks1 = over(plain, column_of(plain, column1), False)
    (segments_,) = after([segments], blocks1[:1])
    x, dy, labels, begin = arrange(inputs[0], cotangent[0], segments_)
    blocks2 = over(twin, column_of(twin, after(column2, [*blocks1, x])), False)
    pieces1 = over_core(lay, blocks1)
    *pieces1, x, labels = after([*pieces1, x, labels], blocks2[:1])
    qx, kx, vx, mixed, gains = attend(plain, x, labels, pieces1)
    near = lay.to_core(blocks2[0])
    blocks2[1:] = after(blocks2[1:], [mixed])
    pieces2 = [*blocks2, near, *[lay.to_core(block) for block in blocks2[1:]]]
    deep_pieces = []
    if not whole_tiles:
        first = depth + hidden
        for piece in pieces2:
            part = piece[:, first:].reshape(lay.rep, own, 4, depth).transpose(0, 2, 1, 3)
            deep_pieces.append(part.reshape(-1, depth))
    middle, middle_grad, middle_low, active, contract_all, out_weight, keep2, send2, second_norms, *deep_out = feed(
        twin, x, mixed, dy, gains, pieces2, deep_pieces
    )
    if not whole_tiles:
        keep2, send2 = [
            jnp.concatenate(
                [
                    wide[:, :, : depth + hidden],
                    part.reshape(lay.plane, lay.rep, 4, own, depth).transpose(0, 1, 3, 2, 4).reshape(lay.plane, -1, 4 * depth),
                ],
                axis=2,
            )
            for wide, part in zip((keep2, send2), deep_out)
        ]
    chip2 = lay.to_core(send2)
    dox = mixed_back(middle_low, mixed, out_weight)
    keep2, chip2 = after([keep2, chip2], [dox])
    own2, *low2 = chip_sum(twin, keep2, chip2)
    got2 = send_over(twin, low2, False)
    (dox,) = after([dox], low2)
    packed = attend_back(qx, kx, vx, dox)
    input_gradient, first_norms = input_back(plain, x, packed, gains, middle_grad, pieces1)
    keep1, send1 = project_back(plain, x, packed, gains, first_norms, second_norms, own)
    own2, send1, *got2 = after([own2, send1, *got2], [])
    own2, *low2 = plane_sum(twin, own2, got2)
    got2 = send_over(twin, low2, True)
    own1, *low1 = chip_sum(plain, keep1, lay.to_core(send1))
    got1 = send_over(plain, low1, False)
    (middle,) = after([middle], low1)
    outputs, input_gradient = finish(begin, middle, active, contract_all, input_gradient, rows)
    own1, *got1 = after([own1, *got1], [outputs])
    spans = [[(0, own, (0, depth))], [(0, own, (depth, depth + hidden))]]
    spans.append([(j * own, own, (depth + hidden + j * depth, depth + hidden + (j + 1) * depth)) for j in range(4)])
    momenta2, variances2, directions2, sums2 = moments(
        spans, (1, 2, 3), [own2, *got2], [], 1, masters[1:4],
        (moment_out, moment_expand, moment_contract), (square_out, square_expand, square_contract),
    )
    own1, *low1 = plane_sum(plain, own1, got1)
    got1 = send_over(plain, low1, True)
    momenta1, variances1, directions1, sums1 = moments(
        [[(0, own, (0, width))], [(0, 4, (width, width + 4, True))]], (0, 4), [own1, *got1], [sums2], count, (attend_in, layer_norms),
        (moment_in, moment_norms), (square_in, square_norms),
    )
    sums = exchange(lay, sums1)
    directions = (directions1[0], *directions2, directions1[1])
    updated, trust_table = update(sums, masters, directions)
    momenta = (momenta1[0], *momenta2, momenta1[1])
    variances = (variances1[0], *variances2, variances1[1])
    return (outputs[None], input_gradient[None], *updated, *momenta, *variances, trust_table)


def solution(mesh):
    placed = (
        P(("dp", "rep"), None, None),
        P(("dp", "rep"), None),
        P(("dp", "rep"), None, None),
        P(("dp", "rep"), None),
        P(("dp", "rep"), None),
        P(("dp", "rep"), None),
        P(("dp", "rep"), None),
        P(None, ("dp", "rep")),
        P(("dp", "rep"), None),
        P(("dp", "rep"), None),
        P(("dp", "rep"), None),
        P(("dp", "rep"), None),
        P(None, ("dp", "rep")),
        P(("dp", "rep"), None),
        P(("dp", "rep"), None),
        P(("dp", "rep"), None),
        P(("dp", "rep"), None),
        P(None, ("dp", "rep")),
    )
    return jax.shard_map(
        partial(body, (Layout(mesh, False), Layout(mesh, True))),
        mesh=mesh,
        in_specs=placed,
        out_specs=(
            P(("dp", "rep"), None, None),
            P(("dp", "rep"), None, None),
            P(("dp", "rep"), None),
            P(("dp", "rep"), None),
            P(("dp", "rep"), None),
            P(("dp", "rep"), None),
            P(None, ("dp", "rep")),
            P(("dp", "rep"), None),
            P(("dp", "rep"), None),
            P(("dp", "rep"), None),
            P(("dp", "rep"), None),
            P(None, ("dp", "rep")),
            P(("dp", "rep"), None),
            P(("dp", "rep"), None),
            P(("dp", "rep"), None),
            P(("dp", "rep"), None),
            P(None, ("dp", "rep")),
            P(),
        ),
        check_vma=False,
    )
```

```python
from functools import partial
import math

import jax
import jax.numpy as jnp
from jax import lax
from jax.experimental import pallas as pl
from jax.experimental.pallas import tpu as pltpu
from jax.sharding import PartitionSpec as P

HEADS = 8
HEAD_DIM = 64


EPSILON = 1e-05
ADAM_EPSILON = 1e-06
DECAY = 0.01
RATE = 0.5
BETA = 0.5
LANES = 128
HALF = 64
BIG = 1e30
FEATS = 4
TILE = 256
THIN = 32
CHUNK = 352
DEEP_CHUNK = 528
GELU_ONE = 0.7978845608028654
GELU_CUBE = 0.044715 * GELU_ONE
VMEM = pltpu.MemorySpace.VMEM
AXES = ("dp", "rep")


def params(mebibytes):
    return pltpu.CompilerParams(vmem_limit_bytes=mebibytes * 1024 * 1024)


def dot(a, b, ca, cb):
    return lax.dot_general(a, b, (((ca,), (cb,)), ((), ())), preferred_element_type=jnp.float32)


def normalize(values):
    center = values - jnp.mean(values, axis=-1, keepdims=True)
    scale = lax.rsqrt(jnp.mean(center * center, axis=-1, keepdims=True) + EPSILON)
    return center * scale, scale


class Layout:
    def __init__(self, mesh, mixed):
        self.dp = mesh.shape["dp"]
        self.rep = mesh.shape["rep"]
        self.plane = self.dp // 2
        self.mixed = mixed and self.plane == self.rep

    def pairs(self, move):
        pairs = []
        for p in range(self.plane):
            for c in range(2):
                for z in range(self.rep):
                    q, d, w = move(p, c, z)
                    pairs.append(((p * 2 + c) * self.rep + z, (q * 2 + d) * self.rep + w))
        return pairs

    def over(self, value, i, first):
        def move(p, c, z):
            along_z = (first == (c == 0)) if self.mixed else first
            return (p, c, (z + i) % self.rep) if along_z else (p ^ i, c, z)

        return lax.ppermute(value, AXES, self.pairs(move))

    def to_core(self, value):
        return lax.ppermute(value, AXES, self.pairs(lambda p, c, z: (p, 1 - c, z)))

    def core(self):
        return lax.rem(lax.axis_index("dp"), 2)

    def partner(self, side, i, first, sign):
        along_z = lax.rem(lax.axis_index("rep") + (sign * i) % self.rep, self.rep)
        in_plane = lax.div(lax.axis_index("dp"), 2) ^ i
        if not self.mixed:
            return along_z if first else in_plane
        return jnp.where(side == 0, along_z, in_plane) if first else jnp.where(side == 0, in_plane, along_z)

    def device(self, side, second, first):
        plain = (2 * second + side) * self.rep + first
        return jnp.where(side == 0, plain, (2 * first + side) * self.rep + second) if self.mixed else plain


def row_blocks(lay, side, second, rows):
    firsts = lay.rep
    if lay.mixed:
        return [(j * rows, pl.multiple_of(lay.device(side, second, j) * rows, rows), rows) for j in range(firsts)]
    return [(0, pl.multiple_of(lay.device(side, second, 0) * rows, firsts * rows), firsts * rows)]


def assemble(lay, pieces, full_ref, columns):
    count = len(pieces) // 2
    for i, piece in enumerate(pieces):
        side = lay.core() if i < count else 1 - lay.core()
        second = lay.partner(side, i % count, False, -1)
        for at, to, rows in row_blocks(lay, side, second, piece.shape[0] // lay.rep):
            full_ref[pl.ds(to, rows), :] = piece[at : at + rows, columns]


def assemble_deep(lay, pieces, full_ref, first):
    count = len(pieces) // 2
    width = full_ref.shape[1]
    for i, piece in enumerate(pieces):
        side = lay.core() if i < count else 1 - lay.core()
        second = lay.partner(side, i % count, False, -1)
        rows = piece.shape[0] // lay.rep
        for z in range(lay.rep):
            to = pl.multiple_of(lay.device(side, second, z) * 4 * rows, 4 * rows)
            for j in range(4):
                source = piece[z * rows : (z + 1) * rows, first + j * width : first + (j + 1) * width]
                full_ref[pl.ds(to + j * rows, rows), :] = source


def split_rows(lay, full_ref, keep_ref, send_ref, lanes):
    for target, side in ((keep_ref, lay.core()), (send_ref, 1 - lay.core())):
        for second in range(target.shape[0]):
            for at, source, rows in row_blocks(lay, side, second, target.shape[1] // lay.rep):
                target[second, at : at + rows, lanes] = full_ref[pl.ds(source, rows), :].astype(target.dtype)


def split_deep(lay, full_ref, keep_ref, send_ref, first):
    width = full_ref.shape[1]
    rows = keep_ref.shape[1] // lay.rep
    for target, side in ((keep_ref, lay.core()), (send_ref, 1 - lay.core())):
        for second in range(target.shape[0]):
            for z in range(lay.rep):
                source = pl.multiple_of(lay.device(side, second, z) * 4 * rows, 4 * rows)
                for j in range(4):
                    part = full_ref[pl.ds(source + j * rows, rows), :]
                    columns = slice(first + j * width, first + (j + 1) * width)
                    target[second, z * rows : (z + 1) * rows, columns] = part.astype(target.dtype)


def row_chunks(rows, size):
    return [(at, min(size, rows - at)) for at in range(0, rows, size)]


def windows(rows):
    half = (rows - THIN) // 2
    span = half + THIN
    spans = [(at, TILE, 0, span) for at in range(0, half, TILE)]
    spans.append((half, THIN, 0, rows))
    return spans + [(at, TILE, half, span) for at in range(span, rows, TILE)]


def arrange_kernel(inputs, cotangent, segments, x, dy, labels, begin, room):
    tokens = segments.shape[1]
    half = tokens // 2
    memory = inputs.shape[0] - tokens
    segment = segments[...].astype(jnp.float32)
    ahead = pltpu.roll(jnp.broadcast_to(segment, (8, tokens)), tokens - half + 1, 1)[:1]
    lane = lax.broadcasted_iota(jnp.int32, (1, tokens), 1)
    fits = (segment == ahead) & (lane <= half)
    start = jnp.sum(jnp.where(fits, lane.astype(jnp.float32), 0.0), axis=1, keepdims=True)
    begin[...] = jnp.broadcast_to(start, begin.shape)
    row = lax.broadcasted_iota(jnp.int32, (half, LANES), 0).astype(jnp.float32)
    early = row < start
    thin = lax.broadcasted_iota(jnp.int32, (THIN, LANES), 0) < memory
    for source, target in ((inputs, x), (cotangent, dy)):
        for at in range(0, inputs.shape[1], LANES):
            columns = slice(at, at + LANES)
            room[: inputs.shape[0]] = source[:, columns].astype(jnp.float32)
            left, right = room[memory : memory + half], room[memory + half : memory + tokens]
            target[:half, columns] = jnp.where(early, right, left).astype(target.dtype)
            target[half : half + THIN, columns] = jnp.where(thin, room[:THIN], 0.0).astype(target.dtype)
            target[half + THIN :, columns] = jnp.where(early, left, right).astype(target.dtype)
    left = jnp.transpose(jnp.broadcast_to(segment[:, :half], (LANES, half)))
    right = jnp.transpose(jnp.broadcast_to(segment[:, half:], (LANES, half)))
    labels[:half] = jnp.where(early, right, left).astype(jnp.int32)
    labels[half : half + THIN] = jnp.where(thin, -1, -2)
    labels[half + THIN :] = jnp.where(early, left, right).astype(jnp.int32)


def arrange(inputs, cotangent, segments):
    width = inputs.shape[1]
    rows = segments.shape[1] + THIN
    return pl.pallas_call(
        arrange_kernel,
        out_shape=(
            jax.ShapeDtypeStruct((rows, width), inputs.dtype),
            jax.ShapeDtypeStruct((rows, width), inputs.dtype),
            jax.ShapeDtypeStruct((rows, LANES), jnp.int32),
            jax.ShapeDtypeStruct((8, LANES), jnp.float32),
        ),
        in_specs=[pl.BlockSpec(memory_space=VMEM)] * 3,
        out_specs=[pl.BlockSpec(memory_space=VMEM)] * 4,
        scratch_shapes=[pltpu.VMEM((rows, LANES), jnp.float32)],
        compiler_params=params(8),
        name="arrange",
    )(inputs, cotangent, segments)


def finish_kernel(begin, middle, active, contract, grad_in, outputs, grad_out, room):
    rows = outputs.shape[0]
    half = (middle.shape[0] - THIN) // 2
    memory = rows - 2 * half
    wide = room.shape[1]
    row = lax.broadcasted_iota(jnp.int32, (half, wide), 0).astype(jnp.float32)
    early = row < begin[:1, :1]

    def place(value, target, columns):
        left, right = value[:half], value[half + THIN :]
        room[:THIN] = value[half : half + THIN]
        room[memory : memory + half] = jnp.where(early, right, left)
        room[memory + half : rows] = jnp.where(early, left, right)
        target[:, columns] = room[:rows].astype(target.dtype)

    for at in range(0, middle.shape[1], wide):
        columns = slice(at, at + wide)
        place(middle[:, columns] + dot(active[...], contract[:, columns], 1, 0), outputs, columns)
        place(grad_in[:, columns].astype(jnp.float32), grad_out, columns)


def finish(begin, middle, active, contract, grad_in, rows):
    width = middle.shape[1]
    return pl.pallas_call(
        finish_kernel,
        out_shape=[jax.ShapeDtypeStruct((rows, width), grad_in.dtype)] * 2,
        in_specs=[pl.BlockSpec(memory_space=VMEM)] * 5,
        out_specs=[pl.BlockSpec(memory_space=VMEM)] * 2,
        scratch_shapes=[pltpu.VMEM((middle.shape[0], 256), jnp.float32)],
        compiler_params=params(10),
        name="finish",
    )(begin, middle, active, contract, grad_in)


def attend_kernel(lay, count, x, labels, *refs):
    pieces = refs[:count]
    qx, kx, vx, mixed, gains, weight, qs = refs[count:]
    rows = x.shape[0]
    width = mixed.shape[1]
    assemble(lay, pieces, weight, slice(None))
    gains[...] = jnp.transpose(weight[:, 3 * width :].astype(jnp.float32))[:8]
    gain, bias = gains[0:1], gains[1:2]

    def one_chunk(i, carry):
        span = pl.ds(pl.multiple_of(i * CHUNK, CHUNK), CHUNK)
        normed, _ = normalize(x[span].astype(jnp.float32))
        first = (normed * gain + bias).astype(jnp.bfloat16)
        lane = lax.broadcasted_iota(jnp.int32, (CHUNK, LANES), 1)
        low = lane < HALF
        feature = lane % HALF
        label = labels[span]
        blocked = ((feature < FEATS) & (label >= 0) & (feature != label)) | (feature == FEATS)
        query_side = jnp.where(blocked, -BIG, 0.0)
        marked = ((feature < FEATS) & (feature == label)) | ((feature == FEATS) & (label == -2))
        key_side = jnp.where(marked | (feature > FEATS), 1.0, 0.0)
        sides = (query_side, key_side, jnp.ones_like(key_side))
        for kind, target in enumerate((qs, kx, vx)):
            whole = dot(first, weight[:, kind * width : (kind + 1) * width], 1, 0)
            whole = whole.astype(jnp.bfloat16).astype(jnp.float32)
            for pair in range(width // LANES):
                part = whole[:, pair * LANES : (pair + 1) * LANES]
                if kind == 0:
                    part = part * (1.0 / math.sqrt(HEAD_DIM))
                at = 2 * pair * LANES
                target[span, at : at + LANES] = jnp.where(low, part, sides[kind]).astype(jnp.bfloat16)
                target[span, at + LANES : at + 2 * LANES] = jnp.where(low, sides[kind], part).astype(jnp.bfloat16)
        return carry

    lax.fori_loop(0, rows // CHUNK, one_chunk, 0)

    def one_pair(pair, carry):
        columns = pl.ds(pl.multiple_of(pair * LANES, LANES), LANES)
        for at, size, key_at, key_size in windows(rows):
            span = pl.ds(at, size)
            seen = pl.ds(key_at, key_size)
            lane = lax.broadcasted_iota(jnp.int32, (size, LANES), 1)
            low = lane < HALF
            feature = lane % HALF
            got = []
            for side in range(2):
                head = pl.ds(pl.multiple_of((2 * pair + side) * LANES, LANES), LANES)
                queries = qs[span, head]
                scores = dot(queries, kx[seen, head], 1, 1)
                highest = jnp.max(scores, axis=1, keepdims=True)
                raised = jnp.exp(scores - highest).astype(jnp.bfloat16)
                found = dot(raised, vx[seen, head], 1, 0)
                total = -(highest + jnp.log(found))
                first = total.astype(jnp.bfloat16).astype(jnp.float32)
                second = (total - first).astype(jnp.bfloat16).astype(jnp.float32)
                third = total - first - second
                values = jnp.where(feature == 5, first, jnp.where(feature == 6, second, third))
                place = (feature > FEATS) & (feature < 8) & (low if side else ~low)
                qx[span, head] = jnp.where(place, values, queries.astype(jnp.float32)).astype(jnp.bfloat16)
                got.append(found)
            over = pltpu.roll(jnp.where(low, got[1], got[0]), HALF, 1)
            mixed[span, columns] = (jnp.where(low, got[0], got[1]) / over).astype(jnp.bfloat16)
        return carry

    lax.fori_loop(0, width // LANES, one_pair, 0)


def attend(lay, x, labels, pieces):
    rows, width = x.shape
    wide = jax.ShapeDtypeStruct((rows, 2 * width), jnp.bfloat16)
    depth = len(pieces) * pieces[0].shape[0]
    return pl.pallas_call(
        partial(attend_kernel, lay, len(pieces)),
        out_shape=(
            wide,
            wide,
            wide,
            jax.ShapeDtypeStruct((rows, width), jnp.bfloat16),
            jax.ShapeDtypeStruct((8, width), jnp.float32),
        ),
        in_specs=[pl.BlockSpec(memory_space=VMEM)] * (2 + len(pieces)),
        out_specs=[pl.BlockSpec(memory_space=VMEM)] * 5,
        scratch_shapes=[
            pltpu.VMEM((depth, pieces[0].shape[1]), jnp.bfloat16),
            pltpu.VMEM((rows, 2 * width), jnp.bfloat16),
        ],
        compiler_params=params(16),
        name="attend",
    )(x, labels, *pieces)


def attend_back_kernel(qx, kx, vx, dox, packed, total):
    rows = qx.shape[0]
    width = packed.shape[1] // 3

    def one_pair(pair, carry):
        heads = [pl.ds(pl.multiple_of((2 * pair + side) * LANES, LANES), LANES) for side in range(2)]
        spots = [pl.ds(pl.multiple_of(kind * width + pair * LANES, LANES), LANES) for kind in range(3)]
        total[...] = jnp.zeros_like(total)
        for at, size, query_at, query_size in windows(rows):
            span = pl.ds(at, size)
            seen = pl.ds(query_at, query_size)
            low = lax.broadcasted_iota(jnp.int32, (size, LANES), 1) < HALF
            got = []
            for side in range(2):
                head = heads[side]
                keys = kx[span, head]
                queries = qx[seen, head]
                upstream = dox[seen, head]
                attention = jnp.exp(dot(keys, queries, 1, 1))
                grad = dot(vx[span, head], upstream, 1, 1)
                scores = (attention * grad).astype(jnp.bfloat16)
                got.append((dot(scores, queries, 1, 0), dot(attention.astype(jnp.bfloat16), upstream, 1, 0)))
                total[side, seen] += dot(scores, keys, 0, 0)
            packed[span, spots[1]] = jnp.where(low, got[0][0], got[1][0]).astype(jnp.bfloat16)
            packed[span, spots[2]] = jnp.where(low, got[0][1], got[1][1]).astype(jnp.bfloat16)
        low = lax.broadcasted_iota(jnp.int32, (rows, LANES), 1) < HALF
        packed[:, spots[0]] = (jnp.where(low, total[0], total[1]) * (1.0 / math.sqrt(HEAD_DIM))).astype(jnp.bfloat16)
        return carry

    lax.fori_loop(0, width // LANES, one_pair, 0)


def attend_back(qx, kx, vx, dox):
    rows, wide = qx.shape
    return pl.pallas_call(
        attend_back_kernel,
        out_shape=jax.ShapeDtypeStruct((rows, 3 * wide // 2), jnp.bfloat16),
        in_specs=[pl.BlockSpec(memory_space=VMEM)] * 4,
        out_specs=pl.BlockSpec(memory_space=VMEM),
        scratch_shapes=[pltpu.VMEM((2, rows, LANES), jnp.float32)],
        compiler_params=params(16),
        name="attend_back",
    )(qx, kx, vx, dox)


def norm_back(grad, normed, scale, gain):
    scaled = grad * gain
    return scale * (
        scaled
        - jnp.mean(scaled, axis=-1, keepdims=True)
        - normed * jnp.mean(scaled * normed, axis=-1, keepdims=True)
    )


def feed_kernel(lay, count, deep_count, x, mixed, dy, gains, *refs):
    pieces = refs[:count]
    deep_pieces = refs[count : count + deep_count]
    outs = refs[count + deep_count : -5]
    middle, middle_grad, middle_low, active, contract, out_weight, keep2, send2, norm_grads, *deep_out = outs
    wide, hidden_grad, second, block, deep_block = refs[-5:]
    rows, width = x.shape
    hidden = contract.shape[0]
    assemble(lay, pieces, wide, slice(0, width + hidden))
    if deep_count:
        assemble(lay, deep_pieces, contract, slice(None))
    else:
        assemble_deep(lay, pieces, contract, width + hidden)
    out_weight[...] = wide[:, :width]
    gain, bias = gains[2:3], gains[3:4]
    zero = jnp.zeros((1, width), jnp.float32)

    def one_chunk(i, carry):
        gain_sum, bias_sum = carry
        span = pl.ds(i * DEEP_CHUNK, DEEP_CHUNK)
        start = x[span].astype(jnp.float32) + dot(mixed[span], wide[:, :width], 1, 0)
        middle[span] = start
        normed, scale = normalize(start)
        low = (normed * gain + bias).astype(jnp.bfloat16)
        second[span] = low
        for start in range(0, hidden, 512):
            part = slice(start, start + 512)
            up = dot(low, wide[:, width + start : width + start + 512], 1, 0)
            square = up * up
            half = 0.5 + 0.5 * jnp.tanh(up * (GELU_ONE + GELU_CUBE * square))
            act = up * half
            active[span, part] = act.astype(jnp.bfloat16)
            slope = half + act * ((1.0 - half) * (2.0 * GELU_ONE + 6.0 * GELU_CUBE * square))
            hidden_grad[span, part] = (dot(dy[span], contract[part], 1, 1) * slope).astype(jnp.bfloat16)
        back = dot(hidden_grad[span], wide[:, width:], 1, 1)
        gain_sum = gain_sum + jnp.sum(back * normed, axis=0, keepdims=True)
        bias_sum = bias_sum + jnp.sum(back, axis=0, keepdims=True)
        grad = dy[span].astype(jnp.float32) + norm_back(back, normed, scale, gain)
        middle_grad[span] = grad
        middle_low[span] = grad.astype(jnp.bfloat16)
        return gain_sum, bias_sum

    sums = (zero, zero)
    for i in range(rows // DEEP_CHUNK):
        sums = one_chunk(i, sums)
    gain_sum, bias_sum = sums
    norm_grads[...] = jnp.concatenate([gain_sum, bias_sum, jnp.zeros((6, width), jnp.float32)], axis=0)

    def one_block(i, carry):
        columns = pl.ds(pl.multiple_of(i * 512, 512), 512)
        deep_block[columns] = dot(active[:, columns], dy[...], 0, 0)
        block[...] = dot(second[...], hidden_grad[:, columns], 0, 0)
        split_rows(lay, block, keep2, send2, pl.ds(pl.multiple_of(width + i * 512, 512), 512))
        return carry

    lax.fori_loop(0, hidden // 512, one_block, 0)
    if deep_count:
        split_rows(lay, deep_block, *deep_out, slice(0, width))
    else:
        split_deep(lay, deep_block, keep2, send2, width + hidden)
    block[...] = dot(mixed[...], middle_low[...], 0, 0)
    split_rows(lay, block, keep2, send2, slice(0, width))


def feed(lay, x, mixed, dy, gains, pieces, deep_pieces):
    rows, width = x.shape
    plane = len(pieces) // 2
    deep = pieces[0].shape[0]
    columns = pieces[0].shape[1]
    hidden = 4 * width
    out_shape = [
        jax.ShapeDtypeStruct((rows, width), jnp.float32),
        jax.ShapeDtypeStruct((rows, width), jnp.float32),
        jax.ShapeDtypeStruct((rows, width), jnp.bfloat16),
        jax.ShapeDtypeStruct((rows, hidden), jnp.bfloat16),
        jax.ShapeDtypeStruct((hidden, width), jnp.bfloat16),
        jax.ShapeDtypeStruct((width, width), jnp.bfloat16),
        jax.ShapeDtypeStruct((plane, deep, columns), jnp.bfloat16),
        jax.ShapeDtypeStruct((plane, deep, columns), jnp.bfloat16),
        jax.ShapeDtypeStruct((8, width), jnp.float32),
    ]
    if deep_pieces:
        out_shape.append(jax.ShapeDtypeStruct((plane, 4 * deep, width), jnp.bfloat16))
        out_shape.append(jax.ShapeDtypeStruct((plane, 4 * deep, width), jnp.bfloat16))
    return pl.pallas_call(
        partial(feed_kernel, lay, len(pieces), len(deep_pieces)),
        out_shape=out_shape,
        in_specs=[pl.BlockSpec(memory_space=VMEM)] * (4 + len(pieces) + len(deep_pieces)),
        out_specs=[pl.BlockSpec(memory_space=VMEM)] * len(out_shape),
        scratch_shapes=[
            pltpu.VMEM((width, width + hidden), jnp.bfloat16),
            pltpu.VMEM((rows, hidden), jnp.bfloat16),
            pltpu.VMEM((rows, width), jnp.bfloat16),
            pltpu.VMEM((width, 512), jnp.float32),
            pltpu.VMEM((hidden, width), jnp.float32),
        ],
        compiler_params=params(26),
        name="feed",
    )(x, mixed, dy, gains, *pieces, *deep_pieces)


def mixed_back_kernel(middle_low, mixed, out_weight, dox):
    rows, width = mixed.shape

    def one_chunk(i, carry):
        span = pl.ds(pl.multiple_of(i * DEEP_CHUNK, DEEP_CHUNK), DEEP_CHUNK)
        mixed_grad = dot(middle_low[span], out_weight[...], 1, 1).astype(jnp.bfloat16).astype(jnp.float32)
        lane = lax.broadcasted_iota(jnp.int32, (DEEP_CHUNK, LANES), 1)
        left = lane < HALF
        feature = lane % HALF
        for pair in range(width // LANES):
            columns = slice(pair * LANES, (pair + 1) * LANES)
            piece = mixed_grad[:, columns]
            product = piece * mixed[span, columns].astype(jnp.float32)
            for side in range(2):
                mine = left if side == 0 else ~left
                delta = -jnp.sum(jnp.where(mine, product, 0.0), axis=1, keepdims=True)
                one = delta.astype(jnp.bfloat16).astype(jnp.float32)
                two = (delta - one).astype(jnp.bfloat16).astype(jnp.float32)
                three = delta - one - two
                extra = jnp.where(feature == 0, one, jnp.where(feature == 1, two, jnp.where(feature == 2, three, 0.0)))
                head = (2 * pair + side) * LANES
                dox[span, head : head + LANES] = jnp.where(mine, piece, extra).astype(jnp.bfloat16)
        return carry

    lax.fori_loop(0, rows // DEEP_CHUNK, one_chunk, 0)


def mixed_back(middle_low, mixed, out_weight):
    rows, width = mixed.shape
    return pl.pallas_call(
        mixed_back_kernel,
        out_shape=jax.ShapeDtypeStruct((rows, 2 * width), jnp.bfloat16),
        in_specs=[pl.BlockSpec(memory_space=VMEM)] * 3,
        out_specs=pl.BlockSpec(memory_space=VMEM),
        compiler_params=params(10),
        name="mixed_back",
    )(middle_low, mixed, out_weight)


def project_back_kernel(lay, x, packed, gains, first_norms, second_norms, keep, send, first, block):
    rows, width = x.shape
    gain, bias = gains[0:1], gains[1:2]

    def one_chunk(i, carry):
        span = pl.ds(pl.multiple_of(i * CHUNK, CHUNK), CHUNK)
        normed, _ = normalize(x[span].astype(jnp.float32))
        first[span] = (normed * gain + bias).astype(jnp.bfloat16)
        return carry

    lax.fori_loop(0, rows // CHUNK, one_chunk, 0)

    def one_block(i, carry):
        columns = pl.ds(pl.multiple_of(i * 512, 512), 512)
        block[...] = dot(first[...], packed[:, columns], 0, 0)
        split_rows(lay, block, keep, send, columns)
        return carry

    lax.fori_loop(0, packed.shape[1] // 512, one_block, 0)
    fill = jnp.zeros((LANES - 4, width), jnp.float32)
    norms = jnp.concatenate([first_norms[:2], second_norms[:2], fill], axis=0)
    block[:, :LANES] = jnp.transpose(norms)
    split_rows(lay, block.at[:, :LANES], keep, send, slice(packed.shape[1], packed.shape[1] + LANES))


def project_back(lay, x, packed, gains, first_norms, second_norms, own):
    rows, width = x.shape
    shape = (lay.plane, lay.rep * own, packed.shape[1] + LANES)
    return pl.pallas_call(
        partial(project_back_kernel, lay),
        out_shape=(jax.ShapeDtypeStruct(shape, jnp.bfloat16), jax.ShapeDtypeStruct(shape, jnp.bfloat16)),
        in_specs=[pl.BlockSpec(memory_space=VMEM)] * 5,
        out_specs=[pl.BlockSpec(memory_space=VMEM)] * 2,
        scratch_shapes=[pltpu.VMEM((rows, width), jnp.bfloat16), pltpu.VMEM((width, 512), jnp.float32)],
        compiler_params=params(10),
        name="project_back",
    )(x, packed, gains, first_norms, second_norms)


def input_back_kernel(lay, x, packed, gains, middle_grad, *refs):
    pieces = refs[:-3]
    grad_in, norm_grads, weight = refs[-3:]
    rows, width = x.shape
    assemble(lay, pieces, weight, slice(None))
    gain = gains[0:1]
    zero = jnp.zeros((1, width), jnp.float32)

    def one_chunk(i, carry):
        gain_sum, bias_sum = carry
        span = pl.ds(pl.multiple_of(i * CHUNK, CHUNK), CHUNK)
        normed, scale = normalize(x[span].astype(jnp.float32))
        back = dot(packed[span], weight[:, : 3 * width], 1, 1)
        grad_in[span] = (middle_grad[span] + norm_back(back, normed, scale, gain)).astype(jnp.bfloat16)
        gain_sum = gain_sum + jnp.sum(back * normed, axis=0, keepdims=True)
        return gain_sum, bias_sum + jnp.sum(back, axis=0, keepdims=True)

    gain_sum, bias_sum = lax.fori_loop(0, rows // CHUNK, one_chunk, (zero, zero))
    norm_grads[...] = jnp.concatenate([gain_sum, bias_sum, jnp.zeros((6, width), jnp.float32)], axis=0)


def input_back(lay, x, packed, gains, middle_grad, pieces):
    rows, width = x.shape
    return pl.pallas_call(
        partial(input_back_kernel, lay),
        out_shape=(jax.ShapeDtypeStruct((rows, width), jnp.bfloat16), jax.ShapeDtypeStruct((8, width), jnp.float32)),
        in_specs=[pl.BlockSpec(memory_space=VMEM)] * (4 + len(pieces)),
        out_specs=[pl.BlockSpec(memory_space=VMEM)] * 2,
        scratch_shapes=[pltpu.VMEM((width, pieces[0].shape[1]), jnp.bfloat16)],
        compiler_params=params(10),
        name="input_back",
    )(x, packed, gains, middle_grad, *pieces)


def pack_kernel(weight, norms, out):
    rows, width = weight.shape
    out[:, :width] = weight[...].astype(out.dtype)
    same = lax.broadcasted_iota(jnp.int32, (rows, rows), 0) == lax.broadcasted_iota(jnp.int32, (rows, rows), 1)
    lane = lax.broadcasted_iota(jnp.int32, (rows, LANES), 1)
    tile = jnp.zeros((rows, LANES), jnp.float32)
    for j in range(norms.shape[0]):
        column = jnp.sum(jnp.where(same, norms[j : j + 1, :], 0.0), axis=1, keepdims=True)
        tile = jnp.where(lane == j, column, tile)
    out[:, width:] = tile.astype(out.dtype)


def pack(weight, norms):
    rows, width = weight.shape
    return pl.pallas_call(
        pack_kernel,
        out_shape=jax.ShapeDtypeStruct((rows, width + LANES), jnp.bfloat16),
        in_specs=[pl.BlockSpec(memory_space=VMEM)] * 2,
        out_specs=pl.BlockSpec(memory_space=VMEM),
        compiler_params=params(4),
        name="pack",
    )(weight, norms)


def column_kernel(lay, *refs):
    out = refs[-1]
    got = [ref[...].astype(jnp.float32) for ref in refs[:-1]]
    parts = []
    for j in range(len(got)):
        part = got[0]
        for i in range(1, len(got)):
            part = jnp.where(lay.partner(lay.core(), i, True, -1) == j, got[i], part)
        parts.append(part)
    out[...] = jnp.concatenate(parts, axis=0).astype(out.dtype)


def column_of(lay, shards):
    rows, cols = shards[0].shape
    return pl.pallas_call(
        partial(column_kernel, lay),
        out_shape=jax.ShapeDtypeStruct((len(shards) * rows, cols), shards[0].dtype),
        in_specs=[pl.BlockSpec(memory_space=VMEM)] * len(shards),
        out_specs=pl.BlockSpec(memory_space=VMEM),
        compiler_params=params(4),
        name="column",
    )(*shards)


def chip_sum_kernel(lay, keep, got, *outs):
    for i, ref in enumerate(outs):
        at = lay.partner(lay.core(), i, False, 1)
        ref[...] = (keep[at].astype(jnp.float32) + got[at].astype(jnp.float32)).astype(ref.dtype)


def chip_sum(lay, keep, got):
    plane, rows, cols = keep.shape
    return pl.pallas_call(
        partial(chip_sum_kernel, lay),
        out_shape=[jax.ShapeDtypeStruct((rows, cols), jnp.float32)]
        + [jax.ShapeDtypeStruct((rows, cols), jnp.bfloat16)] * (plane - 1),
        in_specs=[pl.BlockSpec(memory_space=VMEM)] * 2,
        out_specs=[pl.BlockSpec(memory_space=VMEM)] * plane,
        compiler_params=params(14),
        name="chip_sum",
    )(keep, got)


def plane_sum_kernel(lay, own, *refs):
    got, outs = refs[: lay.plane - 1], refs[lay.plane - 1 :]
    rows = outs[0].shape[0]
    total = own[...]
    for ref in got:
        total = total + ref[...].astype(jnp.float32)
    for i, ref in enumerate(outs):
        at = lay.partner(lay.core(), i, True, 1)
        part = total[:rows]
        for j in range(1, lay.rep):
            part = jnp.where(at == j, total[j * rows : (j + 1) * rows], part)
        ref[...] = part.astype(ref.dtype)


def plane_sum(lay, own, got):
    rows, cols = own.shape
    reps = lay.rep
    return pl.pallas_call(
        partial(plane_sum_kernel, lay),
        out_shape=[jax.ShapeDtypeStruct((rows // reps, cols), jnp.float32)]
        + [jax.ShapeDtypeStruct((rows // reps, cols), jnp.bfloat16)] * (reps - 1),
        in_specs=[pl.BlockSpec(memory_space=VMEM)] * (1 + len(got)),
        out_specs=[pl.BlockSpec(memory_space=VMEM)] * reps,
        compiler_params=params(10),
        name="plane_sum",
    )(own, *got)


def full_sum(value):
    return jnp.sum(jnp.sum(value, axis=1, keepdims=True), axis=0, keepdims=True)


def turned(columns):
    rows, count = columns.shape
    same = lax.broadcasted_iota(jnp.int32, (rows, rows), 0) == lax.broadcasted_iota(jnp.int32, (rows, rows), 1)
    line = lax.broadcasted_iota(jnp.int32, (count, rows), 0)
    out = jnp.zeros((count, rows), jnp.float32)
    for j in range(count):
        row = jnp.sum(jnp.where(same, columns[:, j : j + 1], 0.0), axis=0, keepdims=True)
        out = jnp.where(line == j, row, out)
    return out


def moments_kernel(pieces_of, first_index, reps, more, *refs):
    n = len(pieces_of)
    grads, others, arrays = refs[:reps], refs[reps : reps + more], refs[reps + more :]
    total = grads[0][...]
    for ref in grads[1:]:
        total = total + ref[...].astype(jnp.float32)
    weights, firsts, seconds = arrays[:n], arrays[n : 2 * n], arrays[2 * n : 3 * n]
    momenta, variances, directions = arrays[3 * n : 4 * n], arrays[4 * n : 5 * n], arrays[5 * n : 6 * n]
    sums = arrays[6 * n]
    lane = lax.broadcasted_iota(jnp.int32, (1, LANES), 1)
    row = others[0][0] if more else jnp.zeros((1, LANES), jnp.float32)
    for i, parts in enumerate(pieces_of):
        weight_sum = jnp.zeros((1, 1), jnp.float32)
        step_sum = jnp.zeros((1, 1), jnp.float32)
        for at, size, columns in parts:
            rows = slice(at, at + size)
            gradient = total[:, columns[0] : columns[1]]
            if len(columns) > 2:
                gradient = turned(gradient)
            weight = weights[i][rows]
            momentum = BETA * firsts[i][rows] + (1.0 - BETA) * gradient
            variance = BETA * seconds[i][rows] + (1.0 - BETA) * gradient * gradient
            direction = momentum / (jnp.sqrt(variance) + ADAM_EPSILON) + DECAY * weight
            momenta[i][rows] = momentum
            variances[i][rows] = variance
            directions[i][rows] = direction
            weight_sum = weight_sum + full_sum(weight * weight)
            step_sum = step_sum + full_sum(direction * direction)
        row = jnp.where(lane == first_index[i], weight_sum, row)
        row = jnp.where(lane == 5 + first_index[i], step_sum, row)
    sums[...] = jnp.broadcast_to(row, sums.shape)


def moments(pieces_of, first_index, grads, others, copies, weights, firsts, seconds):
    arrays = [*grads, *others, *weights, *firsts, *seconds]
    shapes = [jax.ShapeDtypeStruct(weight.shape, jnp.float32) for weight in weights]
    outs = pl.pallas_call(
        partial(moments_kernel, pieces_of, first_index, len(grads), len(others)),
        out_shape=shapes * 3 + [jax.ShapeDtypeStruct((copies, 1, LANES), jnp.float32)],
        in_specs=[pl.BlockSpec(memory_space=VMEM)] * len(arrays),
        out_specs=[pl.BlockSpec(memory_space=VMEM)] * (3 * len(weights) + 1),
        compiler_params=params(8),
        name="moments",
    )(*arrays)
    n = len(weights)
    return outs[:n], outs[n : 2 * n], outs[2 * n : 3 * n], outs[3 * n]


def update_kernel(n, sums, *refs):
    weights, directions, updated, table = refs[:n], refs[n : 2 * n], refs[2 * n : 3 * n], refs[3 * n]
    norms = jnp.sqrt(jnp.sum(sums[...], axis=0))
    row = lax.broadcasted_iota(jnp.int32, table.shape, 0)
    lane = lax.broadcasted_iota(jnp.int32, table.shape, 1)
    out = jnp.zeros(table.shape, jnp.float32)
    for i in range(n):
        weight_norm = norms[:, i : i + 1]
        step_norm = norms[:, 5 + i : 6 + i]
        ratio = weight_norm / step_norm
        updated[i][...] = weights[i][...] - RATE * ratio * directions[i][...]
        column = jnp.where(row == 0, weight_norm, jnp.where(row == 1, step_norm, ratio))
        out = jnp.where(lane == i, column, out)
    table[...] = out


def update(sums, weights, directions):
    n = len(weights)
    outs = pl.pallas_call(
        partial(update_kernel, n),
        out_shape=[jax.ShapeDtypeStruct(weight.shape, jnp.float32) for weight in weights]
        + [jax.ShapeDtypeStruct((3, n), jnp.float32)],
        in_specs=[pl.BlockSpec(memory_space=VMEM)] * (1 + 2 * n),
        out_specs=[pl.BlockSpec(memory_space=VMEM)] * (n + 1),
        compiler_params=params(6),
        name="update",
    )(sums, *weights, *directions)
    return outs[:n], outs[n]


def over(lay, value, first):
    return [value] + [lay.over(value, i, first) for i in range(1, lay.rep if first else lay.plane)]


def send_over(lay, parts, first):
    return [lay.over(part, i, first) for i, part in enumerate(parts, 1)]


def over_core(lay, blocks):
    return blocks + [lay.to_core(block) for block in blocks]


def after(values, others):
    count = len(values)
    return list(lax.optimization_barrier((*values, *others))[:count])


def exchange(lay, value):
    return lax.all_to_all(value, AXES, 0, 0)


def body(
    lay,
    inputs,
    segments,
    cotangent,
    attend_in,
    attend_out,
    expand,
    contract,
    layer_norms,
    moment_in,
    moment_out,
    moment_expand,
    moment_contract,
    moment_norms,
    square_in,
    square_out,
    square_expand,
    square_contract,
    square_norms,
):
    plain, twin = lay
    lay = plain
    masters = (attend_in, attend_out, expand, contract, layer_norms)
    width = attend_in.shape[1]
    depth = attend_out.shape[1]
    hidden = expand.shape[1]
    own = attend_in.shape[0]
    count = lay.dp * lay.rep
    whole_tiles = own % 16 == 0
    shard1 = pack(attend_in, layer_norms)
    column1 = over(plain, shard1, True)
    rows = inputs.shape[1]
    attend_out_, expand_, contract_ = after([attend_out, expand, contract], [shard1])
    deep = [contract_[j * own : (j + 1) * own] for j in range(4)]
    shard2 = jnp.concatenate([part.astype(jnp.bfloat16) for part in (attend_out_, expand_, *deep)], axis=1)
    (shard2,) = after([shard2], column1[1:])
    column2 = over(twin, shard2, True)
    blocks1 = over(plain, column_of(plain, column1), False)
    (segments_,) = after([segments], blocks1[:1])
    x, dy, labels, begin = arrange(inputs[0], cotangent[0], segments_)
    blocks2 = over(twin, column_of(twin, after(column2, [*blocks1, x])), False)
    pieces1 = over_core(lay, blocks1)
    *pieces1, x, labels = after([*pieces1, x, labels], blocks2[:1])
    qx, kx, vx, mixed, gains = attend(plain, x, labels, pieces1)
    near = lay.to_core(blocks2[0])
    blocks2[1:] = after(blocks2[1:], [mixed])
    pieces2 = [*blocks2, near, *[lay.to_core(block) for block in blocks2[1:]]]
    deep_pieces = []
    if not whole_tiles:
        first = depth + hidden
        for piece in pieces2:
            part = piece[:, first:].reshape(lay.rep, own, 4, depth).transpose(0, 2, 1, 3)
            deep_pieces.append(part.reshape(-1, depth))
    middle, middle_grad, middle_low, active, contract_all, out_weight, keep2, send2, second_norms, *deep_out = feed(
        twin, x, mixed, dy, gains, pieces2, deep_pieces
    )
    if not whole_tiles:
        keep2, send2 = [
            jnp.concatenate(
                [
                    wide[:, :, : depth + hidden],
                    part.reshape(lay.plane, lay.rep, 4, own, depth).transpose(0, 1, 3, 2, 4).reshape(lay.plane, -1, 4 * depth),
                ],
                axis=2,
            )
            for wide, part in zip((keep2, send2), deep_out)
        ]
    chip2 = lay.to_core(send2)
    dox = mixed_back(middle_low, mixed, out_weight)
    keep2, chip2 = after([keep2, chip2], [dox])
    own2, *low2 = chip_sum(twin, keep2, chip2)
    got2 = send_over(twin, low2, False)
    (dox,) = after([dox], low2)
    packed = attend_back(qx, kx, vx, dox)
    input_gradient, first_norms = input_back(plain, x, packed, gains, middle_grad, pieces1)
    keep1, send1 = project_back(plain, x, packed, gains, first_norms, second_norms, own)
    own2, send1, *got2 = after([own2, send1, *got2], [])
    own2, *low2 = plane_sum(twin, own2, got2)
    got2 = send_over(twin, low2, True)
    own1, *low1 = chip_sum(plain, keep1, lay.to_core(send1))
    got1 = send_over(plain, low1, False)
    (middle,) = after([middle], low1)
    outputs, input_gradient = finish(begin, middle, active, contract_all, input_gradient, rows)
    own1, *got1 = after([own1, *got1], [outputs])
    spans = [[(0, own, (0, depth))], [(0, own, (depth, depth + hidden))]]
    spans.append([(j * own, own, (depth + hidden + j * depth, depth + hidden + (j + 1) * depth)) for j in range(4)])
    momenta2, variances2, directions2, sums2 = moments(
        spans, (1, 2, 3), [own2, *got2], [], 1, masters[1:4],
        (moment_out, moment_expand, moment_contract), (square_out, square_expand, square_contract),
    )
    own1, *low1 = plane_sum(plain, own1, got1)
    got1 = send_over(plain, low1, True)
    momenta1, variances1, directions1, sums1 = moments(
        [[(0, own, (0, width))], [(0, 4, (width, width + 4, True))]], (0, 4), [own1, *got1], [sums2], count, (attend_in, layer_norms),
        (moment_in, moment_norms), (square_in, square_norms),
    )
    sums = exchange(lay, sums1)
    directions = (directions1[0], *directions2, directions1[1])
    updated, trust_table = update(sums, masters, directions)
    momenta = (momenta1[0], *momenta2, momenta1[1])
    variances = (variances1[0], *variances2, variances1[1])
    return (outputs[None], input_gradient[None], *updated, *momenta, *variances, trust_table)


def solution(mesh):
    placed = (
        P(("dp", "rep"), None, None),
        P(("dp", "rep"), None),
        P(("dp", "rep"), None, None),
        P(("dp", "rep"), None),
        P(("dp", "rep"), None),
        P(("dp", "rep"), None),
        P(("dp", "rep"), None),
        P(None, ("dp", "rep")),
        P(("dp", "rep"), None),
        P(("dp", "rep"), None),
        P(("dp", "rep"), None),
        P(("dp", "rep"), None),
        P(None, ("dp", "rep")),
        P(("dp", "rep"), None),
        P(("dp", "rep"), None),
        P(("dp", "rep"), None),
        P(("dp", "rep"), None),
        P(None, ("dp", "rep")),
    )
    return jax.shard_map(
        partial(body, (Layout(mesh, False), Layout(mesh, True))),
        mesh=mesh,
        in_specs=placed,
        out_specs=(
            P(("dp", "rep"), None, None),
            P(("dp", "rep"), None, None),
            P(("dp", "rep"), None),
            P(("dp", "rep"), None),
            P(("dp", "rep"), None),
            P(("dp", "rep"), None),
            P(None, ("dp", "rep")),
            P(("dp", "rep"), None),
            P(("dp", "rep"), None),
            P(("dp", "rep"), None),
            P(("dp", "rep"), None),
            P(None, ("dp", "rep")),
            P(("dp", "rep"), None),
            P(("dp", "rep"), None),
            P(("dp", "rep"), None),
            P(("dp", "rep"), None),
            P(None, ("dp", "rep")),
            P(),
        ),
        check_vma=False,
    )
```

```python
from functools import partial
import math

import jax
import jax.numpy as jnp
from jax import lax
from jax.experimental import pallas as pl
from jax.experimental.pallas import tpu as pltpu
from jax.sharding import PartitionSpec as P

HEADS = 8
HEAD_DIM = 64


EPSILON = 1e-05
ADAM_EPSILON = 1e-06
DECAY = 0.01
RATE = 0.5
BETA = 0.5
LANES = 128
HALF = 64
BIG = 1e30
FEATS = 4
TILE = 256
THIN = 32
CHUNK = 352
DEEP_CHUNK = 528
GELU_ONE = 0.7978845608028654
GELU_CUBE = 0.044715 * GELU_ONE
VMEM = pltpu.MemorySpace.VMEM
AXES = ("dp", "rep")


def params(mebibytes):
    return pltpu.CompilerParams(vmem_limit_bytes=mebibytes * 1024 * 1024)


def dot(a, b, ca, cb):
    return lax.dot_general(a, b, (((ca,), (cb,)), ((), ())), preferred_element_type=jnp.float32)


def normalize(values):
    center = values - jnp.mean(values, axis=-1, keepdims=True)
    scale = lax.rsqrt(jnp.mean(center * center, axis=-1, keepdims=True) + EPSILON)
    return center * scale, scale


class Layout:
    def __init__(self, mesh, mixed):
        self.dp = mesh.shape["dp"]
        self.rep = mesh.shape["rep"]
        self.plane = self.dp // 2
        self.mixed = mixed and self.plane == self.rep

    def pairs(self, move):
        pairs = []
        for p in range(self.plane):
            for c in range(2):
                for z in range(self.rep):
                    q, d, w = move(p, c, z)
                    pairs.append(((p * 2 + c) * self.rep + z, (q * 2 + d) * self.rep + w))
        return pairs

    def over(self, value, i, first):
        def move(p, c, z):
            along_z = (first == (c == 0)) if self.mixed else first
            return (p, c, (z + i) % self.rep) if along_z else (p ^ i, c, z)

        return lax.ppermute(value, AXES, self.pairs(move))

    def to_core(self, value):
        return lax.ppermute(value, AXES, self.pairs(lambda p, c, z: (p, 1 - c, z)))

    def core(self):
        return lax.rem(lax.axis_index("dp"), 2)

    def partner(self, side, i, first, sign):
        along_z = lax.rem(lax.axis_index("rep") + (sign * i) % self.rep, self.rep)
        in_plane = lax.div(lax.axis_index("dp"), 2) ^ i
        if not self.mixed:
            return along_z if first else in_plane
        return jnp.where(side == 0, along_z, in_plane) if first else jnp.where(side == 0, in_plane, along_z)

    def device(self, side, second, first):
        plain = (2 * second + side) * self.rep + first
        return jnp.where(side == 0, plain, (2 * first + side) * self.rep + second) if self.mixed else plain


def row_blocks(lay, side, second, rows):
    firsts = lay.rep
    if lay.mixed:
        return [(j * rows, pl.multiple_of(lay.device(side, second, j) * rows, rows), rows) for j in range(firsts)]
    return [(0, pl.multiple_of(lay.device(side, second, 0) * rows, firsts * rows), firsts * rows)]


def assemble(lay, pieces, full_ref, columns):
    count = len(pieces) // 2
    for i, piece in enumerate(pieces):
        side = lay.core() if i < count else 1 - lay.core()
        second = lay.partner(side, i % count, False, -1)
        for at, to, rows in row_blocks(lay, side, second, piece.shape[0] // lay.rep):
            full_ref[pl.ds(to, rows), :] = piece[at : at + rows, columns]


def assemble_deep(lay, pieces, full_ref, first):
    count = len(pieces) // 2
    width = full_ref.shape[1]
    for i, piece in enumerate(pieces):
        side = lay.core() if i < count else 1 - lay.core()
        second = lay.partner(side, i % count, False, -1)
        rows = piece.shape[0] // lay.rep
        for z in range(lay.rep):
            to = pl.multiple_of(lay.device(side, second, z) * 4 * rows, 4 * rows)
            for j in range(4):
                source = piece[z * rows : (z + 1) * rows, first + j * width : first + (j + 1) * width]
                full_ref[pl.ds(to + j * rows, rows), :] = source


def split_rows(lay, full_ref, keep_ref, send_ref, lanes):
    for target, side in ((keep_ref, lay.core()), (send_ref, 1 - lay.core())):
        for second in range(target.shape[0]):
            for at, source, rows in row_blocks(lay, side, second, target.shape[1] // lay.rep):
                target[second, at : at + rows, lanes] = full_ref[pl.ds(source, rows), :].astype(target.dtype)


def split_deep(lay, full_ref, keep_ref, send_ref, first):
    width = full_ref.shape[1]
    rows = keep_ref.shape[1] // lay.rep
    for target, side in ((keep_ref, lay.core()), (send_ref, 1 - lay.core())):
        for second in range(target.shape[0]):
            for z in range(lay.rep):
                source = pl.multiple_of(lay.device(side, second, z) * 4 * rows, 4 * rows)
                for j in range(4):
                    part = full_ref[pl.ds(source + j * rows, rows), :]
                    columns = slice(first + j * width, first + (j + 1) * width)
                    target[second, z * rows : (z + 1) * rows, columns] = part.astype(target.dtype)


def row_chunks(rows, size):
    return [(at, min(size, rows - at)) for at in range(0, rows, size)]


def windows(rows):
    half = (rows - THIN) // 2
    span = half + THIN
    spans = [(at, TILE, 0, span) for at in range(0, half, TILE)]
    spans.append((half, THIN, 0, rows))
    return spans + [(at, TILE, half, span) for at in range(span, rows, TILE)]


def arrange_kernel(inputs, cotangent, segments, x, dy, labels, begin, room):
    tokens = segments.shape[1]
    half = tokens // 2
    memory = inputs.shape[0] - tokens
    segment = segments[...].astype(jnp.float32)
    ahead = pltpu.roll(jnp.broadcast_to(segment, (8, tokens)), tokens - half + 1, 1)[:1]
    lane = lax.broadcasted_iota(jnp.int32, (1, tokens), 1)
    fits = (segment == ahead) & (lane <= half)
    start = jnp.sum(jnp.where(fits, lane.astype(jnp.float32), 0.0), axis=1, keepdims=True)
    begin[...] = jnp.broadcast_to(start, begin.shape)
    row = lax.broadcasted_iota(jnp.int32, (half, LANES), 0).astype(jnp.float32)
    early = row < start
    thin = lax.broadcasted_iota(jnp.int32, (THIN, LANES), 0) < memory
    for source, target in ((inputs, x), (cotangent, dy)):
        for at in range(0, inputs.shape[1], LANES):
            columns = slice(at, at + LANES)
            room[: inputs.shape[0]] = source[:, columns].astype(jnp.float32)
            left, right = room[memory : memory + half], room[memory + half : memory + tokens]
            target[:half, columns] = jnp.where(early, right, left).astype(target.dtype)
            target[half : half + THIN, columns] = jnp.where(thin, room[:THIN], 0.0).astype(target.dtype)
            target[half + THIN :, columns] = jnp.where(early, left, right).astype(target.dtype)
    left = jnp.transpose(jnp.broadcast_to(segment[:, :half], (LANES, half)))
    right = jnp.transpose(jnp.broadcast_to(segment[:, half:], (LANES, half)))
    labels[:half] = jnp.where(early, right, left).astype(jnp.int32)
    labels[half : half + THIN] = jnp.where(thin, -1, -2)
    labels[half + THIN :] = jnp.where(early, left, right).astype(jnp.int32)


def arrange(inputs, cotangent, segments):
    width = inputs.shape[1]
    rows = segments.shape[1] + THIN
    return pl.pallas_call(
        arrange_kernel,
        out_shape=(
            jax.ShapeDtypeStruct((rows, width), inputs.dtype),
            jax.ShapeDtypeStruct((rows, width), inputs.dtype),
            jax.ShapeDtypeStruct((rows, LANES), jnp.int32),
            jax.ShapeDtypeStruct((8, LANES), jnp.float32),
        ),
        in_specs=[pl.BlockSpec(memory_space=VMEM)] * 3,
        out_specs=[pl.BlockSpec(memory_space=VMEM)] * 4,
        scratch_shapes=[pltpu.VMEM((rows, LANES), jnp.float32)],
        compiler_params=params(8),
        name="arrange",
    )(inputs, cotangent, segments)


def finish_kernel(begin, middle, active, contract, grad_in, outputs, grad_out, room):
    rows = outputs.shape[0]
    half = (middle.shape[0] - THIN) // 2
    memory = rows - 2 * half
    wide = room.shape[1]
    row = lax.broadcasted_iota(jnp.int32, (half, wide), 0).astype(jnp.float32)
    early = row < begin[:1, :1]

    def place(value, target, columns):
        left, right = value[:half], value[half + THIN :]
        room[:THIN] = value[half : half + THIN]
        room[memory : memory + half] = jnp.where(early, right, left)
        room[memory + half : rows] = jnp.where(early, left, right)
        target[:, columns] = room[:rows].astype(target.dtype)

    for at in range(0, middle.shape[1], wide):
        columns = slice(at, at + wide)
        place(middle[:, columns] + dot(active[...], contract[:, columns], 1, 0), outputs, columns)
        place(grad_in[:, columns].astype(jnp.float32), grad_out, columns)


def finish(begin, middle, active, contract, grad_in, rows):
    width = middle.shape[1]
    return pl.pallas_call(
        finish_kernel,
        out_shape=[jax.ShapeDtypeStruct((rows, width), grad_in.dtype)] * 2,
        in_specs=[pl.BlockSpec(memory_space=VMEM)] * 5,
        out_specs=[pl.BlockSpec(memory_space=VMEM)] * 2,
        scratch_shapes=[pltpu.VMEM((middle.shape[0], 256), jnp.float32)],
        compiler_params=params(10),
        name="finish",
    )(begin, middle, active, contract, grad_in)


def attend_kernel(lay, count, x, labels, *refs):
    pieces = refs[:count]
    qx, kx, vx, mixed, gains, weight, qs = refs[count:]
    rows = x.shape[0]
    width = mixed.shape[1]
    assemble(lay, pieces, weight, slice(None))
    gains[...] = jnp.transpose(weight[:, 3 * width :].astype(jnp.float32))[:8]
    gain, bias = gains[0:1], gains[1:2]

    def one_chunk(i, carry):
        span = pl.ds(pl.multiple_of(i * CHUNK, CHUNK), CHUNK)
        normed, _ = normalize(x[span].astype(jnp.float32))
        first = (normed * gain + bias).astype(jnp.bfloat16)
        lane = lax.broadcasted_iota(jnp.int32, (CHUNK, LANES), 1)
        low = lane < HALF
        feature = lane % HALF
        label = labels[span]
        blocked = ((feature < FEATS) & (label >= 0) & (feature != label)) | (feature == FEATS)
        query_side = jnp.where(blocked, -BIG, 0.0)
        marked = ((feature < FEATS) & (feature == label)) | ((feature == FEATS) & (label == -2))
        key_side = jnp.where(marked | (feature > FEATS), 1.0, 0.0)
        sides = (query_side, key_side, jnp.ones_like(key_side))
        for kind, target in enumerate((qs, kx, vx)):
            whole = dot(first, weight[:, kind * width : (kind + 1) * width], 1, 0)
            whole = whole.astype(jnp.bfloat16).astype(jnp.float32)
            for pair in range(width // LANES):
                part = whole[:, pair * LANES : (pair + 1) * LANES]
                if kind == 0:
                    part = part * (1.0 / math.sqrt(HEAD_DIM))
                at = 2 * pair * LANES
                target[span, at : at + LANES] = jnp.where(low, part, sides[kind]).astype(jnp.bfloat16)
                target[span, at + LANES : at + 2 * LANES] = jnp.where(low, sides[kind], part).astype(jnp.bfloat16)
        return carry

    lax.fori_loop(0, rows // CHUNK, one_chunk, 0)

    def one_pair(pair, carry):
        columns = pl.ds(pl.multiple_of(pair * LANES, LANES), LANES)
        for at, size, key_at, key_size in windows(rows):
            span = pl.ds(at, size)
            seen = pl.ds(key_at, key_size)
            lane = lax.broadcasted_iota(jnp.int32, (size, LANES), 1)
            low = lane < HALF
            feature = lane % HALF
            got = []
            for side in range(2):
                head = pl.ds(pl.multiple_of((2 * pair + side) * LANES, LANES), LANES)
                queries = qs[span, head]
                scores = dot(queries, kx[seen, head], 1, 1)
                highest = jnp.max(scores, axis=1, keepdims=True)
                raised = jnp.exp(scores - highest).astype(jnp.bfloat16)
                found = dot(raised, vx[seen, head], 1, 0)
                total = -(highest + jnp.log(found))
                first = total.astype(jnp.bfloat16).astype(jnp.float32)
                second = (total - first).astype(jnp.bfloat16).astype(jnp.float32)
                third = total - first - second
                values = jnp.where(feature == 5, first, jnp.where(feature == 6, second, third))
                place = (feature > FEATS) & (feature < 8) & (low if side else ~low)
                qx[span, head] = jnp.where(place, values, queries.astype(jnp.float32)).astype(jnp.bfloat16)
                got.append(found)
            over = pltpu.roll(jnp.where(low, got[1], got[0]), HALF, 1)
            mixed[span, columns] = (jnp.where(low, got[0], got[1]) / over).astype(jnp.bfloat16)
        return carry

    lax.fori_loop(0, width // LANES, one_pair, 0)


def attend(lay, x, labels, pieces):
    rows, width = x.shape
    wide = jax.ShapeDtypeStruct((rows, 2 * width), jnp.bfloat16)
    depth = len(pieces) * pieces[0].shape[0]
    return pl.pallas_call(
        partial(attend_kernel, lay, len(pieces)),
        out_shape=(
            wide,
            wide,
            wide,
            jax.ShapeDtypeStruct((rows, width), jnp.bfloat16),
            jax.ShapeDtypeStruct((8, width), jnp.float32),
        ),
        in_specs=[pl.BlockSpec(memory_space=VMEM)] * (2 + len(pieces)),
        out_specs=[pl.BlockSpec(memory_space=VMEM)] * 5,
        scratch_shapes=[
            pltpu.VMEM((depth, pieces[0].shape[1]), jnp.bfloat16),
            pltpu.VMEM((rows, 2 * width), jnp.bfloat16),
        ],
        compiler_params=params(16),
        name="attend",
    )(x, labels, *pieces)


def attend_back_kernel(qx, kx, vx, dox, packed, total):
    rows = qx.shape[0]
    width = packed.shape[1] // 3

    def one_pair(pair, carry):
        heads = [pl.ds(pl.multiple_of((2 * pair + side) * LANES, LANES), LANES) for side in range(2)]
        spots = [pl.ds(pl.multiple_of(kind * width + pair * LANES, LANES), LANES) for kind in range(3)]
        total[...] = jnp.zeros_like(total)
        for at, size, query_at, query_size in windows(rows):
            span = pl.ds(at, size)
            seen = pl.ds(query_at, query_size)
            low = lax.broadcasted_iota(jnp.int32, (size, LANES), 1) < HALF
            got = []
            for side in range(2):
                head = heads[side]
                keys = kx[span, head]
                queries = qx[seen, head]
                upstream = dox[seen, head]
                attention = jnp.exp(dot(keys, queries, 1, 1))
                grad = dot(vx[span, head], upstream, 1, 1)
                scores = (attention * grad).astype(jnp.bfloat16)
                got.append((dot(scores, queries, 1, 0), dot(attention.astype(jnp.bfloat16), upstream, 1, 0)))
                total[side, seen] += dot(scores, keys, 0, 0)
            packed[span, spots[1]] = jnp.where(low, got[0][0], got[1][0]).astype(jnp.bfloat16)
            packed[span, spots[2]] = jnp.where(low, got[0][1], got[1][1]).astype(jnp.bfloat16)
        low = lax.broadcasted_iota(jnp.int32, (rows, LANES), 1) < HALF
        packed[:, spots[0]] = (jnp.where(low, total[0], total[1]) * (1.0 / math.sqrt(HEAD_DIM))).astype(jnp.bfloat16)
        return carry

    lax.fori_loop(0, width // LANES, one_pair, 0)


def attend_back(qx, kx, vx, dox):
    rows, wide = qx.shape
    return pl.pallas_call(
        attend_back_kernel,
        out_shape=jax.ShapeDtypeStruct((rows, 3 * wide // 2), jnp.bfloat16),
        in_specs=[pl.BlockSpec(memory_space=VMEM)] * 4,
        out_specs=pl.BlockSpec(memory_space=VMEM),
        scratch_shapes=[pltpu.VMEM((2, rows, LANES), jnp.float32)],
        compiler_params=params(16),
        name="attend_back",
    )(qx, kx, vx, dox)


def norm_back(grad, normed, scale, gain):
    scaled = grad * gain
    return scale * (
        scaled
        - jnp.mean(scaled, axis=-1, keepdims=True)
        - normed * jnp.mean(scaled * normed, axis=-1, keepdims=True)
    )


def feed_kernel(lay, count, deep_count, x, mixed, dy, gains, *refs):
    pieces = refs[:count]
    deep_pieces = refs[count : count + deep_count]
    outs = refs[count + deep_count : -5]
    middle, middle_grad, middle_low, active, contract, out_weight, keep2, send2, norm_grads, *deep_out = outs
    wide, hidden_grad, second, block, deep_block = refs[-5:]
    rows, width = x.shape
    hidden = contract.shape[0]
    assemble(lay, pieces, wide, slice(0, width + hidden))
    if deep_count:
        assemble(lay, deep_pieces, contract, slice(None))
    else:
        assemble_deep(lay, pieces, contract, width + hidden)
    out_weight[...] = wide[:, :width]
    gain, bias = gains[2:3], gains[3:4]
    zero = jnp.zeros((1, width), jnp.float32)

    def one_chunk(i, carry):
        gain_sum, bias_sum = carry
        span = pl.ds(i * DEEP_CHUNK, DEEP_CHUNK)
        start = x[span].astype(jnp.float32) + dot(mixed[span], wide[:, :width], 1, 0)
        middle[span] = start
        normed, scale = normalize(start)
        low = (normed * gain + bias).astype(jnp.bfloat16)
        second[span] = low
        for start in range(0, hidden, 512):
            part = slice(start, start + 512)
            up = dot(low, wide[:, width + start : width + start + 512], 1, 0)
            square = up * up
            half = 0.5 + 0.5 * jnp.tanh(up * (GELU_ONE + GELU_CUBE * square))
            act = up * half
            active[span, part] = act.astype(jnp.bfloat16)
            slope = half + act * ((1.0 - half) * (2.0 * GELU_ONE + 6.0 * GELU_CUBE * square))
            hidden_grad[span, part] = (dot(dy[span], contract[part], 1, 1) * slope).astype(jnp.bfloat16)
        back = dot(hidden_grad[span], wide[:, width:], 1, 1)
        gain_sum = gain_sum + jnp.sum(back * normed, axis=0, keepdims=True)
        bias_sum = bias_sum + jnp.sum(back, axis=0, keepdims=True)
        grad = dy[span].astype(jnp.float32) + norm_back(back, normed, scale, gain)
        middle_grad[span] = grad
        middle_low[span] = grad.astype(jnp.bfloat16)
        return gain_sum, bias_sum

    sums = (zero, zero)
    for i in range(rows // DEEP_CHUNK):
        sums = one_chunk(i, sums)
    gain_sum, bias_sum = sums
    norm_grads[...] = jnp.concatenate([gain_sum, bias_sum, jnp.zeros((6, width), jnp.float32)], axis=0)

    def one_block(i, carry):
        columns = pl.ds(pl.multiple_of(i * 512, 512), 512)
        deep_block[columns] = dot(active[:, columns], dy[...], 0, 0)
        block[...] = dot(second[...], hidden_grad[:, columns], 0, 0)
        split_rows(lay, block, keep2, send2, pl.ds(pl.multiple_of(width + i * 512, 512), 512))
        return carry

    lax.fori_loop(0, hidden // 512, one_block, 0)
    if deep_count:
        split_rows(lay, deep_block, *deep_out, slice(0, width))
    else:
        split_deep(lay, deep_block, keep2, send2, width + hidden)
    block[...] = dot(mixed[...], middle_low[...], 0, 0)
    split_rows(lay, block, keep2, send2, slice(0, width))


def feed(lay, x, mixed, dy, gains, pieces, deep_pieces):
    rows, width = x.shape
    plane = len(pieces) // 2
    deep = pieces[0].shape[0]
    columns = pieces[0].shape[1]
    hidden = 4 * width
    out_shape = [
        jax.ShapeDtypeStruct((rows, width), jnp.float32),
        jax.ShapeDtypeStruct((rows, width), jnp.float32),
        jax.ShapeDtypeStruct((rows, width), jnp.bfloat16),
        jax.ShapeDtypeStruct((rows, hidden), jnp.bfloat16),
        jax.ShapeDtypeStruct((hidden, width), jnp.bfloat16),
        jax.ShapeDtypeStruct((width, width), jnp.bfloat16),
        jax.ShapeDtypeStruct((plane, deep, columns), jnp.bfloat16),
        jax.ShapeDtypeStruct((plane, deep, columns), jnp.bfloat16),
        jax.ShapeDtypeStruct((8, width), jnp.float32),
    ]
    if deep_pieces:
        out_shape.append(jax.ShapeDtypeStruct((plane, 4 * deep, width), jnp.bfloat16))
        out_shape.append(jax.ShapeDtypeStruct((plane, 4 * deep, width), jnp.bfloat16))
    return pl.pallas_call(
        partial(feed_kernel, lay, len(pieces), len(deep_pieces)),
        out_shape=out_shape,
        in_specs=[pl.BlockSpec(memory_space=VMEM)] * (4 + len(pieces) + len(deep_pieces)),
        out_specs=[pl.BlockSpec(memory_space=VMEM)] * len(out_shape),
        scratch_shapes=[
            pltpu.VMEM((width, width + hidden), jnp.bfloat16),
            pltpu.VMEM((rows, hidden), jnp.bfloat16),
            pltpu.VMEM((rows, width), jnp.bfloat16),
            pltpu.VMEM((width, 512), jnp.float32),
            pltpu.VMEM((hidden, width), jnp.float32),
        ],
        compiler_params=params(26),
        name="feed",
    )(x, mixed, dy, gains, *pieces, *deep_pieces)


def mixed_back_kernel(middle_low, mixed, out_weight, dox):
    rows, width = mixed.shape

    def one_chunk(i, carry):
        span = pl.ds(pl.multiple_of(i * DEEP_CHUNK, DEEP_CHUNK), DEEP_CHUNK)
        mixed_grad = dot(middle_low[span], out_weight[...], 1, 1).astype(jnp.bfloat16).astype(jnp.float32)
        lane = lax.broadcasted_iota(jnp.int32, (DEEP_CHUNK, LANES), 1)
        left = lane < HALF
        feature = lane % HALF
        for pair in range(width // LANES):
            columns = slice(pair * LANES, (pair + 1) * LANES)
            piece = mixed_grad[:, columns]
            product = piece * mixed[span, columns].astype(jnp.float32)
            for side in range(2):
                mine = left if side == 0 else ~left
                delta = -jnp.sum(jnp.where(mine, product, 0.0), axis=1, keepdims=True)
                one = delta.astype(jnp.bfloat16).astype(jnp.float32)
                two = (delta - one).astype(jnp.bfloat16).astype(jnp.float32)
                three = delta - one - two
                extra = jnp.where(feature == 0, one, jnp.where(feature == 1, two, jnp.where(feature == 2, three, 0.0)))
                head = (2 * pair + side) * LANES
                dox[span, head : head + LANES] = jnp.where(mine, piece, extra).astype(jnp.bfloat16)
        return carry

    lax.fori_loop(0, rows // DEEP_CHUNK, one_chunk, 0)


def mixed_back(middle_low, mixed, out_weight):
    rows, width = mixed.shape
    return pl.pallas_call(
        mixed_back_kernel,
        out_shape=jax.ShapeDtypeStruct((rows, 2 * width), jnp.bfloat16),
        in_specs=[pl.BlockSpec(memory_space=VMEM)] * 3,
        out_specs=pl.BlockSpec(memory_space=VMEM),
        compiler_params=params(10),
        name="mixed_back",
    )(middle_low, mixed, out_weight)


def project_back_kernel(lay, x, packed, gains, first_norms, second_norms, keep, send, first, block):
    rows, width = x.shape
    gain, bias = gains[0:1], gains[1:2]

    def one_chunk(i, carry):
        span = pl.ds(i * CHUNK, CHUNK)
        normed, _ = normalize(x[span].astype(jnp.float32))
        first[span] = (normed * gain + bias).astype(jnp.bfloat16)
        return carry

    for i in range(rows // CHUNK):
        one_chunk(i, 0)

    def one_block(i, carry):
        columns = pl.ds(pl.multiple_of(i * 512, 512), 512)
        block[...] = dot(first[...], packed[:, columns], 0, 0)
        split_rows(lay, block, keep, send, columns)
        return carry

    lax.fori_loop(0, packed.shape[1] // 512, one_block, 0)
    fill = jnp.zeros((LANES - 4, width), jnp.float32)
    norms = jnp.concatenate([first_norms[:2], second_norms[:2], fill], axis=0)
    block[:, :LANES] = jnp.transpose(norms)
    split_rows(lay, block.at[:, :LANES], keep, send, slice(packed.shape[1], packed.shape[1] + LANES))


def project_back(lay, x, packed, gains, first_norms, second_norms, own):
    rows, width = x.shape
    shape = (lay.plane, lay.rep * own, packed.shape[1] + LANES)
    return pl.pallas_call(
        partial(project_back_kernel, lay),
        out_shape=(jax.ShapeDtypeStruct(shape, jnp.bfloat16), jax.ShapeDtypeStruct(shape, jnp.bfloat16)),
        in_specs=[pl.BlockSpec(memory_space=VMEM)] * 5,
        out_specs=[pl.BlockSpec(memory_space=VMEM)] * 2,
        scratch_shapes=[pltpu.VMEM((rows, width), jnp.bfloat16), pltpu.VMEM((width, 512), jnp.float32)],
        compiler_params=params(10),
        name="project_back",
    )(x, packed, gains, first_norms, second_norms)


def input_back_kernel(lay, x, packed, gains, middle_grad, *refs):
    pieces = refs[:-3]
    grad_in, norm_grads, weight = refs[-3:]
    rows, width = x.shape
    assemble(lay, pieces, weight, slice(None))
    gain = gains[0:1]
    zero = jnp.zeros((1, width), jnp.float32)

    def one_chunk(i, carry):
        gain_sum, bias_sum = carry
        span = pl.ds(i * CHUNK, CHUNK)
        normed, scale = normalize(x[span].astype(jnp.float32))
        back = dot(packed[span], weight[:, : 3 * width], 1, 1)
        grad_in[span] = (middle_grad[span] + norm_back(back, normed, scale, gain)).astype(jnp.bfloat16)
        gain_sum = gain_sum + jnp.sum(back * normed, axis=0, keepdims=True)
        return gain_sum, bias_sum + jnp.sum(back, axis=0, keepdims=True)

    sums = (zero, zero)
    for i in range(rows // CHUNK):
        sums = one_chunk(i, sums)
    gain_sum, bias_sum = sums
    norm_grads[...] = jnp.concatenate([gain_sum, bias_sum, jnp.zeros((6, width), jnp.float32)], axis=0)


def input_back(lay, x, packed, gains, middle_grad, pieces):
    rows, width = x.shape
    return pl.pallas_call(
        partial(input_back_kernel, lay),
        out_shape=(jax.ShapeDtypeStruct((rows, width), jnp.bfloat16), jax.ShapeDtypeStruct((8, width), jnp.float32)),
        in_specs=[pl.BlockSpec(memory_space=VMEM)] * (4 + len(pieces)),
        out_specs=[pl.BlockSpec(memory_space=VMEM)] * 2,
        scratch_shapes=[pltpu.VMEM((width, pieces[0].shape[1]), jnp.bfloat16)],
        compiler_params=params(10),
        name="input_back",
    )(x, packed, gains, middle_grad, *pieces)


def pack_kernel(weight, norms, out):
    rows, width = weight.shape
    out[:, :width] = weight[...].astype(out.dtype)
    same = lax.broadcasted_iota(jnp.int32, (rows, rows), 0) == lax.broadcasted_iota(jnp.int32, (rows, rows), 1)
    lane = lax.broadcasted_iota(jnp.int32, (rows, LANES), 1)
    tile = jnp.zeros((rows, LANES), jnp.float32)
    for j in range(norms.shape[0]):
        column = jnp.sum(jnp.where(same, norms[j : j + 1, :], 0.0), axis=1, keepdims=True)
        tile = jnp.where(lane == j, column, tile)
    out[:, width:] = tile.astype(out.dtype)


def pack(weight, norms):
    rows, width = weight.shape
    return pl.pallas_call(
        pack_kernel,
        out_shape=jax.ShapeDtypeStruct((rows, width + LANES), jnp.bfloat16),
        in_specs=[pl.BlockSpec(memory_space=VMEM)] * 2,
        out_specs=pl.BlockSpec(memory_space=VMEM),
        compiler_params=params(4),
        name="pack",
    )(weight, norms)


def column_kernel(lay, *refs):
    out = refs[-1]
    got = [ref[...].astype(jnp.float32) for ref in refs[:-1]]
    parts = []
    for j in range(len(got)):
        part = got[0]
        for i in range(1, len(got)):
            part = jnp.where(lay.partner(lay.core(), i, True, -1) == j, got[i], part)
        parts.append(part)
    out[...] = jnp.concatenate(parts, axis=0).astype(out.dtype)


def column_of(lay, shards):
    rows, cols = shards[0].shape
    return pl.pallas_call(
        partial(column_kernel, lay),
        out_shape=jax.ShapeDtypeStruct((len(shards) * rows, cols), shards[0].dtype),
        in_specs=[pl.BlockSpec(memory_space=VMEM)] * len(shards),
        out_specs=pl.BlockSpec(memory_space=VMEM),
        compiler_params=params(4),
        name="column",
    )(*shards)


def chip_sum_kernel(lay, keep, got, *outs):
    for i, ref in enumerate(outs):
        at = lay.partner(lay.core(), i, False, 1)
        ref[...] = (keep[at].astype(jnp.float32) + got[at].astype(jnp.float32)).astype(ref.dtype)


def chip_sum(lay, keep, got):
    plane, rows, cols = keep.shape
    return pl.pallas_call(
        partial(chip_sum_kernel, lay),
        out_shape=[jax.ShapeDtypeStruct((rows, cols), jnp.float32)]
        + [jax.ShapeDtypeStruct((rows, cols), jnp.bfloat16)] * (plane - 1),
        in_specs=[pl.BlockSpec(memory_space=VMEM)] * 2,
        out_specs=[pl.BlockSpec(memory_space=VMEM)] * plane,
        compiler_params=params(14),
        name="chip_sum",
    )(keep, got)


def plane_sum_kernel(lay, own, *refs):
    got, outs = refs[: lay.plane - 1], refs[lay.plane - 1 :]
    rows = outs[0].shape[0]
    total = own[...]
    for ref in got:
        total = total + ref[...].astype(jnp.float32)
    for i, ref in enumerate(outs):
        at = lay.partner(lay.core(), i, True, 1)
        part = total[:rows]
        for j in range(1, lay.rep):
            part = jnp.where(at == j, total[j * rows : (j + 1) * rows], part)
        ref[...] = part.astype(ref.dtype)


def plane_sum(lay, own, got):
    rows, cols = own.shape
    reps = lay.rep
    return pl.pallas_call(
        partial(plane_sum_kernel, lay),
        out_shape=[jax.ShapeDtypeStruct((rows // reps, cols), jnp.float32)]
        + [jax.ShapeDtypeStruct((rows // reps, cols), jnp.bfloat16)] * (reps - 1),
        in_specs=[pl.BlockSpec(memory_space=VMEM)] * (1 + len(got)),
        out_specs=[pl.BlockSpec(memory_space=VMEM)] * reps,
        compiler_params=params(10),
        name="plane_sum",
    )(own, *got)


def full_sum(value):
    return jnp.sum(jnp.sum(value, axis=1, keepdims=True), axis=0, keepdims=True)


def turned(columns):
    rows, count = columns.shape
    same = lax.broadcasted_iota(jnp.int32, (rows, rows), 0) == lax.broadcasted_iota(jnp.int32, (rows, rows), 1)
    line = lax.broadcasted_iota(jnp.int32, (count, rows), 0)
    out = jnp.zeros((count, rows), jnp.float32)
    for j in range(count):
        row = jnp.sum(jnp.where(same, columns[:, j : j + 1], 0.0), axis=0, keepdims=True)
        out = jnp.where(line == j, row, out)
    return out


def moments_kernel(pieces_of, first_index, reps, more, *refs):
    n = len(pieces_of)
    grads, others, arrays = refs[:reps], refs[reps : reps + more], refs[reps + more :]
    total = grads[0][...]
    for ref in grads[1:]:
        total = total + ref[...].astype(jnp.float32)
    weights, firsts, seconds = arrays[:n], arrays[n : 2 * n], arrays[2 * n : 3 * n]
    momenta, variances, directions = arrays[3 * n : 4 * n], arrays[4 * n : 5 * n], arrays[5 * n : 6 * n]
    sums = arrays[6 * n]
    lane = lax.broadcasted_iota(jnp.int32, (1, LANES), 1)
    row = others[0][0] if more else jnp.zeros((1, LANES), jnp.float32)
    for i, parts in enumerate(pieces_of):
        weight_sum = jnp.zeros((1, 1), jnp.float32)
        step_sum = jnp.zeros((1, 1), jnp.float32)
        for at, size, columns in parts:
            rows = slice(at, at + size)
            gradient = total[:, columns[0] : columns[1]]
            if len(columns) > 2:
                gradient = turned(gradient)
            weight = weights[i][rows]
            momentum = BETA * firsts[i][rows] + (1.0 - BETA) * gradient
            variance = BETA * seconds[i][rows] + (1.0 - BETA) * gradient * gradient
            direction = momentum / (jnp.sqrt(variance) + ADAM_EPSILON) + DECAY * weight
            momenta[i][rows] = momentum
            variances[i][rows] = variance
            directions[i][rows] = direction
            weight_sum = weight_sum + full_sum(weight * weight)
            step_sum = step_sum + full_sum(direction * direction)
        row = jnp.where(lane == first_index[i], weight_sum, row)
        row = jnp.where(lane == 5 + first_index[i], step_sum, row)
    sums[...] = jnp.broadcast_to(row, sums.shape)


def moments(pieces_of, first_index, grads, others, copies, weights, firsts, seconds):
    arrays = [*grads, *others, *weights, *firsts, *seconds]
    shapes = [jax.ShapeDtypeStruct(weight.shape, jnp.float32) for weight in weights]
    outs = pl.pallas_call(
        partial(moments_kernel, pieces_of, first_index, len(grads), len(others)),
        out_shape=shapes * 3 + [jax.ShapeDtypeStruct((copies, 1, LANES), jnp.float32)],
        in_specs=[pl.BlockSpec(memory_space=VMEM)] * len(arrays),
        out_specs=[pl.BlockSpec(memory_space=VMEM)] * (3 * len(weights) + 1),
        compiler_params=params(8),
        name="moments",
    )(*arrays)
    n = len(weights)
    return outs[:n], outs[n : 2 * n], outs[2 * n : 3 * n], outs[3 * n]


def update_kernel(n, sums, *refs):
    weights, directions, updated, table = refs[:n], refs[n : 2 * n], refs[2 * n : 3 * n], refs[3 * n]
    norms = jnp.sqrt(jnp.sum(sums[...], axis=0))
    row = lax.broadcasted_iota(jnp.int32, table.shape, 0)
    lane = lax.broadcasted_iota(jnp.int32, table.shape, 1)
    out = jnp.zeros(table.shape, jnp.float32)
    for i in range(n):
        weight_norm = norms[:, i : i + 1]
        step_norm = norms[:, 5 + i : 6 + i]
        ratio = weight_norm / step_norm
        updated[i][...] = weights[i][...] - RATE * ratio * directions[i][...]
        column = jnp.where(row == 0, weight_norm, jnp.where(row == 1, step_norm, ratio))
        out = jnp.where(lane == i, column, out)
    table[...] = out


def update(sums, weights, directions):
    n = len(weights)
    outs = pl.pallas_call(
        partial(update_kernel, n),
        out_shape=[jax.ShapeDtypeStruct(weight.shape, jnp.float32) for weight in weights]
        + [jax.ShapeDtypeStruct((3, n), jnp.float32)],
        in_specs=[pl.BlockSpec(memory_space=VMEM)] * (1 + 2 * n),
        out_specs=[pl.BlockSpec(memory_space=VMEM)] * (n + 1),
        compiler_params=params(6),
        name="update",
    )(sums, *weights, *directions)
    return outs[:n], outs[n]


def over(lay, value, first):
    return [value] + [lay.over(value, i, first) for i in range(1, lay.rep if first else lay.plane)]


def send_over(lay, parts, first):
    return [lay.over(part, i, first) for i, part in enumerate(parts, 1)]


def over_core(lay, blocks):
    return blocks + [lay.to_core(block) for block in blocks]


def after(values, others):
    count = len(values)
    return list(lax.optimization_barrier((*values, *others))[:count])


def exchange(lay, value):
    return lax.all_to_all(value, AXES, 0, 0)


def body(
    lay,
    inputs,
    segments,
    cotangent,
    attend_in,
    attend_out,
    expand,
    contract,
    layer_norms,
    moment_in,
    moment_out,
    moment_expand,
    moment_contract,
    moment_norms,
    square_in,
    square_out,
    square_expand,
    square_contract,
    square_norms,
):
    plain, twin = lay
    lay = plain
    masters = (attend_in, attend_out, expand, contract, layer_norms)
    width = attend_in.shape[1]
    depth = attend_out.shape[1]
    hidden = expand.shape[1]
    own = attend_in.shape[0]
    count = lay.dp * lay.rep
    whole_tiles = own % 16 == 0
    shard1 = pack(attend_in, layer_norms)
    column1 = over(plain, shard1, True)
    rows = inputs.shape[1]
    attend_out_, expand_, contract_ = after([attend_out, expand, contract], [shard1])
    deep = [contract_[j * own : (j + 1) * own] for j in range(4)]
    shard2 = jnp.concatenate([part.astype(jnp.bfloat16) for part in (attend_out_, expand_, *deep)], axis=1)
    (shard2,) = after([shard2], column1[1:])
    column2 = over(twin, shard2, True)
    blocks1 = over(plain, column_of(plain, column1), False)
    (segments_,) = after([segments], blocks1[:1])
    x, dy, labels, begin = arrange(inputs[0], cotangent[0], segments_)
    blocks2 = over(twin, column_of(twin, after(column2, [*blocks1, x])), False)
    pieces1 = over_core(lay, blocks1)
    *pieces1, x, labels = after([*pieces1, x, labels], blocks2[:1])
    qx, kx, vx, mixed, gains = attend(plain, x, labels, pieces1)
    near = lay.to_core(blocks2[0])
    blocks2[1:] = after(blocks2[1:], [mixed])
    pieces2 = [*blocks2, near, *[lay.to_core(block) for block in blocks2[1:]]]
    deep_pieces = []
    if not whole_tiles:
        first = depth + hidden
        for piece in pieces2:
            part = piece[:, first:].reshape(lay.rep, own, 4, depth).transpose(0, 2, 1, 3)
            deep_pieces.append(part.reshape(-1, depth))
    middle, middle_grad, middle_low, active, contract_all, out_weight, keep2, send2, second_norms, *deep_out = feed(
        twin, x, mixed, dy, gains, pieces2, deep_pieces
    )
    if not whole_tiles:
        keep2, send2 = [
            jnp.concatenate(
                [
                    wide[:, :, : depth + hidden],
                    part.reshape(lay.plane, lay.rep, 4, own, depth).transpose(0, 1, 3, 2, 4).reshape(lay.plane, -1, 4 * depth),
                ],
                axis=2,
            )
            for wide, part in zip((keep2, send2), deep_out)
        ]
    chip2 = lay.to_core(send2)
    dox = mixed_back(middle_low, mixed, out_weight)
    keep2, chip2 = after([keep2, chip2], [dox])
    own2, *low2 = chip_sum(twin, keep2, chip2)
    got2 = send_over(twin, low2, False)
    (dox,) = after([dox], low2)
    packed = attend_back(qx, kx, vx, dox)
    input_gradient, first_norms = input_back(plain, x, packed, gains, middle_grad, pieces1)
    keep1, send1 = project_back(plain, x, packed, gains, first_norms, second_norms, own)
    own2, send1, *got2 = after([own2, send1, *got2], [])
    own2, *low2 = plane_sum(twin, own2, got2)
    got2 = send_over(twin, low2, True)
    own1, *low1 = chip_sum(plain, keep1, lay.to_core(send1))
    got1 = send_over(plain, low1, False)
    (middle,) = after([middle], low1)
    outputs, input_gradient = finish(begin, middle, active, contract_all, input_gradient, rows)
    own1, *got1 = after([own1, *got1], [outputs])
    spans = [[(0, own, (0, depth))], [(0, own, (depth, depth + hidden))]]
    spans.append([(j * own, own, (depth + hidden + j * depth, depth + hidden + (j + 1) * depth)) for j in range(4)])
    momenta2, variances2, directions2, sums2 = moments(
        spans, (1, 2, 3), [own2, *got2], [], 1, masters[1:4],
        (moment_out, moment_expand, moment_contract), (square_out, square_expand, square_contract),
    )
    own1, *low1 = plane_sum(plain, own1, got1)
    got1 = send_over(plain, low1, True)
    momenta1, variances1, directions1, sums1 = moments(
        [[(0, own, (0, width))], [(0, 4, (width, width + 4, True))]], (0, 4), [own1, *got1], [sums2], count, (attend_in, layer_norms),
        (moment_in, moment_norms), (square_in, square_norms),
    )
    sums = exchange(lay, sums1)
    directions = (directions1[0], *directions2, directions1[1])
    updated, trust_table = update(sums, masters, directions)
    momenta = (momenta1[0], *momenta2, momenta1[1])
    variances = (variances1[0], *variances2, variances1[1])
    return (outputs[None], input_gradient[None], *updated, *momenta, *variances, trust_table)


def solution(mesh):
    placed = (
        P(("dp", "rep"), None, None),
        P(("dp", "rep"), None),
        P(("dp", "rep"), None, None),
        P(("dp", "rep"), None),
        P(("dp", "rep"), None),
        P(("dp", "rep"), None),
        P(("dp", "rep"), None),
        P(None, ("dp", "rep")),
        P(("dp", "rep"), None),
        P(("dp", "rep"), None),
        P(("dp", "rep"), None),
        P(("dp", "rep"), None),
        P(None, ("dp", "rep")),
        P(("dp", "rep"), None),
        P(("dp", "rep"), None),
        P(("dp", "rep"), None),
        P(("dp", "rep"), None),
        P(None, ("dp", "rep")),
    )
    return jax.shard_map(
        partial(body, (Layout(mesh, False), Layout(mesh, True))),
        mesh=mesh,
        in_specs=placed,
        out_specs=(
            P(("dp", "rep"), None, None),
            P(("dp", "rep"), None, None),
            P(("dp", "rep"), None),
            P(("dp", "rep"), None),
            P(("dp", "rep"), None),
            P(("dp", "rep"), None),
            P(None, ("dp", "rep")),
            P(("dp", "rep"), None),
            P(("dp", "rep"), None),
            P(("dp", "rep"), None),
            P(("dp", "rep"), None),
            P(None, ("dp", "rep")),
            P(("dp", "rep"), None),
            P(("dp", "rep"), None),
            P(("dp", "rep"), None),
            P(("dp", "rep"), None),
            P(None, ("dp", "rep")),
            P(),
        ),
        check_vma=False,
    )
```
